32 devices in a mesh: dp: 8 (over z, y), ctx: 4 (over x, core).
Axes of the slice: x: 2, y: 2, z: 4, core: 2. Of those that a mesh axis runs over, the one named last changes fastest.
Arguments:
- tokens: bfloat16 [8, 1024, 2048], P('dp', 'ctx'), may hold values from -6 to 6
- cotangent: bfloat16 [8, 1024, 2048], P('dp', 'ctx'), may hold values from -6 to 6
- domain_ids: int32 [8], P('dp'), may hold values from 0 to 31
- domain_counts: int32 [32], replicated, may hold values from 1024 to 4096
- domain_numer: int32 [32], replicated, may hold values from 1 to 8
- domain_denom: int32 [32], replicated, may hold values from 1 to 8
- attention_gain: bfloat16 [2048], replicated, may hold values from 0.5 to 1.5
- query_gain: bfloat16 [128], replicated, may hold values from 0.796875 to 1.796875
- key_gain: bfloat16 [128], replicated, may hold values from 0.796875 to 1.796875
- query_proj: bfloat16 [2048, 2048], P('dp', 'ctx'), may hold values from -0.125 to 0.125
- key_proj: bfloat16 [2048, 1024], P('dp', 'ctx'), may hold values from -0.125 to 0.125
- value_proj: bfloat16 [2048, 1024], P('dp', 'ctx'), may hold values from -0.125 to 0.125
- gating_proj: bfloat16 [2048, 2048], P('dp', 'ctx'), may hold values from -0.125 to 0.125
- output_proj: bfloat16 [2048, 2048], P('ctx', 'dp'), may hold values from -1 to 1
- swiglu_gain: bfloat16 [2048], replicated, may hold values from 0.5 to 1.5
- swiglu_gate: bfloat16 [2048, 6144], P('dp', 'ctx'), may hold values from -0.125 to 0.125
- swiglu_up: bfloat16 [2048, 6144], P('dp', 'ctx'), may hold values from -0.125 to 0.125
- swiglu_down: bfloat16 [6144, 2048], P('ctx', 'dp'), may hold values from -0.109375 to 0.109375
Outputs:
- layer_out: bfloat16 [8, 1024, 2048], P('dp', 'ctx')
- input_grad: bfloat16 [8, 1024, 2048], P('dp', 'ctx')
- attention_gain_grad: float32 [2048], replicated
- query_gain_grad: float32 [128], replicated
- key_gain_grad: float32 [128], replicated
- query_proj_grad: float32 [2048, 2048], P('dp', 'ctx')
- key_proj_grad: float32 [2048, 1024], P('dp', 'ctx')
- value_proj_grad: float32 [2048, 1024], P('dp', 'ctx')
- gating_proj_grad: float32 [2048, 2048], P('dp', 'ctx')
- output_proj_grad: float32 [2048, 2048], P('ctx', 'dp')
- swiglu_gain_grad: float32 [2048], replicated
- swiglu_gate_grad: float32 [2048, 6144], P('dp', 'ctx')
- swiglu_up_grad: float32 [2048, 6144], P('dp', 'ctx')
- swiglu_down_grad: float32 [6144, 2048], P('ctx', 'dp')
The draws below stay inside these ranges and needn't reach their ends.
All inputs are finite; a program needn't handle non-finite values.
Results may differ from the reference program's by a relative error of at most 0.019.
Values may be sent and summed in bfloat16 or wider, within the bound.
A program may use at most 192 MiB of HBM per device.

```python
import jax
import jax.numpy as jnp
from jax import lax

D = 2048
H = 16
KVH = 8
HD = 128
FF = 6144
LENGTH = 1024
NDOM = 32
SEQS = 8


def touch_ends(values, rng, least, high):
    longest = values.shape.index(max(values.shape))
    spots = []
    for shift in (0, 1):
        where = [jax.random.randint(jax.random.fold_in(rng, axis), (), 0, length) for axis, length in enumerate(values.shape)]
        where[longest] = (where[longest] + shift) % values.shape[longest]
        spots.append(tuple(where))
    return values.at[spots[0]].set(least).at[spots[1]].set(high)


def with_spikes(values, key, source, target, blocks, factor):
    owner, partner = [(jnp.arange(values.shape[axis_at]) // (values.shape[axis_at] // blocks)).reshape([-1 if axis == axis_at else 1 for axis in range(values.ndim)]) for axis_at in (source, target)]
    chosen = jax.random.permutation(key, blocks)[partner]
    strong = (owner == chosen) | (owner == (partner + blocks // 2) % blocks)
    return jnp.where(strong, factor * values, values)


def level_of(key, extent, cuts, smallest, top_value):
    factor_of = 1.0
    for axis_at, parts in cuts:
        heights = jax.random.uniform(jax.random.fold_in(jax.random.fold_in(key, 6), axis_at), (parts,), jnp.float32, smallest / len(cuts), top_value / len(cuts))
        factor_of = factor_of * jnp.repeat(jnp.exp(heights), extent[axis_at] // parts).reshape((-1,) + (1,) * (len(extent) - 1 - axis_at))
    return factor_of


def normal_values(stream_key, dims, scale, bound, cuts=(), kind=jnp.bfloat16):
    entries = jax.random.normal(stream_key, dims, jnp.float32) * scale
    if len(cuts) > 0:
        entries = level_of(stream_key, dims, cuts, -0.22, 0.18) * entries
    return jnp.clip(entries, min=-bound, max=bound).astype(kind)


def noise_with(key, extent, spread, bound, pieces, heavy, kind=jnp.bfloat16):
    values = spread * jax.random.normal(key, extent, jnp.float32)
    if pieces:
        values = values * level_of(key, extent, pieces, -0.22, 0.18)
    return jnp.clip(with_spikes(values, jax.random.fold_in(key, 3), *heavy), -bound, bound).astype(kind)


def setup_inputs(seed: int = 0) -> dict:
    arg_keys = jax.random.split(jax.random.key(seed), 19)
    return {
        "tokens": noise_with(arg_keys[0], (SEQS, LENGTH, D), 1.0, 6.0, ((0, 8), (1, 4)), (0, 2, 8, 2.0)),
        "cotangent": normal_values(arg_keys[1], (SEQS, LENGTH, D), 1.0, 6.0, ((0, 8), (1, 4))),
        "domain_ids": touch_ends(jax.random.randint(arg_keys[2], (SEQS,), 0, NDOM), jax.random.fold_in(arg_keys[2], 1), 0, NDOM - 1).astype(jnp.int32),
        "domain_counts": touch_ends(jax.random.randint(arg_keys[3], (NDOM,), LENGTH, 4 * LENGTH + 1), jax.random.fold_in(arg_keys[3], 1), LENGTH, 4 * LENGTH).astype(jnp.int32),
        "domain_numer": touch_ends(jax.random.randint(arg_keys[4], (NDOM,), 1, 9), jax.random.fold_in(arg_keys[4], 1), 1, 8).astype(jnp.int32),
        "domain_denom": touch_ends(jax.random.randint(arg_keys[5], (NDOM,), 1, 9), jax.random.fold_in(arg_keys[5], 1), 1, 8).astype(jnp.int32),
        "attention_gain": jnp.clip(1.0 + 0.1 * jax.random.normal(arg_keys[6], (D,), jnp.float32), 0.5, 1.5).astype(jnp.bfloat16),
        "query_gain": jnp.clip(jax.random.uniform(arg_keys[7], (HD,), jnp.float32, 0.796875, 1.796875), 0.796875, 1.796875).astype(jnp.bfloat16),
        "key_gain": jnp.clip(jax.random.uniform(arg_keys[8], (HD,), jnp.float32, 0.796875, 1.796875), 0.796875, 1.796875).astype(jnp.bfloat16),
        "query_proj": normal_values(arg_keys[9], (D, H * HD), D ** -0.5, 0.125, ((0, 8), (1, 4))),
        "key_proj": normal_values(arg_keys[10], (D, KVH * HD), D ** -0.5, 0.125, ((0, 8), (1, 4))),
        "value_proj": normal_values(arg_keys[11], (D, KVH * HD), D ** -0.5, 0.125, ((0, 8), (1, 4))),
        "gating_proj": normal_values(arg_keys[12], (D, H * HD), D ** -0.5, 0.125, ((0, 8), (1, 4))),
        "output_proj": normal_values(arg_keys[13], (H * HD, D), (max(1, H * HD // 64)) ** -0.5, 1.0, ((0, 4), (1, 8))),
        "swiglu_gain": jnp.clip(1.0 + 0.1 * jax.random.normal(arg_keys[14], (D,), jnp.float32), 0.5, 1.5).astype(jnp.bfloat16),
        "swiglu_gate": normal_values(arg_keys[15], (D, FF), D ** -0.5, 0.125, ((0, 8), (1, 4))),
        "swiglu_up": normal_values(arg_keys[16], (D, FF), D ** -0.5, 0.125, ((0, 8), (1, 4))),
        "swiglu_down": normal_values(arg_keys[17], (FF, D), (FF // 2) ** -0.5, 0.109375, ((0, 4), (1, 8))),
    }


@jax.custom_vjp
def low(v):
    return lax.optimization_barrier(v.astype(jnp.bfloat16)).astype(jnp.float32)

@jax.custom_vjp
def low_back(v):
    return v

def low_keep(v):
    return (low(v), None)

def low_pass(kept, grad):
    return (grad,)

def back_keep(v):
    return (v, None)

def back_low(kept, grad):
    return (low(grad),)
low.defvjp(low_keep, low_pass)
low_back.defvjp(back_keep, back_low)
EPSILON = 1e-06
ROPE_BASE = 1000000.0
HIGHEST = lax.Precision.HIGHEST

def matmul_high(left, right):
    return jnp.dot(left, right, precision=HIGHEST, preferred_element_type=jnp.float32)

def rope_tables(positions, head_width):
    halfway = head_width // 2
    inverse = 1.0 / ROPE_BASE ** (jnp.arange(halfway, dtype=jnp.float32) * (2.0 / head_width))
    angles = positions.astype(jnp.float32)[:, None] * inverse[None, :]
    return (jnp.cos(angles), jnp.sin(angles))

def rotate(tensor, cosine, sine):
    halfway = tensor.shape[-1] // 2
    first_half = tensor[..., :halfway]
    second_half = tensor[..., halfway:]
    return jnp.concatenate([first_half * cosine - second_half * sine, second_half * cosine + first_half * sine], -1)

def head_norm(tensor, gain_vec):
    return tensor * lax.rsqrt(lax.optimization_barrier(jnp.mean(tensor * tensor, -1, keepdims=True)) + EPSILON) * gain_vec

def attend_sequence(queries, keys_seq, values_seq, causal):
    scaling = queries.shape[-1] ** (-0.5)
    scores = jnp.einsum('qgjd,kgd->gjqk', queries, keys_seq, precision=HIGHEST) * scaling
    scores = low_back(scores)
    scores = jnp.where(causal, scores, -1e+30)
    highest = lax.optimization_barrier(jnp.max(scores, -1, keepdims=True))
    exp_vals = jnp.exp(scores - highest)
    attn_probs = low(exp_vals / lax.optimization_barrier(jnp.sum(exp_vals, -1, keepdims=True)))
    return jnp.einsum('gjqk,kgd->qgjd', attn_probs, values_seq, precision=HIGHEST)

def layer(inputs, params, cosine, sine, causal):
    attention_gain, query_gain, key_gain, query_proj, key_proj, value_proj, gating_proj, output_proj, swiglu_gain, swiglu_gate, swiglu_up, swiglu_down = params
    seq_count = inputs.shape[0]
    seq_len = inputs.shape[1]
    flat_rows = inputs.reshape(seq_count * seq_len, D)
    inverse_in = lax.rsqrt(lax.optimization_barrier(jnp.mean(flat_rows * flat_rows, -1, keepdims=True)) + EPSILON)
    normed = low(flat_rows * inverse_in * attention_gain)
    queries = low_back(matmul_high(normed, query_proj)).reshape(seq_count, seq_len, H, HD)
    keys_all = low_back(matmul_high(normed, key_proj)).reshape(seq_count, seq_len, KVH, HD)
    values_all = low(low_back(matmul_high(normed, value_proj))).reshape(seq_count, seq_len, KVH, HD)
    gate_pre = low_back(matmul_high(normed, gating_proj))
    cos_rows = cosine[:, None, :]
    sin_rows = sine[:, None, :]
    queries = low(rotate(head_norm(queries, query_gain), cos_rows, sin_rows))
    queries = queries.reshape(seq_count, seq_len, KVH, H // KVH, HD)
    keys_all = low(rotate(head_norm(keys_all, key_gain), cos_rows, sin_rows))
    attend_block = jax.checkpoint(lambda seq_items: attend_sequence(seq_items[0], seq_items[1], seq_items[2], causal))
    attended = lax.map(attend_block, (queries, keys_all, values_all))
    attended = low_back(attended.reshape(seq_count * seq_len, H * HD))
    mixed = low(attended * jax.nn.sigmoid(gate_pre))
    branch = low_back(matmul_high(mixed, output_proj))
    hidden = flat_rows + branch
    inverse_mid = lax.rsqrt(lax.optimization_barrier(jnp.mean(hidden * hidden, -1, keepdims=True)) + EPSILON)
    normed_mid = low(hidden * inverse_mid * swiglu_gain)
    gate_ff = low_back(matmul_high(normed_mid, swiglu_gate))
    up_val = low_back(matmul_high(normed_mid, swiglu_up))
    activation = low(gate_ff * jax.nn.sigmoid(gate_ff) * up_val)
    outcome = low_back(matmul_high(activation, swiglu_down))
    return (hidden + outcome).reshape(seq_count, seq_len, D)

def reference(tokens, cotangent, domain_ids, domain_counts, domain_numer, domain_denom, attention_gain, query_gain, key_gain, query_proj, key_proj, value_proj, gating_proj, output_proj, swiglu_gain, swiglu_gate, swiglu_up, swiglu_down):
    ratio = domain_numer.astype(jnp.float32) / domain_denom.astype(jnp.float32) * LENGTH / domain_counts.astype(jnp.float32)
    factor = ratio[domain_ids]
    params = tuple((weight_array.astype(jnp.float32) for weight_array in (attention_gain, query_gain, key_gain, query_proj, key_proj, value_proj, gating_proj, output_proj, swiglu_gain, swiglu_gate, swiglu_up, swiglu_down)))
    positions = jnp.arange(LENGTH, dtype=jnp.int32)
    cosine, sine = rope_tables(positions, HD)
    causal = positions[:, None] >= positions[None, :]
    grouped = max(1, min(SEQS, 4096 // LENGTH))
    while SEQS % grouped != 0:
        grouped = grouped - 1
    inputs = tokens.astype(jnp.float32).reshape(SEQS // grouped, grouped, LENGTH, D)
    weighted = (cotangent.astype(jnp.float32) * factor[:, None, None]).reshape(SEQS // grouped, grouped, LENGTH, D)

    def scan_step(running, pair):

        def forward(inputs_part, params_part):
            return layer(inputs_part, params_part, cosine, sine, causal)
        result, pullback = jax.vjp(forward, pair[0], params)
        grad_input, grad_params = pullback(pair[1])
        running = tuple((sofar + addend for sofar, addend in zip(running, grad_params)))
        return (running, (result.astype(jnp.bfloat16), grad_input.astype(jnp.bfloat16)))
    zero_grads = tuple((jnp.zeros_like(weight_array) for weight_array in params))
    grads, (outputs, input_grads) = lax.scan(scan_step, zero_grads, (inputs, weighted))
    layer_out = outputs.reshape(SEQS, LENGTH, D)
    input_grad = input_grads.reshape(SEQS, LENGTH, D)
    return (layer_out, input_grad, grads[0], grads[1], grads[2], grads[3], grads[4], grads[5], grads[6], grads[7], grads[8], grads[9], grads[10], grads[11])
```

```python
import functools

import jax
import jax.numpy as jnp
from jax import lax
from jax.experimental import pallas as pl
from jax.experimental.pallas import tpu as pltpu
from jax.sharding import Mesh
from jax.sharding import PartitionSpec as P

LENGTH = 1024

EPSILON = 1e-06
ROPE_BASE = 1000000.0
MESH = pl.DeviceIdType.MESH
BF16 = jnp.bfloat16
F32 = jnp.float32


def dot_nn(left, right):
    return jnp.dot(left, right, preferred_element_type=F32)


def dot_tn(left, right):
    return lax.dot_general(left, right, (((0,), (0,)), ((), ())), preferred_element_type=F32)


def dot_nt(left, right):
    return lax.dot_general(left, right, (((1,), (1,)), ((), ())), preferred_element_type=F32)


def rope_tables(positions, head_width):
    halfway = head_width // 2
    inverse = 1.0 / ROPE_BASE ** (jnp.arange(halfway, dtype=F32) * (2.0 / head_width))
    angles = positions.astype(F32)[:, None] * inverse[None, :]
    return (jnp.cos(angles), jnp.sin(angles))


def rotate(tensor, cosine, sine):
    halfway = tensor.shape[-1] // 2
    first_half = tensor[..., :halfway]
    second_half = tensor[..., halfway:]
    return jnp.concatenate(
        [first_half * cosine - second_half * sine, second_half * cosine + first_half * sine], -1
    )


def unrotate(grads_in, cosine, sine):
    halfway = grads_in.shape[-1] // 2
    first_half = grads_in[..., :halfway]
    second_half = grads_in[..., halfway:]
    return jnp.concatenate(
        [first_half * cosine + second_half * sine, second_half * cosine - first_half * sine], -1
    )


def norm_back(grads_in, values_in, inverse, gain_vec):
    scaled = grads_in * gain_vec
    return inverse * scaled - values_in * (inverse * inverse * inverse) * jnp.mean(
        scaled * values_in, -1, keepdims=True
    )


def greet(neighbours):
    barrier = pltpu.get_barrier_semaphore()
    for neighbour in neighbours:
        pl.semaphore_signal(barrier, inc=1, device_id=neighbour, device_id_type=MESH)
    pl.semaphore_wait(barrier, len(neighbours))


def gather_kernel(rows, s_ref, out_ref, local_sem, send, recv):
    y, x, c = lax.axis_index("y"), lax.axis_index("x"), lax.axis_index("c")
    to_y, to_x, to_c = {"y": 1 - y}, {"x": 1 - x}, {"c": 1 - c}
    greet((to_y, to_x, to_c))
    half = rows // 2
    low, high = pl.ds(0, half), pl.ds(half, half)

    def remote(index, source, target, device):
        return pltpu.make_async_remote_copy(
            src_ref=source,
            dst_ref=target,
            send_sem=send.at[index],
            recv_sem=recv.at[index],
            device_id=device,
            device_id_type=MESH,
        )

    mine = out_ref.at[y, x, c]
    from_x = out_ref.at[y, 1 - x, c]
    from_y = out_ref.at[1 - y, x, c]
    diagonal = out_ref.at[1 - y, 1 - x, c]
    x_low = remote(0, s_ref.at[low], mine.at[low], to_x)
    y_high = remote(1, s_ref.at[high], mine.at[high], to_y)
    x_high = remote(2, s_ref.at[high], mine.at[high], to_x)
    y_low = remote(3, s_ref.at[low], mine.at[low], to_y)
    c_own = remote(4, s_ref, mine, to_c)
    local = pltpu.make_async_copy(s_ref, mine, local_sem)
    for copy in (x_low, y_high, x_high, y_low, c_own, local):
        copy.start()
    x_low.wait_recv()
    forward_y = remote(5, from_x.at[low], from_x.at[low], to_y)
    forward_y.start()
    y_high.wait_recv()
    forward_x = remote(6, from_y.at[high], from_y.at[high], to_x)
    forward_x.start()
    x_high.wait_recv()
    c_x = remote(7, from_x, from_x, to_c)
    c_x.start()
    y_low.wait_recv()
    c_y = remote(8, from_y, from_y, to_c)
    c_y.start()
    forward_y.wait_recv()
    c_low = remote(9, diagonal.at[low], diagonal.at[low], to_c)
    c_low.start()
    forward_x.wait_recv()
    c_high = remote(10, diagonal.at[high], diagonal.at[high], to_c)
    c_high.start()
    for copy in (c_own, c_x, c_y, c_low, c_high):
        copy.wait()
    for copy in (x_low, y_high, x_high, y_low, forward_y, forward_x):
        copy.wait_send()
    local.wait()


def gather_tokens(shard):
    rows, width = shard.shape
    return pl.pallas_call(
        functools.partial(gather_kernel, rows),
        out_shape=jax.ShapeDtypeStruct((2, 2, 2, rows, width), shard.dtype),
        in_specs=[pl.BlockSpec(memory_space=pltpu.VMEM)],
        out_specs=pl.BlockSpec(memory_space=pl.ANY),
        scratch_shapes=[
            pltpu.SemaphoreType.DMA,
            pltpu.SemaphoreType.DMA((11,)),
            pltpu.SemaphoreType.DMA((11,)),
        ],
        compiler_params=pltpu.CompilerParams(collective_id=0, has_side_effects=True),
        name="gather_tokens",
    )(shard).reshape(8 * rows, width)


def scatter_kernel(rows, parts_ref, out_ref, own, got, x_diag, y_diag, x_got, y_got, load_sem, send, recv):
    y, x, c = lax.axis_index("y"), lax.axis_index("x"), lax.axis_index("c")
    to_y, to_x, to_c = {"y": 1 - y}, {"x": 1 - x}, {"c": 1 - c}
    half = rows // 2
    low, high = pl.ds(0, half), pl.ds(half, half)
    targets = ((1 - y, 1 - x), (1 - y, x), (y, 1 - x), (y, x))
    loads = [
        pltpu.make_async_copy(parts_ref.at[a, b, c], own.at[i], load_sem.at[i])
        for i, (a, b) in enumerate(targets)
    ]
    for load in loads:
        load.start()
    greet((to_y, to_x, to_c))

    def remote(index, source, target, device):
        return pltpu.make_async_remote_copy(
            src_ref=source,
            dst_ref=target,
            send_sem=send.at[index],
            recv_sem=recv.at[index],
            device_id=device,
            device_id_type=MESH,
        )

    crossing = [
        remote(i, parts_ref.at[a, b, 1 - c], got.at[i], to_c) for i, (a, b) in enumerate(targets)
    ]
    for copy in crossing:
        copy.start()
    step = 64

    def add_into(target, start, count, *others):
        @pl.loop(0, count // step)
        def _(i):
            at = pl.ds(start + i * step, step)
            total = target[at].astype(F32)
            for other, base in others:
                total = total + other[pl.ds(base + i * step, step)].astype(F32)
            target[at] = total.astype(target.dtype)

    def cores(i):
        loads[i].wait()
        crossing[i].wait_recv()
        add_into(own.at[i], 0, rows, (got.at[i], 0))

    cores(0)
    diag_x = remote(4, own.at[0, low], x_diag, to_x)
    diag_y = remote(5, own.at[0, high], y_diag, to_y)
    diag_x.start()
    diag_y.start()
    cores(1)
    y_high = remote(6, own.at[1, high], y_got.at[high], to_y)
    y_high.start()
    cores(2)
    x_low = remote(7, own.at[2, low], x_got.at[low], to_x)
    x_low.start()
    cores(3)
    diag_x.wait_recv()
    add_into(own.at[1], 0, half, (x_diag, 0))
    y_low = remote(8, own.at[1, low], y_got.at[low], to_y)
    y_low.start()
    diag_y.wait_recv()
    add_into(own.at[2], half, half, (y_diag, 0))
    x_high = remote(9, own.at[2, high], x_got.at[high], to_x)
    x_high.start()
    y_high.wait_recv()
    x_low.wait_recv()
    y_low.wait_recv()
    x_high.wait_recv()

    @pl.loop(0, rows // step)
    def _(i):
        at = pl.ds(i * step, step)
        out_ref[at] = own[3, at].astype(F32) + x_got[at].astype(F32) + y_got[at].astype(F32)

    for copy in (*crossing, diag_x, diag_y, y_high, x_low, y_low, x_high):
        copy.wait_send()


def scatter_tokens(parts):
    rows, width = parts.shape[0] // 8, parts.shape[1]
    return pl.pallas_call(
        functools.partial(scatter_kernel, rows),
        out_shape=jax.ShapeDtypeStruct((rows, width), F32),
        in_specs=[pl.BlockSpec(memory_space=pl.ANY)],
        out_specs=pl.BlockSpec(memory_space=pltpu.VMEM),
        scratch_shapes=[
            pltpu.VMEM((4, rows, width), parts.dtype),
            pltpu.VMEM((4, rows, width), parts.dtype),
            pltpu.VMEM((rows // 2, width), parts.dtype),
            pltpu.VMEM((rows // 2, width), parts.dtype),
            pltpu.VMEM((rows, width), parts.dtype),
            pltpu.VMEM((rows, width), parts.dtype),
            pltpu.SemaphoreType.DMA((4,)),
            pltpu.SemaphoreType.DMA((10,)),
            pltpu.SemaphoreType.DMA((10,)),
        ],
        compiler_params=pltpu.CompilerParams(collective_id=1, has_side_effects=True),
        name="scatter_tokens",
    )(parts.reshape(2, 2, 2, rows, width))


def swap_y(value):
    return lax.ppermute(value, "y", [(0, 1), (1, 0)])


def in_y_order(mine, theirs, axis):
    first = lax.axis_index("y") == 0
    return jnp.where(
        first, jnp.concatenate([mine, theirs], axis), jnp.concatenate([theirs, mine], axis)
    )


def column_half(weight, which):
    half = weight.shape[1] // 2
    return lax.dynamic_slice_in_dim(weight, which * half, half, 1)


def pack_half(weights, which):
    return jnp.concatenate([column_half(weight, which) for weight in weights], 1)


def gather_weights(weights):
    y = lax.axis_index("y")
    mine, theirs = pack_half(weights, y), pack_half(weights, 1 - y)
    rows = in_y_order(mine, swap_y(theirs), 0)
    return lax.all_gather(rows, "z", axis=0, tiled=True)


def scatter_grads(grad):
    return lax.psum_scatter(grad.astype(BF16), "z", scatter_dimension=0, tiled=True)


def finish_grads(part, widths):
    y = lax.axis_index("y")
    half = part.shape[0] // 2
    mine = lax.dynamic_slice_in_dim(part, y * half, half, 0)
    theirs = swap_y(lax.dynamic_slice_in_dim(part, (1 - y) * half, half, 0))
    outs, start = [], 0
    for width in widths:
        piece = slice(start, start + width)
        outs.append(in_y_order(mine[:, piece], theirs[:, piece], 1).astype(F32))
        start += width
    return outs


def softmax_forward(queries, keys_seq, values_seq, causal):
    scaling = queries.shape[-1] ** (-0.5)
    scores = jnp.einsum("sqjd,skd->sjqk", queries, keys_seq, preferred_element_type=F32) * scaling
    scores = jnp.where(causal, scores, -1e30)
    highest = jnp.max(scores, -1, keepdims=True)
    exp_vals = jnp.exp(scores - highest)
    row_totals = jnp.sum(exp_vals, -1, keepdims=True)
    attn_probs = (exp_vals / row_totals).astype(BF16)
    attended = jnp.einsum("sjqk,skd->sqjd", attn_probs, values_seq, preferred_element_type=F32)
    return (attended, highest[..., 0] + jnp.log(row_totals[..., 0]))


def softmax_backward(queries, keys_seq, values_seq, log_total, upstream, causal):
    scaling = queries.shape[-1] ** (-0.5)
    scores = jnp.einsum("sqjd,skd->sjqk", queries, keys_seq, preferred_element_type=F32) * scaling
    scores = jnp.where(causal, scores, -1e30)
    attn_probs = jnp.exp(scores - log_total[..., None])
    dprobs = jnp.einsum("sqjd,skd->sjqk", upstream, values_seq, preferred_element_type=F32)
    centre = jnp.sum(dprobs * attn_probs, -1, keepdims=True)
    dscores = (attn_probs * (dprobs - centre)).astype(BF16)
    dqueries = (
        jnp.einsum("sjqk,skd->sqjd", dscores, keys_seq, preferred_element_type=F32) * scaling
    )
    key_grads = (
        jnp.einsum("sjqk,sqjd->skd", dscores, queries, preferred_element_type=F32) * scaling
    )
    value_grads = jnp.einsum(
        "sjqk,sqjd->skd", attn_probs.astype(BF16), upstream, preferred_element_type=F32
    )
    return (dqueries, key_grads, value_grads)


def attention_weights(query_proj, key_proj, value_proj, gating_proj, output_proj):
    return (
        lax.all_gather(query_proj, "dp", axis=0, tiled=True),
        lax.all_gather(key_proj, "dp", axis=0, tiled=True),
        lax.all_gather(value_proj, "dp", axis=0, tiled=True),
        lax.all_gather(gating_proj, "dp", axis=0, tiled=True),
        lax.all_gather(output_proj, "dp", axis=1, tiled=True),
    )


def swiglu_weights(swiglu_gate, swiglu_up, swiglu_down):
    return (
        lax.all_gather(swiglu_gate, "dp", axis=0, tiled=True),
        lax.all_gather(swiglu_up, "dp", axis=0, tiled=True),
        lax.all_gather(swiglu_down, "dp", axis=1, tiled=True),
    )


def softmax_forward_mapped(seq_items, causal):
    queries, keys_seq, values_seq = seq_items
    scaling = queries.shape[-1] ** (-0.5)
    scores = (
        jnp.einsum("qgjd,kgd->gjqk", queries, keys_seq, preferred_element_type=jnp.float32)
        * scaling
    )
    scores = jnp.where(causal, scores, -1e30)
    highest = jnp.max(scores, -1, keepdims=True)
    exp_vals = jnp.exp(scores - highest)
    row_totals = jnp.sum(exp_vals, -1, keepdims=True)
    attn_probs = (exp_vals / row_totals).astype(jnp.bfloat16)
    attended = jnp.einsum(
        "gjqk,kgd->qgjd", attn_probs, values_seq, preferred_element_type=jnp.float32
    )
    return (attended, highest[..., 0] + jnp.log(row_totals[..., 0]))


def softmax_backward_mapped(seq_items, causal):
    queries, keys_seq, values_seq, log_total, upstream = seq_items
    scaling = queries.shape[-1] ** (-0.5)
    scores = (
        jnp.einsum("qgjd,kgd->gjqk", queries, keys_seq, preferred_element_type=jnp.float32)
        * scaling
    )
    scores = jnp.where(causal, scores, -1e30)
    attn_probs = jnp.exp(scores - log_total[..., None])
    dprobs = jnp.einsum("qgjd,kgd->gjqk", upstream, values_seq, preferred_element_type=jnp.float32)
    centre = jnp.sum(dprobs * attn_probs, -1, keepdims=True)
    dscores = (attn_probs * (dprobs - centre)).astype(jnp.bfloat16)
    dqueries = (
        jnp.einsum("gjqk,kgd->qgjd", dscores, keys_seq, preferred_element_type=jnp.float32)
        * scaling
    )
    key_grads = (
        jnp.einsum("gjqk,qgjd->kgd", dscores, queries, preferred_element_type=jnp.float32) * scaling
    )
    value_grads = jnp.einsum(
        "gjqk,qgjd->kgd",
        attn_probs.astype(jnp.bfloat16),
        upstream,
        preferred_element_type=jnp.float32,
    )
    key_rows = key_grads.shape[0]
    return (dqueries, key_grads.reshape(key_rows, -1), value_grads.reshape(key_rows, -1))


def per_device_wide(
    tokens,
    cotangent,
    domain_ids,
    domain_counts,
    domain_numer,
    domain_denom,
    attention_gain,
    query_gain,
    key_gain,
    query_proj,
    key_proj,
    value_proj,
    gating_proj,
    output_proj,
    swiglu_gain,
    swiglu_gate,
    swiglu_up,
    swiglu_down,
):
    seq_count, local_len, model_width = tokens.shape
    full_len = local_len * lax.axis_size("ctx")
    local_rows = seq_count * local_len
    all_rows = seq_count * full_len
    head_dim = query_gain.shape[0]
    local_heads = query_proj.shape[1] // head_dim
    local_kv = key_proj.shape[1] // head_dim
    group_size = local_heads // local_kv
    positions = jnp.arange(full_len, dtype=jnp.int32)
    causal = positions[:, None] >= positions[None, :]
    cosine, sine = rope_tables(positions, head_dim)
    cos_rows = cosine[:, None, :]
    sin_rows = sine[:, None, :]
    inputs = tokens.reshape(local_rows, model_width).astype(jnp.float32)
    inverse_in = lax.rsqrt(jnp.mean(inputs * inputs, -1, keepdims=True) + EPSILON)
    gain_in = attention_gain.astype(jnp.float32)
    normed = (inputs * inverse_in * gain_in).astype(jnp.bfloat16)
    normed_all = lax.all_gather(
        normed.reshape(seq_count, local_len, model_width), "ctx", axis=1, tiled=True
    ).reshape(all_rows, model_width)
    attn_full = attention_weights(query_proj, key_proj, value_proj, gating_proj, output_proj)
    query_raw = dot_nn(normed_all, attn_full[0]).reshape(
        seq_count, full_len, local_heads, head_dim
    )
    key_raw = dot_nn(normed_all, attn_full[1]).reshape(seq_count, full_len, local_kv, head_dim)
    value_low = (
        dot_nn(normed_all, attn_full[2])
        .astype(jnp.bfloat16)
        .reshape(seq_count, full_len, local_kv, head_dim)
    )
    gate_pre = dot_nn(normed_all, attn_full[3])
    query_scale = query_gain.astype(jnp.float32)
    key_scale = key_gain.astype(jnp.float32)
    query_inv = lax.rsqrt(jnp.mean(query_raw * query_raw, -1, keepdims=True) + EPSILON)
    key_inv = lax.rsqrt(jnp.mean(key_raw * key_raw, -1, keepdims=True) + EPSILON)
    query_low = rotate(query_raw * query_inv * query_scale, cos_rows, sin_rows).astype(jnp.bfloat16)
    key_low = rotate(key_raw * key_inv * key_scale, cos_rows, sin_rows).astype(jnp.bfloat16)
    query_groups = query_low.reshape(seq_count, full_len, local_kv, group_size, head_dim)
    attended, log_total = lax.map(
        lambda seq_items: softmax_forward_mapped(seq_items, causal), (query_groups, key_low, value_low)
    )
    attended = attended.reshape(all_rows, local_heads * head_dim)
    gate_sig = jax.nn.sigmoid(gate_pre)
    mixed = (attended * gate_sig).astype(jnp.bfloat16)
    branch_part = dot_nn(mixed, attn_full[4]).reshape(seq_count, full_len, model_width)
    branch = lax.psum_scatter(branch_part, "ctx", scatter_dimension=1, tiled=True).reshape(
        local_rows, model_width
    )
    hidden = inputs + branch
    inverse_mid = lax.rsqrt(jnp.mean(hidden * hidden, -1, keepdims=True) + EPSILON)
    gain_mid = swiglu_gain.astype(jnp.float32)
    normed_mid = (hidden * inverse_mid * gain_mid).astype(jnp.bfloat16)
    normed_mid_all = lax.all_gather(
        normed_mid.reshape(seq_count, local_len, model_width), "ctx", axis=1, tiled=True
    ).reshape(all_rows, model_width)
    swiglu_full = swiglu_weights(swiglu_gate, swiglu_up, swiglu_down)
    gate_ff = dot_nn(normed_mid_all, swiglu_full[0])
    up_val = dot_nn(normed_mid_all, swiglu_full[1])
    gate_sigma = jax.nn.sigmoid(gate_ff)
    silu_val = gate_ff * gate_sigma
    activation = (silu_val * up_val).astype(jnp.bfloat16)
    down_part = dot_nn(activation, swiglu_full[2]).reshape(seq_count, full_len, model_width)
    ffn_branch = (
        lax.psum_scatter(down_part.astype(jnp.bfloat16), "ctx", scatter_dimension=1, tiled=True)
        .astype(jnp.float32)
        .reshape(local_rows, model_width)
    )
    layer_out = (hidden + ffn_branch).astype(jnp.bfloat16)
    domain_table = (
        domain_ids[:, None] == jnp.arange(domain_counts.shape[0], dtype=jnp.int32)[None, :]
    ).astype(jnp.float32)
    ratio = (
        domain_numer.astype(jnp.float32)
        / domain_denom.astype(jnp.float32)
        * LENGTH
        / domain_counts.astype(jnp.float32)
    )
    factor = jnp.sum(domain_table * ratio[None, :], 1)
    upstream = (cotangent.astype(jnp.float32) * factor[:, None, None]).reshape(
        local_rows, model_width
    )
    swiglu_back = swiglu_weights(swiglu_gate, swiglu_up, swiglu_down)
    out_low = upstream.astype(jnp.bfloat16)
    out_all = lax.all_gather(
        out_low.reshape(seq_count, local_len, model_width), "ctx", axis=1, tiled=True
    ).reshape(all_rows, model_width)
    dactivation = dot_nt(out_all, swiglu_back[2])
    dgate_low = (dactivation * up_val * gate_sigma * (1.0 + gate_ff * (1.0 - gate_sigma))).astype(
        jnp.bfloat16
    )
    dup_low = (dactivation * silu_val).astype(jnp.bfloat16)
    grad_down = dot_tn(activation, out_all)
    grad_gate = dot_tn(normed_mid_all, dgate_low)
    grad_up = dot_tn(normed_mid_all, dup_low)
    dmid_part = dot_nt(dgate_low, swiglu_back[0]) + dot_nt(dup_low, swiglu_back[1])
    dnormed_mid = lax.psum_scatter(
        dmid_part.reshape(seq_count, full_len, model_width), "ctx", scatter_dimension=1, tiled=True
    ).reshape(local_rows, model_width)
    grad_gain_mid = jnp.sum(dnormed_mid * hidden * inverse_mid, 0)
    dhidden = upstream + norm_back(dnormed_mid, hidden, inverse_mid, gain_mid)
    swiglu_grads = (
        lax.psum_scatter(
            grad_gate.astype(jnp.bfloat16), "dp", scatter_dimension=0, tiled=True
        ).astype(jnp.float32),
        lax.psum_scatter(
            grad_up.astype(jnp.bfloat16), "dp", scatter_dimension=0, tiled=True
        ).astype(jnp.float32),
        lax.psum_scatter(
            grad_down.astype(jnp.bfloat16), "dp", scatter_dimension=1, tiled=True
        ).astype(jnp.float32),
    )
    attn_back = attention_weights(query_proj, key_proj, value_proj, gating_proj, output_proj)
    dbranch_low = dhidden.astype(jnp.bfloat16)
    dbranch_all = lax.all_gather(
        dbranch_low.reshape(seq_count, local_len, model_width), "ctx", axis=1, tiled=True
    ).reshape(all_rows, model_width)
    grad_output = dot_tn(mixed, dbranch_all)
    dmixed = dot_nt(dbranch_all, attn_back[4])
    dattended_low = (dmixed * gate_sig).astype(jnp.bfloat16)
    dgating_low = (dmixed * attended * gate_sig * (1.0 - gate_sig)).astype(jnp.bfloat16)
    upstream_heads = dattended_low.reshape(seq_count, full_len, local_kv, group_size, head_dim)
    dquery_rot, dkey_rot, dvalue_sum = lax.map(
        lambda seq_items: softmax_backward_mapped(seq_items, causal),
        (query_groups, key_low, value_low, log_total, upstream_heads),
    )
    dvalue_low = dvalue_sum.reshape(all_rows, local_kv * head_dim).astype(jnp.bfloat16)
    dquery_normed = unrotate(
        dquery_rot.reshape(seq_count, full_len, local_heads, head_dim), cos_rows, sin_rows
    )
    dkey_normed = unrotate(
        dkey_rot.reshape(seq_count, full_len, local_kv, head_dim), cos_rows, sin_rows
    )
    grad_query_gain = jnp.sum(dquery_normed * query_raw * query_inv, (0, 1, 2))
    grad_key_gain = jnp.sum(dkey_normed * key_raw * key_inv, (0, 1, 2))
    dquery_low = (
        norm_back(dquery_normed, query_raw, query_inv, query_scale)
        .reshape(all_rows, -1)
        .astype(jnp.bfloat16)
    )
    dkey_low = (
        norm_back(dkey_normed, key_raw, key_inv, key_scale)
        .reshape(all_rows, -1)
        .astype(jnp.bfloat16)
    )
    dnormed_part = (
        dot_nt(dquery_low, attn_back[0])
        + dot_nt(dkey_low, attn_back[1])
        + dot_nt(dvalue_low, attn_back[2])
        + dot_nt(dgating_low, attn_back[3])
    )
    dnormed = (
        lax.psum_scatter(
            dnormed_part.reshape(seq_count, full_len, model_width).astype(jnp.bfloat16),
            "ctx",
            scatter_dimension=1,
            tiled=True,
        )
        .astype(jnp.float32)
        .reshape(local_rows, model_width)
    )
    grad_gain_in = jnp.sum(dnormed * inputs * inverse_in, 0)
    input_grad = (dhidden + norm_back(dnormed, inputs, inverse_in, gain_in)).astype(jnp.bfloat16)
    grad_query = dot_tn(normed_all, dquery_low)
    grad_key = dot_tn(normed_all, dkey_low)
    grad_value = dot_tn(normed_all, dvalue_low)
    grad_gating = dot_tn(normed_all, dgating_low)
    attention_grads = (
        lax.psum_scatter(
            grad_query.astype(jnp.bfloat16), "dp", scatter_dimension=0, tiled=True
        ).astype(jnp.float32),
        lax.psum_scatter(
            grad_key.astype(jnp.bfloat16), "dp", scatter_dimension=0, tiled=True
        ).astype(jnp.float32),
        lax.psum_scatter(
            grad_value.astype(jnp.bfloat16), "dp", scatter_dimension=0, tiled=True
        ).astype(jnp.float32),
        lax.psum_scatter(
            grad_gating.astype(jnp.bfloat16), "dp", scatter_dimension=0, tiled=True
        ).astype(jnp.float32),
        lax.psum_scatter(
            grad_output.astype(jnp.bfloat16), "dp", scatter_dimension=1, tiled=True
        ).astype(jnp.float32),
    )
    gain_grads = lax.psum(
        (grad_gain_in, grad_gain_mid, grad_query_gain, grad_key_gain), ("dp", "ctx")
    )
    return (
        layer_out.reshape(seq_count, local_len, model_width),
        input_grad.reshape(seq_count, local_len, model_width),
        gain_grads[0],
        gain_grads[2],
        gain_grads[3],
        attention_grads[0],
        attention_grads[1],
        attention_grads[2],
        attention_grads[3],
        attention_grads[4],
        gain_grads[1],
        swiglu_grads[0],
        swiglu_grads[1],
        swiglu_grads[2],
    )


def per_device(
    tokens,
    cotangent,
    domain_ids,
    domain_counts,
    domain_numer,
    domain_denom,
    attention_gain,
    query_gain,
    key_gain,
    query_proj,
    key_proj,
    value_proj,
    gating_proj,
    output_proj,
    swiglu_gain,
    swiglu_gate,
    swiglu_up,
    swiglu_down,
):
    seq_count, local_len, width = tokens.shape
    rows = seq_count * local_len
    full_len = local_len * lax.axis_size("x") * lax.axis_size("c")
    seqs = seq_count * lax.axis_size("y")
    head = query_gain.shape[0]
    kv_cols = key_proj.shape[1] // 2
    q_cols = query_proj.shape[1] // 2
    ff_cols = swiglu_gate.shape[1] // 2
    heads = q_cols // head
    positions = jnp.arange(full_len, dtype=jnp.int32)
    causal = positions[:, None] >= positions[None, :]
    cosine, sine = rope_tables(positions, head)
    cos_rows, sin_rows = cosine[:, None, :], sine[:, None, :]

    inputs = tokens.reshape(rows, width).astype(F32)
    inverse_in = lax.rsqrt(jnp.mean(inputs * inputs, -1, keepdims=True) + EPSILON)
    gain_in = attention_gain.astype(F32)
    normed = (inputs * inverse_in * gain_in).astype(BF16)

    w_qkv = gather_weights((query_proj, key_proj, value_proj))
    normed_all = gather_tokens(normed)
    gating_proj, output_t, normed_all = lax.optimization_barrier(
        (gating_proj, output_proj.T, normed_all)
    )
    w_go = gather_weights((gating_proj, output_t))
    w_gu = gather_weights((swiglu_gate, swiglu_up))
    w_dt = gather_weights((swiglu_down.T,))

    domain_table = (
        domain_ids[:, None] == jnp.arange(domain_counts.shape[0], dtype=jnp.int32)[None, :]
    ).astype(F32)
    ratio = (
        domain_numer.astype(F32) / domain_denom.astype(F32) * LENGTH / domain_counts.astype(F32)
    )
    factor = jnp.sum(domain_table * ratio[None, :], 1)
    upstream = (cotangent.astype(F32) * factor[:, None, None]).reshape(rows, width)
    out_low = upstream.astype(BF16)
    out_all = gather_tokens(out_low)

    qkv = dot_nn(normed_all, w_qkv)
    query_raw = qkv[:, :q_cols].reshape(seqs, full_len, heads, head)
    key_raw = qkv[:, q_cols : q_cols + kv_cols].reshape(seqs, full_len, 1, head)
    value_low = qkv[:, q_cols + kv_cols :].astype(BF16).reshape(seqs, full_len, head)
    query_scale, key_scale = query_gain.astype(F32), key_gain.astype(F32)
    query_inv = lax.rsqrt(jnp.mean(query_raw * query_raw, -1, keepdims=True) + EPSILON)
    key_inv = lax.rsqrt(jnp.mean(key_raw * key_raw, -1, keepdims=True) + EPSILON)
    query_low = rotate(query_raw * query_inv * query_scale, cos_rows, sin_rows).astype(BF16)
    key_low = rotate(key_raw * key_inv * key_scale, cos_rows, sin_rows).astype(BF16)
    key_low = key_low.reshape(seqs, full_len, head)
    attended, log_total = softmax_forward(query_low, key_low, value_low, causal)
    attended = attended.reshape(seqs * full_len, q_cols)

    w_g, w_ot = w_go[:, :q_cols], w_go[:, q_cols:]
    gate_sig = jax.nn.sigmoid(dot_nn(normed_all, w_g))
    mixed = (attended * gate_sig).astype(BF16)
    branch = scatter_tokens(dot_nt(mixed, w_ot).astype(BF16))
    hidden = inputs + branch
    inverse_mid = lax.rsqrt(jnp.mean(hidden * hidden, -1, keepdims=True) + EPSILON)
    gain_mid = swiglu_gain.astype(F32)
    normed_mid = (hidden * inverse_mid * gain_mid).astype(BF16)
    mid_all = gather_tokens(normed_mid)

    gate_up = dot_nn(mid_all, w_gu)
    gate_ff, up_val = gate_up[:, :ff_cols], gate_up[:, ff_cols:]
    sigma = jax.nn.sigmoid(gate_ff)
    silu = gate_ff * sigma
    activation = (silu * up_val).astype(BF16)
    part_dt = scatter_grads(dot_tn(out_all, activation))

    dact = dot_nn(out_all, w_dt)
    dgate = (dact * up_val * sigma * (1.0 + gate_ff * (1.0 - sigma))).astype(BF16)
    dup = (dact * silu).astype(BF16)
    dgu = jnp.concatenate([dgate, dup], 1)
    dnormed_mid = scatter_tokens(dot_nt(dgu, w_gu).astype(BF16))
    part_gu = scatter_grads(dot_tn(mid_all, dgu))
    grad_gain_mid = jnp.sum(dnormed_mid * hidden * inverse_mid, 0)
    dhidden = upstream + norm_back(dnormed_mid, hidden, inverse_mid, gain_mid)
    dbranch_all = gather_tokens(dhidden.astype(BF16))

    ffn_branch = scatter_tokens(dot_nt(activation, w_dt).astype(BF16))
    layer_out = (hidden + ffn_branch).astype(BF16)

    grad_ot = dot_tn(dbranch_all, mixed)
    dmixed = dot_nn(dbranch_all, w_ot)
    dattended = (dmixed * gate_sig).astype(BF16)
    dgating = (dmixed * attended * gate_sig * (1.0 - gate_sig)).astype(BF16)
    grad_g = dot_tn(normed_all, dgating)
    part_go = scatter_grads(jnp.concatenate([grad_g.astype(BF16), grad_ot.astype(BF16)], 1))
    dquery_rot, dkey_rot, dvalue_sum = softmax_backward(
        query_low,
        key_low,
        value_low,
        log_total,
        dattended.reshape(seqs, full_len, heads, head),
        causal,
    )
    dvalue = dvalue_sum.reshape(seqs * full_len, head).astype(BF16)
    dquery_n = unrotate(dquery_rot, cos_rows, sin_rows)
    dkey_n = unrotate(dkey_rot.reshape(seqs, full_len, 1, head), cos_rows, sin_rows)
    grad_query_gain = jnp.sum(dquery_n * query_raw * query_inv, (0, 1, 2))
    grad_key_gain = jnp.sum(dkey_n * key_raw * key_inv, (0, 1, 2))
    dquery = norm_back(dquery_n, query_raw, query_inv, query_scale).astype(BF16)
    dkey = norm_back(dkey_n, key_raw, key_inv, key_scale).astype(BF16)
    dqkv = jnp.concatenate(
        [dquery.reshape(seqs * full_len, -1), dkey.reshape(seqs * full_len, -1), dvalue], 1
    )
    part_qkv = scatter_grads(dot_tn(normed_all, dqkv))
    dnormed = scatter_tokens((dot_nt(dqkv, w_qkv) + dot_nt(dgating, w_g)).astype(BF16))
    grad_gain_in = jnp.sum(dnormed * inputs * inverse_in, 0)
    input_grad = (dhidden + norm_back(dnormed, inputs, inverse_in, gain_in)).astype(BF16)

    grad_down_t = finish_grads(part_dt, (ff_cols,))[0]
    grad_gate, grad_up = finish_grads(part_gu, (ff_cols, ff_cols))
    grad_gating, grad_output_t = finish_grads(part_go, (q_cols, q_cols))
    grad_query, grad_key, grad_value = finish_grads(part_qkv, (q_cols, kv_cols, kv_cols))
    gain_grads = lax.psum(
        (grad_gain_in, grad_gain_mid, grad_query_gain, grad_key_gain), ("z", "y", "x", "c")
    )
    shape = (seq_count, local_len, width)
    return (
        layer_out.reshape(shape),
        input_grad.reshape(shape),
        gain_grads[0],
        gain_grads[2],
        gain_grads[3],
        grad_query,
        grad_key,
        grad_value,
        grad_gating,
        grad_output_t.T,
        gain_grads[1],
        grad_gate,
        grad_up,
        grad_down_t.T,
    )


def solution(mesh):
    if (mesh.shape["dp"], mesh.shape["ctx"]) == (8, 4):
        body = per_device
        mesh = Mesh(mesh.devices.reshape(4, 2, 2, 2), ("z", "y", "x", "c"))
        dp, ctx = ("z", "y"), ("x", "c")
    else:
        body = per_device_wide
        dp, ctx = "dp", "ctx"
    tokens, weight, turned = P(dp, ctx, None), P(dp, ctx), P(ctx, dp)
    return jax.shard_map(
        body,
        mesh=mesh,
        in_specs=(tokens, tokens, P(dp), *[P()] * 6, *[weight] * 4, turned, P(), weight, weight, turned),
        out_specs=(tokens, tokens, *[P()] * 3, *[weight] * 4, turned, P(), weight, weight, turned),
        check_vma=False,
    )
```

```python
import functools

import jax
import jax.numpy as jnp
from jax import lax
from jax.experimental import pallas as pl
from jax.experimental.pallas import tpu as pltpu
from jax.sharding import Mesh
from jax.sharding import PartitionSpec as P

LENGTH = 1024

EPSILON = 1e-06
ROPE_BASE = 1000000.0
MESH = pl.DeviceIdType.MESH
BF16 = jnp.bfloat16
F32 = jnp.float32
VMEM_BYTES = 62 * 2**20


def micros(count):
    return pl.CostEstimate(flops=0, transcendentals=0, bytes_accessed=count * 3_300_000)


def dot_nn(left, right):
    return jnp.dot(left, right, preferred_element_type=F32)


def dot_tn(left, right):
    return lax.dot_general(left, right, (((0,), (0,)), ((), ())), preferred_element_type=F32)


def dot_nt(left, right):
    return lax.dot_general(left, right, (((1,), (1,)), ((), ())), preferred_element_type=F32)


def rope_tables(positions, head_width):
    halfway = head_width // 2
    inverse = 1.0 / ROPE_BASE ** (jnp.arange(halfway, dtype=F32) * (2.0 / head_width))
    angles = positions.astype(F32)[:, None] * inverse[None, :]
    return (jnp.cos(angles), jnp.sin(angles))


def rotate(tensor, cosine, sine):
    halfway = tensor.shape[-1] // 2
    first_half = tensor[..., :halfway]
    second_half = tensor[..., halfway:]
    return jnp.concatenate(
        [first_half * cosine - second_half * sine, second_half * cosine + first_half * sine], -1
    )


def unrotate(grads_in, cosine, sine):
    halfway = grads_in.shape[-1] // 2
    first_half = grads_in[..., :halfway]
    second_half = grads_in[..., halfway:]
    return jnp.concatenate(
        [first_half * cosine + second_half * sine, second_half * cosine - first_half * sine], -1
    )


def norm_back(grads_in, values_in, inverse, gain_vec):
    scaled = grads_in * gain_vec
    return inverse * scaled - values_in * (inverse * inverse * inverse) * jnp.mean(
        scaled * values_in, -1, keepdims=True
    )


def greet(neighbours):
    barrier = pltpu.get_barrier_semaphore()
    for neighbour in neighbours:
        pl.semaphore_signal(barrier, inc=1, device_id=neighbour, device_id_type=MESH)
    pl.semaphore_wait(barrier, len(neighbours))


def remote_copies(send, recv, device):
    def remote(index, source, target, axis):
        return pltpu.make_async_remote_copy(
            src_ref=source,
            dst_ref=target,
            send_sem=send.at[index],
            recv_sem=recv.at[index],
            device_id=device[axis],
            device_id_type=MESH,
        )

    return remote


def place():
    y, x, c = lax.axis_index("y"), lax.axis_index("x"), lax.axis_index("c")
    return y, x, c, {"y": {"y": 1 - y}, "x": {"x": 1 - x}, "c": {"c": 1 - c}}


def gather_steps(s_ref, out_ref, local_sem, send, recv, split=True):
    y, x, c, device = place()
    remote = remote_copies(send, recv, device)
    half = s_ref.shape[0] // 2
    low, high = pl.ds(0, half), pl.ds(half, half)
    mine = out_ref.at[y, x, c]
    from_x = out_ref.at[y, 1 - x, c]
    from_y = out_ref.at[1 - y, x, c]
    diagonal = out_ref.at[1 - y, 1 - x, c]
    x_low = remote(0, s_ref.at[low], mine.at[low], "x")
    y_high = remote(1, s_ref.at[high], mine.at[high], "y")
    x_high = remote(2, s_ref.at[high], mine.at[high], "x")
    y_low = remote(3, s_ref.at[low], mine.at[low], "y")
    c_own = remote(4, s_ref, mine, "c")
    local = pltpu.make_async_copy(s_ref, mine, local_sem)
    forward_y = remote(5, from_x.at[low], from_x.at[low], "y")
    over_x = from_y.at[high] if split else from_y
    forward_x = remote(6, over_x, over_x, "x")
    c_x = remote(7, from_x, from_x, "c")
    c_y = remote(8, from_y, from_y, "c")
    c_low = remote(9, diagonal.at[low], diagonal.at[low], "c")
    over_c = diagonal.at[high] if split else diagonal
    c_high = remote(10, over_c, over_c, "c")

    def begin():
        for copy in (x_low, y_high, x_high, y_low, c_own, local):
            copy.start()

    def forward():
        x_low.wait_recv()
        if split:
            forward_y.start()
        y_high.wait_recv()
        if split:
            forward_x.start()

    def across():
        if not split:
            y_low.wait_recv()
            forward_x.start()
        x_high.wait_recv()
        c_x.start()
        if split:
            y_low.wait_recv()
        c_y.start()

    def finish():
        if split:
            forward_y.wait_recv()
            c_low.start()
        forward_x.wait_recv()
        c_high.start()
        for copy in (c_own, c_x, c_y, *((c_low,) if split else ()), c_high):
            copy.wait()
        for copy in (x_low, y_high, x_high, y_low, *((forward_y,) if split else ()), forward_x):
            copy.wait_send()
        local.wait()

    return begin, forward, across, finish


GATHER_SEMAPHORES = (
    pltpu.SemaphoreType.DMA,
    pltpu.SemaphoreType.DMA((11,)),
    pltpu.SemaphoreType.DMA((11,)),
)


def swap_steps(pieces, sources, outs, local_sem, send, recv, wanted=None):
    y, _, _, device = place()
    remote = remote_copies(send, recv, device)
    copies, locals_ = [], []
    for i, (source, out, first, count, at) in enumerate(pieces):
        if wanted is not None and not wanted(out):
            continue
        rows, cols = sources[source].shape
        target = outs[out].at[pl.ds(pl.multiple_of(y * rows, rows), rows), pl.ds(at, count)]

        def half(which):
            start = pl.multiple_of(which * (cols // 2) + first, 128)
            return sources[source].at[:, pl.ds(start, count)]

        copies.append(remote(i, half(1 - y), target, "y"))
        locals_.append(pltpu.make_async_copy(half(y), target, local_sem.at[i]))

    def begin():
        for copy in (*copies, *locals_):
            copy.start()

    def finish():
        for copy in (*copies, *locals_):
            copy.wait()

    return begin, finish


def swap_plan(groups):
    weights, pieces, widths = [], [], []
    for group in groups:
        width = 0
        for weight, first, count in group:
            index = next((i for i, w in enumerate(weights) if w is weight), len(weights))
            if index == len(weights):
                weights.append(weight)
            pieces.append((index, len(widths), first, count, width))
            width += count
        widths.append(width)
    rows = 2 * weights[0].shape[0]
    shapes = tuple(jax.ShapeDtypeStruct((rows, width), BF16) for width in widths)
    count = len(pieces)
    semaphores = [pltpu.SemaphoreType.DMA((count,))] * 3
    return weights, pieces, shapes, semaphores


def swap_kernel(pieces, count, *refs):
    begin, finish = swap_steps(pieces, refs[:count], refs[count:-3], *refs[-3:])
    greet((place()[3]["y"],))
    begin()
    finish()


def swap_weights(*groups):
    weights, pieces, shapes, semaphores = swap_plan(groups)
    return pl.pallas_call(
        functools.partial(swap_kernel, pieces, len(weights)),
        out_shape=shapes,
        in_specs=[pl.BlockSpec(memory_space=pltpu.VMEM)] * len(weights),
        out_specs=(pl.BlockSpec(memory_space=pl.ANY),) * len(shapes),
        scratch_shapes=semaphores,
        compiler_params=pltpu.CompilerParams(collective_id=4, has_side_effects=True),
        cost_estimate=micros(15),
        name="swap_weights",
    )(*weights)


def gather_kernel(split, *refs):
    source, out, *sems = refs
    begin, forward, across, finish = gather_steps(source, out, *sems, split)
    greet(tuple(place()[3].values()))
    begin()
    forward()
    across()
    finish()


def gather_tokens(shard):
    rows, width = shard.shape
    return pl.pallas_call(
        functools.partial(gather_kernel, True),
        out_shape=jax.ShapeDtypeStruct((2, 2, 2, rows, width), shard.dtype),
        in_specs=[pl.BlockSpec(memory_space=pltpu.VMEM)],
        out_specs=pl.BlockSpec(memory_space=pl.ANY),
        scratch_shapes=list(GATHER_SEMAPHORES),
        compiler_params=pltpu.CompilerParams(collective_id=1, has_side_effects=True),
        cost_estimate=micros(42),
        name="gather_tokens",
    )(shard).reshape(8 * rows, width)


def line_steps(rows_ref, out_ref, local_sem, send, recv):
    z = lax.axis_index("z")
    rows = rows_ref.shape[0]
    pair, middle = z + 1 - 2 * lax.rem(z, 2), 3 - z
    inner = (z == 1) | (z == 2)

    def at(index):
        return out_ref.at[pl.ds(pl.multiple_of(index * rows, rows), rows)]

    def remote(index, source, target, peer):
        return pltpu.make_async_remote_copy(
            src_ref=source,
            dst_ref=target,
            send_sem=send.at[index],
            recv_sem=recv.at[index],
            device_id={"z": peer},
            device_id_type=MESH,
        )

    far = middle + 1 - 2 * lax.rem(middle, 2)
    own_pair = remote(0, rows_ref, at(z), pair)
    own_middle = remote(1, rows_ref, at(z), middle)
    pair_middle = remote(2, at(pair), at(pair), middle)
    middle_pair = remote(3, at(middle), at(middle), pair)
    far_pair = remote(4, at(far), at(far), pair)
    local = pltpu.make_async_copy(rows_ref, at(z), local_sem)

    def begin():
        local.start()
        own_pair.start()
        pl.when(inner)(own_middle.start)

    def second():
        own_pair.wait_recv()

        @pl.when(inner)
        def _():
            pair_middle.start()
            own_middle.wait_recv()
            middle_pair.start()

    def third():
        @pl.when(inner)
        def _():
            pair_middle.wait_recv()
            far_pair.start()

    def finish():
        @pl.when(inner)
        def _():
            for copy in (own_middle, pair_middle, middle_pair, far_pair):
                copy.wait_send()

        @pl.when(jnp.logical_not(inner))
        def _():
            middle_pair.wait_recv()
            far_pair.wait_recv()

        own_pair.wait_send()
        local.wait()

    def peers():
        return pair, middle, inner

    return begin, second, third, finish, peers


def greet_line(others, pair, middle, inner):
    barrier = pltpu.get_barrier_semaphore()
    for other in (*others, {"z": pair}):
        pl.semaphore_signal(barrier, inc=1, device_id=other, device_id_type=MESH)

    @pl.when(inner)
    def _():
        pl.semaphore_signal(barrier, inc=1, device_id={"z": middle}, device_id_type=MESH)

    count = len(others) + 1
    pl.semaphore_wait(barrier, jnp.where(inner, count + 1, count))


def gather_swap_kernel(pieces, count, source, *refs):
    out, line_out, outs, scratch = refs[count], refs[count + 1], refs[count + 2 : -10], refs[-10:]
    line, sems = scratch[0], scratch[1:]
    begin, forward, across, finish = gather_steps(source, out, *sems[:3], False)
    line_begin, line_second, line_third, line_finish, peers = line_steps(line, line_out, *sems[3:6])
    targets = (line, *outs)
    early, early_done = swap_steps(pieces, refs[:count], targets, *sems[6:], lambda out: out == 0)
    swap, swapped = swap_steps(pieces, refs[:count], targets, *sems[6:], lambda out: out > 0)
    greet_line(tuple(place()[3].values()), *peers())
    early()
    begin()
    early_done()
    line_begin()
    line_second()
    forward()
    across()
    swap()
    line_third()
    finish()
    line_finish()
    swapped()


def gather_and_swap(shard, *groups):
    rows, width = shard.shape
    weights, pieces, shapes, semaphores = swap_plan(groups)
    line, shapes = shapes[0], shapes[1:]
    whole = jax.ShapeDtypeStruct((4 * line.shape[0], line.shape[1]), line.dtype)
    gathered, lined, *swapped = pl.pallas_call(
        functools.partial(gather_swap_kernel, pieces, len(weights)),
        out_shape=(jax.ShapeDtypeStruct((2, 2, 2, rows, width), shard.dtype), whole, *shapes),
        in_specs=[pl.BlockSpec(memory_space=pltpu.VMEM)] * (1 + len(weights)),
        out_specs=(pl.BlockSpec(memory_space=pl.ANY),) * (2 + len(shapes)),
        scratch_shapes=[
            pltpu.VMEM(line.shape, line.dtype),
            *GATHER_SEMAPHORES,
            pltpu.SemaphoreType.DMA,
            pltpu.SemaphoreType.DMA((5,)),
            pltpu.SemaphoreType.DMA((5,)),
            *semaphores,
        ],
        compiler_params=pltpu.CompilerParams(collective_id=2, has_side_effects=True),
        cost_estimate=micros(65),
        name="gather_and_swap",
    )(shard, *weights)
    return gathered.reshape(8 * rows, width), lined, swapped


def scatter_steps(windows, lefts, rights, out_ref, left_vmem, right_vmem, own, away, got, x_diag, y_diag, x_got, y_got, load_sem, send, recv):
    y, x, c, device = place()
    remote = remote_copies(send, recv, device)
    rows, width = own.shape[1:]
    half, both = rows // 2, 2 * rows
    low, high = pl.ds(0, half), pl.ds(half, half)
    targets = ((1 - y, 1 - x), (1 - y, x), (y, 1 - x), (y, x))
    starts = [pl.multiple_of((a * 2 + b) * both, both) for a, b in targets]
    count = len(lefts)
    right_loads = [
        pltpu.make_async_copy(
            rights[j].at[:, pl.ds(windows[j], right_vmem[j].shape[1])], right_vmem[j], load_sem.at[j]
        )
        for j in range(count)
    ]
    left_loads = [
        [
            pltpu.make_async_copy(
                lefts[j].at[pl.ds(start, both)], left_vmem[j].at[i], load_sem.at[count * (i + 1) + j]
            )
            for j in range(count)
        ]
        for i, start in enumerate(starts)
    ]
    crossing = [remote(i, away.at[i], got.at[i], "c") for i in range(4)]
    diag_x = remote(4, own.at[0, low], x_diag, "x")
    diag_y = remote(5, own.at[0, high], y_diag, "y")
    y_high = remote(6, own.at[1, high], y_got.at[high], "y")
    x_low = remote(7, own.at[2, low], x_got.at[low], "x")
    y_low = remote(8, own.at[1, low], y_got.at[low], "y")
    x_high = remote(9, own.at[2, high], x_got.at[high], "x")
    step, tile = 64, 512

    def add_into(target, start, size, other, base):
        @pl.loop(0, size // step)
        def _(i):
            at, there = pl.ds(start + i * step, step), pl.ds(base + i * step, step)
            target[at] = (target[at].astype(F32) + other[there].astype(F32)).astype(target.dtype)

    mine, others = pl.ds(c * rows, rows), pl.ds((1 - c) * rows, rows)

    def product(i):
        for load in left_loads[i]:
            load.wait()

        @pl.loop(0, width // tile)
        def _(n):
            cols = pl.ds(pl.multiple_of(n * tile, tile), tile)
            for part, target in ((others, away), (mine, own)):
                total = dot_nt(left_vmem[0][i, part], right_vmem[0][cols])
                for j in range(1, count):
                    total = total + dot_nt(left_vmem[j][i, part], right_vmem[j][cols])
                target[i, :, cols] = total.astype(target.dtype)

        crossing[i].start()

    def cores(i):
        crossing[i].wait_recv()
        add_into(own.at[i], 0, rows, got.at[i], 0)

    def load():
        for copy in right_loads:
            copy.start()
        for copies in left_loads:
            for copy in copies:
                copy.start()

    def first_a():
        for copy in right_loads:
            copy.wait()
        product(0)
        product(1)

    def first_b():
        cores(0)
        diag_x.start()
        diag_y.start()
        product(2)
        cores(1)
        y_high.start()

    def first_c():
        product(3)
        cores(2)
        x_low.start()

    def first():
        first_a()
        first_b()
        first_c()

    first.parts = (first_a, first_b, first_c)

    def second():
        diag_x.wait_recv()
        add_into(own.at[1], 0, half, x_diag, 0)
        y_low.start()
        diag_y.wait_recv()
        add_into(own.at[2], half, half, y_diag, 0)
        x_high.start()
        cores(3)

    def finish():
        for copy in (y_high, x_low, y_low, x_high):
            copy.wait_recv()

        @pl.loop(0, rows // step)
        def _(i):
            at = pl.ds(i * step, step)
            out_ref[at] = own[3, at].astype(F32) + x_got[at].astype(F32) + y_got[at].astype(F32)

        for copy in (*crossing, diag_x, diag_y, y_high, x_low, y_low, x_high):
            copy.wait_send()

    return load, first, second, finish


def scatter_scratch(group):
    lefts, rights = [item[0] for item in group], [item[1] for item in group]
    rows, width = lefts[0].shape[0] // 8, rights[0].shape[0]
    scratch = [
        *[pltpu.VMEM((4, 2 * rows, left.shape[1]), BF16) for left in lefts],
        *[pltpu.VMEM((width, left.shape[1]), BF16) for left in lefts],
        pltpu.VMEM((4, rows, width), BF16),
        pltpu.VMEM((4, rows, width), BF16),
        pltpu.VMEM((4, rows, width), BF16),
        pltpu.VMEM((rows // 2, width), BF16),
        pltpu.VMEM((rows // 2, width), BF16),
        pltpu.VMEM((rows, width), BF16),
        pltpu.VMEM((rows, width), BF16),
        pltpu.SemaphoreType.DMA((5 * len(group),)),
        pltpu.SemaphoreType.DMA((10,)),
        pltpu.SemaphoreType.DMA((10,)),
    ]
    return lefts + rights, scratch, jax.ShapeDtypeStruct((rows, width), F32)


def scatter_kernel(windows, *refs):
    count = len(windows)
    lefts, rights, out_ref, scratch = refs[:count], refs[count : 2 * count], refs[2 * count], refs[2 * count + 1 :]
    load, first, second, finish = scatter_steps(
        windows, lefts, rights, out_ref, scratch[:count], scratch[count : 2 * count], *scratch[2 * count :]
    )
    load()
    greet(tuple(place()[3].values()))
    first()
    second()
    finish()


def scatter_products(*group):
    operands, scratch, total = scatter_scratch(group)
    return pl.pallas_call(
        functools.partial(scatter_kernel, [item[2] for item in group]),
        out_shape=total,
        in_specs=[pl.BlockSpec(memory_space=pl.ANY)] * len(operands),
        out_specs=pl.BlockSpec(memory_space=pltpu.VMEM),
        scratch_shapes=scratch,
        compiler_params=pltpu.CompilerParams(
            collective_id=10 + sum(item[0].shape[1] for item in group) // 256, has_side_effects=True
        ),
        cost_estimate=micros(48),
        name="scatter_products",
    )(*operands)


def line_scatter_steps(grad_ref, own, from_edge, from_middle, inward, load_sem, send, recv):
    z = lax.axis_index("z")
    rows = own.shape[1]
    pair, middle = z + 1 - 2 * lax.rem(z, 2), 3 - z
    inner = (z == 1) | (z == 2)
    edge = jnp.logical_not(inner)
    far = middle + 1 - 2 * lax.rem(middle, 2)

    def block(index):
        return grad_ref.at[pl.ds(pl.multiple_of(index * rows, rows), rows)]

    def remote(index, source, target, peer):
        return pltpu.make_async_remote_copy(
            src_ref=source,
            dst_ref=target,
            send_sem=send.at[index],
            recv_sem=recv.at[index],
            device_id={"z": peer},
            device_id_type=MESH,
        )

    indices = (far, middle, pair, z)
    loads = [
        pltpu.make_async_copy(block(index), own.at[i], load_sem.at[i])
        for i, index in enumerate(indices)
    ]
    edge_far = remote(0, own.at[1], from_edge.at[0], pair)
    edge_near = remote(1, own.at[0], from_edge.at[1], pair)
    edge_pair = remote(2, own.at[2], from_edge.at[2], pair)
    inner_far = remote(3, own.at[0], from_middle.at[0], middle)
    inner_near = remote(4, own.at[1], from_middle.at[1], middle)
    outward = remote(5, own.at[2], inward, pair)
    step = 128

    def add_into(target, other):
        @pl.loop(0, rows // step)
        def _(i):
            at = pl.ds(i * step, step)
            target[at] = (target[at].astype(F32) + other[at].astype(F32)).astype(target.dtype)

    def load():
        for copy in loads:
            copy.start()

    def begin():
        for copy in loads:
            copy.wait()

        @pl.when(edge)
        def _():
            for copy in (edge_far, edge_near, edge_pair):
                copy.start()

    def second():
        @pl.when(inner)
        def _():
            edge_far.wait_recv()
            add_into(own.at[0], from_edge.at[0])
            inner_far.start()

    def third():
        @pl.when(inner)
        def _():
            edge_near.wait_recv()
            add_into(own.at[1], from_edge.at[1])
            inner_near.start()
            inner_far.wait_recv()
            add_into(own.at[2], from_middle.at[0])
            outward.start()

    def finish():
        @pl.when(inner)
        def _():
            edge_pair.wait_recv()
            add_into(own.at[3], from_edge.at[2])
            inner_near.wait_recv()
            add_into(own.at[3], from_middle.at[1])
            for copy in (inner_far, inner_near, outward):
                copy.wait_send()

        @pl.when(edge)
        def _():
            outward.wait_recv()
            add_into(own.at[3], inward)
            for copy in (edge_far, edge_near, edge_pair):
                copy.wait_send()

    return load, begin, second, third, finish, (pair, middle, inner)


def total_steps(near, far, near_send, near_recv, far_send, far_recv):
    z, y, x, c = (lax.axis_index(name) for name in "zyxc")
    here = (y * 2 + x) * 2 + c
    others = [
        {"y": lax.rem(y + i // 4, 2), "x": lax.rem(x + i // 2 % 2, 2), "c": lax.rem(c + i % 2, 2)}
        for i in range(1, 8)
    ]
    levels = [{"z": lax.rem(z + i, 4)} for i in range(1, 4)]

    def remote(index, source, target, send, recv, device):
        return pltpu.make_async_remote_copy(
            src_ref=source,
            dst_ref=target,
            send_sem=send.at[index],
            recv_sem=recv.at[index],
            device_id=device,
            device_id_type=MESH,
        )

    around = [
        remote(i, near.at[here], near.at[here], near_send, near_recv, other)
        for i, other in enumerate(others)
    ]
    along = [
        remote(i, far.at[z], far.at[z], far_send, far_recv, level) for i, level in enumerate(levels)
    ]

    def begin():
        for copy in around:
            copy.start()

    def second():
        for copy in around:
            copy.wait()
        total = near[0]
        for i in range(1, 8):
            total = total + near[i]
        far[z] = total
        for copy in along:
            copy.start()

    def finish():
        for copy in along:
            copy.wait()
        total = far[0]
        for i in range(1, 4):
            total = total + far[i]
        return total

    return begin, second, finish, here, others, levels


def tail_kernel(windows, *refs):
    count = len(windows)
    lefts, rights, refs = refs[:count], refs[count : 2 * count], refs[2 * count :]
    grad_ref, tokens_ref, inverse_ref, *refs = refs
    gains, (out_ref, mine_ref, theirs_ref, total_ref), scratch = refs[:3], refs[3:7], refs[7:]
    size = 2 * count + 10
    load, first, second, finish = scatter_steps(
        windows, lefts, rights, out_ref, scratch[:count], scratch[count : 2 * count], *scratch[2 * count : size]
    )
    line, (swap_sem,), total = scratch[size : size + 7], scratch[size + 7 : size + 8], scratch[size + 8 :]
    line_load, line_begin, line_second, line_third, line_finish, peers = line_scatter_steps(grad_ref, *line)
    near, far = total[:2]
    total_begin, total_second, total_finish, here, others, levels = total_steps(*total)
    y = lax.axis_index("y")
    load()
    line_load()
    width = out_ref.shape[1]
    near[here, :, pl.ds(width, width)] = gains[0][...]
    head = gains[1].shape[1]
    near[here, :, pl.ds(2 * width, head)] = gains[1][...]
    near[here, :, pl.ds(2 * width + head, head)] = gains[2][...]
    greet(others + levels)
    line_begin()
    first()
    line_second()
    second()
    line_third()
    finish()
    rows, step = out_ref.shape[0], 32

    def gain_part(i, part):
        at = pl.ds(i * step, step)
        return part + jnp.sum(
            out_ref[at] * tokens_ref[at].astype(F32) * inverse_ref[at], 0, keepdims=True
        )

    near[here, :, pl.ds(0, width)] = lax.fori_loop(
        0, rows // step, gain_part, jnp.zeros((1, width), F32)
    )
    total_begin()
    line_finish()
    summed = line[0].at[3]
    half = theirs_ref.shape[0]
    swap = pltpu.make_async_remote_copy(
        src_ref=summed.at[pl.ds(pl.multiple_of((1 - y) * half, half), half)],
        dst_ref=theirs_ref,
        send_sem=swap_sem.at[0],
        recv_sem=swap_sem.at[1],
        device_id={"y": 1 - y},
        device_id_type=MESH,
    )
    swap.start()
    total_second()
    mine_ref[...] = summed[pl.ds(pl.multiple_of(y * half, half), half)]
    total_ref[...] = total_finish()
    swap.wait()


def tail(group, grad, tokens, inverse, gains):
    operands, scratch, total = scatter_scratch(group)
    rows, cols = grad.shape[0] // 4, grad.shape[1]
    length = 2 * total.shape[1] + 2 * gains[1].size
    half = jax.ShapeDtypeStruct((rows // 2, cols), BF16)
    whole = pl.BlockSpec(memory_space=pltpu.VMEM)
    block = lambda count: pltpu.VMEM((count, rows, cols), BF16)
    dma = pltpu.SemaphoreType.DMA
    return pl.pallas_call(
        functools.partial(tail_kernel, [item[2] for item in group]),
        out_shape=(total, half, half, jax.ShapeDtypeStruct((1, length), F32)),
        in_specs=[pl.BlockSpec(memory_space=pl.ANY)] * (len(operands) + 1) + [whole] * 5,
        out_specs=(whole,) * 4,
        scratch_shapes=[
            *scratch,
            block(4), block(3), block(2), pltpu.VMEM((rows, cols), BF16), dma((4,)), dma((6,)), dma((6,)),
            dma((2,)),
            pltpu.VMEM((8, 1, length), F32), pltpu.VMEM((4, 1, length), F32), dma((7,)), dma((7,)), dma((3,)), dma((3,)),
        ],
        compiler_params=pltpu.CompilerParams(
            collective_id=0, has_side_effects=True, vmem_limit_bytes=VMEM_BYTES
        ),
        cost_estimate=micros(52),
        name="tail",
    )(*operands, grad, tokens, inverse, *(gain.reshape(1, -1) for gain in gains))


def swap_y(value):
    return lax.ppermute(value, "y", [(0, 1), (1, 0)])


def in_y_order(mine, theirs, axis):
    count = mine.shape[axis]
    return lax.dynamic_slice_in_dim(
        jnp.concatenate([mine, theirs, mine], axis), lax.axis_index("y") * count, 2 * count, axis
    )


def gather_rows(rows):
    return lax.all_gather(rows, "z", axis=0, tiled=True)


def scatter_grads(grad):
    return lax.psum_scatter(grad.astype(BF16), "z", scatter_dimension=0, tiled=True)


def their_rows(part):
    half = part.shape[0] // 2
    return swap_y(
        lax.dynamic_slice_in_dim(part, (1 - lax.axis_index("y")) * half, half, 0)
    )


def join_pieces(plan, y, mine_of, theirs_of, outs):
    for source, first, width, out, at, turned in plan:
        half = outs[out].shape[0 if turned else 1] // 2
        cols = pl.ds(first, width)
        for which, piece in ((y, mine_of(source, cols)), (1 - y, theirs_of(source, cols))):
            target = pl.ds(pl.multiple_of(which * half + at, 128), width)
            if turned:
                outs[out][target, :] = piece.astype(F32).T
            else:
                outs[out][:, target] = piece.astype(F32)


def join_kernel(plan, count, y_rows, *refs):
    y = lax.axis_index("y")
    parts, theirs, outs = refs[:count], refs[count : 2 * count], refs[2 * count :]
    mine = pl.ds(pl.multiple_of(y * y_rows, y_rows), y_rows)
    own = lambda source, cols: parts[source][mine, cols]
    got = lambda source, cols: theirs[source][:, cols]
    join_pieces(plan, y, own, got, outs)


def join_grads(parts, theirs, plan, shapes):
    whole = pl.BlockSpec(memory_space=pltpu.VMEM)
    return pl.pallas_call(
        functools.partial(join_kernel, plan, len(parts), theirs[0].shape[0]),
        out_shape=tuple(jax.ShapeDtypeStruct(shape, F32) for shape in shapes),
        in_specs=[whole] * (2 * len(parts)),
        out_specs=(whole,) * len(shapes),
        compiler_params=pltpu.CompilerParams(vmem_limit_bytes=VMEM_BYTES),
        cost_estimate=micros(5),
        name="join_grads",
    )(*parts, *theirs)


def last_join_kernel(plan, mine, theirs, total, *outs):
    gains, grads, start = outs[:4], outs[4:], 0
    for gain in gains:
        gain[...] = total[:, pl.ds(start, gain.shape[1])]
        start += gain.shape[1]
    y = lax.axis_index("y")
    join_pieces(plan, y, lambda _, cols: mine[:, cols], lambda _, cols: theirs[:, cols], grads)


def join_last(mine, theirs, total, plan, sizes, shapes):
    whole = pl.BlockSpec(memory_space=pltpu.VMEM)
    outs = (*((1, size) for size in sizes), *shapes)
    return pl.pallas_call(
        functools.partial(last_join_kernel, plan),
        out_shape=tuple(jax.ShapeDtypeStruct(shape, F32) for shape in outs),
        in_specs=[whole] * 3,
        out_specs=(whole,) * len(outs),
        cost_estimate=micros(4),
        name="join_last",
    )(mine, theirs, total)


def normed_rope(raw, gain, cosine, sine):
    inverse = lax.rsqrt(jnp.mean(raw * raw, -1, keepdims=True) + EPSILON)
    scaled = raw * inverse * gain
    turned = pltpu.roll(scaled, scaled.shape[-1] // 2, 1)
    return (scaled * cosine + turned * sine).astype(BF16)


def normed_rope_back(grad, raw, gain, cosine, sine):
    inverse = lax.rsqrt(jnp.mean(raw * raw, -1, keepdims=True) + EPSILON)
    straight = grad * cosine - pltpu.roll(grad, grad.shape[-1] // 2, 1) * sine
    gain_part = jnp.sum(straight * (raw * inverse), 0, keepdims=True)
    return norm_back(straight, raw, inverse, gain).astype(BF16), gain_part


def causal_scores(query, keys, first, scaling):
    scores = dot_nt(query, keys) * scaling
    rows = lax.broadcasted_iota(jnp.int32, scores.shape, 0) + first
    columns = lax.broadcasted_iota(jnp.int32, scores.shape, 1)
    return jnp.where(rows >= columns, scores, -1e30)


def attend_kernel(
    heads, head, block, normed_ref, w_ref, wg_ref, low_ref, qg_ref, kg_ref, cos_ref, sin_ref,
    raw_ref, out_ref, log_ref, gate_ref, mixed_ref, all_ref, key_ref, value_ref, *sems,
):
    seq, step, steps = pl.program_id(0), pl.program_id(1), pl.num_programs(1)
    tick = seq * steps + step
    scaling = head**-0.5
    at = heads * head
    begin, forward, across, finish = gather_steps(low_ref, all_ref, *sems)

    @pl.when(tick == 0)
    def _():
        greet(tuple(place()[3].values()))
        begin()

    pl.when(tick == 3)(forward)
    pl.when(tick == 6)(across)
    raw_ref[...] = dot_nn(normed_ref[...], w_ref[...])
    here = pl.ds(pl.multiple_of(step * block, block), block)
    cosine, sine = cos_ref[here], sin_ref[here]
    key_ref[here] = normed_rope(raw_ref[:, at : at + head], kg_ref[...], cosine, sine)
    value_ref[here] = raw_ref[:, at + head :].astype(BF16)

    for i in range(key_ref.shape[0] // block):

        @pl.when(step == i)
        def _():
            seen = pl.ds(0, (i + 1) * block)

            @pl.loop(0, heads)
            def _(h):
                cols = pl.ds(pl.multiple_of(h * head, head), head)
                query = normed_rope(raw_ref[:, cols], qg_ref[...], cosine, sine)
                scores = causal_scores(query, key_ref[seen], i * block, scaling)
                highest = jnp.max(scores, -1, keepdims=True)
                exp_vals = jnp.exp(scores - highest)
                total = jnp.sum(exp_vals, -1, keepdims=True)
                probs = (exp_vals / total).astype(BF16)
                out_ref[:, cols] = dot_nn(probs, value_ref[seen])
                log_ref[h] = highest + jnp.log(total)

    gate = jax.nn.sigmoid(dot_nn(normed_ref[...], wg_ref[...]))
    gate_ref[...] = gate
    mixed_ref[...] = (out_ref[...] * gate).astype(BF16)
    pl.when(tick == pl.num_programs(0) * steps - 1)(finish)


def attend(normed, weights, gates, low, query_gain, key_gain, cosine, sine, heads, head, length, block=256):
    rows, width = normed.shape
    cols = weights.shape[1]
    seqs, steps = rows // length, length // block
    whole = lambda shape: pl.BlockSpec(
        shape, lambda s, i: (0,) * len(shape), pipeline_mode=pl.Buffered(1)
    )
    part = lambda cols: pl.BlockSpec((block, cols), lambda s, i: (s * steps + i, 0))
    *outs, gathered = pl.pallas_call(
        functools.partial(attend_kernel, heads, head, block),
        out_shape=(
            jax.ShapeDtypeStruct((rows, cols), F32),
            jax.ShapeDtypeStruct((rows, heads * head), F32),
            jax.ShapeDtypeStruct((heads, rows, 1), F32),
            jax.ShapeDtypeStruct((rows, heads * head), F32),
            jax.ShapeDtypeStruct((rows, heads * head), BF16),
            jax.ShapeDtypeStruct((2, 2, 2, *low.shape), low.dtype),
        ),
        grid=(seqs, steps),
        in_specs=[
            part(width),
            whole((width, cols)),
            whole((width, heads * head)),
            pl.BlockSpec(memory_space=pl.ANY),
            whole((1, head)),
            whole((1, head)),
            whole((length, head)),
            whole((length, head)),
        ],
        out_specs=(
            part(cols),
            part(heads * head),
            pl.BlockSpec((heads, block, 1), lambda s, i: (0, s * steps + i, 0)),
            part(heads * head),
            part(heads * head),
            pl.BlockSpec(memory_space=pl.ANY),
        ),
        scratch_shapes=[
            pltpu.VMEM((length, head), BF16),
            pltpu.VMEM((length, head), BF16),
            *GATHER_SEMAPHORES,
        ],
        compiler_params=pltpu.CompilerParams(collective_id=3, has_side_effects=True),
        cost_estimate=micros(42),
        name="attend",
    )(normed, weights, gates, low, query_gain, key_gain, cosine, sine)
    return *outs, gathered.reshape(rows, width)


def add_products(step, total_ref, start, left_ref, right, tile=1024):
    cols = slice(start, start + right.shape[1])

    @pl.loop(0, left_ref.shape[1] // tile)
    def _(m):
        at = pl.ds(pl.multiple_of(m * tile, tile), tile)
        part = dot_tn(left_ref[:, at], right)

        @pl.when(step == 0)
        def _():
            total_ref[at, cols] = part

        @pl.when(step > 0)
        def _():
            total_ref[at, cols] += part


def store_low(step, total_ref, out_ref, tile=256):
    @pl.when(step == pl.num_programs(0) - 1)
    def _():
        @pl.loop(0, total_ref.shape[0] // tile)
        def _(m):
            at = pl.ds(m * tile, tile)
            out_ref[at] = total_ref[at].astype(BF16)


def gate_back_kernel(
    normed_ref, branch_ref, w_ref, attended_ref, gate_ref, mixed_ref,
    dattended_ref, dgating_ref, grad_ref, total_ref,
):
    step = pl.program_id(0)
    dmixed = dot_nn(branch_ref[...], w_ref[...])
    gate = gate_ref[...]
    dattended_ref[...] = (dmixed * gate).astype(BF16)
    dgating = (dmixed * attended_ref[...] * gate * (1.0 - gate)).astype(BF16)
    dgating_ref[...] = dgating
    add_products(step, total_ref, 0, normed_ref, dgating)
    add_products(step, total_ref, dgating.shape[1], branch_ref, mixed_ref[...])
    store_low(step, total_ref, grad_ref)


def gate_back(normed, branch, weights, attended, gate, mixed, block=1024):
    rows, width = normed.shape
    cols = attended.shape[1]
    part = lambda cols: pl.BlockSpec((block, cols), lambda i: (i, 0))
    return pl.pallas_call(
        gate_back_kernel,
        out_shape=(
            jax.ShapeDtypeStruct((rows, cols), BF16),
            jax.ShapeDtypeStruct((rows, cols), BF16),
            jax.ShapeDtypeStruct((width, 2 * cols), BF16),
        ),
        grid=(rows // block,),
        in_specs=[
            part(width),
            part(width),
            pl.BlockSpec((width, cols), lambda i: (0, 1)),
            part(cols),
            part(cols),
            part(cols),
        ],
        out_specs=(part(cols), part(cols), pl.BlockSpec((width, 2 * cols), lambda i: (0, 0))),
        scratch_shapes=[pltpu.VMEM((width, 2 * cols), F32)],
        compiler_params=pltpu.CompilerParams(vmem_limit_bytes=VMEM_BYTES),
        cost_estimate=micros(25),
        name="gate_back",
    )(normed, branch, weights, attended, gate, mixed)


def feed_kernel(count, tile, mid_ref, low_ref, w_ref, act_ref, dgu_ref, grad_ref, total_ref):
    step = pl.program_id(0)

    @pl.loop(0, count // tile)
    def _(j):
        start = pl.multiple_of(j * tile, tile)
        at, after = pl.ds(start, tile), pl.ds(pl.multiple_of(count + start, tile), tile)
        last = pl.ds(pl.multiple_of(2 * count + start, tile), tile)
        gate = dot_nn(mid_ref[...], w_ref[:, at])
        up = dot_nn(mid_ref[...], w_ref[:, after])
        dact = dot_nn(low_ref[...], w_ref[:, last])
        sigma = jax.nn.sigmoid(gate)
        silu = gate * sigma
        act_ref[:, at] = (silu * up).astype(BF16)
        dgu_ref[:, at] = (dact * up * sigma * (1.0 + gate * (1.0 - sigma))).astype(BF16)
        dgu_ref[:, after] = (dact * silu).astype(BF16)

    add_products(step, total_ref, 0, mid_ref, dgu_ref[...])
    add_products(step, total_ref, 2 * count, low_ref, act_ref[...])
    store_low(step, total_ref, grad_ref)


def feed_forward(mid, low, weights, block=1024):
    rows, width = mid.shape
    count = weights.shape[1] // 3
    part = lambda cols: pl.BlockSpec((block, cols), lambda i: (i, 0))
    whole = pl.BlockSpec(weights.shape, lambda i: (0, 0), pipeline_mode=pl.Buffered(1))
    return pl.pallas_call(
        functools.partial(feed_kernel, count, 256),
        out_shape=(
            jax.ShapeDtypeStruct((rows, count), BF16),
            jax.ShapeDtypeStruct((rows, 2 * count), BF16),
            jax.ShapeDtypeStruct(weights.shape, BF16),
        ),
        grid=(rows // block,),
        in_specs=[part(width), part(width), whole],
        out_specs=(part(count), part(2 * count), whole),
        scratch_shapes=[pltpu.VMEM(weights.shape, F32)],
        compiler_params=pltpu.CompilerParams(vmem_limit_bytes=VMEM_BYTES),
        cost_estimate=micros(40),
        name="feed_forward",
    )(mid, low, weights)


def attend_back_kernel(
    heads, head, block, windows, raw_ref, up_ref, log_ref, qg_ref, kg_ref, cos_ref, sin_ref, *refs
):
    count = len(windows)
    lefts, rights, refs = refs[:count], refs[count : 2 * count], refs[2 * count :]
    out_ref, qg_out, kg_out, sum_ref, key_ref, value_ref, dkey_ref, dvalue_ref, *scratch = refs
    seq, step, steps = pl.program_id(0), pl.program_id(1), pl.num_programs(1)
    tick = seq * steps + step
    scaling = head**-0.5
    at = heads * head
    blocks = raw_ref.shape[0] // block
    load, first, second, finish = scatter_steps(
        windows, lefts, rights, sum_ref, scratch[:count], scratch[count : 2 * count], *scratch[2 * count :]
    )

    @pl.when(tick == 0)
    def _():
        load()
        greet(tuple(place()[3].values()))
        qg_out[...] = jnp.zeros_like(qg_out)
        kg_out[...] = jnp.zeros_like(kg_out)

    for i, part in enumerate(first.parts):
        pl.when(tick == i)(part)
    pl.when(tick == 5)(second)

    @pl.when(step == 0)
    def _():
        key_ref[...] = normed_rope(
            raw_ref[:, at : at + head], kg_ref[...], cos_ref[...], sin_ref[...]
        )
        value_ref[...] = raw_ref[:, at + head :].astype(BF16)
        dkey_ref[...] = jnp.zeros_like(dkey_ref)
        dvalue_ref[...] = jnp.zeros_like(dvalue_ref)

    for i in range(blocks):

        @pl.when(step == i)
        def _():
            rows, seen = pl.ds(i * block, block), pl.ds(0, (i + 1) * block)

            @pl.loop(0, heads)
            def _(h):
                cols = pl.ds(pl.multiple_of(h * head, head), head)
                raw = raw_ref[rows, cols]
                query = normed_rope(raw, qg_ref[...], cos_ref[rows], sin_ref[rows])
                scores = causal_scores(query, key_ref[seen], i * block, scaling)
                probs = jnp.exp(scores - log_ref[h])
                upstream = up_ref[:, cols]
                dprobs = dot_nt(upstream, value_ref[seen])
                centre = jnp.sum(dprobs * probs, -1, keepdims=True)
                dscores = (probs * (dprobs - centre)).astype(BF16)
                dkey_ref[seen] += dot_tn(dscores, query)
                dvalue_ref[seen] += dot_tn(probs.astype(BF16), upstream)
                dquery = dot_nn(dscores, key_ref[seen]) * scaling
                grad, part = normed_rope_back(
                    dquery, raw, qg_ref[...], cos_ref[rows], sin_ref[rows]
                )
                out_ref[rows, cols] = grad
                qg_out[...] += part

    @pl.when(step == blocks - 1)
    def _():
        grad, part = normed_rope_back(
            dkey_ref[...] * scaling,
            raw_ref[:, at : at + head],
            kg_ref[...],
            cos_ref[...],
            sin_ref[...],
        )
        out_ref[:, at : at + head] = grad
        out_ref[:, at + head :] = dvalue_ref[...].astype(BF16)
        kg_out[...] += part

    pl.when(tick == pl.num_programs(0) * steps - 1)(finish)


def attend_back(
    raw, upstream, logs, query_gain, key_gain, cosine, sine, heads, head, length, group, block=256
):
    rows = raw.shape[0]
    operands, scratch, total = scatter_scratch(group)
    seqs, steps = rows // length, length // block
    whole = lambda shape: pl.BlockSpec(shape, lambda s, i: (0,) * len(shape))
    return pl.pallas_call(
        functools.partial(attend_back_kernel, heads, head, block, [item[2] for item in group]),
        out_shape=(
            jax.ShapeDtypeStruct(raw.shape, BF16),
            jax.ShapeDtypeStruct((1, head), F32),
            jax.ShapeDtypeStruct((1, head), F32),
            total,
        ),
        grid=(seqs, steps),
        in_specs=[
            pl.BlockSpec((length, raw.shape[1]), lambda s, i: (s, 0)),
            pl.BlockSpec((block, heads * head), lambda s, i: (s * steps + i, 0)),
            pl.BlockSpec((heads, block, 1), lambda s, i: (0, s * steps + i, 0)),
            whole((1, head)),
            whole((1, head)),
            whole((length, head)),
            whole((length, head)),
            *[pl.BlockSpec(memory_space=pl.ANY)] * len(operands),
        ],
        out_specs=(
            pl.BlockSpec((length, raw.shape[1]), lambda s, i: (s, 0)),
            whole((1, head)),
            whole((1, head)),
            whole(total.shape),
        ),
        scratch_shapes=[
            pltpu.VMEM((length, head), BF16),
            pltpu.VMEM((length, head), BF16),
            pltpu.VMEM((length, head), F32),
            pltpu.VMEM((length, head), F32),
            *scratch,
        ],
        compiler_params=pltpu.CompilerParams(
            collective_id=5, has_side_effects=True, vmem_limit_bytes=VMEM_BYTES
        ),
        cost_estimate=micros(48),
        name="attend_back",
    )(raw, upstream, logs, query_gain, key_gain, cosine, sine, *operands)


def attention_weights(query_proj, key_proj, value_proj, gating_proj, output_proj):
    return (
        lax.all_gather(query_proj, "dp", axis=0, tiled=True),
        lax.all_gather(key_proj, "dp", axis=0, tiled=True),
        lax.all_gather(value_proj, "dp", axis=0, tiled=True),
        lax.all_gather(gating_proj, "dp", axis=0, tiled=True),
        lax.all_gather(output_proj, "dp", axis=1, tiled=True),
    )


def swiglu_weights(swiglu_gate, swiglu_up, swiglu_down):
    return (
        lax.all_gather(swiglu_gate, "dp", axis=0, tiled=True),
        lax.all_gather(swiglu_up, "dp", axis=0, tiled=True),
        lax.all_gather(swiglu_down, "dp", axis=1, tiled=True),
    )


def softmax_forward_mapped(seq_items, causal):
    queries, keys_seq, values_seq = seq_items
    scaling = queries.shape[-1] ** (-0.5)
    scores = (
        jnp.einsum("qgjd,kgd->gjqk", queries, keys_seq, preferred_element_type=jnp.float32)
        * scaling
    )
    scores = jnp.where(causal, scores, -1e30)
    highest = jnp.max(scores, -1, keepdims=True)
    exp_vals = jnp.exp(scores - highest)
    row_totals = jnp.sum(exp_vals, -1, keepdims=True)
    attn_probs = (exp_vals / row_totals).astype(jnp.bfloat16)
    attended = jnp.einsum(
        "gjqk,kgd->qgjd", attn_probs, values_seq, preferred_element_type=jnp.float32
    )
    return (attended, highest[..., 0] + jnp.log(row_totals[..., 0]))


def softmax_backward_mapped(seq_items, causal):
    queries, keys_seq, values_seq, log_total, upstream = seq_items
    scaling = queries.shape[-1] ** (-0.5)
    scores = (
        jnp.einsum("qgjd,kgd->gjqk", queries, keys_seq, preferred_element_type=jnp.float32)
        * scaling
    )
    scores = jnp.where(causal, scores, -1e30)
    attn_probs = jnp.exp(scores - log_total[..., None])
    dprobs = jnp.einsum("qgjd,kgd->gjqk", upstream, values_seq, preferred_element_type=jnp.float32)
    centre = jnp.sum(dprobs * attn_probs, -1, keepdims=True)
    dscores = (attn_probs * (dprobs - centre)).astype(jnp.bfloat16)
    dqueries = (
        jnp.einsum("gjqk,kgd->qgjd", dscores, keys_seq, preferred_element_type=jnp.float32)
        * scaling
    )
    key_grads = (
        jnp.einsum("gjqk,qgjd->kgd", dscores, queries, preferred_element_type=jnp.float32) * scaling
    )
    value_grads = jnp.einsum(
        "gjqk,qgjd->kgd",
        attn_probs.astype(jnp.bfloat16),
        upstream,
        preferred_element_type=jnp.float32,
    )
    key_rows = key_grads.shape[0]
    return (dqueries, key_grads.reshape(key_rows, -1), value_grads.reshape(key_rows, -1))


def per_device_wide(
    tokens,
    cotangent,
    domain_ids,
    domain_counts,
    domain_numer,
    domain_denom,
    attention_gain,
    query_gain,
    key_gain,
    query_proj,
    key_proj,
    value_proj,
    gating_proj,
    output_proj,
    swiglu_gain,
    swiglu_gate,
    swiglu_up,
    swiglu_down,
):
    seq_count, local_len, model_width = tokens.shape
    full_len = local_len * lax.axis_size("ctx")
    local_rows = seq_count * local_len
    all_rows = seq_count * full_len
    head_dim = query_gain.shape[0]
    local_heads = query_proj.shape[1] // head_dim
    local_kv = key_proj.shape[1] // head_dim
    group_size = local_heads // local_kv
    positions = jnp.arange(full_len, dtype=jnp.int32)
    causal = positions[:, None] >= positions[None, :]
    cosine, sine = rope_tables(positions, head_dim)
    cos_rows = cosine[:, None, :]
    sin_rows = sine[:, None, :]
    inputs = tokens.reshape(local_rows, model_width).astype(jnp.float32)
    inverse_in = lax.rsqrt(jnp.mean(inputs * inputs, -1, keepdims=True) + EPSILON)
    gain_in = attention_gain.astype(jnp.float32)
    normed = (inputs * inverse_in * gain_in).astype(jnp.bfloat16)
    normed_all = lax.all_gather(
        normed.reshape(seq_count, local_len, model_width), "ctx", axis=1, tiled=True
    ).reshape(all_rows, model_width)
    attn_full = attention_weights(query_proj, key_proj, value_proj, gating_proj, output_proj)
    query_raw = dot_nn(normed_all, attn_full[0]).reshape(
        seq_count, full_len, local_heads, head_dim
    )
    key_raw = dot_nn(normed_all, attn_full[1]).reshape(seq_count, full_len, local_kv, head_dim)
    value_low = (
        dot_nn(normed_all, attn_full[2])
        .astype(jnp.bfloat16)
        .reshape(seq_count, full_len, local_kv, head_dim)
    )
    gate_pre = dot_nn(normed_all, attn_full[3])
    query_scale = query_gain.astype(jnp.float32)
    key_scale = key_gain.astype(jnp.float32)
    query_inv = lax.rsqrt(jnp.mean(query_raw * query_raw, -1, keepdims=True) + EPSILON)
    key_inv = lax.rsqrt(jnp.mean(key_raw * key_raw, -1, keepdims=True) + EPSILON)
    query_low = rotate(query_raw * query_inv * query_scale, cos_rows, sin_rows).astype(jnp.bfloat16)
    key_low = rotate(key_raw * key_inv * key_scale, cos_rows, sin_rows).astype(jnp.bfloat16)
    query_groups = query_low.reshape(seq_count, full_len, local_kv, group_size, head_dim)
    attended, log_total = lax.map(
        lambda seq_items: softmax_forward_mapped(seq_items, causal), (query_groups, key_low, value_low)
    )
    attended = attended.reshape(all_rows, local_heads * head_dim)
    gate_sig = jax.nn.sigmoid(gate_pre)
    mixed = (attended * gate_sig).astype(jnp.bfloat16)
    branch_part = dot_nn(mixed, attn_full[4]).reshape(seq_count, full_len, model_width)
    branch = lax.psum_scatter(branch_part, "ctx", scatter_dimension=1, tiled=True).reshape(
        local_rows, model_width
    )
    hidden = inputs + branch
    inverse_mid = lax.rsqrt(jnp.mean(hidden * hidden, -1, keepdims=True) + EPSILON)
    gain_mid = swiglu_gain.astype(jnp.float32)
    normed_mid = (hidden * inverse_mid * gain_mid).astype(jnp.bfloat16)
    normed_mid_all = lax.all_gather(
        normed_mid.reshape(seq_count, local_len, model_width), "ctx", axis=1, tiled=True
    ).reshape(all_rows, model_width)
    swiglu_full = swiglu_weights(swiglu_gate, swiglu_up, swiglu_down)
    gate_ff = dot_nn(normed_mid_all, swiglu_full[0])
    up_val = dot_nn(normed_mid_all, swiglu_full[1])
    gate_sigma = jax.nn.sigmoid(gate_ff)
    silu_val = gate_ff * gate_sigma
    activation = (silu_val * up_val).astype(jnp.bfloat16)
    down_part = dot_nn(activation, swiglu_full[2]).reshape(seq_count, full_len, model_width)
    ffn_branch = (
        lax.psum_scatter(down_part.astype(jnp.bfloat16), "ctx", scatter_dimension=1, tiled=True)
        .astype(jnp.float32)
        .reshape(local_rows, model_width)
    )
    layer_out = (hidden + ffn_branch).astype(jnp.bfloat16)
    domain_table = (
        domain_ids[:, None] == jnp.arange(domain_counts.shape[0], dtype=jnp.int32)[None, :]
    ).astype(jnp.float32)
    ratio = (
        domain_numer.astype(jnp.float32)
        / domain_denom.astype(jnp.float32)
        * LENGTH
        / domain_counts.astype(jnp.float32)
    )
    factor = jnp.sum(domain_table * ratio[None, :], 1)
    upstream = (cotangent.astype(jnp.float32) * factor[:, None, None]).reshape(
        local_rows, model_width
    )
    swiglu_back = swiglu_weights(swiglu_gate, swiglu_up, swiglu_down)
    out_low = upstream.astype(jnp.bfloat16)
    out_all = lax.all_gather(
        out_low.reshape(seq_count, local_len, model_width), "ctx", axis=1, tiled=True
    ).reshape(all_rows, model_width)
    dactivation = dot_nt(out_all, swiglu_back[2])
    dgate_low = (dactivation * up_val * gate_sigma * (1.0 + gate_ff * (1.0 - gate_sigma))).astype(
        jnp.bfloat16
    )
    dup_low = (dactivation * silu_val).astype(jnp.bfloat16)
    grad_down = dot_tn(activation, out_all)
    grad_gate = dot_tn(normed_mid_all, dgate_low)
    grad_up = dot_tn(normed_mid_all, dup_low)
    dmid_part = dot_nt(dgate_low, swiglu_back[0]) + dot_nt(dup_low, swiglu_back[1])
    dnormed_mid = lax.psum_scatter(
        dmid_part.reshape(seq_count, full_len, model_width), "ctx", scatter_dimension=1, tiled=True
    ).reshape(local_rows, model_width)
    grad_gain_mid = jnp.sum(dnormed_mid * hidden * inverse_mid, 0)
    dhidden = upstream + norm_back(dnormed_mid, hidden, inverse_mid, gain_mid)
    swiglu_grads = (
        lax.psum_scatter(
            grad_gate.astype(jnp.bfloat16), "dp", scatter_dimension=0, tiled=True
        ).astype(jnp.float32),
        lax.psum_scatter(
            grad_up.astype(jnp.bfloat16), "dp", scatter_dimension=0, tiled=True
        ).astype(jnp.float32),
        lax.psum_scatter(
            grad_down.astype(jnp.bfloat16), "dp", scatter_dimension=1, tiled=True
        ).astype(jnp.float32),
    )
    attn_back = attention_weights(query_proj, key_proj, value_proj, gating_proj, output_proj)
    dbranch_low = dhidden.astype(jnp.bfloat16)
    dbranch_all = lax.all_gather(
        dbranch_low.reshape(seq_count, local_len, model_width), "ctx", axis=1, tiled=True
    ).reshape(all_rows, model_width)
    grad_output = dot_tn(mixed, dbranch_all)
    dmixed = dot_nt(dbranch_all, attn_back[4])
    dattended_low = (dmixed * gate_sig).astype(jnp.bfloat16)
    dgating_low = (dmixed * attended * gate_sig * (1.0 - gate_sig)).astype(jnp.bfloat16)
    upstream_heads = dattended_low.reshape(seq_count, full_len, local_kv, group_size, head_dim)
    dquery_rot, dkey_rot, dvalue_sum = lax.map(
        lambda seq_items: softmax_backward_mapped(seq_items, causal),
        (query_groups, key_low, value_low, log_total, upstream_heads),
    )
    dvalue_low = dvalue_sum.reshape(all_rows, local_kv * head_dim).astype(jnp.bfloat16)
    dquery_normed = unrotate(
        dquery_rot.reshape(seq_count, full_len, local_heads, head_dim), cos_rows, sin_rows
    )
    dkey_normed = unrotate(
        dkey_rot.reshape(seq_count, full_len, local_kv, head_dim), cos_rows, sin_rows
    )
    grad_query_gain = jnp.sum(dquery_normed * query_raw * query_inv, (0, 1, 2))
    grad_key_gain = jnp.sum(dkey_normed * key_raw * key_inv, (0, 1, 2))
    dquery_low = (
        norm_back(dquery_normed, query_raw, query_inv, query_scale)
        .reshape(all_rows, -1)
        .astype(jnp.bfloat16)
    )
    dkey_low = (
        norm_back(dkey_normed, key_raw, key_inv, key_scale)
        .reshape(all_rows, -1)
        .astype(jnp.bfloat16)
    )
    dnormed_part = (
        dot_nt(dquery_low, attn_back[0])
        + dot_nt(dkey_low, attn_back[1])
        + dot_nt(dvalue_low, attn_back[2])
        + dot_nt(dgating_low, attn_back[3])
    )
    dnormed = (
        lax.psum_scatter(
            dnormed_part.reshape(seq_count, full_len, model_width).astype(jnp.bfloat16),
            "ctx",
            scatter_dimension=1,
            tiled=True,
        )
        .astype(jnp.float32)
        .reshape(local_rows, model_width)
    )
    grad_gain_in = jnp.sum(dnormed * inputs * inverse_in, 0)
    input_grad = (dhidden + norm_back(dnormed, inputs, inverse_in, gain_in)).astype(jnp.bfloat16)
    grad_query = dot_tn(normed_all, dquery_low)
    grad_key = dot_tn(normed_all, dkey_low)
    grad_value = dot_tn(normed_all, dvalue_low)
    grad_gating = dot_tn(normed_all, dgating_low)
    attention_grads = (
        lax.psum_scatter(
            grad_query.astype(jnp.bfloat16), "dp", scatter_dimension=0, tiled=True
        ).astype(jnp.float32),
        lax.psum_scatter(
            grad_key.astype(jnp.bfloat16), "dp", scatter_dimension=0, tiled=True
        ).astype(jnp.float32),
        lax.psum_scatter(
            grad_value.astype(jnp.bfloat16), "dp", scatter_dimension=0, tiled=True
        ).astype(jnp.float32),
        lax.psum_scatter(
            grad_gating.astype(jnp.bfloat16), "dp", scatter_dimension=0, tiled=True
        ).astype(jnp.float32),
        lax.psum_scatter(
            grad_output.astype(jnp.bfloat16), "dp", scatter_dimension=1, tiled=True
        ).astype(jnp.float32),
    )
    gain_grads = lax.psum(
        (grad_gain_in, grad_gain_mid, grad_query_gain, grad_key_gain), ("dp", "ctx")
    )
    return (
        layer_out.reshape(seq_count, local_len, model_width),
        input_grad.reshape(seq_count, local_len, model_width),
        gain_grads[0],
        gain_grads[2],
        gain_grads[3],
        attention_grads[0],
        attention_grads[1],
        attention_grads[2],
        attention_grads[3],
        attention_grads[4],
        gain_grads[1],
        swiglu_grads[0],
        swiglu_grads[1],
        swiglu_grads[2],
    )


def per_device(
    tokens,
    cotangent,
    domain_ids,
    domain_counts,
    domain_numer,
    domain_denom,
    attention_gain,
    query_gain,
    key_gain,
    query_proj,
    key_proj,
    value_proj,
    gating_proj,
    output_proj,
    swiglu_gain,
    swiglu_gate,
    swiglu_up,
    swiglu_down,
):
    seq_count, local_len, width = tokens.shape
    rows = seq_count * local_len
    full_len = local_len * lax.axis_size("x") * lax.axis_size("c")
    seqs = seq_count * lax.axis_size("y")
    head = query_gain.shape[0]
    kv_cols = key_proj.shape[1] // 2
    q_cols = query_proj.shape[1] // 2
    ff_cols = swiglu_gate.shape[1] // 2
    heads = q_cols // head
    cosine, sine = rope_tables(jnp.arange(full_len, dtype=jnp.int32), head)
    cos_rows = jnp.concatenate([cosine, cosine], 1)
    sin_rows = jnp.concatenate([-sine, sine], 1)

    inputs = tokens.reshape(rows, width).astype(F32)
    inverse_in = lax.rsqrt(jnp.mean(inputs * inputs, -1, keepdims=True) + EPSILON)
    gain_in = attention_gain.astype(F32)
    normed = (inputs * inverse_in * gain_in).astype(BF16)

    domain_table = (
        domain_ids[:, None] == jnp.arange(domain_counts.shape[0], dtype=jnp.int32)[None, :]
    ).astype(F32)
    ratio = (
        domain_numer.astype(F32) / domain_denom.astype(F32) * LENGTH / domain_counts.astype(F32)
    )
    factor = jnp.sum(domain_table * ratio[None, :], 1)
    upstream = (cotangent.astype(F32) * factor[:, None, None]).reshape(rows, width)
    out_low = upstream.astype(BF16)

    down_t, output_t = swiglu_down.T, output_proj.T
    split, rest = ff_cols * 2 // 3, ff_cols - ff_cols * 2 // 3
    (rows_go,) = swap_weights([(gating_proj, 0, q_cols), (output_t, 0, q_cols)])
    w_go = gather_rows(rows_go)
    feed = (swiglu_gate, swiglu_up, down_t)
    normed, out_low, cos_rows, sin_rows, rows_go = lax.optimization_barrier(
        (normed, out_low, cos_rows, sin_rows, rows_go)
    )
    normed_all, w_qkv, (rows_first, rows_last) = gather_and_swap(
        normed,
        [(query_proj, 0, q_cols), (key_proj, 0, kv_cols), (value_proj, 0, kv_cols)],
        [(w, 0, split) for w in feed], [(w, split, rest) for w in feed]
    )
    w_first = gather_rows(rows_first)
    w_last = gather_rows(rows_last)

    query_scale, key_scale = query_gain.astype(F32)[None], key_gain.astype(F32)[None]
    qkv, attended, logs, gate_sig, mixed, out_all = attend(
        normed_all, w_qkv, w_go, out_low, query_scale, key_scale, cos_rows, sin_rows, heads, head, full_len
    )
    branch = scatter_products((mixed, w_go, q_cols))
    hidden = inputs + branch
    inverse_mid = lax.rsqrt(jnp.mean(hidden * hidden, -1, keepdims=True) + EPSILON)
    gain_mid = swiglu_gain.astype(F32)
    normed_mid = (hidden * inverse_mid * gain_mid).astype(BF16)
    mid_all = gather_tokens(normed_mid)

    act_first, dgu_first, grad_first = feed_forward(mid_all, out_all, w_first)
    part_first = scatter_grads(grad_first)
    w_last, grad_first = lax.optimization_barrier((w_last, grad_first))
    act_last, dgu_last, grad_last = feed_forward(mid_all, out_all, w_last)
    dgu_last, grad_last = lax.optimization_barrier((dgu_last, grad_last))
    part_last = scatter_grads(grad_last)
    dnormed_mid = scatter_products((dgu_first, w_first, 0), (dgu_last, w_last, 0))
    grad_gain_mid = jnp.sum(dnormed_mid * hidden * inverse_mid, 0)
    dhidden = upstream + norm_back(dnormed_mid, hidden, inverse_mid, gain_mid)
    dbranch_all = gather_tokens(dhidden.astype(BF16))
    dbranch_all, part_first = lax.optimization_barrier((dbranch_all, part_first))

    theirs_first = their_rows(part_first)
    dattended, dgating, grad_go = gate_back(
        normed_all, dbranch_all, w_go, attended, gate_sig, mixed
    )
    dattended, theirs_first, grad_go = lax.optimization_barrier((dattended, theirs_first, grad_go))
    part_go = scatter_grads(grad_go)
    dqkv, grad_query_gain, grad_key_gain, ffn_branch = attend_back(
        qkv, dattended, logs, query_scale, key_scale, cos_rows, sin_rows, heads, head, full_len,
        ((act_first, w_first, 2 * split), (act_last, w_last, 2 * rest)),
    )
    grad_query_gain, grad_key_gain = grad_query_gain[0], grad_key_gain[0]
    grad_qkv = dot_tn(normed_all, dqkv).astype(BF16)
    dqkv, grad_qkv, part_last = lax.optimization_barrier((dqkv, grad_qkv, part_last))
    theirs_last = their_rows(part_last)
    dnormed, mine_qkv, theirs_qkv, totals = tail(
        ((dqkv, w_qkv, 0), (dgating, w_go, 0)),
        grad_qkv,
        tokens.reshape(rows, width),
        inverse_in,
        (grad_gain_mid, grad_query_gain, grad_key_gain),
    )
    dnormed, part_go = lax.optimization_barrier((dnormed, part_go))
    input_grad = (dhidden + norm_back(dnormed, inputs, inverse_in, gain_in)).astype(BF16)
    layer_out = (hidden + ffn_branch).astype(BF16)

    plan = [(0, i * split, split, i, 0, i == 2) for i in range(3)]
    plan += [(1, i * rest, rest, i, split, i == 2) for i in range(3)]
    plan += [(2, 0, q_cols, 3, 0, False), (2, q_cols, q_cols, 4, 0, True)]
    weights = (swiglu_gate, swiglu_up, swiglu_down, gating_proj, output_proj)
    grad_gate, grad_up, grad_down, grad_gating, grad_output = join_grads(
        (part_first, part_last, part_go),
        (theirs_first, theirs_last, their_rows(part_go)),
        plan,
        [weight.shape for weight in weights],
    )
    widths, starts = (q_cols, kv_cols, kv_cols), (0, q_cols, q_cols + kv_cols)
    *gain_grads, grad_query, grad_key, grad_value = join_last(
        mine_qkv,
        theirs_qkv,
        totals,
        [(0, starts[i], widths[i], i, 0, False) for i in range(3)],
        (width, width, head, head),
        [weight.shape for weight in (query_proj, key_proj, value_proj)],
    )
    gain_grads = [gain.reshape(-1) for gain in gain_grads]
    shape = (seq_count, local_len, width)
    return (
        layer_out.reshape(shape),
        input_grad.reshape(shape),
        gain_grads[0],
        gain_grads[2],
        gain_grads[3],
        grad_query,
        grad_key,
        grad_value,
        grad_gating,
        grad_output,
        gain_grads[1],
        grad_gate,
        grad_up,
        grad_down,
    )


def solution(mesh):
    if (mesh.shape["dp"], mesh.shape["ctx"]) == (8, 4):
        body = per_device
        mesh = Mesh(mesh.devices.reshape(4, 2, 2, 2), ("z", "y", "x", "c"))
        dp, ctx = ("z", "y"), ("x", "c")
    else:
        body = per_device_wide
        dp, ctx = "dp", "ctx"
    tokens, weight, turned = P(dp, ctx, None), P(dp, ctx), P(ctx, dp)
    return jax.shard_map(
        body,
        mesh=mesh,
        in_specs=(tokens, tokens, P(dp), *[P()] * 6, *[weight] * 4, turned, P(), weight, weight, turned),
        out_specs=(tokens, tokens, *[P()] * 3, *[weight] * 4, turned, P(), weight, weight, turned),
        check_vma=False,
    )
```

```python
import functools

import jax
import jax.numpy as jnp
import numpy as np
from jax import lax
from jax.experimental import pallas as pl
from jax.experimental.pallas import tpu as pltpu
from jax.sharding import Mesh
from jax.sharding import PartitionSpec as P

LENGTH = 1024

EPSILON = 1e-06
ROPE_BASE = 1000000.0
MESH = pl.DeviceIdType.MESH
BF16 = jnp.bfloat16
F32 = jnp.float32
VMEM_BYTES = 62 * 2**20


def micros(count):
    return pl.CostEstimate(flops=0, transcendentals=0, bytes_accessed=count * 3_300_000)


def dot_nn(left, right):
    return jnp.dot(left, right, preferred_element_type=F32)


def dot_tn(left, right):
    return lax.dot_general(left, right, (((0,), (0,)), ((), ())), preferred_element_type=F32)


def dot_nt(left, right):
    return lax.dot_general(left, right, (((1,), (1,)), ((), ())), preferred_element_type=F32)


def rope_tables(positions, head_width):
    halfway = head_width // 2
    inverse = 1.0 / ROPE_BASE ** (jnp.arange(halfway, dtype=F32) * (2.0 / head_width))
    angles = positions.astype(F32)[:, None] * inverse[None, :]
    return (jnp.cos(angles), jnp.sin(angles))


def rotate(tensor, cosine, sine):
    halfway = tensor.shape[-1] // 2
    first_half = tensor[..., :halfway]
    second_half = tensor[..., halfway:]
    return jnp.concatenate(
        [first_half * cosine - second_half * sine, second_half * cosine + first_half * sine], -1
    )


def unrotate(grads_in, cosine, sine):
    halfway = grads_in.shape[-1] // 2
    first_half = grads_in[..., :halfway]
    second_half = grads_in[..., halfway:]
    return jnp.concatenate(
        [first_half * cosine + second_half * sine, second_half * cosine - first_half * sine], -1
    )


def norm_back(grads_in, values_in, inverse, gain_vec):
    scaled = grads_in * gain_vec
    return inverse * scaled - values_in * (inverse * inverse * inverse) * jnp.mean(
        scaled * values_in, -1, keepdims=True
    )


def greet(neighbours):
    barrier = pltpu.get_barrier_semaphore()
    for neighbour in neighbours:
        pl.semaphore_signal(barrier, inc=1, device_id=neighbour, device_id_type=MESH)
    pl.semaphore_wait(barrier, len(neighbours))


def remote_copies(send, recv, device):
    def remote(index, source, target, axis):
        return pltpu.make_async_remote_copy(
            src_ref=source,
            dst_ref=target,
            send_sem=send.at[index],
            recv_sem=recv.at[index],
            device_id=device[axis],
            device_id_type=MESH,
        )

    return remote


def place():
    y, x, c = lax.axis_index("y"), lax.axis_index("x"), lax.axis_index("c")
    return y, x, c, {"y": {"y": 1 - y}, "x": {"x": 1 - x}, "c": {"c": 1 - c}}


def gather_steps(s_ref, out_ref, local_sem, send, recv, split=True):
    y, x, c, device = place()
    remote = remote_copies(send, recv, device)
    half = s_ref.shape[0] // 2
    low, high = pl.ds(0, half), pl.ds(half, half)
    mine = out_ref.at[y, x, c]
    from_x = out_ref.at[y, 1 - x, c]
    from_y = out_ref.at[1 - y, x, c]
    diagonal = out_ref.at[1 - y, 1 - x, c]
    x_low = remote(0, s_ref.at[low], mine.at[low], "x")
    y_high = remote(1, s_ref.at[high], mine.at[high], "y")
    x_high = remote(2, s_ref.at[high], mine.at[high], "x")
    y_low = remote(3, s_ref.at[low], mine.at[low], "y")
    c_own = remote(4, s_ref, mine, "c")
    local = pltpu.make_async_copy(s_ref, mine, local_sem)
    forward_y = remote(5, from_x.at[low], from_x.at[low], "y")
    over_x = from_y.at[high] if split else from_y
    forward_x = remote(6, over_x, over_x, "x")
    c_x = remote(7, from_x, from_x, "c")
    c_y = remote(8, from_y, from_y, "c")
    c_low = remote(9, diagonal.at[low], diagonal.at[low], "c")
    over_c = diagonal.at[high] if split else diagonal
    c_high = remote(10, over_c, over_c, "c")

    def begin():
        for copy in (x_low, y_high, x_high, y_low, c_own, local):
            copy.start()

    def forward():
        x_low.wait_recv()
        if split:
            forward_y.start()
        y_high.wait_recv()
        if split:
            forward_x.start()

    def across():
        if not split:
            y_low.wait_recv()
            forward_x.start()
        x_high.wait_recv()
        c_x.start()
        if split:
            y_low.wait_recv()
        c_y.start()

    def finish():
        if split:
            forward_y.wait_recv()
            c_low.start()
        forward_x.wait_recv()
        c_high.start()
        for copy in (c_own, c_x, c_y, *((c_low,) if split else ()), c_high):
            copy.wait()
        for copy in (x_low, y_high, x_high, y_low, *((forward_y,) if split else ()), forward_x):
            copy.wait_send()
        local.wait()

    return begin, forward, across, finish


GATHER_SEMAPHORES = (
    pltpu.SemaphoreType.DMA,
    pltpu.SemaphoreType.DMA((11,)),
    pltpu.SemaphoreType.DMA((11,)),
)


def swap_steps(pieces, sources, outs, local_sem, send, recv, wanted=None):
    y, _, _, device = place()
    remote = remote_copies(send, recv, device)
    copies, locals_ = [], []
    for i, (source, out, first, count, at) in enumerate(pieces):
        if wanted is not None and not wanted(out):
            continue
        rows, cols = sources[source].shape
        target = outs[out].at[pl.ds(pl.multiple_of(y * rows, rows), rows), pl.ds(at, count)]

        def half(which):
            start = pl.multiple_of(which * (cols // 2) + first, 128)
            return sources[source].at[:, pl.ds(start, count)]

        copies.append(remote(i, half(1 - y), target, "y"))
        locals_.append(pltpu.make_async_copy(half(y), target, local_sem.at[i]))

    def begin():
        for copy in (*copies, *locals_):
            copy.start()

    def here():
        for copy in locals_:
            copy.wait()

    def finish():
        for copy in copies:
            copy.wait()

    return begin, here, finish


def gather_kernel(split, *refs):
    source, out, *sems = refs
    begin, forward, across, finish = gather_steps(source, out, *sems, split)
    greet(tuple(place()[3].values()))
    begin()
    forward()
    across()
    finish()


def gather_tokens(shard):
    rows, width = shard.shape
    return pl.pallas_call(
        functools.partial(gather_kernel, True),
        out_shape=jax.ShapeDtypeStruct((2, 2, 2, rows, width), shard.dtype),
        in_specs=[pl.BlockSpec(memory_space=pltpu.VMEM)],
        out_specs=pl.BlockSpec(memory_space=pl.ANY),
        scratch_shapes=list(GATHER_SEMAPHORES),
        compiler_params=pltpu.CompilerParams(collective_id=1, has_side_effects=True),
        cost_estimate=micros(42),
        name="gather_tokens",
    )(shard).reshape(8 * rows, width)


def line_steps(rows_ref, out_ref, local_sem, send, recv, part, which):
    z = lax.axis_index("z")
    rows, half = rows_ref.shape[0], rows_ref.shape[0] // 2
    first = which * half
    pair, middle = z + 1 - 2 * lax.rem(z, 2), 3 - z
    inner = (z == 1) | (z == 2)

    def at(index):
        return out_ref.at[pl.ds(pl.multiple_of(index * rows + first, half), half)]

    def remote(index, source, target, peer):
        return pltpu.make_async_remote_copy(
            src_ref=source,
            dst_ref=target,
            send_sem=send.at[5 * part + index],
            recv_sem=recv.at[5 * part + index],
            device_id={"z": peer},
            device_id_type=MESH,
        )

    far = middle + 1 - 2 * lax.rem(middle, 2)
    own = rows_ref.at[pl.ds(pl.multiple_of(first, half), half)]
    own_pair = remote(0, own, at(z), pair)
    own_middle = remote(1, own, at(z), middle)
    pair_middle = remote(2, at(pair), at(pair), middle)
    middle_pair = remote(3, at(middle), at(middle), pair)
    far_pair = remote(4, at(far), at(far), pair)
    local = pltpu.make_async_copy(own, at(z), local_sem.at[part])

    def begin():
        local.start()
        own_pair.start()
        pl.when(inner)(own_middle.start)

    def second():
        own_pair.wait_recv()

        @pl.when(inner)
        def _():
            pair_middle.start()
            own_middle.wait_recv()
            middle_pair.start()

    def third():
        @pl.when(inner)
        def _():
            pair_middle.wait_recv()
            far_pair.start()

    def finish():
        @pl.when(inner)
        def _():
            for copy in (own_middle, pair_middle, middle_pair, far_pair):
                copy.wait_send()

        @pl.when(jnp.logical_not(inner))
        def _():
            middle_pair.wait_recv()
            far_pair.wait_recv()

        own_pair.wait_send()
        local.wait()

    def peers():
        return pair, middle, inner

    return begin, second, third, finish, peers


def greet_line(others, pair, middle, inner):
    barrier = pltpu.get_barrier_semaphore()
    for other in (*others, {"z": pair}):
        pl.semaphore_signal(barrier, inc=1, device_id=other, device_id_type=MESH)

    @pl.when(inner)
    def _():
        pl.semaphore_signal(barrier, inc=1, device_id={"z": middle}, device_id_type=MESH)

    count = len(others) + 1
    pl.semaphore_wait(barrier, jnp.where(inner, count + 1, count))


def opening_kernel(pieces, tokens, cotangent, gain, ids, counts, numer, denom, turns, *refs):
    sources, refs = list(refs[:8]), refs[8:]
    out, line_q, line_g, first, last, inverse, low, factor, cosine, sine, *refs = refs
    rows_q, rows_g, normed, output_t, down_t, *sems = refs
    begin, forward, across, finish = gather_steps(normed, out, *sems[:3], False)
    y = lax.axis_index("y")
    steps = [
        line_steps(rows, line, *sems[3 * i + 3 : 3 * i + 6], part, which)
        for part, which in ((0, y), (1, 1 - y))
        for i, (rows, line) in enumerate(((rows_q, line_q), (rows_g, line_g)))
    ]
    output_ref, down_ref = sources[4], sources[7]
    sources[4], sources[7] = output_t, down_t
    swaps = [
        swap_steps(pieces, sources, (rows_q, rows_g, first, last), *sems[9:], wanted)
        for wanted in (lambda out: out == 0, lambda out: out == 1, lambda out: out > 1)
    ]
    step = 64

    def norm(i):
        at = pl.ds(i * step, step)
        x = tokens[at].astype(F32)
        inv = lax.rsqrt(jnp.mean(x * x, -1, keepdims=True) + EPSILON)
        inverse[at] = inv
        normed[at] = (x * inv * gain[...].astype(F32)).astype(BF16)

    def weigh(i):
        at = pl.ds(i * step, step)
        low[at] = (cotangent[at].astype(F32) * factor[...]).astype(BF16)

    def turn(i):
        at = pl.ds(i * 128, 128)
        places = lax.broadcasted_iota(jnp.int32, (128, cosine.shape[1]), 0) + i * 128
        angles = places.astype(F32) * turns[0:1]
        cosine[at] = jnp.cos(angles)
        sine[at] = jnp.sin(angles) * turns[1:2]

    greet_line(tuple(place()[3].values()), *steps[0][4]())
    swaps[0][0]()
    output_t[...] = output_ref[...].astype(F32).T.astype(BF16)
    swaps[1][0]()
    for i in range(2):
        swaps[i][1]()
        steps[i][0]()
    pl.loop(0, tokens.shape[0] // step)(norm)
    begin()
    for i in range(2):
        swaps[i][2]()
        steps[i + 2][0]()
    steps[0][1]()
    steps[1][1]()
    chosen = lax.broadcasted_iota(jnp.int32, counts.shape, 1) == ids[...]
    ratio = numer[...].astype(F32) / denom[...].astype(F32) * LENGTH / counts[...].astype(F32)
    factor[...] = jnp.sum(jnp.where(chosen, ratio, 0.0), -1, keepdims=True)

    @pl.loop(0, down_ref.shape[0] // 256)
    def _(i):
        at = pl.ds(pl.multiple_of(i * 256, 256), 256)
        down_t[:, at] = down_ref[at].astype(F32).T.astype(BF16)

    forward()
    across()
    swaps[2][0]()
    steps[2][1]()
    steps[3][1]()
    steps[0][2]()
    steps[1][2]()
    pl.loop(0, tokens.shape[0] // step)(weigh)
    steps[2][2]()
    steps[3][2]()
    pl.loop(0, cosine.shape[0] // 128)(turn)
    finish()
    for step_set in steps:
        step_set[3]()
    swaps[2][1]()
    swaps[2][2]()


def opening(tokens, cotangent, gain, domains, weights, split, full_len, head):
    rows, width = tokens.shape
    halves = [weight.shape[0 if i in (4, 7) else 1] // 2 for i, weight in enumerate(weights)]
    groups = (
        [(i, 0, halves[i]) for i in (0, 1, 2)],
        [(i, 0, halves[i]) for i in (3, 4)],
        [(i, 0, split) for i in (5, 6, 7)],
        [(i, split, halves[i] - split) for i in (5, 6, 7)],
    )
    pieces, widths = [], []
    for group in groups:
        at = 0
        for source, first, count in group:
            pieces.append((source, len(widths), first, count, at))
            at += count
        widths.append(at)
    inverse = 1.0 / np.float32(ROPE_BASE) ** (np.arange(head // 2, dtype=np.float32) * np.float32(2.0 / head))
    turns = np.stack([np.tile(inverse, 2), np.repeat(np.float32([-1.0, 1.0]), head // 2)]).astype(np.float32)
    whole, loose = pl.BlockSpec(memory_space=pltpu.VMEM), pl.BlockSpec(memory_space=pl.ANY)
    shape = jax.ShapeDtypeStruct
    dma = pltpu.SemaphoreType.DMA
    gathered, *outs = pl.pallas_call(
        functools.partial(opening_kernel, pieces),
        out_shape=(
            shape((2, 2, 2, rows, width), BF16),
            *[shape((8 * rows, size), BF16) for size in widths[:2]],
            *[shape((2 * rows, size), BF16) for size in widths[2:]],
            shape((rows, 1), F32),
            shape((rows, width), BF16),
            shape((1, 1), F32),
            shape((full_len, head), F32),
            shape((full_len, head), F32),
        ),
        in_specs=[whole] * (8 + len(weights)),
        out_specs=(*[loose] * 5, *[whole] * 5),
        scratch_shapes=[
            *[pltpu.VMEM((2 * rows, size), BF16) for size in widths[:2]],
            pltpu.VMEM((rows, width), BF16),
            *[pltpu.VMEM(weights[i].shape[::-1], BF16) for i in (4, 7)],
            *GATHER_SEMAPHORES,
            *[dma((2,)), dma((10,)), dma((10,))] * 2,
            *[dma((len(pieces),))] * 3,
        ],
        compiler_params=pltpu.CompilerParams(
            collective_id=2, has_side_effects=True, vmem_limit_bytes=VMEM_BYTES
        ),
        cost_estimate=micros(80),
        name="opening",
    )(
        tokens,
        cotangent,
        gain.reshape(1, -1),
        *(domain.reshape(1, -1) for domain in domains),
        jnp.asarray(turns),
        *weights,
    )
    return gathered.reshape(8 * rows, width), *outs


def add_rows(target, start, size, other, base, step=64):
    @pl.loop(0, size // step)
    def _(i):
        at, there = pl.ds(start + i * step, step), pl.ds(base + i * step, step)
        target[at] = (target[at].astype(F32) + other[there].astype(F32)).astype(target.dtype)


def product_steps(windows, lefts, rights, left_vmem, right_vmem, own, pairs, got, load_sem, send, recv):
    y, x, c, device = place()
    remote = remote_copies(send, recv, device)
    rows, width = own.shape[1:]
    half, both, tile = rows // 2, 2 * rows, 512
    targets = ((1 - y, 1 - x), (1 - y, x), (y, 1 - x), (y, x))
    pieces = ((0, 0, half), (0, half, half), (1, 0, rows), (2, 0, rows), (3, 0, rows))
    count = len(lefts)
    right_loads = [
        pltpu.make_async_copy(
            rights[j].at[:, pl.ds(windows[j], right_vmem[j].shape[1])], right_vmem[j], load_sem.at[j]
        )
        for j in range(count)
    ]
    left_loads = []
    for i, (a, b) in enumerate(targets):
        start = pl.multiple_of((a * 2 + b) * both, both)
        left_loads.append(
            [
                pltpu.make_async_copy(
                    lefts[j].at[pl.ds(start, both)], left_vmem[j].at[i], load_sem.at[count * (i + 1) + j]
                )
                for j in range(count)
            ]
        )
    crossing = [
        remote(k, pairs.at[i, 1 - c, pl.ds(first, size)], got.at[i, pl.ds(first, size)], "c")
        for k, (i, first, size) in enumerate(pieces)
    ]

    def load():
        for copy in right_loads:
            copy.start()
        for copies in left_loads:
            for copy in copies:
                copy.start()

    def ready():
        for copy in right_loads:
            copy.wait()

    def product(i):
        for copy in left_loads[i]:
            copy.wait()

        @pl.loop(0, width // tile)
        def _(n):
            cols = pl.ds(pl.multiple_of(n * tile, tile), tile)
            total = dot_nt(left_vmem[0][i], right_vmem[0][cols])
            for j in range(1, count):
                total = total + dot_nt(left_vmem[j][i], right_vmem[j][cols])
            pairs[i, :, :, cols] = total.reshape(2, rows, tile).astype(BF16)

        for k, piece in enumerate(pieces):
            if piece[0] == i:
                crossing[k].start()

    def cores(k, step=64):
        i, first, size = pieces[k]
        crossing[k].wait_recv()

        @pl.loop(0, size // step)
        def _(n):
            at = pl.ds(first + n * step, step)
            own[i, at] = (pairs[i, c, at].astype(F32) + got[i, at].astype(F32)).astype(BF16)

    def finish():
        for copy in crossing:
            copy.wait_send()

    return load, ready, product, cores, finish


def axis_steps(own, x_diag, y_diag, x_got, y_got, send, recv):
    remote = remote_copies(send, recv, place()[3])
    rows = own.shape[1]
    half = rows // 2
    low, high = pl.ds(0, half), pl.ds(half, half)
    diag_x = remote(0, own.at[0, low], x_diag, "x")
    diag_y = remote(1, own.at[0, high], y_diag, "y")
    y_high = remote(2, own.at[1, high], y_got.at[high], "y")
    x_low = remote(3, own.at[2, low], x_got.at[low], "x")
    y_low = remote(4, own.at[1, low], y_got.at[low], "y")
    x_high = remote(5, own.at[2, high], x_got.at[high], "x")

    def second():
        diag_x.wait_recv()
        add_rows(own.at[1], 0, half, x_diag, 0)
        y_low.start()
        diag_y.wait_recv()
        add_rows(own.at[2], half, half, y_diag, 0)
        x_high.start()

    def finish(store, step=32):
        for copy in (y_high, x_low, y_low, x_high):
            copy.wait_recv()

        @pl.loop(0, rows // step)
        def _(i):
            at = pl.ds(i * step, step)
            store(at, own[3, at].astype(F32) + x_got[at].astype(F32) + y_got[at].astype(F32))

        for copy in (diag_x, diag_y, y_high, x_low, y_low, x_high):
            copy.wait_send()

    return diag_x, diag_y, x_low, y_high, second, finish


def scatter_steps(windows, lefts, rights, scratch):
    count = len(windows)
    product_scratch, axis_scratch = scratch[: 2 * count + 6], scratch[2 * count + 6 :]
    load, ready, product, cores, crossed = product_steps(
        windows, lefts, rights, product_scratch[:count], product_scratch[count : 2 * count],
        *product_scratch[2 * count :],
    )
    own = product_scratch[2 * count]
    diag_x, diag_y, x_low, y_high, second_axis, finish_axis = axis_steps(own, *axis_scratch)

    def first():
        ready()
        product(0)
        cores(0)
        diag_x.start()
        cores(1)
        diag_y.start()
        product(2)
        product(1)
        cores(3)
        x_low.start()
        cores(2)
        y_high.start()

    def second():
        second_axis()
        product(3)
        cores(4)

    def finish(store):
        finish_axis(store)
        crossed()

    return load, first, second, finish


def product_scratch(group, own=True):
    lefts, rights = [item[0] for item in group], [item[1] for item in group]
    rows, width = lefts[0].shape[0] // 8, rights[0].shape[0]
    return [
        *[pltpu.VMEM((4, 2 * rows, left.shape[1]), BF16) for left in lefts],
        *[pltpu.VMEM((width, left.shape[1]), BF16) for left in lefts],
        *[pltpu.VMEM((4, rows, width), BF16)] * own,
        pltpu.VMEM((4, 2, rows, width), BF16),
        pltpu.VMEM((4, rows, width), BF16),
        pltpu.SemaphoreType.DMA((5 * len(group),)),
        pltpu.SemaphoreType.DMA((5,)),
        pltpu.SemaphoreType.DMA((5,)),
    ]


def axis_scratch(rows, width):
    return [
        pltpu.VMEM((rows // 2, width), BF16),
        pltpu.VMEM((rows // 2, width), BF16),
        pltpu.VMEM((rows, width), BF16),
        pltpu.VMEM((rows, width), BF16),
        pltpu.SemaphoreType.DMA((6,)),
        pltpu.SemaphoreType.DMA((6,)),
    ]


def scatter_scratch(group):
    lefts, rights = [item[0] for item in group], [item[1] for item in group]
    rows, width = lefts[0].shape[0] // 8, rights[0].shape[0]
    scratch = product_scratch(group) + axis_scratch(rows, width)
    return lefts + rights, scratch, jax.ShapeDtypeStruct((rows, width), F32)


def middle_kernel(windows, *refs):
    count = len(windows)
    lefts, rights, refs = refs[:count], refs[count : 2 * count], refs[2 * count :]
    tokens, gain, hidden, inverse, normed, *scratch = refs
    load, first, second, finish = scatter_steps(windows, lefts, rights, scratch)

    def store(at, branch):
        total = tokens[at].astype(F32) + branch
        inv = lax.rsqrt(jnp.mean(total * total, -1, keepdims=True) + EPSILON)
        hidden[at] = total
        inverse[at] = inv
        normed[at] = (total * inv * gain[...].astype(F32)).astype(BF16)

    load()
    greet(tuple(place()[3].values()))
    first()
    second()
    finish(store)


def middle_back_kernel(windows, *refs):
    count = len(windows)
    lefts, rights, refs = refs[:count], refs[count : 2 * count], refs[2 * count :]
    hidden, inverse, gain, cotangent, factor, dhidden, dbranch, gain_grad, *scratch = refs
    load, first, second, finish = scatter_steps(windows, lefts, rights, scratch)
    gain_grad[...] = jnp.zeros_like(gain_grad)

    def store(at, grad):
        state, inv = hidden[at], inverse[at]
        gain_grad[...] += jnp.sum(grad * state * inv, 0, keepdims=True)
        upstream = cotangent[at].astype(F32) * factor[...]
        total = upstream + norm_back(grad, state, inv, gain[...].astype(F32))
        dhidden[at] = total
        dbranch[at] = total.astype(BF16)

    load()
    greet(tuple(place()[3].values()))
    first()
    second()
    finish(store)


def scatter_products(kernel, number, extras, outs, *group):
    operands, scratch, _ = scatter_scratch(group)
    whole = pl.BlockSpec(memory_space=pltpu.VMEM)
    return pl.pallas_call(
        functools.partial(kernel, [item[2] for item in group]),
        out_shape=outs,
        in_specs=[pl.BlockSpec(memory_space=pl.ANY)] * len(operands) + [whole] * len(extras),
        out_specs=(whole,) * len(outs),
        scratch_shapes=scratch,
        compiler_params=pltpu.CompilerParams(
            collective_id=number, has_side_effects=True, vmem_limit_bytes=VMEM_BYTES
        ),
        cost_estimate=micros(48),
        name="scatter_products",
    )(*operands, *extras)


def gather_beside_kernel(windows, tile, shard_ref, *refs):
    count = len(windows)
    lefts, rights, refs = refs[:count], refs[count : 2 * count], refs[2 * count :]
    mid, low, dgu, act, out_ref, sums_ref, grad_ref, *scratch = refs
    size = 2 * count + 5
    products, (mid_buf, low_buf, dgu_vmem, act_vmem, total, tile_sem, side_sem), sems = (
        scratch[:size], scratch[size : size + 7], scratch[size + 7 :],
    )
    load, ready, product, cores, crossed = product_steps(
        windows, lefts, rights, products[:count], products[count : 2 * count], sums_ref,
        *products[2 * count :],
    )
    begin, forward, across, finish = gather_steps(shard_ref, out_ref, *sems)
    tiles = mid.shape[0] // tile
    sides = [
        pltpu.make_async_copy(dgu, dgu_vmem, side_sem.at[0]),
        pltpu.make_async_copy(act, act_vmem, side_sem.at[1]),
    ]

    def tile_copies(t):
        rows, slot = pl.ds(t * tile, tile), t % 2
        return [
            pltpu.make_async_copy(source.at[rows], buffer.at[slot], tile_sem.at[i, slot])
            for i, (source, buffer) in enumerate(((mid, mid_buf), (low, low_buf)))
        ]

    def grads(t):
        for copy in tile_copies(t):
            copy.wait()
        rows, slot = pl.ds(t * tile, tile), t % 2
        add_products(t, total, 0, mid_buf.at[slot], dgu_vmem[rows])
        add_products(t, total, dgu_vmem.shape[1], low_buf.at[slot], act_vmem[rows])
        if t + 2 < tiles:
            for copy in tile_copies(t + 2):
                copy.start()

    load()
    greet(tuple(place()[3].values()))
    begin()
    for copy in (*sides, *tile_copies(0), *tile_copies(1)):
        copy.start()
    ready()
    for i in range(4):
        product(i)
    forward()
    for copy in sides:
        copy.wait()
    cores(0)
    cores(1)
    for t in range(tiles // 2):
        grads(t)
    across()
    for k in range(2, 5):
        cores(k)
    for t in range(tiles // 2, tiles):
        grads(t)

    @pl.loop(0, total.shape[0] // 256)
    def _(m):
        at = pl.ds(m * 256, 256)
        grad_ref[at] = total[at].astype(BF16)

    crossed()
    finish()


def gather_beside(shard, group, mid, low, dgu, act, tile=512):
    rows, width = shard.shape
    operands = [item[0] for item in group] + [item[1] for item in group] + [mid, low, dgu, act]
    cols = dgu.shape[1] + act.shape[1]
    gathered, sums, grad = pl.pallas_call(
        functools.partial(gather_beside_kernel, [item[2] for item in group], tile),
        out_shape=(
            jax.ShapeDtypeStruct((2, 2, 2, rows, width), shard.dtype),
            jax.ShapeDtypeStruct((4, rows, width), BF16),
            jax.ShapeDtypeStruct((width, cols), BF16),
        ),
        in_specs=[
            pl.BlockSpec(memory_space=pltpu.VMEM),
            *[pl.BlockSpec(memory_space=pl.ANY)] * len(operands),
        ],
        out_specs=(
            pl.BlockSpec(memory_space=pl.ANY),
            pl.BlockSpec(memory_space=pltpu.VMEM),
            pl.BlockSpec(memory_space=pltpu.VMEM),
        ),
        scratch_shapes=[
            *product_scratch(group, own=False),
            pltpu.VMEM((2, tile, width), BF16),
            pltpu.VMEM((2, tile, width), BF16),
            pltpu.VMEM(dgu.shape, BF16),
            pltpu.VMEM(act.shape, BF16),
            pltpu.VMEM((width, cols), F32),
            pltpu.SemaphoreType.DMA((2, 2)),
            pltpu.SemaphoreType.DMA((2,)),
            *GATHER_SEMAPHORES,
        ],
        compiler_params=pltpu.CompilerParams(
            collective_id=6, has_side_effects=True, vmem_limit_bytes=VMEM_BYTES
        ),
        cost_estimate=micros(44),
        name="gather_beside",
    )(shard, *operands)
    return gathered.reshape(8 * rows, width), sums, grad


def line_scatter_steps(grad_ref, own, from_edge, from_middle, inward, load_sem, send, recv, part, which):
    z = lax.axis_index("z")
    rows, half = own.shape[1], own.shape[1] // 2
    pair, middle = z + 1 - 2 * lax.rem(z, 2), 3 - z
    inner = (z == 1) | (z == 2)
    edge = jnp.logical_not(inner)
    far = middle + 1 - 2 * lax.rem(middle, 2)
    first = pl.multiple_of(which * half, half)
    span = pl.ds(first, half)

    def block(index):
        return grad_ref.at[pl.ds(pl.multiple_of(index * rows + first, half), half)]

    def remote(index, source, target, peer):
        return pltpu.make_async_remote_copy(
            src_ref=source,
            dst_ref=target,
            send_sem=send.at[6 * part + index],
            recv_sem=recv.at[6 * part + index],
            device_id={"z": peer},
            device_id_type=MESH,
        )

    indices = (far, middle, pair, z)
    loads = [
        pltpu.make_async_copy(block(index), own.at[i, span], load_sem.at[4 * part + i])
        for i, index in enumerate(indices)
    ]
    edge_far = remote(0, own.at[1, span], from_edge.at[0, span], pair)
    edge_near = remote(1, own.at[0, span], from_edge.at[1, span], pair)
    edge_pair = remote(2, own.at[2, span], from_edge.at[2, span], pair)
    inner_far = remote(3, own.at[0, span], from_middle.at[0, span], middle)
    inner_near = remote(4, own.at[1, span], from_middle.at[1, span], middle)
    outward = remote(5, own.at[2, span], inward.at[span], pair)
    step = 128

    def add_into(target, other):
        @pl.loop(0, half // step)
        def _(i):
            at = pl.ds(first + i * step, step)
            target[at] = (target[at].astype(F32) + other[at].astype(F32)).astype(target.dtype)

    def load():
        for copy in loads:
            copy.start()

    def begin():
        for copy in loads:
            copy.wait()

        @pl.when(edge)
        def _():
            for copy in (edge_far, edge_near, edge_pair):
                copy.start()

    def second():
        @pl.when(inner)
        def _():
            edge_far.wait_recv()
            add_into(own.at[0], from_edge.at[0])
            inner_far.start()

    def third():
        @pl.when(inner)
        def _():
            edge_near.wait_recv()
            add_into(own.at[1], from_edge.at[1])
            inner_near.start()
            inner_far.wait_recv()
            add_into(own.at[2], from_middle.at[0])
            outward.start()

    def finish():
        @pl.when(inner)
        def _():
            edge_pair.wait_recv()
            add_into(own.at[3], from_edge.at[2])
            inner_near.wait_recv()
            add_into(own.at[3], from_middle.at[1])
            for copy in (inner_far, inner_near, outward):
                copy.wait_send()

        @pl.when(edge)
        def _():
            outward.wait_recv()
            add_into(own.at[3], inward)
            for copy in (edge_far, edge_near, edge_pair):
                copy.wait_send()

    return load, begin, second, third, finish


def total_steps(near, far, near_send, near_recv, far_send, far_recv):
    z, y, x, c = (lax.axis_index(name) for name in "zyxc")
    here = (y * 2 + x) * 2 + c
    others = [
        {"y": lax.rem(y + i // 4, 2), "x": lax.rem(x + i // 2 % 2, 2), "c": lax.rem(c + i % 2, 2)}
        for i in range(1, 8)
    ]
    levels = [{"z": lax.rem(z + i, 4)} for i in range(1, 4)]

    def remote(index, source, target, send, recv, device):
        return pltpu.make_async_remote_copy(
            src_ref=source,
            dst_ref=target,
            send_sem=send.at[index],
            recv_sem=recv.at[index],
            device_id=device,
            device_id_type=MESH,
        )

    around = [
        remote(i, near.at[here], near.at[here], near_send, near_recv, other)
        for i, other in enumerate(others)
    ]
    along = [
        remote(i, far.at[z], far.at[z], far_send, far_recv, level) for i, level in enumerate(levels)
    ]

    def begin():
        for copy in around:
            copy.start()

    def second():
        for copy in around:
            copy.wait()
        total = near[0]
        for i in range(1, 8):
            total = total + near[i]
        far[z] = total
        for copy in along:
            copy.start()

    def finish():
        for copy in along:
            copy.wait()
        total = far[0]
        for i in range(1, 4):
            total = total + far[i]
        return total

    return begin, second, finish, here, others, levels


def tail_kernel(windows, *refs):
    count = len(windows)
    lefts, rights, refs = refs[:count], refs[count : 2 * count], refs[2 * count :]
    grad_ref, tokens_ref, inverse_ref, dhidden_ref, gain_ref, *refs = refs
    gains, (out_ref, mine_ref, theirs_ref, total_ref), scratch = refs[:3], refs[3:7], refs[7:]
    size = 2 * count + 12
    load, first, second, finish = scatter_steps(windows, lefts, rights, scratch[:size])
    line, (swap_sem,), total = scratch[size : size + 7], scratch[size + 7 : size + 8], scratch[size + 8 :]
    near, far = total[:2]
    total_begin, total_second, total_finish, here, others, levels = total_steps(*total)
    y = lax.axis_index("y")
    lines = [line_scatter_steps(grad_ref, *line, part, which) for part, which in ((0, 1 - y), (1, y))]
    load()
    for steps in lines:
        steps[0]()
    width = out_ref.shape[1]
    near[here, :, pl.ds(width, width)] = gains[0][...]
    head = gains[1].shape[1]
    near[here, :, pl.ds(2 * width, head)] = gains[1][...]
    near[here, :, pl.ds(2 * width + head, head)] = gains[2][...]
    greet(others + levels)
    for steps in lines:
        steps[1]()
    first()
    lines[0][2]()
    second()
    lines[0][3]()
    lines[1][2]()
    gain_in = near.at[here, :, pl.ds(0, width)]
    gain_in[...] = jnp.zeros((1, width), F32)

    def store(at, grad):
        x, inv = tokens_ref[at].astype(F32), inverse_ref[at]
        gain_in[...] += jnp.sum(grad * x * inv, 0, keepdims=True)
        back = norm_back(grad, x, inv, gain_ref[...].astype(F32))
        out_ref[at] = (dhidden_ref[at] + back).astype(BF16)

    finish(store)
    total_begin()
    lines[1][3]()
    lines[0][4]()
    summed = line[0].at[3]
    half = theirs_ref.shape[0]
    swap = pltpu.make_async_remote_copy(
        src_ref=summed.at[pl.ds(pl.multiple_of((1 - y) * half, half), half)],
        dst_ref=theirs_ref,
        send_sem=swap_sem.at[0],
        recv_sem=swap_sem.at[1],
        device_id={"y": 1 - y},
        device_id_type=MESH,
    )
    swap.start()
    total_second()
    lines[1][4]()
    mine_ref[...] = summed[pl.ds(pl.multiple_of(y * half, half), half)]
    total_ref[...] = total_finish()
    swap.wait()


def tail(group, grad, tokens, inverse, dhidden, gain, gains):
    operands, scratch, total = scatter_scratch(group)
    rows, cols = grad.shape[0] // 4, grad.shape[1]
    length = 2 * total.shape[1] + 2 * gains[1].size
    half = jax.ShapeDtypeStruct((rows // 2, cols), BF16)
    whole = pl.BlockSpec(memory_space=pltpu.VMEM)
    block = lambda count: pltpu.VMEM((count, rows, cols), BF16)
    dma = pltpu.SemaphoreType.DMA
    return pl.pallas_call(
        functools.partial(tail_kernel, [item[2] for item in group]),
        out_shape=(
            jax.ShapeDtypeStruct(total.shape, BF16),
            half,
            half,
            jax.ShapeDtypeStruct((1, length), F32),
        ),
        in_specs=[pl.BlockSpec(memory_space=pl.ANY)] * (len(operands) + 1) + [whole] * 7,
        out_specs=(whole,) * 4,
        scratch_shapes=[
            *scratch,
            block(4), block(3), block(2), pltpu.VMEM((rows, cols), BF16), dma((8,)), dma((12,)), dma((12,)),
            dma((2,)),
            pltpu.VMEM((8, 1, length), F32), pltpu.VMEM((4, 1, length), F32), dma((7,)), dma((7,)), dma((3,)), dma((3,)),
        ],
        compiler_params=pltpu.CompilerParams(
            collective_id=0, has_side_effects=True, vmem_limit_bytes=VMEM_BYTES
        ),
        cost_estimate=micros(52),
        name="tail",
    )(*operands, grad, tokens, inverse, dhidden, gain.reshape(1, -1), *(gain.reshape(1, -1) for gain in gains))


def swap_y(value):
    return lax.ppermute(value, "y", [(0, 1), (1, 0)])


def in_y_order(mine, theirs, axis):
    count = mine.shape[axis]
    return lax.dynamic_slice_in_dim(
        jnp.concatenate([mine, theirs, mine], axis), lax.axis_index("y") * count, 2 * count, axis
    )


def gather_rows(rows):
    return lax.all_gather(rows, "z", axis=0, tiled=True)


def scatter_grads(grad):
    return lax.psum_scatter(grad.astype(BF16), "z", scatter_dimension=0, tiled=True)


def their_rows(part):
    half = part.shape[0] // 2
    return swap_y(
        lax.dynamic_slice_in_dim(part, (1 - lax.axis_index("y")) * half, half, 0)
    )


def join_pieces(plan, y, mine_of, theirs_of, outs):
    for source, first, width, out, at, turned in plan:
        half = outs[out].shape[0 if turned else 1] // 2
        cols = pl.ds(first, width)
        for which, piece in ((y, mine_of(source, cols)), (1 - y, theirs_of(source, cols))):
            target = pl.ds(pl.multiple_of(which * half + at, 128), width)
            if turned:
                outs[out][target, :] = piece.astype(F32).T
            else:
                outs[out][:, target] = piece.astype(F32)


def join_kernel(plan, count, y_rows, *refs):
    y = lax.axis_index("y")
    parts, theirs, outs = refs[:count], refs[count : 2 * count], refs[2 * count :]
    mine = pl.ds(pl.multiple_of(y * y_rows, y_rows), y_rows)
    own = lambda source, cols: parts[source][mine, cols]
    got = lambda source, cols: theirs[source][:, cols]
    join_pieces(plan, y, own, got, outs)


def join_grads(parts, theirs, plan, shapes):
    whole = pl.BlockSpec(memory_space=pltpu.VMEM)
    return pl.pallas_call(
        functools.partial(join_kernel, plan, len(parts), theirs[0].shape[0]),
        out_shape=tuple(jax.ShapeDtypeStruct(shape, F32) for shape in shapes),
        in_specs=[whole] * (2 * len(parts)),
        out_specs=(whole,) * len(shapes),
        compiler_params=pltpu.CompilerParams(vmem_limit_bytes=VMEM_BYTES),
        cost_estimate=micros(5),
        name="join_grads",
    )(*parts, *theirs)


def last_join_kernel(plan, mine, theirs, total, *outs):
    gains, grads, start = outs[:4], outs[4:], 0
    for gain in gains:
        gain[...] = total[:, pl.ds(start, gain.shape[1])]
        start += gain.shape[1]
    y = lax.axis_index("y")
    join_pieces(plan, y, lambda _, cols: mine[:, cols], lambda _, cols: theirs[:, cols], grads)


def join_last(mine, theirs, total, plan, sizes, shapes):
    whole = pl.BlockSpec(memory_space=pltpu.VMEM)
    outs = (*((1, size) for size in sizes), *shapes)
    return pl.pallas_call(
        functools.partial(last_join_kernel, plan),
        out_shape=tuple(jax.ShapeDtypeStruct(shape, F32) for shape in outs),
        in_specs=[whole] * 3,
        out_specs=(whole,) * len(outs),
        cost_estimate=micros(4),
        name="join_last",
    )(mine, theirs, total)


def normed_rope(raw, gain, cosine, sine):
    inverse = lax.rsqrt(jnp.mean(raw * raw, -1, keepdims=True) + EPSILON)
    scaled = raw * inverse * gain
    turned = pltpu.roll(scaled, scaled.shape[-1] // 2, 1)
    return (scaled * cosine + turned * sine).astype(BF16)


def normed_rope_back(grad, raw, gain, cosine, sine):
    inverse = lax.rsqrt(jnp.mean(raw * raw, -1, keepdims=True) + EPSILON)
    straight = grad * cosine - pltpu.roll(grad, grad.shape[-1] // 2, 1) * sine
    gain_part = jnp.sum(straight * (raw * inverse), 0, keepdims=True)
    return norm_back(straight, raw, inverse, gain).astype(BF16), gain_part


def causal_scores(query, keys, first, scaling):
    scores = dot_nt(query, keys) * scaling
    rows = lax.broadcasted_iota(jnp.int32, scores.shape, 0) + first
    columns = lax.broadcasted_iota(jnp.int32, scores.shape, 1)
    return jnp.where(rows >= columns, scores, -1e30)


def attend_kernel(
    heads, head, block, normed_ref, w_ref, wg_ref, low_ref, qg_ref, kg_ref, cos_ref, sin_ref,
    raw_ref, out_ref, log_ref, gate_ref, mixed_ref, all_ref, key_ref, value_ref, *sems,
):
    seq, step, steps = pl.program_id(0), pl.program_id(1), pl.num_programs(1)
    tick = seq * steps + step
    scaling = head**-0.5
    at = heads * head
    begin, forward, across, finish = gather_steps(low_ref, all_ref, *sems)

    @pl.when(tick == 0)
    def _():
        greet(tuple(place()[3].values()))
        begin()

    pl.when(tick == 3)(forward)
    pl.when(tick == 6)(across)
    raw_ref[...] = dot_nn(normed_ref[...], w_ref[...])
    here = pl.ds(pl.multiple_of(step * block, block), block)
    cosine, sine = cos_ref[here], sin_ref[here]
    key_ref[here] = normed_rope(raw_ref[:, at : at + head], kg_ref[...], cosine, sine)
    value_ref[here] = raw_ref[:, at + head :].astype(BF16)

    for i in range(key_ref.shape[0] // block):

        @pl.when(step == i)
        def _():
            seen = pl.ds(0, (i + 1) * block)

            @pl.loop(0, heads)
            def _(h):
                cols = pl.ds(pl.multiple_of(h * head, head), head)
                query = normed_rope(raw_ref[:, cols], qg_ref[...], cosine, sine)
                scores = causal_scores(query, key_ref[seen], i * block, scaling)
                highest = jnp.max(scores, -1, keepdims=True)
                exp_vals = jnp.exp(scores - highest)
                total = jnp.sum(exp_vals, -1, keepdims=True)
                probs = (exp_vals / total).astype(BF16)
                out_ref[:, cols] = dot_nn(probs, value_ref[seen])
                log_ref[h] = highest + jnp.log(total)

    gate = jax.nn.sigmoid(dot_nn(normed_ref[...], wg_ref[...]))
    gate_ref[...] = gate
    mixed_ref[...] = (out_ref[...] * gate).astype(BF16)
    pl.when(tick == pl.num_programs(0) * steps - 1)(finish)


def attend(normed, weights, gates, low, query_gain, key_gain, cosine, sine, heads, head, length, block=256):
    rows, width = normed.shape
    cols = weights.shape[1]
    seqs, steps = rows // length, length // block
    whole = lambda shape: pl.BlockSpec(
        shape, lambda s, i: (0,) * len(shape), pipeline_mode=pl.Buffered(1)
    )
    part = lambda cols: pl.BlockSpec((block, cols), lambda s, i: (s * steps + i, 0))
    *outs, gathered = pl.pallas_call(
        functools.partial(attend_kernel, heads, head, block),
        out_shape=(
            jax.ShapeDtypeStruct((rows, cols), F32),
            jax.ShapeDtypeStruct((rows, heads * head), F32),
            jax.ShapeDtypeStruct((heads, rows, 1), F32),
            jax.ShapeDtypeStruct((rows, heads * head), F32),
            jax.ShapeDtypeStruct((rows, heads * head), BF16),
            jax.ShapeDtypeStruct((2, 2, 2, *low.shape), low.dtype),
        ),
        grid=(seqs, steps),
        in_specs=[
            part(width),
            whole((width, cols)),
            whole((width, heads * head)),
            pl.BlockSpec(memory_space=pl.ANY),
            whole((1, head)),
            whole((1, head)),
            whole((length, head)),
            whole((length, head)),
        ],
        out_specs=(
            part(cols),
            part(heads * head),
            pl.BlockSpec((heads, block, 1), lambda s, i: (0, s * steps + i, 0)),
            part(heads * head),
            part(heads * head),
            pl.BlockSpec(memory_space=pl.ANY),
        ),
        scratch_shapes=[
            pltpu.VMEM((length, head), BF16),
            pltpu.VMEM((length, head), BF16),
            *GATHER_SEMAPHORES,
        ],
        compiler_params=pltpu.CompilerParams(collective_id=3, has_side_effects=True),
        cost_estimate=micros(42),
        name="attend",
    )(normed, weights, gates, low, query_gain, key_gain, cosine, sine)
    return *outs, gathered.reshape(rows, width)


def add_products(step, total_ref, start, left_ref, right, tile=1024):
    cols = slice(start, start + right.shape[1])

    @pl.loop(0, left_ref.shape[1] // tile)
    def _(m):
        at = pl.ds(pl.multiple_of(m * tile, tile), tile)
        part = dot_tn(left_ref[:, at], right)
        if isinstance(step, int):
            total_ref[at, cols] = total_ref[at, cols] + part if step else part
            return

        @pl.when(step == 0)
        def _():
            total_ref[at, cols] = part

        @pl.when(step > 0)
        def _():
            total_ref[at, cols] += part


def store_low(step, total_ref, out_ref, tile=256):
    @pl.when(step == pl.num_programs(0) - 1)
    def _():
        @pl.loop(0, total_ref.shape[0] // tile)
        def _(m):
            at = pl.ds(m * tile, tile)
            out_ref[at] = total_ref[at].astype(BF16)


def gate_back_kernel(
    normed_ref, branch_ref, w_ref, attended_ref, gate_ref, mixed_ref,
    dattended_ref, dgating_ref, grad_ref, total_ref,
):
    step = pl.program_id(0)
    dmixed = dot_nn(branch_ref[...], w_ref[...])
    gate = gate_ref[...]
    dattended_ref[...] = (dmixed * gate).astype(BF16)
    dgating = (dmixed * attended_ref[...] * gate * (1.0 - gate)).astype(BF16)
    dgating_ref[...] = dgating
    add_products(step, total_ref, 0, normed_ref, dgating)
    add_products(step, total_ref, dgating.shape[1], branch_ref, mixed_ref[...])
    store_low(step, total_ref, grad_ref)


def gate_back(normed, branch, weights, attended, gate, mixed, block=1024):
    rows, width = normed.shape
    cols = attended.shape[1]
    part = lambda cols: pl.BlockSpec((block, cols), lambda i: (i, 0))
    return pl.pallas_call(
        gate_back_kernel,
        out_shape=(
            jax.ShapeDtypeStruct((rows, cols), BF16),
            jax.ShapeDtypeStruct((rows, cols), BF16),
            jax.ShapeDtypeStruct((width, 2 * cols), BF16),
        ),
        grid=(rows // block,),
        in_specs=[
            part(width),
            part(width),
            pl.BlockSpec((width, cols), lambda i: (0, 1)),
            part(cols),
            part(cols),
            part(cols),
        ],
        out_specs=(part(cols), part(cols), pl.BlockSpec((width, 2 * cols), lambda i: (0, 0))),
        scratch_shapes=[pltpu.VMEM((width, 2 * cols), F32)],
        compiler_params=pltpu.CompilerParams(vmem_limit_bytes=VMEM_BYTES),
        cost_estimate=micros(25),
        name="gate_back",
    )(normed, branch, weights, attended, gate, mixed)


def feed_kernel(count, tile, mid_ref, low_ref, w_ref, act_ref, dgu_ref, *grads):
    step = pl.program_id(0)

    @pl.loop(0, count // tile)
    def _(j):
        start = pl.multiple_of(j * tile, tile)
        at, after = pl.ds(start, tile), pl.ds(pl.multiple_of(count + start, tile), tile)
        last = pl.ds(pl.multiple_of(2 * count + start, tile), tile)
        gate = dot_nn(mid_ref[...], w_ref[:, at])
        up = dot_nn(mid_ref[...], w_ref[:, after])
        dact = dot_nn(low_ref[...], w_ref[:, last])
        sigma = jax.nn.sigmoid(gate)
        silu = gate * sigma
        act_ref[:, at] = (silu * up).astype(BF16)
        dgu_ref[:, at] = (dact * up * sigma * (1.0 + gate * (1.0 - sigma))).astype(BF16)
        dgu_ref[:, after] = (dact * silu).astype(BF16)

    if grads:
        grad_ref, total_ref = grads
        add_products(step, total_ref, 0, mid_ref, dgu_ref[...])
        add_products(step, total_ref, 2 * count, low_ref, act_ref[...])
        store_low(step, total_ref, grad_ref)


def feed_forward(mid, low, weights, grads, block):
    rows, width = mid.shape
    count = weights.shape[1] // 3
    part = lambda cols: pl.BlockSpec((block, cols), lambda i: (i, 0))
    whole = pl.BlockSpec(weights.shape, lambda i: (0, 0), pipeline_mode=pl.Buffered(1))
    return pl.pallas_call(
        functools.partial(feed_kernel, count, 256),
        out_shape=(
            jax.ShapeDtypeStruct((rows, count), BF16),
            jax.ShapeDtypeStruct((rows, 2 * count), BF16),
            *[jax.ShapeDtypeStruct(weights.shape, BF16)] * grads,
        ),
        grid=(rows // block,),
        in_specs=[part(width), part(width), whole],
        out_specs=(part(count), part(2 * count), *[whole] * grads),
        scratch_shapes=[pltpu.VMEM(weights.shape, F32)] * grads,
        compiler_params=pltpu.CompilerParams(vmem_limit_bytes=VMEM_BYTES),
        cost_estimate=micros(41 if grads else 14),
        name="feed_forward",
    )(mid, low, weights)


def attend_back_kernel(
    heads, head, block, raw_ref, up_ref, log_ref, qg_ref, kg_ref, cos_ref, sin_ref, sums_ref,
    out_ref, qg_out, kg_out, sum_ref, key_ref, value_ref, dkey_ref, dvalue_ref, own, load_sem, *scratch,
):
    seq, step, steps = pl.program_id(0), pl.program_id(1), pl.num_programs(1)
    tick = seq * steps + step
    scaling = head**-0.5
    at = heads * head
    blocks = raw_ref.shape[0] // block
    diag_x, diag_y, x_low, y_high, second, finish = axis_steps(own, *scratch)

    @pl.when(tick == 0)
    def _():
        load = pltpu.make_async_copy(sums_ref, own, load_sem)
        load.start()
        device = place()[3]
        greet((device["y"], device["x"]))
        load.wait()
        for copy in (diag_x, diag_y, x_low, y_high):
            copy.start()
        qg_out[...] = jnp.zeros_like(qg_out)
        kg_out[...] = jnp.zeros_like(kg_out)

    pl.when(tick == 4)(second)

    @pl.when(step == 0)
    def _():
        key_ref[...] = normed_rope(
            raw_ref[:, at : at + head], kg_ref[...], cos_ref[...], sin_ref[...]
        )
        value_ref[...] = raw_ref[:, at + head :].astype(BF16)
        dkey_ref[...] = jnp.zeros_like(dkey_ref)
        dvalue_ref[...] = jnp.zeros_like(dvalue_ref)

    for i in range(blocks):

        @pl.when(step == i)
        def _():
            rows, seen = pl.ds(i * block, block), pl.ds(0, (i + 1) * block)

            @pl.loop(0, heads)
            def _(h):
                cols = pl.ds(pl.multiple_of(h * head, head), head)
                raw = raw_ref[rows, cols]
                query = normed_rope(raw, qg_ref[...], cos_ref[rows], sin_ref[rows])
                scores = causal_scores(query, key_ref[seen], i * block, scaling)
                probs = jnp.exp(scores - log_ref[h])
                upstream = up_ref[:, cols]
                dprobs = dot_nt(upstream, value_ref[seen])
                centre = jnp.sum(dprobs * probs, -1, keepdims=True)
                dscores = (probs * (dprobs - centre)).astype(BF16)
                dkey_ref[seen] += dot_tn(dscores, query)
                dvalue_ref[seen] += dot_tn(probs.astype(BF16), upstream)
                dquery = dot_nn(dscores, key_ref[seen]) * scaling
                grad, part = normed_rope_back(
                    dquery, raw, qg_ref[...], cos_ref[rows], sin_ref[rows]
                )
                out_ref[rows, cols] = grad
                qg_out[...] += part

    @pl.when(step == blocks - 1)
    def _():
        grad, part = normed_rope_back(
            dkey_ref[...] * scaling,
            raw_ref[:, at : at + head],
            kg_ref[...],
            cos_ref[...],
            sin_ref[...],
        )
        out_ref[:, at : at + head] = grad
        out_ref[:, at + head :] = dvalue_ref[...].astype(BF16)
        kg_out[...] += part

    @pl.when(tick == pl.num_programs(0) * steps - 1)
    def _():
        def store(rows, value):
            sum_ref[rows] = value

        finish(store)


def attend_back(
    raw, upstream, logs, query_gain, key_gain, cosine, sine, sums, heads, head, length, block=256
):
    rows = raw.shape[0]
    total = jax.ShapeDtypeStruct(sums.shape[1:], F32)
    seqs, steps = rows // length, length // block
    whole = lambda shape: pl.BlockSpec(shape, lambda s, i: (0,) * len(shape))
    return pl.pallas_call(
        functools.partial(attend_back_kernel, heads, head, block),
        out_shape=(
            jax.ShapeDtypeStruct(raw.shape, BF16),
            jax.ShapeDtypeStruct((1, head), F32),
            jax.ShapeDtypeStruct((1, head), F32),
            total,
        ),
        grid=(seqs, steps),
        in_specs=[
            pl.BlockSpec((length, raw.shape[1]), lambda s, i: (s, 0)),
            pl.BlockSpec((block, heads * head), lambda s, i: (s * steps + i, 0)),
            pl.BlockSpec((heads, block, 1), lambda s, i: (0, s * steps + i, 0)),
            whole((1, head)),
            whole((1, head)),
            whole((length, head)),
            whole((length, head)),
            pl.BlockSpec(memory_space=pl.ANY),
        ],
        out_specs=(
            pl.BlockSpec((length, raw.shape[1]), lambda s, i: (s, 0)),
            whole((1, head)),
            whole((1, head)),
            whole(total.shape),
        ),
        scratch_shapes=[
            pltpu.VMEM((length, head), BF16),
            pltpu.VMEM((length, head), BF16),
            pltpu.VMEM((length, head), F32),
            pltpu.VMEM((length, head), F32),
            pltpu.VMEM(sums.shape, BF16),
            pltpu.SemaphoreType.DMA,
            *axis_scratch(*sums.shape[1:]),
        ],
        compiler_params=pltpu.CompilerParams(
            collective_id=5, has_side_effects=True, vmem_limit_bytes=VMEM_BYTES
        ),
        cost_estimate=micros(40),
        name="attend_back",
    )(raw, upstream, logs, query_gain, key_gain, cosine, sine, sums)


def attention_weights(query_proj, key_proj, value_proj, gating_proj, output_proj):
    return (
        lax.all_gather(query_proj, "dp", axis=0, tiled=True),
        lax.all_gather(key_proj, "dp", axis=0, tiled=True),
        lax.all_gather(value_proj, "dp", axis=0, tiled=True),
        lax.all_gather(gating_proj, "dp", axis=0, tiled=True),
        lax.all_gather(output_proj, "dp", axis=1, tiled=True),
    )


def swiglu_weights(swiglu_gate, swiglu_up, swiglu_down):
    return (
        lax.all_gather(swiglu_gate, "dp", axis=0, tiled=True),
        lax.all_gather(swiglu_up, "dp", axis=0, tiled=True),
        lax.all_gather(swiglu_down, "dp", axis=1, tiled=True),
    )


def softmax_forward_mapped(seq_items, causal):
    queries, keys_seq, values_seq = seq_items
    scaling = queries.shape[-1] ** (-0.5)
    scores = (
        jnp.einsum("qgjd,kgd->gjqk", queries, keys_seq, preferred_element_type=jnp.float32)
        * scaling
    )
    scores = jnp.where(causal, scores, -1e30)
    highest = jnp.max(scores, -1, keepdims=True)
    exp_vals = jnp.exp(scores - highest)
    row_totals = jnp.sum(exp_vals, -1, keepdims=True)
    attn_probs = (exp_vals / row_totals).astype(jnp.bfloat16)
    attended = jnp.einsum(
        "gjqk,kgd->qgjd", attn_probs, values_seq, preferred_element_type=jnp.float32
    )
    return (attended, highest[..., 0] + jnp.log(row_totals[..., 0]))


def softmax_backward_mapped(seq_items, causal):
    queries, keys_seq, values_seq, log_total, upstream = seq_items
    scaling = queries.shape[-1] ** (-0.5)
    scores = (
        jnp.einsum("qgjd,kgd->gjqk", queries, keys_seq, preferred_element_type=jnp.float32)
        * scaling
    )
    scores = jnp.where(causal, scores, -1e30)
    attn_probs = jnp.exp(scores - log_total[..., None])
    dprobs = jnp.einsum("qgjd,kgd->gjqk", upstream, values_seq, preferred_element_type=jnp.float32)
    centre = jnp.sum(dprobs * attn_probs, -1, keepdims=True)
    dscores = (attn_probs * (dprobs - centre)).astype(jnp.bfloat16)
    dqueries = (
        jnp.einsum("gjqk,kgd->qgjd", dscores, keys_seq, preferred_element_type=jnp.float32)
        * scaling
    )
    key_grads = (
        jnp.einsum("gjqk,qgjd->kgd", dscores, queries, preferred_element_type=jnp.float32) * scaling
    )
    value_grads = jnp.einsum(
        "gjqk,qgjd->kgd",
        attn_probs.astype(jnp.bfloat16),
        upstream,
        preferred_element_type=jnp.float32,
    )
    key_rows = key_grads.shape[0]
    return (dqueries, key_grads.reshape(key_rows, -1), value_grads.reshape(key_rows, -1))


def per_device_wide(
    tokens,
    cotangent,
    domain_ids,
    domain_counts,
    domain_numer,
    domain_denom,
    attention_gain,
    query_gain,
    key_gain,
    query_proj,
    key_proj,
    value_proj,
    gating_proj,
    output_proj,
    swiglu_gain,
    swiglu_gate,
    swiglu_up,
    swiglu_down,
):
    seq_count, local_len, model_width = tokens.shape
    full_len = local_len * lax.axis_size("ctx")
    local_rows = seq_count * local_len
    all_rows = seq_count * full_len
    head_dim = query_gain.shape[0]
    local_heads = query_proj.shape[1] // head_dim
    local_kv = key_proj.shape[1] // head_dim
    group_size = local_heads // local_kv
    positions = jnp.arange(full_len, dtype=jnp.int32)
    causal = positions[:, None] >= positions[None, :]
    cosine, sine = rope_tables(positions, head_dim)
    cos_rows = cosine[:, None, :]
    sin_rows = sine[:, None, :]
    inputs = tokens.reshape(local_rows, model_width).astype(jnp.float32)
    inverse_in = lax.rsqrt(jnp.mean(inputs * inputs, -1, keepdims=True) + EPSILON)
    gain_in = attention_gain.astype(jnp.float32)
    normed = (inputs * inverse_in * gain_in).astype(jnp.bfloat16)
    normed_all = lax.all_gather(
        normed.reshape(seq_count, local_len, model_width), "ctx", axis=1, tiled=True
    ).reshape(all_rows, model_width)
    attn_full = attention_weights(query_proj, key_proj, value_proj, gating_proj, output_proj)
    query_raw = dot_nn(normed_all, attn_full[0]).reshape(
        seq_count, full_len, local_heads, head_dim
    )
    key_raw = dot_nn(normed_all, attn_full[1]).reshape(seq_count, full_len, local_kv, head_dim)
    value_low = (
        dot_nn(normed_all, attn_full[2])
        .astype(jnp.bfloat16)
        .reshape(seq_count, full_len, local_kv, head_dim)
    )
    gate_pre = dot_nn(normed_all, attn_full[3])
    query_scale = query_gain.astype(jnp.float32)
    key_scale = key_gain.astype(jnp.float32)
    query_inv = lax.rsqrt(jnp.mean(query_raw * query_raw, -1, keepdims=True) + EPSILON)
    key_inv = lax.rsqrt(jnp.mean(key_raw * key_raw, -1, keepdims=True) + EPSILON)
    query_low = rotate(query_raw * query_inv * query_scale, cos_rows, sin_rows).astype(jnp.bfloat16)
    key_low = rotate(key_raw * key_inv * key_scale, cos_rows, sin_rows).astype(jnp.bfloat16)
    query_groups = query_low.reshape(seq_count, full_len, local_kv, group_size, head_dim)
    attended, log_total = lax.map(
        lambda seq_items: softmax_forward_mapped(seq_items, causal), (query_groups, key_low, value_low)
    )
    attended = attended.reshape(all_rows, local_heads * head_dim)
    gate_sig = jax.nn.sigmoid(gate_pre)
    mixed = (attended * gate_sig).astype(jnp.bfloat16)
    branch_part = dot_nn(mixed, attn_full[4]).reshape(seq_count, full_len, model_width)
    branch = lax.psum_scatter(branch_part, "ctx", scatter_dimension=1, tiled=True).reshape(
        local_rows, model_width
    )
    hidden = inputs + branch
    inverse_mid = lax.rsqrt(jnp.mean(hidden * hidden, -1, keepdims=True) + EPSILON)
    gain_mid = swiglu_gain.astype(jnp.float32)
    normed_mid = (hidden * inverse_mid * gain_mid).astype(jnp.bfloat16)
    normed_mid_all = lax.all_gather(
        normed_mid.reshape(seq_count, local_len, model_width), "ctx", axis=1, tiled=True
    ).reshape(all_rows, model_width)
    swiglu_full = swiglu_weights(swiglu_gate, swiglu_up, swiglu_down)
    gate_ff = dot_nn(normed_mid_all, swiglu_full[0])
    up_val = dot_nn(normed_mid_all, swiglu_full[1])
    gate_sigma = jax.nn.sigmoid(gate_ff)
    silu_val = gate_ff * gate_sigma
    activation = (silu_val * up_val).astype(jnp.bfloat16)
    down_part = dot_nn(activation, swiglu_full[2]).reshape(seq_count, full_len, model_width)
    ffn_branch = (
        lax.psum_scatter(down_part.astype(jnp.bfloat16), "ctx", scatter_dimension=1, tiled=True)
        .astype(jnp.float32)
        .reshape(local_rows, model_width)
    )
    layer_out = (hidden + ffn_branch).astype(jnp.bfloat16)
    domain_table = (
        domain_ids[:, None] == jnp.arange(domain_counts.shape[0], dtype=jnp.int32)[None, :]
    ).astype(jnp.float32)
    ratio = (
        domain_numer.astype(jnp.float32)
        / domain_denom.astype(jnp.float32)
        * LENGTH
        / domain_counts.astype(jnp.float32)
    )
    factor = jnp.sum(domain_table * ratio[None, :], 1)
    upstream = (cotangent.astype(jnp.float32) * factor[:, None, None]).reshape(
        local_rows, model_width
    )
    swiglu_back = swiglu_weights(swiglu_gate, swiglu_up, swiglu_down)
    out_low = upstream.astype(jnp.bfloat16)
    out_all = lax.all_gather(
        out_low.reshape(seq_count, local_len, model_width), "ctx", axis=1, tiled=True
    ).reshape(all_rows, model_width)
    dactivation = dot_nt(out_all, swiglu_back[2])
    dgate_low = (dactivation * up_val * gate_sigma * (1.0 + gate_ff * (1.0 - gate_sigma))).astype(
        jnp.bfloat16
    )
    dup_low = (dactivation * silu_val).astype(jnp.bfloat16)
    grad_down = dot_tn(activation, out_all)
    grad_gate = dot_tn(normed_mid_all, dgate_low)
    grad_up = dot_tn(normed_mid_all, dup_low)
    dmid_part = dot_nt(dgate_low, swiglu_back[0]) + dot_nt(dup_low, swiglu_back[1])
    dnormed_mid = lax.psum_scatter(
        dmid_part.reshape(seq_count, full_len, model_width), "ctx", scatter_dimension=1, tiled=True
    ).reshape(local_rows, model_width)
    grad_gain_mid = jnp.sum(dnormed_mid * hidden * inverse_mid, 0)
    dhidden = upstream + norm_back(dnormed_mid, hidden, inverse_mid, gain_mid)
    swiglu_grads = (
        lax.psum_scatter(
            grad_gate.astype(jnp.bfloat16), "dp", scatter_dimension=0, tiled=True
        ).astype(jnp.float32),
        lax.psum_scatter(
            grad_up.astype(jnp.bfloat16), "dp", scatter_dimension=0, tiled=True
        ).astype(jnp.float32),
        lax.psum_scatter(
            grad_down.astype(jnp.bfloat16), "dp", scatter_dimension=1, tiled=True
        ).astype(jnp.float32),
    )
    attn_back = attention_weights(query_proj, key_proj, value_proj, gating_proj, output_proj)
    dbranch_low = dhidden.astype(jnp.bfloat16)
    dbranch_all = lax.all_gather(
        dbranch_low.reshape(seq_count, local_len, model_width), "ctx", axis=1, tiled=True
    ).reshape(all_rows, model_width)
    grad_output = dot_tn(mixed, dbranch_all)
    dmixed = dot_nt(dbranch_all, attn_back[4])
    dattended_low = (dmixed * gate_sig).astype(jnp.bfloat16)
    dgating_low = (dmixed * attended * gate_sig * (1.0 - gate_sig)).astype(jnp.bfloat16)
    upstream_heads = dattended_low.reshape(seq_count, full_len, local_kv, group_size, head_dim)
    dquery_rot, dkey_rot, dvalue_sum = lax.map(
        lambda seq_items: softmax_backward_mapped(seq_items, causal),
        (query_groups, key_low, value_low, log_total, upstream_heads),
    )
    dvalue_low = dvalue_sum.reshape(all_rows, local_kv * head_dim).astype(jnp.bfloat16)
    dquery_normed = unrotate(
        dquery_rot.reshape(seq_count, full_len, local_heads, head_dim), cos_rows, sin_rows
    )
    dkey_normed = unrotate(
        dkey_rot.reshape(seq_count, full_len, local_kv, head_dim), cos_rows, sin_rows
    )
    grad_query_gain = jnp.sum(dquery_normed * query_raw * query_inv, (0, 1, 2))
    grad_key_gain = jnp.sum(dkey_normed * key_raw * key_inv, (0, 1, 2))
    dquery_low = (
        norm_back(dquery_normed, query_raw, query_inv, query_scale)
        .reshape(all_rows, -1)
        .astype(jnp.bfloat16)
    )
    dkey_low = (
        norm_back(dkey_normed, key_raw, key_inv, key_scale)
        .reshape(all_rows, -1)
        .astype(jnp.bfloat16)
    )
    dnormed_part = (
        dot_nt(dquery_low, attn_back[0])
        + dot_nt(dkey_low, attn_back[1])
        + dot_nt(dvalue_low, attn_back[2])
        + dot_nt(dgating_low, attn_back[3])
    )
    dnormed = (
        lax.psum_scatter(
            dnormed_part.reshape(seq_count, full_len, model_width).astype(jnp.bfloat16),
            "ctx",
            scatter_dimension=1,
            tiled=True,
        )
        .astype(jnp.float32)
        .reshape(local_rows, model_width)
    )
    grad_gain_in = jnp.sum(dnormed * inputs * inverse_in, 0)
    input_grad = (dhidden + norm_back(dnormed, inputs, inverse_in, gain_in)).astype(jnp.bfloat16)
    grad_query = dot_tn(normed_all, dquery_low)
    grad_key = dot_tn(normed_all, dkey_low)
    grad_value = dot_tn(normed_all, dvalue_low)
    grad_gating = dot_tn(normed_all, dgating_low)
    attention_grads = (
        lax.psum_scatter(
            grad_query.astype(jnp.bfloat16), "dp", scatter_dimension=0, tiled=True
        ).astype(jnp.float32),
        lax.psum_scatter(
            grad_key.astype(jnp.bfloat16), "dp", scatter_dimension=0, tiled=True
        ).astype(jnp.float32),
        lax.psum_scatter(
            grad_value.astype(jnp.bfloat16), "dp", scatter_dimension=0, tiled=True
        ).astype(jnp.float32),
        lax.psum_scatter(
            grad_gating.astype(jnp.bfloat16), "dp", scatter_dimension=0, tiled=True
        ).astype(jnp.float32),
        lax.psum_scatter(
            grad_output.astype(jnp.bfloat16), "dp", scatter_dimension=1, tiled=True
        ).astype(jnp.float32),
    )
    gain_grads = lax.psum(
        (grad_gain_in, grad_gain_mid, grad_query_gain, grad_key_gain), ("dp", "ctx")
    )
    return (
        layer_out.reshape(seq_count, local_len, model_width),
        input_grad.reshape(seq_count, local_len, model_width),
        gain_grads[0],
        gain_grads[2],
        gain_grads[3],
        attention_grads[0],
        attention_grads[1],
        attention_grads[2],
        attention_grads[3],
        attention_grads[4],
        gain_grads[1],
        swiglu_grads[0],
        swiglu_grads[1],
        swiglu_grads[2],
    )


def per_device(
    tokens,
    cotangent,
    domain_ids,
    domain_counts,
    domain_numer,
    domain_denom,
    attention_gain,
    query_gain,
    key_gain,
    query_proj,
    key_proj,
    value_proj,
    gating_proj,
    output_proj,
    swiglu_gain,
    swiglu_gate,
    swiglu_up,
    swiglu_down,
):
    seq_count, local_len, width = tokens.shape
    rows = seq_count * local_len
    full_len = local_len * lax.axis_size("x") * lax.axis_size("c")
    seqs = seq_count * lax.axis_size("y")
    head = query_gain.shape[0]
    kv_cols = key_proj.shape[1] // 2
    q_cols = query_proj.shape[1] // 2
    ff_cols = swiglu_gate.shape[1] // 2
    heads = q_cols // head
    split, rest = ff_cols * 2 // 3, ff_cols - ff_cols * 2 // 3
    tokens, cotangent = tokens.reshape(rows, width), cotangent.reshape(rows, width)
    (
        normed_all, w_qkv, w_go, rows_first, rows_last, inverse_in, out_low, factor, cos_rows, sin_rows,
    ) = opening(
        tokens,
        cotangent,
        attention_gain,
        (domain_ids, domain_counts, domain_numer, domain_denom),
        (
            query_proj, key_proj, value_proj, gating_proj, output_proj, swiglu_gate, swiglu_up, swiglu_down,
        ),
        split,
        full_len,
        head,
    )
    w_first = gather_rows(rows_first)
    w_last = gather_rows(rows_last)

    query_scale, key_scale = query_gain.astype(F32)[None], key_gain.astype(F32)[None]
    qkv, attended, logs, gate_sig, mixed, out_all = attend(
        normed_all, w_qkv, w_go, out_low, query_scale, key_scale, cos_rows, sin_rows, heads, head, full_len
    )
    wide, column = jax.ShapeDtypeStruct((rows, width), F32), jax.ShapeDtypeStruct((rows, 1), F32)
    low = jax.ShapeDtypeStruct((rows, width), BF16)
    gain_mid = swiglu_gain.reshape(1, -1)
    hidden, inverse_mid, normed_mid = scatter_products(
        middle_kernel, 7, (tokens, gain_mid), (wide, column, low), (mixed, w_go, q_cols)
    )
    mid_all = gather_tokens(normed_mid)

    act_first, dgu_first, grad_first = feed_forward(mid_all, out_all, w_first, True, 1024)
    part_first = scatter_grads(grad_first)
    w_last, grad_first = lax.optimization_barrier((w_last, grad_first))
    act_last, dgu_last = feed_forward(mid_all, out_all, w_last, False, 512)
    dhidden, dbranch, grad_gain_mid = scatter_products(
        middle_back_kernel,
        8,
        (hidden, inverse_mid, gain_mid, cotangent, factor),
        (wide, low, jax.ShapeDtypeStruct((1, width), F32)),
        (dgu_first, w_first, 0),
        (dgu_last, w_last, 0),
    )
    dbranch_all, ffn_sums, grad_last = gather_beside(
        dbranch,
        ((act_first, w_first, 2 * split), (act_last, w_last, 2 * rest)),
        mid_all,
        out_all,
        dgu_last,
        act_last,
    )
    part_last = scatter_grads(grad_last)
    dbranch_all, part_first = lax.optimization_barrier((dbranch_all, part_first))

    theirs_first = their_rows(part_first)
    dattended, dgating, grad_go = gate_back(
        normed_all, dbranch_all, w_go, attended, gate_sig, mixed
    )
    dattended, theirs_first, grad_go = lax.optimization_barrier((dattended, theirs_first, grad_go))
    part_go = scatter_grads(grad_go)
    dqkv, grad_query_gain, grad_key_gain, ffn_branch = attend_back(
        qkv, dattended, logs, query_scale, key_scale, cos_rows, sin_rows, ffn_sums, heads, head, full_len
    )
    grad_query_gain, grad_key_gain = grad_query_gain[0], grad_key_gain[0]
    dqkv, part_last = lax.optimization_barrier((dqkv, part_last))
    theirs_last = their_rows(part_last)
    layer_out = (hidden + ffn_branch).astype(BF16)
    grad_qkv = dot_tn(normed_all, dqkv).astype(BF16)
    plan = [(0, i * split, split, i, 0, i == 2) for i in range(3)]
    plan += [(1, i * rest, rest, i, split, i == 2) for i in range(3)]
    grad_gate, grad_up, grad_down = join_grads(
        (part_first, part_last),
        (theirs_first, theirs_last),
        plan,
        [weight.shape for weight in (swiglu_gate, swiglu_up, swiglu_down)],
    )
    grad_qkv, layer_out, grad_gate, grad_up, grad_down = lax.optimization_barrier(
        (grad_qkv, layer_out, grad_gate, grad_up, grad_down)
    )
    input_grad, mine_qkv, theirs_qkv, totals = tail(
        ((dqkv, w_qkv, 0), (dgating, w_go, 0)),
        grad_qkv,
        tokens,
        inverse_in,
        dhidden,
        attention_gain,
        (grad_gain_mid, grad_query_gain, grad_key_gain),
    )
    input_grad, part_go = lax.optimization_barrier((input_grad, part_go))
    theirs_go = their_rows(part_go)
    grad_gating, grad_output = join_grads(
        (part_go,),
        (theirs_go,),
        [(0, 0, q_cols, 0, 0, False), (0, q_cols, q_cols, 1, 0, True)],
        (gating_proj.shape, output_proj.shape),
    )
    widths, starts = (q_cols, kv_cols, kv_cols), (0, q_cols, q_cols + kv_cols)
    *gain_grads, grad_query, grad_key, grad_value = join_last(
        mine_qkv,
        theirs_qkv,
        totals,
        [(0, starts[i], widths[i], i, 0, False) for i in range(3)],
        (width, width, head, head),
        [weight.shape for weight in (query_proj, key_proj, value_proj)],
    )
    gain_grads = [gain.reshape(-1) for gain in gain_grads]
    shape = (seq_count, local_len, width)
    return (
        layer_out.reshape(shape),
        input_grad.reshape(shape),
        gain_grads[0],
        gain_grads[2],
        gain_grads[3],
        grad_query,
        grad_key,
        grad_value,
        grad_gating,
        grad_output,
        gain_grads[1],
        grad_gate,
        grad_up,
        grad_down,
    )


def solution(mesh):
    if (mesh.shape["dp"], mesh.shape["ctx"]) == (8, 4):
        body = per_device
        mesh = Mesh(mesh.devices.reshape(4, 2, 2, 2), ("z", "y", "x", "c"))
        dp, ctx = ("z", "y"), ("x", "c")
    else:
        body = per_device_wide
        dp, ctx = "dp", "ctx"
    tokens, weight, turned = P(dp, ctx, None), P(dp, ctx), P(ctx, dp)
    return jax.shard_map(
        body,
        mesh=mesh,
        in_specs=(tokens, tokens, P(dp), *[P()] * 6, *[weight] * 4, turned, P(), weight, weight, turned),
        out_specs=(tokens, tokens, *[P()] * 3, *[weight] * 4, turned, P(), weight, weight, turned),
        check_vma=False,
    )
```

```python
import functools

import jax
import jax.numpy as jnp
import numpy as np
from jax import lax
from jax.experimental import pallas as pl
from jax.experimental.pallas import tpu as pltpu
from jax.sharding import Mesh
from jax.sharding import PartitionSpec as P

LENGTH = 1024

EPSILON = 1e-06
ROPE_BASE = 1000000.0
MESH = pl.DeviceIdType.MESH
BF16 = jnp.bfloat16
F32 = jnp.float32
VMEM_BYTES = 62 * 2**20


def micros(count):
    return pl.CostEstimate(flops=0, transcendentals=0, bytes_accessed=count * 3_300_000)


def dot_nn(left, right):
    return jnp.dot(left, right, preferred_element_type=F32)


def dot_tn(left, right):
    return lax.dot_general(left, right, (((0,), (0,)), ((), ())), preferred_element_type=F32)


def dot_nt(left, right):
    return lax.dot_general(left, right, (((1,), (1,)), ((), ())), preferred_element_type=F32)


def rope_tables(positions, head_width):
    halfway = head_width // 2
    inverse = 1.0 / ROPE_BASE ** (jnp.arange(halfway, dtype=F32) * (2.0 / head_width))
    angles = positions.astype(F32)[:, None] * inverse[None, :]
    return (jnp.cos(angles), jnp.sin(angles))


def rotate(tensor, cosine, sine):
    halfway = tensor.shape[-1] // 2
    first_half = tensor[..., :halfway]
    second_half = tensor[..., halfway:]
    return jnp.concatenate(
        [first_half * cosine - second_half * sine, second_half * cosine + first_half * sine], -1
    )


def unrotate(grads_in, cosine, sine):
    halfway = grads_in.shape[-1] // 2
    first_half = grads_in[..., :halfway]
    second_half = grads_in[..., halfway:]
    return jnp.concatenate(
        [first_half * cosine + second_half * sine, second_half * cosine - first_half * sine], -1
    )


def norm_back(grads_in, values_in, inverse, gain_vec):
    scaled = grads_in * gain_vec
    return inverse * scaled - values_in * (inverse * inverse * inverse) * jnp.mean(
        scaled * values_in, -1, keepdims=True
    )


def greet(neighbours):
    barrier = pltpu.get_barrier_semaphore()
    for neighbour in neighbours:
        pl.semaphore_signal(barrier, inc=1, device_id=neighbour, device_id_type=MESH)
    pl.semaphore_wait(barrier, len(neighbours))


def remote_copies(send, recv, device):
    def remote(index, source, target, axis):
        return pltpu.make_async_remote_copy(
            src_ref=source,
            dst_ref=target,
            send_sem=send.at[index],
            recv_sem=recv.at[index],
            device_id=device[axis],
            device_id_type=MESH,
        )

    return remote


def place():
    y, x, c = lax.axis_index("y"), lax.axis_index("x"), lax.axis_index("c")
    return y, x, c, {"y": {"y": 1 - y}, "x": {"x": 1 - x}, "c": {"c": 1 - c}}


def gather_steps(s_ref, out_ref, local_sem, send, recv, split=True):
    y, x, c, device = place()
    remote = remote_copies(send, recv, device)
    half = s_ref.shape[0] // 2
    low, high = pl.ds(0, half), pl.ds(half, half)
    mine = out_ref.at[y, x, c]
    from_x = out_ref.at[y, 1 - x, c]
    from_y = out_ref.at[1 - y, x, c]
    diagonal = out_ref.at[1 - y, 1 - x, c]
    x_low = remote(0, s_ref.at[low], mine.at[low], "x")
    y_high = remote(1, s_ref.at[high], mine.at[high], "y")
    x_high = remote(2, s_ref.at[high], mine.at[high], "x")
    y_low = remote(3, s_ref.at[low], mine.at[low], "y")
    c_own = remote(4, s_ref, mine, "c")
    local = pltpu.make_async_copy(s_ref, mine, local_sem)
    forward_y = remote(5, from_x.at[low], from_x.at[low], "y")
    over_x = from_y.at[high] if split else from_y
    forward_x = remote(6, over_x, over_x, "x")
    c_x = remote(7, from_x, from_x, "c")
    c_y = remote(8, from_y, from_y, "c")
    c_low = remote(9, diagonal.at[low], diagonal.at[low], "c")
    over_c = diagonal.at[high] if split else diagonal
    c_high = remote(10, over_c, over_c, "c")

    def begin():
        for copy in (x_low, y_high, x_high, y_low, c_own, local):
            copy.start()

    def forward():
        x_low.wait_recv()
        if split:
            forward_y.start()
        y_high.wait_recv()
        if split:
            forward_x.start()

    def across():
        if not split:
            y_low.wait_recv()
            forward_x.start()
        x_high.wait_recv()
        c_x.start()
        if split:
            y_low.wait_recv()
        c_y.start()

    def finish():
        if split:
            forward_y.wait_recv()
            c_low.start()
        forward_x.wait_recv()
        c_high.start()
        for copy in (c_own, c_x, c_y, *((c_low,) if split else ()), c_high):
            copy.wait()
        for copy in (x_low, y_high, x_high, y_low, *((forward_y,) if split else ()), forward_x):
            copy.wait_send()
        local.wait()

    return begin, forward, across, finish


GATHER_SEMAPHORES = (
    pltpu.SemaphoreType.DMA,
    pltpu.SemaphoreType.DMA((11,)),
    pltpu.SemaphoreType.DMA((11,)),
)


def swap_steps(pieces, sources, outs, local_sem, send, recv, wanted=None):
    y, _, _, device = place()
    remote = remote_copies(send, recv, device)
    copies, locals_ = [], []
    for i, (source, out, first, count, at) in enumerate(pieces):
        if wanted is not None and not wanted(out):
            continue
        rows, cols = sources[source].shape
        target = outs[out].at[pl.ds(pl.multiple_of(y * rows, rows), rows), pl.ds(at, count)]

        def half(which):
            start = pl.multiple_of(which * (cols // 2) + first, 128)
            return sources[source].at[:, pl.ds(start, count)]

        copies.append(remote(i, half(1 - y), target, "y"))
        locals_.append(pltpu.make_async_copy(half(y), target, local_sem.at[i]))

    def begin():
        for copy in (*copies, *locals_):
            copy.start()

    def here():
        for copy in locals_:
            copy.wait()

    def finish():
        for copy in copies:
            copy.wait()

    return begin, here, finish


def gather_kernel(split, *refs):
    source, out, *sems = refs
    begin, forward, across, finish = gather_steps(source, out, *sems, split)
    greet(tuple(place()[3].values()))
    begin()
    forward()
    across()
    finish()


def gather_tokens(shard):
    rows, width = shard.shape
    return pl.pallas_call(
        functools.partial(gather_kernel, True),
        out_shape=jax.ShapeDtypeStruct((2, 2, 2, rows, width), shard.dtype),
        in_specs=[pl.BlockSpec(memory_space=pltpu.VMEM)],
        out_specs=pl.BlockSpec(memory_space=pl.ANY),
        scratch_shapes=list(GATHER_SEMAPHORES),
        compiler_params=pltpu.CompilerParams(collective_id=1, has_side_effects=True),
        cost_estimate=micros(42),
        name="gather_tokens",
    )(shard).reshape(8 * rows, width)


def line_steps(rows_ref, out_ref, local_sem, send, recv, part, which):
    z = lax.axis_index("z")
    rows, half = rows_ref.shape[0], rows_ref.shape[0] // 2
    first = which * half
    pair, middle = z + 1 - 2 * lax.rem(z, 2), 3 - z
    inner = (z == 1) | (z == 2)

    def at(index):
        return out_ref.at[pl.ds(pl.multiple_of(index * rows + first, half), half)]

    def remote(index, source, target, peer):
        return pltpu.make_async_remote_copy(
            src_ref=source,
            dst_ref=target,
            send_sem=send.at[5 * part + index],
            recv_sem=recv.at[5 * part + index],
            device_id={"z": peer},
            device_id_type=MESH,
        )

    far = middle + 1 - 2 * lax.rem(middle, 2)
    own = rows_ref.at[pl.ds(pl.multiple_of(first, half), half)]
    own_pair = remote(0, own, at(z), pair)
    own_middle = remote(1, own, at(z), middle)
    pair_middle = remote(2, at(pair), at(pair), middle)
    middle_pair = remote(3, at(middle), at(middle), pair)
    far_pair = remote(4, at(far), at(far), pair)
    local = pltpu.make_async_copy(own, at(z), local_sem.at[part])

    def begin():
        local.start()
        own_pair.start()
        pl.when(inner)(own_middle.start)

    def second():
        own_pair.wait_recv()

        @pl.when(inner)
        def _():
            pair_middle.start()
            own_middle.wait_recv()
            middle_pair.start()

    def third():
        @pl.when(inner)
        def _():
            pair_middle.wait_recv()
            far_pair.start()

    def finish():
        @pl.when(inner)
        def _():
            for copy in (own_middle, pair_middle, middle_pair, far_pair):
                copy.wait_send()

        @pl.when(jnp.logical_not(inner))
        def _():
            middle_pair.wait_recv()
            far_pair.wait_recv()

        own_pair.wait_send()
        local.wait()

    def peers():
        return pair, middle, inner

    return begin, second, third, finish, peers


def greet_line(others, pair, middle, inner):
    barrier = pltpu.get_barrier_semaphore()
    for other in (*others, {"z": pair}):
        pl.semaphore_signal(barrier, inc=1, device_id=other, device_id_type=MESH)

    @pl.when(inner)
    def _():
        pl.semaphore_signal(barrier, inc=1, device_id={"z": middle}, device_id_type=MESH)

    count = len(others) + 1
    pl.semaphore_wait(barrier, jnp.where(inner, count + 1, count))


def opening_kernel(pieces, tokens, cotangent, gain, ids, counts, numer, denom, turns, *refs):
    sources, refs = list(refs[:8]), refs[8:]
    out, line_q, line_g, first, last, inverse, low, factor, cosine, sine, *refs = refs
    rows_q, rows_g, normed, output_t, down_t, *sems = refs
    begin, forward, across, finish = gather_steps(normed, out, *sems[:3], False)
    y = lax.axis_index("y")
    steps = [
        line_steps(rows, line, *sems[3 * i + 3 : 3 * i + 6], part, which)
        for part, which in ((0, y), (1, 1 - y))
        for i, (rows, line) in enumerate(((rows_q, line_q), (rows_g, line_g)))
    ]
    output_ref, down_ref = sources[4], sources[7]
    sources[4], sources[7] = output_t, down_t
    swaps = [
        swap_steps(pieces, sources, (rows_q, rows_g, first, last), *sems[9:], wanted)
        for wanted in (lambda out: out == 0, lambda out: out == 1, lambda out: out > 1)
    ]
    step = 64

    def norm(i):
        at = pl.ds(i * step, step)
        x = tokens[at].astype(F32)
        inv = lax.rsqrt(jnp.mean(x * x, -1, keepdims=True) + EPSILON)
        inverse[at] = inv
        normed[at] = (x * inv * gain[...].astype(F32).reshape(1, -1)).astype(BF16)

    def weigh(i):
        at = pl.ds(i * step, step)
        low[at] = (cotangent[at].astype(F32) * factor[...]).astype(BF16)

    def turn(i):
        at = pl.ds(i * 128, 128)
        places = lax.broadcasted_iota(jnp.int32, (128, cosine.shape[1]), 0) + i * 128
        angles = places.astype(F32) * turns[0:1]
        cosine[at] = jnp.cos(angles)
        sine[at] = jnp.sin(angles) * turns[1:2]

    greet_line(tuple(place()[3].values()), *steps[0][4]())
    swaps[0][0]()
    output_t[...] = output_ref[...].astype(F32).T.astype(BF16)
    swaps[1][0]()
    for i in range(2):
        swaps[i][1]()
        steps[i][0]()
    pl.loop(0, tokens.shape[0] // step)(norm)
    begin()
    for i in range(2):
        swaps[i][2]()
        steps[i + 2][0]()
    steps[0][1]()
    steps[1][1]()
    chosen = lax.broadcasted_iota(jnp.int32, counts.shape, 1) == ids[...]
    ratio = numer[...].astype(F32) / denom[...].astype(F32) * LENGTH / counts[...].astype(F32)
    factor[...] = jnp.sum(jnp.where(chosen, ratio, 0.0), -1, keepdims=True)

    @pl.loop(0, down_ref.shape[0] // 256)
    def _(i):
        at = pl.ds(pl.multiple_of(i * 256, 256), 256)
        down_t[:, at] = down_ref[at].astype(F32).T.astype(BF16)

    forward()
    across()
    swaps[2][0]()
    steps[2][1]()
    steps[3][1]()
    steps[0][2]()
    steps[1][2]()
    pl.loop(0, tokens.shape[0] // step)(weigh)
    steps[2][2]()
    steps[3][2]()
    pl.loop(0, cosine.shape[0] // 128)(turn)
    finish()
    for step_set in steps:
        step_set[3]()
    swaps[2][1]()
    swaps[2][2]()


def opening(tokens, cotangent, gain, domains, weights, split, full_len, head):
    rows, width = tokens.shape
    halves = [weight.shape[0 if i in (4, 7) else 1] // 2 for i, weight in enumerate(weights)]
    groups = (
        [(i, 0, halves[i]) for i in (0, 1, 2)],
        [(i, 0, halves[i]) for i in (3, 4)],
        [(i, 0, split) for i in (5, 6, 7)],
        [(i, split, halves[i] - split) for i in (5, 6, 7)],
    )
    pieces, widths = [], []
    for group in groups:
        at = 0
        for source, first, count in group:
            pieces.append((source, len(widths), first, count, at))
            at += count
        widths.append(at)
    inverse = 1.0 / np.float32(ROPE_BASE) ** (np.arange(head // 2, dtype=np.float32) * np.float32(2.0 / head))
    turns = np.stack([np.tile(inverse, 2), np.repeat(np.float32([-1.0, 1.0]), head // 2)]).astype(np.float32)
    whole, loose = pl.BlockSpec(memory_space=pltpu.VMEM), pl.BlockSpec(memory_space=pl.ANY)
    shape = jax.ShapeDtypeStruct
    dma = pltpu.SemaphoreType.DMA
    gathered, *outs = pl.pallas_call(
        functools.partial(opening_kernel, pieces),
        out_shape=(
            shape((2, 2, 2, rows, width), BF16),
            *[shape((8 * rows, size), BF16) for size in widths[:2]],
            *[shape((2 * rows, size), BF16) for size in widths[2:]],
            shape((rows, 1), F32),
            shape((rows, width), BF16),
            shape((1, 1), F32),
            shape((full_len, head), F32),
            shape((full_len, head), F32),
        ),
        in_specs=[whole] * (8 + len(weights)),
        out_specs=(*[loose] * 5, *[whole] * 5),
        scratch_shapes=[
            *[pltpu.VMEM((2 * rows, size), BF16) for size in widths[:2]],
            pltpu.VMEM((rows, width), BF16),
            *[pltpu.VMEM(weights[i].shape[::-1], BF16) for i in (4, 7)],
            *GATHER_SEMAPHORES,
            *[dma((2,)), dma((10,)), dma((10,))] * 2,
            *[dma((len(pieces),))] * 3,
        ],
        compiler_params=pltpu.CompilerParams(
            collective_id=2, has_side_effects=True, vmem_limit_bytes=VMEM_BYTES
        ),
        cost_estimate=micros(80),
        name="opening",
    )(
        tokens,
        cotangent,
        gain,
        *(domain.reshape(1, -1) for domain in domains),
        jnp.asarray(turns),
        *weights,
    )
    return gathered.reshape(8 * rows, width), *outs


def add_rows(target, start, size, other, base, step=64):
    @pl.loop(0, size // step)
    def _(i):
        at, there = pl.ds(start + i * step, step), pl.ds(base + i * step, step)
        target[at] = (target[at].astype(F32) + other[there].astype(F32)).astype(target.dtype)


def product_steps(windows, lefts, rights, left_vmem, right_vmem, own, pairs, got, load_sem, send, recv):
    y, x, c, device = place()
    remote = remote_copies(send, recv, device)
    rows, width = own.shape[1:]
    half, both, tile = rows // 2, 2 * rows, 256
    targets = ((1 - y, 1 - x), (1 - y, x), (y, 1 - x), (y, x))
    pieces = ((0, 0, half), (0, half, half), (1, 0, rows), (2, 0, rows), (3, 0, rows))
    count = len(lefts)
    right_loads = [
        pltpu.make_async_copy(
            rights[j].at[:, pl.ds(windows[j], right_vmem[j].shape[1])], right_vmem[j], load_sem.at[j]
        )
        for j in range(count)
    ]
    left_loads = []
    for i, (a, b) in enumerate(targets):
        start = pl.multiple_of((a * 2 + b) * both, both)
        left_loads.append(
            [
                pltpu.make_async_copy(
                    lefts[j].at[pl.ds(start, both)], left_vmem[j].at[i], load_sem.at[count * (i + 1) + j]
                )
                for j in range(count)
            ]
        )
    crossing = [
        remote(k, pairs.at[i, 1 - c, pl.ds(first, size)], got.at[i, pl.ds(first, size)], "c")
        for k, (i, first, size) in enumerate(pieces)
    ]

    def load():
        for copy in right_loads:
            copy.start()
        for copies in left_loads:
            for copy in copies:
                copy.start()

    def ready():
        for copy in right_loads:
            copy.wait()

    def product(i):
        for copy in left_loads[i]:
            copy.wait()

        @pl.loop(0, width // tile)
        def _(n):
            cols = pl.ds(pl.multiple_of(n * tile, tile), tile)
            total = dot_nt(left_vmem[0][i], right_vmem[0][cols])
            for j in range(1, count):
                total = total + dot_nt(left_vmem[j][i], right_vmem[j][cols])
            pairs[i, :, :, cols] = total.reshape(2, rows, tile).astype(BF16)

        for k, piece in enumerate(pieces):
            if piece[0] == i:
                crossing[k].start()

    def cores(k, step=64):
        i, first, size = pieces[k]
        crossing[k].wait_recv()

        @pl.loop(0, size // step)
        def _(n):
            at = pl.ds(first + n * step, step)
            own[i, at] = (pairs[i, c, at].astype(F32) + got[i, at].astype(F32)).astype(BF16)

    def finish():
        for copy in crossing:
            copy.wait_send()

    return load, ready, product, cores, finish


def axis_steps(own, x_diag, y_diag, x_got, y_got, send, recv):
    remote = remote_copies(send, recv, place()[3])
    rows = own.shape[1]
    half = rows // 2
    low, high = pl.ds(0, half), pl.ds(half, half)
    diag_x = remote(0, own.at[0, low], x_diag, "x")
    diag_y = remote(1, own.at[0, high], y_diag, "y")
    y_high = remote(2, own.at[1, high], y_got.at[high], "y")
    x_low = remote(3, own.at[2, low], x_got.at[low], "x")
    y_low = remote(4, own.at[1, low], y_got.at[low], "y")
    x_high = remote(5, own.at[2, high], x_got.at[high], "x")

    def second():
        diag_x.wait_recv()
        add_rows(own.at[1], 0, half, x_diag, 0)
        y_low.start()
        diag_y.wait_recv()
        add_rows(own.at[2], half, half, y_diag, 0)
        x_high.start()

    def finish(store, step=32):
        for copy in (y_high, x_low, y_low, x_high):
            copy.wait_recv()

        @pl.loop(0, rows // step)
        def _(i):
            at = pl.ds(i * step, step)
            store(at, own[3, at].astype(F32) + x_got[at].astype(F32) + y_got[at].astype(F32))

        for copy in (diag_x, diag_y, y_high, x_low, y_low, x_high):
            copy.wait_send()

    return diag_x, diag_y, x_low, y_high, second, finish


def scatter_steps(windows, lefts, rights, scratch):
    count = len(windows)
    product_scratch, axis_scratch = scratch[: 2 * count + 6], scratch[2 * count + 6 :]
    load, ready, product, cores, crossed = product_steps(
        windows, lefts, rights, product_scratch[:count], product_scratch[count : 2 * count],
        *product_scratch[2 * count :],
    )
    own = product_scratch[2 * count]
    diag_x, diag_y, x_low, y_high, second_axis, finish_axis = axis_steps(own, *axis_scratch)

    def first():
        ready()
        product(0)
        cores(0)
        diag_x.start()
        cores(1)
        diag_y.start()
        product(2)
        product(1)
        cores(3)
        x_low.start()
        cores(2)
        y_high.start()

    def second():
        second_axis()
        product(3)
        cores(4)

    def finish(store):
        finish_axis(store)
        crossed()

    return load, first, second, finish


def product_scratch(group, own=True):
    lefts, rights = [item[0] for item in group], [item[1] for item in group]
    rows, width = lefts[0].shape[0] // 8, rights[0].shape[0]
    return [
        *[pltpu.VMEM((4, 2 * rows, left.shape[1]), BF16) for left in lefts],
        *[pltpu.VMEM((width, left.shape[1]), BF16) for left in lefts],
        *[pltpu.VMEM((4, rows, width), BF16)] * own,
        pltpu.VMEM((4, 2, rows, width), BF16),
        pltpu.VMEM((4, rows, width), BF16),
        pltpu.SemaphoreType.DMA((5 * len(group),)),
        pltpu.SemaphoreType.DMA((5,)),
        pltpu.SemaphoreType.DMA((5,)),
    ]


def axis_scratch(rows, width):
    return [
        pltpu.VMEM((rows // 2, width), BF16),
        pltpu.VMEM((rows // 2, width), BF16),
        pltpu.VMEM((rows, width), BF16),
        pltpu.VMEM((rows, width), BF16),
        pltpu.SemaphoreType.DMA((6,)),
        pltpu.SemaphoreType.DMA((6,)),
    ]


def scatter_scratch(group):
    lefts, rights = [item[0] for item in group], [item[1] for item in group]
    rows, width = lefts[0].shape[0] // 8, rights[0].shape[0]
    scratch = product_scratch(group) + axis_scratch(rows, width)
    return lefts + rights, scratch, jax.ShapeDtypeStruct((rows, width), F32)


def middle_kernel(windows, *refs):
    count = len(windows)
    lefts, rights, refs = refs[:count], refs[count : 2 * count], refs[2 * count :]
    tokens, gain, hidden, inverse, normed, *scratch = refs
    load, first, second, finish = scatter_steps(windows, lefts, rights, scratch)

    def store(at, branch):
        total = tokens[at].astype(F32) + branch
        inv = lax.rsqrt(jnp.mean(total * total, -1, keepdims=True) + EPSILON)
        hidden[at] = total
        inverse[at] = inv
        normed[at] = (total * inv * gain[...].astype(F32)).astype(BF16)

    load()
    greet(tuple(place()[3].values()))
    first()
    second()
    finish(store)


def middle_back_kernel(windows, *refs):
    count = len(windows)
    lefts, rights, refs = refs[:count], refs[count : 2 * count], refs[2 * count :]
    hidden, inverse, gain, cotangent, factor, dhidden, dbranch, gain_grad, *scratch = refs
    load, first, second, finish = scatter_steps(windows, lefts, rights, scratch)
    gain_grad[...] = jnp.zeros_like(gain_grad)

    def store(at, grad):
        state, inv = hidden[at], inverse[at]
        gain_grad[...] += jnp.sum(grad * state * inv, 0, keepdims=True)
        upstream = cotangent[at].astype(F32) * factor[...]
        total = upstream + norm_back(grad, state, inv, gain[...].astype(F32))
        dhidden[at] = total
        dbranch[at] = total.astype(BF16)

    load()
    greet(tuple(place()[3].values()))
    first()
    second()
    finish(store)


def scatter_products(kernel, number, extras, outs, *group):
    operands, scratch, _ = scatter_scratch(group)
    whole = pl.BlockSpec(memory_space=pltpu.VMEM)
    return pl.pallas_call(
        functools.partial(kernel, [item[2] for item in group]),
        out_shape=outs,
        in_specs=[pl.BlockSpec(memory_space=pl.ANY)] * len(operands) + [whole] * len(extras),
        out_specs=(whole,) * len(outs),
        scratch_shapes=scratch,
        compiler_params=pltpu.CompilerParams(
            collective_id=number, has_side_effects=True, vmem_limit_bytes=VMEM_BYTES
        ),
        cost_estimate=micros(48),
        name="scatter_products",
    )(*operands, *extras)


def gather_beside_kernel(windows, tile, shard_ref, *refs):
    count = len(windows)
    lefts, rights, refs = refs[:count], refs[count : 2 * count], refs[2 * count :]
    mid, low, dgu, act, out_ref, sums_ref, grad_ref, *scratch = refs
    size = 2 * count + 5
    products, (mid_buf, low_buf, dgu_vmem, act_vmem, total, tile_sem, side_sem), sems = (
        scratch[:size], scratch[size : size + 7], scratch[size + 7 :],
    )
    load, ready, product, cores, crossed = product_steps(
        windows, lefts, rights, products[:count], products[count : 2 * count], sums_ref,
        *products[2 * count :],
    )
    begin, forward, across, finish = gather_steps(shard_ref, out_ref, *sems)
    tiles = mid.shape[0] // tile
    sides = [
        pltpu.make_async_copy(dgu, dgu_vmem, side_sem.at[0]),
        pltpu.make_async_copy(act, act_vmem, side_sem.at[1]),
    ]

    def tile_copies(t):
        rows, slot = pl.ds(pl.multiple_of(t * tile, tile), tile), lax.rem(t, 2)
        return [
            pltpu.make_async_copy(source.at[rows], buffer.at[slot], tile_sem.at[i, slot])
            for i, (source, buffer) in enumerate(((mid, mid_buf), (low, low_buf)))
        ]

    load()
    greet(tuple(place()[3].values()))
    begin()
    for copy in (*sides, *tile_copies(0), *tile_copies(1)):
        copy.start()
    ready()
    for i in range(4):
        product(i)
    forward()
    for copy in sides:
        copy.wait()
    cores(0)
    cores(1)

    @pl.loop(0, tiles)
    def _(t):
        for copy in tile_copies(t):
            copy.wait()
        rows, slot = pl.ds(pl.multiple_of(t * tile, tile), tile), lax.rem(t, 2)
        add_products(t, total, 0, mid_buf.at[slot], dgu_vmem.at[rows])
        add_products(t, total, dgu_vmem.shape[1], low_buf.at[slot], act_vmem.at[rows])

        @pl.when(t + 2 < tiles)
        def _():
            for copy in tile_copies(t + 2):
                copy.start()

        @pl.when(t == tiles // 2 - 1)
        def _():
            across()
            for k in range(2, 5):
                cores(k)

    @pl.loop(0, total.shape[0] // 256)
    def _(m):
        at = pl.ds(m * 256, 256)
        grad_ref[at] = total[at].astype(BF16)

    crossed()
    finish()


def gather_beside(shard, group, mid, low, dgu, act, tile=512):
    rows, width = shard.shape
    operands = [item[0] for item in group] + [item[1] for item in group] + [mid, low, dgu, act]
    cols = dgu.shape[1] + act.shape[1]
    gathered, sums, grad = pl.pallas_call(
        functools.partial(gather_beside_kernel, [item[2] for item in group], tile),
        out_shape=(
            jax.ShapeDtypeStruct((2, 2, 2, rows, width), shard.dtype),
            jax.ShapeDtypeStruct((4, rows, width), BF16),
            jax.ShapeDtypeStruct((width, cols), BF16),
        ),
        in_specs=[
            pl.BlockSpec(memory_space=pltpu.VMEM),
            *[pl.BlockSpec(memory_space=pl.ANY)] * len(operands),
        ],
        out_specs=(
            pl.BlockSpec(memory_space=pl.ANY),
            pl.BlockSpec(memory_space=pltpu.VMEM),
            pl.BlockSpec(memory_space=pltpu.VMEM),
        ),
        scratch_shapes=[
            *product_scratch(group, own=False),
            pltpu.VMEM((2, tile, width), BF16),
            pltpu.VMEM((2, tile, width), BF16),
            pltpu.VMEM(dgu.shape, BF16),
            pltpu.VMEM(act.shape, BF16),
            pltpu.VMEM((width, cols), F32),
            pltpu.SemaphoreType.DMA((2, 2)),
            pltpu.SemaphoreType.DMA((2,)),
            *GATHER_SEMAPHORES,
        ],
        compiler_params=pltpu.CompilerParams(
            collective_id=6, has_side_effects=True, vmem_limit_bytes=VMEM_BYTES
        ),
        cost_estimate=micros(44),
        name="gather_beside",
    )(shard, *operands)
    return gathered.reshape(8 * rows, width), sums, grad


def line_scatter_steps(grad_ref, own, from_edge, from_middle, inward, load_sem, send, recv, part, which):
    z = lax.axis_index("z")
    rows, half = own.shape[1], own.shape[1] // 2
    pair, middle = z + 1 - 2 * lax.rem(z, 2), 3 - z
    inner = (z == 1) | (z == 2)
    edge = jnp.logical_not(inner)
    far = middle + 1 - 2 * lax.rem(middle, 2)
    first = pl.multiple_of(which * half, half)
    span = pl.ds(first, half)

    def block(index):
        return grad_ref.at[pl.ds(pl.multiple_of(index * rows + first, half), half)]

    def remote(index, source, target, peer):
        return pltpu.make_async_remote_copy(
            src_ref=source,
            dst_ref=target,
            send_sem=send.at[6 * part + index],
            recv_sem=recv.at[6 * part + index],
            device_id={"z": peer},
            device_id_type=MESH,
        )

    indices = (far, middle, pair, z)
    loads = [
        pltpu.make_async_copy(block(index), own.at[i, span], load_sem.at[4 * part + i])
        for i, index in enumerate(indices)
    ]
    edge_far = remote(0, own.at[1, span], from_edge.at[0, span], pair)
    edge_near = remote(1, own.at[0, span], from_edge.at[1, span], pair)
    edge_pair = remote(2, own.at[2, span], from_edge.at[2, span], pair)
    inner_far = remote(3, own.at[0, span], from_middle.at[0, span], middle)
    inner_near = remote(4, own.at[1, span], from_middle.at[1, span], middle)
    outward = remote(5, own.at[2, span], inward.at[span], pair)
    step = 128

    def add_into(target, other):
        @pl.loop(0, half // step)
        def _(i):
            at = pl.ds(first + i * step, step)
            target[at] = (target[at].astype(F32) + other[at].astype(F32)).astype(target.dtype)

    def load():
        for copy in loads:
            copy.start()

    def begin():
        for copy in loads:
            copy.wait()

        @pl.when(edge)
        def _():
            for copy in (edge_far, edge_near, edge_pair):
                copy.start()

    def second():
        @pl.when(inner)
        def _():
            edge_far.wait_recv()
            add_into(own.at[0], from_edge.at[0])
            inner_far.start()

    def third():
        @pl.when(inner)
        def _():
            edge_near.wait_recv()
            add_into(own.at[1], from_edge.at[1])
            inner_near.start()
            inner_far.wait_recv()
            add_into(own.at[2], from_middle.at[0])
            outward.start()

    def finish():
        @pl.when(inner)
        def _():
            edge_pair.wait_recv()
            add_into(own.at[3], from_edge.at[2])
            inner_near.wait_recv()
            add_into(own.at[3], from_middle.at[1])
            for copy in (inner_far, inner_near, outward):
                copy.wait_send()

        @pl.when(edge)
        def _():
            outward.wait_recv()
            add_into(own.at[3], inward)
            for copy in (edge_far, edge_near, edge_pair):
                copy.wait_send()

    return load, begin, second, third, finish


def total_steps(near, far, near_send, near_recv, far_send, far_recv):
    z, y, x, c = (lax.axis_index(name) for name in "zyxc")
    here = (y * 2 + x) * 2 + c
    others = [
        {"y": lax.rem(y + i // 4, 2), "x": lax.rem(x + i // 2 % 2, 2), "c": lax.rem(c + i % 2, 2)}
        for i in range(1, 8)
    ]
    levels = [{"z": lax.rem(z + i, 4)} for i in range(1, 4)]

    def remote(index, source, target, send, recv, device):
        return pltpu.make_async_remote_copy(
            src_ref=source,
            dst_ref=target,
            send_sem=send.at[index],
            recv_sem=recv.at[index],
            device_id=device,
            device_id_type=MESH,
        )

    around = [
        remote(i, near.at[here], near.at[here], near_send, near_recv, other)
        for i, other in enumerate(others)
    ]
    along = [
        remote(i, far.at[z], far.at[z], far_send, far_recv, level) for i, level in enumerate(levels)
    ]

    def begin():
        for copy in around:
            copy.start()

    def second():
        for copy in around:
            copy.wait()
        total = near[0]
        for i in range(1, 8):
            total = total + near[i]
        far[z] = total
        for copy in along:
            copy.start()

    def finish():
        for copy in along:
            copy.wait()
        total = far[0]
        for i in range(1, 4):
            total = total + far[i]
        return total

    return begin, second, finish, here, others, levels


def tail_kernel(windows, *refs):
    count = len(windows)
    lefts, rights, refs = refs[:count], refs[count : 2 * count], refs[2 * count :]
    grad_ref, tokens_ref, inverse_ref, dhidden_ref, gain_ref, *refs = refs
    gains, (out_ref, mine_ref, theirs_ref, total_ref), scratch = refs[:3], refs[3:7], refs[7:]
    size = 2 * count + 12
    load, first, second, finish = scatter_steps(windows, lefts, rights, scratch[:size])
    line, (swap_sem,), total = scratch[size : size + 7], scratch[size + 7 : size + 8], scratch[size + 8 :]
    near, far = total[:2]
    total_begin, total_second, total_finish, here, others, levels = total_steps(*total)
    y = lax.axis_index("y")
    lines = [line_scatter_steps(grad_ref, *line, part, which) for part, which in ((0, 1 - y), (1, y))]
    load()
    for steps in lines:
        steps[0]()
    width = out_ref.shape[1]
    near[here, :, pl.ds(width, width)] = gains[0][...]
    head = gains[1].shape[1]
    near[here, :, pl.ds(2 * width, head)] = gains[1][...]
    near[here, :, pl.ds(2 * width + head, head)] = gains[2][...]
    greet(others + levels)
    for steps in lines:
        steps[1]()
    first()
    lines[0][2]()
    second()
    lines[0][3]()
    lines[1][2]()
    gain_in = near.at[here, :, pl.ds(0, width)]
    gain_in[...] = jnp.zeros((1, width), F32)

    def store(at, grad):
        x, inv = tokens_ref[at].astype(F32), inverse_ref[at]
        gain_in[...] += jnp.sum(grad * x * inv, 0, keepdims=True)
        back = norm_back(grad, x, inv, gain_ref[...].astype(F32))
        out_ref[at] = (dhidden_ref[at] + back).astype(BF16)

    finish(store)
    total_begin()
    lines[1][3]()
    lines[0][4]()
    summed = line[0].at[3]
    half = theirs_ref.shape[0]
    swap = pltpu.make_async_remote_copy(
        src_ref=summed.at[pl.ds(pl.multiple_of((1 - y) * half, half), half)],
        dst_ref=theirs_ref,
        send_sem=swap_sem.at[0],
        recv_sem=swap_sem.at[1],
        device_id={"y": 1 - y},
        device_id_type=MESH,
    )
    swap.start()
    total_second()
    lines[1][4]()
    mine_ref[...] = summed[pl.ds(pl.multiple_of(y * half, half), half)]
    total_ref[...] = total_finish()
    swap.wait()


def tail(group, grad, tokens, inverse, dhidden, gain, gains):
    operands, scratch, total = scatter_scratch(group)
    rows, cols = grad.shape[0] // 4, grad.shape[1]
    length = 2 * total.shape[1] + 2 * gains[1].size
    half = jax.ShapeDtypeStruct((rows // 2, cols), BF16)
    whole = pl.BlockSpec(memory_space=pltpu.VMEM)
    block = lambda count: pltpu.VMEM((count, rows, cols), BF16)
    dma = pltpu.SemaphoreType.DMA
    return pl.pallas_call(
        functools.partial(tail_kernel, [item[2] for item in group]),
        out_shape=(
            jax.ShapeDtypeStruct(total.shape, BF16),
            half,
            half,
            jax.ShapeDtypeStruct((1, length), F32),
        ),
        in_specs=[pl.BlockSpec(memory_space=pl.ANY)] * (len(operands) + 1) + [whole] * 7,
        out_specs=(whole,) * 4,
        scratch_shapes=[
            *scratch,
            block(4), block(3), block(2), pltpu.VMEM((rows, cols), BF16), dma((8,)), dma((12,)), dma((12,)),
            dma((2,)),
            pltpu.VMEM((8, 1, length), F32), pltpu.VMEM((4, 1, length), F32), dma((7,)), dma((7,)), dma((3,)), dma((3,)),
        ],
        compiler_params=pltpu.CompilerParams(
            collective_id=0, has_side_effects=True, vmem_limit_bytes=VMEM_BYTES
        ),
        cost_estimate=micros(52),
        name="tail",
    )(*operands, grad, tokens, inverse, dhidden, gain.reshape(1, -1), *(gain.reshape(1, -1) for gain in gains))


def swap_y(value):
    return lax.ppermute(value, "y", [(0, 1), (1, 0)])


def in_y_order(mine, theirs, axis):
    count = mine.shape[axis]
    return lax.dynamic_slice_in_dim(
        jnp.concatenate([mine, theirs, mine], axis), lax.axis_index("y") * count, 2 * count, axis
    )


def gather_rows(rows):
    return lax.all_gather(rows, "z", axis=0, tiled=True)


def scatter_grads(grad):
    return lax.psum_scatter(grad.astype(BF16), "z", scatter_dimension=0, tiled=True)


def their_rows(part):
    half = part.shape[0] // 2
    return swap_y(
        lax.dynamic_slice_in_dim(part, (1 - lax.axis_index("y")) * half, half, 0)
    )


def join_pieces(plan, y, mine_of, theirs_of, outs):
    for source, first, width, out, at, turned in plan:
        half = outs[out].shape[0 if turned else 1] // 2
        cols = pl.ds(first, width)
        for which, piece in ((y, mine_of(source, cols)), (1 - y, theirs_of(source, cols))):
            target = pl.ds(pl.multiple_of(which * half + at, 128), width)
            if turned:
                outs[out][target, :] = piece.astype(F32).T
            else:
                outs[out][:, target] = piece.astype(F32)


def join_kernel(plan, count, y_rows, *refs):
    y = lax.axis_index("y")
    parts, theirs, outs = refs[:count], refs[count : 2 * count], refs[2 * count :]
    mine = pl.ds(pl.multiple_of(y * y_rows, y_rows), y_rows)
    own = lambda source, cols: parts[source][mine, cols]
    got = lambda source, cols: theirs[source][:, cols]
    join_pieces(plan, y, own, got, outs)


def join_grads(parts, theirs, plan, shapes):
    whole = pl.BlockSpec(memory_space=pltpu.VMEM)
    return pl.pallas_call(
        functools.partial(join_kernel, plan, len(parts), theirs[0].shape[0]),
        out_shape=tuple(jax.ShapeDtypeStruct(shape, F32) for shape in shapes),
        in_specs=[whole] * (2 * len(parts)),
        out_specs=(whole,) * len(shapes),
        compiler_params=pltpu.CompilerParams(vmem_limit_bytes=VMEM_BYTES),
        cost_estimate=micros(5),
        name="join_grads",
    )(*parts, *theirs)


def last_join_kernel(plan, mine, theirs, total, *outs):
    gains, grads, start = outs[:4], outs[4:], 0
    for gain in gains:
        gain[...] = total[:, pl.ds(start, gain.shape[1])]
        start += gain.shape[1]
    y = lax.axis_index("y")
    join_pieces(plan, y, lambda _, cols: mine[:, cols], lambda _, cols: theirs[:, cols], grads)


def join_last(mine, theirs, total, plan, sizes, shapes):
    whole = pl.BlockSpec(memory_space=pltpu.VMEM)
    outs = (*((1, size) for size in sizes), *shapes)
    return pl.pallas_call(
        functools.partial(last_join_kernel, plan),
        out_shape=tuple(jax.ShapeDtypeStruct(shape, F32) for shape in outs),
        in_specs=[whole] * 3,
        out_specs=(whole,) * len(outs),
        cost_estimate=micros(4),
        name="join_last",
    )(mine, theirs, total)


def normed_rope(raw, gain, cosine, sine):
    inverse = lax.rsqrt(jnp.mean(raw * raw, -1, keepdims=True) + EPSILON)
    scaled = raw * inverse * gain
    turned = pltpu.roll(scaled, scaled.shape[-1] // 2, 1)
    return (scaled * cosine + turned * sine).astype(BF16)


def normed_rope_back(grad, raw, gain, cosine, sine):
    inverse = lax.rsqrt(jnp.mean(raw * raw, -1, keepdims=True) + EPSILON)
    straight = grad * cosine - pltpu.roll(grad, grad.shape[-1] // 2, 1) * sine
    gain_part = jnp.sum(straight * (raw * inverse), 0, keepdims=True)
    return norm_back(straight, raw, inverse, gain).astype(BF16), gain_part


def causal_scores(query, keys, first, scaling):
    scores = dot_nt(query, keys) * scaling
    rows = lax.broadcasted_iota(jnp.int32, scores.shape, 0) + first
    columns = lax.broadcasted_iota(jnp.int32, scores.shape, 1)
    return jnp.where(rows >= columns, scores, -1e30)


def attend_kernel(
    heads, head, block, normed_ref, w_ref, wg_ref, low_ref, qg_ref, kg_ref, cos_ref, sin_ref,
    raw_ref, out_ref, log_ref, gate_ref, mixed_ref, all_ref, key_ref, value_ref, *sems,
):
    seq, step, steps = pl.program_id(0), pl.program_id(1), pl.num_programs(1)
    tick = seq * steps + step
    scaling = head**-0.5
    at = heads * head
    begin, forward, across, finish = gather_steps(low_ref, all_ref, *sems)

    @pl.when(tick == 0)
    def _():
        greet(tuple(place()[3].values()))
        begin()

    pl.when(tick == 3)(forward)
    pl.when(tick == 6)(across)
    raw_ref[...] = dot_nn(normed_ref[...], w_ref[...])
    here = pl.ds(pl.multiple_of(step * block, block), block)
    cosine, sine = cos_ref[here], sin_ref[here]

    @pl.when(tick == 0)
    def _():
        key_ref[...] = jnp.zeros_like(key_ref)
        value_ref[...] = jnp.zeros_like(value_ref)

    key_ref[here] = normed_rope(raw_ref[:, at : at + head], kg_ref[...], cosine, sine)
    value_ref[here] = raw_ref[:, at + head :].astype(BF16)

    for i in range(0, key_ref.shape[0] // block, 2):

        @pl.when(step // 2 == i // 2)
        def _():
            seen = pl.ds(0, (i + 2) * block)

            @pl.loop(0, heads)
            def _(h):
                cols = pl.ds(pl.multiple_of(h * head, head), head)
                query = normed_rope(raw_ref[:, cols], qg_ref[...], cosine, sine)
                scores = causal_scores(query, key_ref[seen], step * block, scaling)
                highest = jnp.max(scores, -1, keepdims=True)
                exp_vals = jnp.exp(scores - highest)
                total = jnp.sum(exp_vals, -1, keepdims=True)
                probs = (exp_vals / total).astype(BF16)
                out_ref[:, cols] = dot_nn(probs, value_ref[seen])
                log_ref[h] = highest + jnp.log(total)

    gate = jax.nn.sigmoid(dot_nn(normed_ref[...], wg_ref[...]))
    gate_ref[...] = gate
    mixed_ref[...] = (out_ref[...] * gate).astype(BF16)
    pl.when(tick == pl.num_programs(0) * steps - 1)(finish)


def attend(normed, weights, gates, low, query_gain, key_gain, cosine, sine, heads, head, length, block=256):
    rows, width = normed.shape
    cols = weights.shape[1]
    seqs, steps = rows // length, length // block
    whole = lambda shape: pl.BlockSpec(
        shape, lambda s, i: (0,) * len(shape), pipeline_mode=pl.Buffered(1)
    )
    part = lambda cols: pl.BlockSpec((block, cols), lambda s, i: (s * steps + i, 0))
    *outs, gathered = pl.pallas_call(
        functools.partial(attend_kernel, heads, head, block),
        out_shape=(
            jax.ShapeDtypeStruct((rows, cols), F32),
            jax.ShapeDtypeStruct((rows, heads * head), F32),
            jax.ShapeDtypeStruct((heads, rows, 1), F32),
            jax.ShapeDtypeStruct((rows, heads * head), F32),
            jax.ShapeDtypeStruct((rows, heads * head), BF16),
            jax.ShapeDtypeStruct((2, 2, 2, *low.shape), low.dtype),
        ),
        grid=(seqs, steps),
        in_specs=[
            part(width),
            whole((width, cols)),
            whole((width, heads * head)),
            pl.BlockSpec(memory_space=pl.ANY),
            whole((1, head)),
            whole((1, head)),
            whole((length, head)),
            whole((length, head)),
        ],
        out_specs=(
            part(cols),
            part(heads * head),
            pl.BlockSpec((heads, block, 1), lambda s, i: (0, s * steps + i, 0)),
            part(heads * head),
            part(heads * head),
            pl.BlockSpec(memory_space=pl.ANY),
        ),
        scratch_shapes=[
            pltpu.VMEM((length, head), BF16),
            pltpu.VMEM((length, head), BF16),
            *GATHER_SEMAPHORES,
        ],
        compiler_params=pltpu.CompilerParams(collective_id=3, has_side_effects=True),
        cost_estimate=micros(42),
        name="attend",
    )(normed, weights, gates, low, query_gain, key_gain, cosine, sine)
    return *outs, gathered.reshape(rows, width)


def add_products(step, total_ref, start, left_ref, right_ref, tile=1024):
    wide = min(512, right_ref.shape[1])

    @pl.loop(0, left_ref.shape[1] // tile)
    def _(m):
        at = pl.ds(pl.multiple_of(m * tile, tile), tile)

        @pl.loop(0, right_ref.shape[1] // wide)
        def _(n):
            cols = pl.ds(pl.multiple_of(start + n * wide, wide), wide)
            part = dot_tn(left_ref[:, at], right_ref[:, pl.ds(pl.multiple_of(n * wide, wide), wide)])

            @pl.when(step == 0)
            def _():
                total_ref[at, cols] = part

            @pl.when(step > 0)
            def _():
                total_ref[at, cols] += part


def store_low(step, total_ref, out_ref, tile=256):
    @pl.when(step == pl.num_programs(0) - 1)
    def _():
        @pl.loop(0, total_ref.shape[0] // tile)
        def _(m):
            at = pl.ds(m * tile, tile)
            out_ref[at] = total_ref[at].astype(BF16)


def grads_kernel(left_ref, right_ref, out_ref, total_ref):
    step = pl.program_id(0)
    add_products(step, total_ref, 0, left_ref, right_ref)
    store_low(step, total_ref, out_ref)


def weight_grads(left, right, block=1024):
    (rows, width), cols = left.shape, right.shape[1]
    part = lambda cols: pl.BlockSpec((block, cols), lambda i: (i, 0))
    return pl.pallas_call(
        grads_kernel,
        out_shape=jax.ShapeDtypeStruct((width, cols), BF16),
        grid=(rows // block,),
        in_specs=[part(width), part(cols)],
        out_specs=pl.BlockSpec((width, cols), lambda i: (0, 0)),
        scratch_shapes=[pltpu.VMEM((width, cols), F32)],
        cost_estimate=micros(11),
        name="weight_grads",
    )(left, right)


def gate_back_kernel(
    normed_ref, branch_ref, w_ref, attended_ref, gate_ref, mixed_ref,
    dattended_ref, dgating_ref, grad_ref, total_ref,
):
    step = pl.program_id(0)
    dmixed = dot_nn(branch_ref[...], w_ref[...])
    gate = gate_ref[...]
    dattended_ref[...] = (dmixed * gate).astype(BF16)
    dgating_ref[...] = (dmixed * attended_ref[...] * gate * (1.0 - gate)).astype(BF16)
    add_products(step, total_ref, 0, normed_ref, dgating_ref)
    add_products(step, total_ref, dgating_ref.shape[1], branch_ref, mixed_ref)
    store_low(step, total_ref, grad_ref)


def gate_back(normed, branch, weights, attended, gate, mixed, block=1024):
    rows, width = normed.shape
    cols = attended.shape[1]
    part = lambda cols: pl.BlockSpec((block, cols), lambda i: (i, 0))
    return pl.pallas_call(
        gate_back_kernel,
        out_shape=(
            jax.ShapeDtypeStruct((rows, cols), BF16),
            jax.ShapeDtypeStruct((rows, cols), BF16),
            jax.ShapeDtypeStruct((width, 2 * cols), BF16),
        ),
        grid=(rows // block,),
        in_specs=[
            part(width),
            part(width),
            pl.BlockSpec((width, cols), lambda i: (0, 1)),
            part(cols),
            part(cols),
            part(cols),
        ],
        out_specs=(part(cols), part(cols), pl.BlockSpec((width, 2 * cols), lambda i: (0, 0))),
        scratch_shapes=[pltpu.VMEM((width, 2 * cols), F32)],
        compiler_params=pltpu.CompilerParams(vmem_limit_bytes=VMEM_BYTES),
        cost_estimate=micros(25),
        name="gate_back",
    )(normed, branch, weights, attended, gate, mixed)


def feed_kernel(count, tile, mid_ref, low_ref, w_ref, act_ref, dgu_ref, *grads):
    step = pl.program_id(0)

    @pl.loop(0, count // tile)
    def _(j):
        start = pl.multiple_of(j * tile, tile)
        at, after = pl.ds(start, tile), pl.ds(pl.multiple_of(count + start, tile), tile)
        last = pl.ds(pl.multiple_of(2 * count + start, tile), tile)
        gate = dot_nn(mid_ref[...], w_ref[:, at])
        up = dot_nn(mid_ref[...], w_ref[:, after])
        dact = dot_nn(low_ref[...], w_ref[:, last])
        sigma = jax.nn.sigmoid(gate)
        silu = gate * sigma
        act_ref[:, at] = (silu * up).astype(BF16)
        dgu_ref[:, at] = (dact * up * sigma * (1.0 + gate * (1.0 - sigma))).astype(BF16)
        dgu_ref[:, after] = (dact * silu).astype(BF16)

    if grads:
        grad_ref, total_ref = grads
        add_products(step, total_ref, 0, mid_ref, dgu_ref)
        add_products(step, total_ref, 2 * count, low_ref, act_ref)
        store_low(step, total_ref, grad_ref)


def feed_forward(mid, low, weights, grads, block):
    rows, width = mid.shape
    count = weights.shape[1] // 3
    part = lambda cols: pl.BlockSpec((block, cols), lambda i: (i, 0))
    whole = pl.BlockSpec(weights.shape, lambda i: (0, 0), pipeline_mode=pl.Buffered(1))
    return pl.pallas_call(
        functools.partial(feed_kernel, count, 256),
        out_shape=(
            jax.ShapeDtypeStruct((rows, count), BF16),
            jax.ShapeDtypeStruct((rows, 2 * count), BF16),
            *[jax.ShapeDtypeStruct(weights.shape, BF16)] * grads,
        ),
        grid=(rows // block,),
        in_specs=[part(width), part(width), whole],
        out_specs=(part(count), part(2 * count), *[whole] * grads),
        scratch_shapes=[pltpu.VMEM(weights.shape, F32)] * grads,
        compiler_params=pltpu.CompilerParams(vmem_limit_bytes=VMEM_BYTES),
        cost_estimate=micros(41 if grads else 14),
        name="feed_forward",
    )(mid, low, weights)


def attend_back_kernel(
    heads, head, block, raw_ref, up_ref, log_ref, qg_ref, kg_ref, cos_ref, sin_ref, sums_ref,
    out_ref, qg_out, kg_out, sum_ref, key_ref, value_ref, dkey_ref, dvalue_ref, own, load_sem, *scratch,
):
    seq, step, steps = pl.program_id(0), pl.program_id(1), pl.num_programs(1)
    tick = seq * steps + step
    scaling = head**-0.5
    at = heads * head
    blocks = raw_ref.shape[0] // block
    diag_x, diag_y, x_low, y_high, second, finish = axis_steps(own, *scratch)

    @pl.when(tick == 0)
    def _():
        load = pltpu.make_async_copy(sums_ref, own, load_sem)
        load.start()
        device = place()[3]
        greet((device["y"], device["x"]))
        load.wait()
        for copy in (diag_x, diag_y, x_low, y_high):
            copy.start()
        qg_out[...] = jnp.zeros_like(qg_out)
        kg_out[...] = jnp.zeros_like(kg_out)

    pl.when(tick == 4)(second)

    @pl.when(step == 0)
    def _():
        key_ref[...] = normed_rope(
            raw_ref[:, at : at + head], kg_ref[...], cos_ref[...], sin_ref[...]
        )
        value_ref[...] = raw_ref[:, at + head :].astype(BF16)
        dkey_ref[...] = jnp.zeros_like(dkey_ref)
        dvalue_ref[...] = jnp.zeros_like(dvalue_ref)

    rows = pl.ds(pl.multiple_of(step * block, block), block)

    for i in range(0, blocks, 2):

        @pl.when(step // 2 == i // 2)
        def _():
            seen = pl.ds(0, (i + 2) * block)

            @pl.loop(0, heads)
            def _(h):
                cols = pl.ds(pl.multiple_of(h * head, head), head)
                raw = raw_ref[rows, cols]
                query = normed_rope(raw, qg_ref[...], cos_ref[rows], sin_ref[rows])
                scores = causal_scores(query, key_ref[seen], step * block, scaling)
                probs = jnp.exp(scores - log_ref[h])
                upstream = up_ref[:, cols]
                dprobs = dot_nt(upstream, value_ref[seen])
                centre = jnp.sum(dprobs * probs, -1, keepdims=True)
                dscores = (probs * (dprobs - centre)).astype(BF16)
                dkey_ref[seen] += dot_tn(dscores, query)
                dvalue_ref[seen] += dot_tn(probs.astype(BF16), upstream)
                dquery = dot_nn(dscores, key_ref[seen]) * scaling
                grad, part = normed_rope_back(
                    dquery, raw, qg_ref[...], cos_ref[rows], sin_ref[rows]
                )
                out_ref[rows, cols] = grad
                qg_out[...] += part

    @pl.when(step == blocks - 1)
    def _():
        grad, part = normed_rope_back(
            dkey_ref[...] * scaling,
            raw_ref[:, at : at + head],
            kg_ref[...],
            cos_ref[...],
            sin_ref[...],
        )
        out_ref[:, at : at + head] = grad
        out_ref[:, at + head :] = dvalue_ref[...].astype(BF16)
        kg_out[...] += part

    @pl.when(tick == pl.num_programs(0) * steps - 1)
    def _():
        def store(rows, value):
            sum_ref[rows] = value

        finish(store)


def attend_back(
    raw, upstream, logs, query_gain, key_gain, cosine, sine, sums, heads, head, length, block=256
):
    rows = raw.shape[0]
    total = jax.ShapeDtypeStruct(sums.shape[1:], F32)
    seqs, steps = rows // length, length // block
    whole = lambda shape: pl.BlockSpec(shape, lambda s, i: (0,) * len(shape))
    return pl.pallas_call(
        functools.partial(attend_back_kernel, heads, head, block),
        out_shape=(
            jax.ShapeDtypeStruct(raw.shape, BF16),
            jax.ShapeDtypeStruct((1, head), F32),
            jax.ShapeDtypeStruct((1, head), F32),
            total,
        ),
        grid=(seqs, steps),
        in_specs=[
            pl.BlockSpec((length, raw.shape[1]), lambda s, i: (s, 0)),
            pl.BlockSpec((block, heads * head), lambda s, i: (s * steps + i, 0)),
            pl.BlockSpec((heads, block, 1), lambda s, i: (0, s * steps + i, 0)),
            whole((1, head)),
            whole((1, head)),
            whole((length, head)),
            whole((length, head)),
            pl.BlockSpec(memory_space=pl.ANY),
        ],
        out_specs=(
            pl.BlockSpec((length, raw.shape[1]), lambda s, i: (s, 0)),
            whole((1, head)),
            whole((1, head)),
            whole(total.shape),
        ),
        scratch_shapes=[
            pltpu.VMEM((length, head), BF16),
            pltpu.VMEM((length, head), BF16),
            pltpu.VMEM((length, head), F32),
            pltpu.VMEM((length, head), F32),
            pltpu.VMEM(sums.shape, BF16),
            pltpu.SemaphoreType.DMA,
            *axis_scratch(*sums.shape[1:]),
        ],
        compiler_params=pltpu.CompilerParams(
            collective_id=5, has_side_effects=True, vmem_limit_bytes=VMEM_BYTES
        ),
        cost_estimate=micros(40),
        name="attend_back",
    )(raw, upstream, logs, query_gain, key_gain, cosine, sine, sums)


def attention_weights(query_proj, key_proj, value_proj, gating_proj, output_proj):
    return (
        lax.all_gather(query_proj, "dp", axis=0, tiled=True),
        lax.all_gather(key_proj, "dp", axis=0, tiled=True),
        lax.all_gather(value_proj, "dp", axis=0, tiled=True),
        lax.all_gather(gating_proj, "dp", axis=0, tiled=True),
        lax.all_gather(output_proj, "dp", axis=1, tiled=True),
    )


def swiglu_weights(swiglu_gate, swiglu_up, swiglu_down):
    return (
        lax.all_gather(swiglu_gate, "dp", axis=0, tiled=True),
        lax.all_gather(swiglu_up, "dp", axis=0, tiled=True),
        lax.all_gather(swiglu_down, "dp", axis=1, tiled=True),
    )


def softmax_forward_mapped(seq_items, causal):
    queries, keys_seq, values_seq = seq_items
    scaling = queries.shape[-1] ** (-0.5)
    scores = (
        jnp.einsum("qgjd,kgd->gjqk", queries, keys_seq, preferred_element_type=jnp.float32)
        * scaling
    )
    scores = jnp.where(causal, scores, -1e30)
    highest = jnp.max(scores, -1, keepdims=True)
    exp_vals = jnp.exp(scores - highest)
    row_totals = jnp.sum(exp_vals, -1, keepdims=True)
    attn_probs = (exp_vals / row_totals).astype(jnp.bfloat16)
    attended = jnp.einsum(
        "gjqk,kgd->qgjd", attn_probs, values_seq, preferred_element_type=jnp.float32
    )
    return (attended, highest[..., 0] + jnp.log(row_totals[..., 0]))


def softmax_backward_mapped(seq_items, causal):
    queries, keys_seq, values_seq, log_total, upstream = seq_items
    scaling = queries.shape[-1] ** (-0.5)
    scores = (
        jnp.einsum("qgjd,kgd->gjqk", queries, keys_seq, preferred_element_type=jnp.float32)
        * scaling
    )
    scores = jnp.where(causal, scores, -1e30)
    attn_probs = jnp.exp(scores - log_total[..., None])
    dprobs = jnp.einsum("qgjd,kgd->gjqk", upstream, values_seq, preferred_element_type=jnp.float32)
    centre = jnp.sum(dprobs * attn_probs, -1, keepdims=True)
    dscores = (attn_probs * (dprobs - centre)).astype(jnp.bfloat16)
    dqueries = (
        jnp.einsum("gjqk,kgd->qgjd", dscores, keys_seq, preferred_element_type=jnp.float32)
        * scaling
    )
    key_grads = (
        jnp.einsum("gjqk,qgjd->kgd", dscores, queries, preferred_element_type=jnp.float32) * scaling
    )
    value_grads = jnp.einsum(
        "gjqk,qgjd->kgd",
        attn_probs.astype(jnp.bfloat16),
        upstream,
        preferred_element_type=jnp.float32,
    )
    key_rows = key_grads.shape[0]
    return (dqueries, key_grads.reshape(key_rows, -1), value_grads.reshape(key_rows, -1))


def per_device_wide(
    tokens,
    cotangent,
    domain_ids,
    domain_counts,
    domain_numer,
    domain_denom,
    attention_gain,
    query_gain,
    key_gain,
    query_proj,
    key_proj,
    value_proj,
    gating_proj,
    output_proj,
    swiglu_gain,
    swiglu_gate,
    swiglu_up,
    swiglu_down,
):
    seq_count, local_len, model_width = tokens.shape
    full_len = local_len * lax.axis_size("ctx")
    local_rows = seq_count * local_len
    all_rows = seq_count * full_len
    head_dim = query_gain.shape[0]
    local_heads = query_proj.shape[1] // head_dim
    local_kv = key_proj.shape[1] // head_dim
    group_size = local_heads // local_kv
    positions = jnp.arange(full_len, dtype=jnp.int32)
    causal = positions[:, None] >= positions[None, :]
    cosine, sine = rope_tables(positions, head_dim)
    cos_rows = cosine[:, None, :]
    sin_rows = sine[:, None, :]
    inputs = tokens.reshape(local_rows, model_width).astype(jnp.float32)
    inverse_in = lax.rsqrt(jnp.mean(inputs * inputs, -1, keepdims=True) + EPSILON)
    gain_in = attention_gain.astype(jnp.float32)
    normed = (inputs * inverse_in * gain_in).astype(jnp.bfloat16)
    normed_all = lax.all_gather(
        normed.reshape(seq_count, local_len, model_width), "ctx", axis=1, tiled=True
    ).reshape(all_rows, model_width)
    attn_full = attention_weights(query_proj, key_proj, value_proj, gating_proj, output_proj)
    query_raw = dot_nn(normed_all, attn_full[0]).reshape(
        seq_count, full_len, local_heads, head_dim
    )
    key_raw = dot_nn(normed_all, attn_full[1]).reshape(seq_count, full_len, local_kv, head_dim)
    value_low = (
        dot_nn(normed_all, attn_full[2])
        .astype(jnp.bfloat16)
        .reshape(seq_count, full_len, local_kv, head_dim)
    )
    gate_pre = dot_nn(normed_all, attn_full[3])
    query_scale = query_gain.astype(jnp.float32)
    key_scale = key_gain.astype(jnp.float32)
    query_inv = lax.rsqrt(jnp.mean(query_raw * query_raw, -1, keepdims=True) + EPSILON)
    key_inv = lax.rsqrt(jnp.mean(key_raw * key_raw, -1, keepdims=True) + EPSILON)
    query_low = rotate(query_raw * query_inv * query_scale, cos_rows, sin_rows).astype(jnp.bfloat16)
    key_low = rotate(key_raw * key_inv * key_scale, cos_rows, sin_rows).astype(jnp.bfloat16)
    query_groups = query_low.reshape(seq_count, full_len, local_kv, group_size, head_dim)
    attended, log_total = lax.map(
        lambda seq_items: softmax_forward_mapped(seq_items, causal), (query_groups, key_low, value_low)
    )
    attended = attended.reshape(all_rows, local_heads * head_dim)
    gate_sig = jax.nn.sigmoid(gate_pre)
    mixed = (attended * gate_sig).astype(jnp.bfloat16)
    branch_part = dot_nn(mixed, attn_full[4]).reshape(seq_count, full_len, model_width)
    branch = lax.psum_scatter(branch_part, "ctx", scatter_dimension=1, tiled=True).reshape(
        local_rows, model_width
    )
    hidden = inputs + branch
    inverse_mid = lax.rsqrt(jnp.mean(hidden * hidden, -1, keepdims=True) + EPSILON)
    gain_mid = swiglu_gain.astype(jnp.float32)
    normed_mid = (hidden * inverse_mid * gain_mid).astype(jnp.bfloat16)
    normed_mid_all = lax.all_gather(
        normed_mid.reshape(seq_count, local_len, model_width), "ctx", axis=1, tiled=True
    ).reshape(all_rows, model_width)
    swiglu_full = swiglu_weights(swiglu_gate, swiglu_up, swiglu_down)
    gate_ff = dot_nn(normed_mid_all, swiglu_full[0])
    up_val = dot_nn(normed_mid_all, swiglu_full[1])
    gate_sigma = jax.nn.sigmoid(gate_ff)
    silu_val = gate_ff * gate_sigma
    activation = (silu_val * up_val).astype(jnp.bfloat16)
    down_part = dot_nn(activation, swiglu_full[2]).reshape(seq_count, full_len, model_width)
    ffn_branch = (
        lax.psum_scatter(down_part.astype(jnp.bfloat16), "ctx", scatter_dimension=1, tiled=True)
        .astype(jnp.float32)
        .reshape(local_rows, model_width)
    )
    layer_out = (hidden + ffn_branch).astype(jnp.bfloat16)
    domain_table = (
        domain_ids[:, None] == jnp.arange(domain_counts.shape[0], dtype=jnp.int32)[None, :]
    ).astype(jnp.float32)
    ratio = (
        domain_numer.astype(jnp.float32)
        / domain_denom.astype(jnp.float32)
        * LENGTH
        / domain_counts.astype(jnp.float32)
    )
    factor = jnp.sum(domain_table * ratio[None, :], 1)
    upstream = (cotangent.astype(jnp.float32) * factor[:, None, None]).reshape(
        local_rows, model_width
    )
    swiglu_back = swiglu_weights(swiglu_gate, swiglu_up, swiglu_down)
    out_low = upstream.astype(jnp.bfloat16)
    out_all = lax.all_gather(
        out_low.reshape(seq_count, local_len, model_width), "ctx", axis=1, tiled=True
    ).reshape(all_rows, model_width)
    dactivation = dot_nt(out_all, swiglu_back[2])
    dgate_low = (dactivation * up_val * gate_sigma * (1.0 + gate_ff * (1.0 - gate_sigma))).astype(
        jnp.bfloat16
    )
    dup_low = (dactivation * silu_val).astype(jnp.bfloat16)
    grad_down = dot_tn(activation, out_all)
    grad_gate = dot_tn(normed_mid_all, dgate_low)
    grad_up = dot_tn(normed_mid_all, dup_low)
    dmid_part = dot_nt(dgate_low, swiglu_back[0]) + dot_nt(dup_low, swiglu_back[1])
    dnormed_mid = lax.psum_scatter(
        dmid_part.reshape(seq_count, full_len, model_width), "ctx", scatter_dimension=1, tiled=True
    ).reshape(local_rows, model_width)
    grad_gain_mid = jnp.sum(dnormed_mid * hidden * inverse_mid, 0)
    dhidden = upstream + norm_back(dnormed_mid, hidden, inverse_mid, gain_mid)
    swiglu_grads = (
        lax.psum_scatter(
            grad_gate.astype(jnp.bfloat16), "dp", scatter_dimension=0, tiled=True
        ).astype(jnp.float32),
        lax.psum_scatter(
            grad_up.astype(jnp.bfloat16), "dp", scatter_dimension=0, tiled=True
        ).astype(jnp.float32),
        lax.psum_scatter(
            grad_down.astype(jnp.bfloat16), "dp", scatter_dimension=1, tiled=True
        ).astype(jnp.float32),
    )
    attn_back = attention_weights(query_proj, key_proj, value_proj, gating_proj, output_proj)
    dbranch_low = dhidden.astype(jnp.bfloat16)
    dbranch_all = lax.all_gather(
        dbranch_low.reshape(seq_count, local_len, model_width), "ctx", axis=1, tiled=True
    ).reshape(all_rows, model_width)
    grad_output = dot_tn(mixed, dbranch_all)
    dmixed = dot_nt(dbranch_all, attn_back[4])
    dattended_low = (dmixed * gate_sig).astype(jnp.bfloat16)
    dgating_low = (dmixed * attended * gate_sig * (1.0 - gate_sig)).astype(jnp.bfloat16)
    upstream_heads = dattended_low.reshape(seq_count, full_len, local_kv, group_size, head_dim)
    dquery_rot, dkey_rot, dvalue_sum = lax.map(
        lambda seq_items: softmax_backward_mapped(seq_items, causal),
        (query_groups, key_low, value_low, log_total, upstream_heads),
    )
    dvalue_low = dvalue_sum.reshape(all_rows, local_kv * head_dim).astype(jnp.bfloat16)
    dquery_normed = unrotate(
        dquery_rot.reshape(seq_count, full_len, local_heads, head_dim), cos_rows, sin_rows
    )
    dkey_normed = unrotate(
        dkey_rot.reshape(seq_count, full_len, local_kv, head_dim), cos_rows, sin_rows
    )
    grad_query_gain = jnp.sum(dquery_normed * query_raw * query_inv, (0, 1, 2))
    grad_key_gain = jnp.sum(dkey_normed * key_raw * key_inv, (0, 1, 2))
    dquery_low = (
        norm_back(dquery_normed, query_raw, query_inv, query_scale)
        .reshape(all_rows, -1)
        .astype(jnp.bfloat16)
    )
    dkey_low = (
        norm_back(dkey_normed, key_raw, key_inv, key_scale)
        .reshape(all_rows, -1)
        .astype(jnp.bfloat16)
    )
    dnormed_part = (
        dot_nt(dquery_low, attn_back[0])
        + dot_nt(dkey_low, attn_back[1])
        + dot_nt(dvalue_low, attn_back[2])
        + dot_nt(dgating_low, attn_back[3])
    )
    dnormed = (
        lax.psum_scatter(
            dnormed_part.reshape(seq_count, full_len, model_width).astype(jnp.bfloat16),
            "ctx",
            scatter_dimension=1,
            tiled=True,
        )
        .astype(jnp.float32)
        .reshape(local_rows, model_width)
    )
    grad_gain_in = jnp.sum(dnormed * inputs * inverse_in, 0)
    input_grad = (dhidden + norm_back(dnormed, inputs, inverse_in, gain_in)).astype(jnp.bfloat16)
    grad_query = dot_tn(normed_all, dquery_low)
    grad_key = dot_tn(normed_all, dkey_low)
    grad_value = dot_tn(normed_all, dvalue_low)
    grad_gating = dot_tn(normed_all, dgating_low)
    attention_grads = (
        lax.psum_scatter(
            grad_query.astype(jnp.bfloat16), "dp", scatter_dimension=0, tiled=True
        ).astype(jnp.float32),
        lax.psum_scatter(
            grad_key.astype(jnp.bfloat16), "dp", scatter_dimension=0, tiled=True
        ).astype(jnp.float32),
        lax.psum_scatter(
            grad_value.astype(jnp.bfloat16), "dp", scatter_dimension=0, tiled=True
        ).astype(jnp.float32),
        lax.psum_scatter(
            grad_gating.astype(jnp.bfloat16), "dp", scatter_dimension=0, tiled=True
        ).astype(jnp.float32),
        lax.psum_scatter(
            grad_output.astype(jnp.bfloat16), "dp", scatter_dimension=1, tiled=True
        ).astype(jnp.float32),
    )
    gain_grads = lax.psum(
        (grad_gain_in, grad_gain_mid, grad_query_gain, grad_key_gain), ("dp", "ctx")
    )
    return (
        layer_out.reshape(seq_count, local_len, model_width),
        input_grad.reshape(seq_count, local_len, model_width),
        gain_grads[0],
        gain_grads[2],
        gain_grads[3],
        attention_grads[0],
        attention_grads[1],
        attention_grads[2],
        attention_grads[3],
        attention_grads[4],
        gain_grads[1],
        swiglu_grads[0],
        swiglu_grads[1],
        swiglu_grads[2],
    )


def per_device(
    tokens,
    cotangent,
    domain_ids,
    domain_counts,
    domain_numer,
    domain_denom,
    attention_gain,
    query_gain,
    key_gain,
    query_proj,
    key_proj,
    value_proj,
    gating_proj,
    output_proj,
    swiglu_gain,
    swiglu_gate,
    swiglu_up,
    swiglu_down,
):
    seq_count, local_len, width = tokens.shape
    rows = seq_count * local_len
    full_len = local_len * lax.axis_size("x") * lax.axis_size("c")
    seqs = seq_count * lax.axis_size("y")
    head = query_gain.shape[0]
    kv_cols = key_proj.shape[1] // 2
    q_cols = query_proj.shape[1] // 2
    ff_cols = swiglu_gate.shape[1] // 2
    heads = q_cols // head
    split, rest = ff_cols * 2 // 3, ff_cols - ff_cols * 2 // 3
    tokens, cotangent = tokens.reshape(rows, width), cotangent.reshape(rows, width)
    (
        normed_all, w_qkv, w_go, rows_first, rows_last, inverse_in, out_low, factor, cos_rows, sin_rows,
    ) = opening(
        tokens,
        cotangent,
        attention_gain,
        (domain_ids, domain_counts, domain_numer, domain_denom),
        (
            query_proj, key_proj, value_proj, gating_proj, output_proj, swiglu_gate, swiglu_up, swiglu_down,
        ),
        split,
        full_len,
        head,
    )
    w_first = gather_rows(rows_first)
    w_last = gather_rows(rows_last)

    query_scale, key_scale = query_gain.astype(F32)[None], key_gain.astype(F32)[None]
    qkv, attended, logs, gate_sig, mixed, out_all = attend(
        normed_all, w_qkv, w_go, out_low, query_scale, key_scale, cos_rows, sin_rows, heads, head, full_len
    )
    wide, column = jax.ShapeDtypeStruct((rows, width), F32), jax.ShapeDtypeStruct((rows, 1), F32)
    low = jax.ShapeDtypeStruct((rows, width), BF16)
    gain_mid = swiglu_gain.reshape(1, -1)
    hidden, inverse_mid, normed_mid = scatter_products(
        middle_kernel, 7, (tokens, gain_mid), (wide, column, low), (mixed, w_go, q_cols)
    )
    mid_all = gather_tokens(normed_mid)

    act_first, dgu_first, grad_first = feed_forward(mid_all, out_all, w_first, True, 1024)
    part_first = scatter_grads(grad_first)
    w_last, grad_first = lax.optimization_barrier((w_last, grad_first))
    act_last, dgu_last = feed_forward(mid_all, out_all, w_last, False, 512)
    dhidden, dbranch, grad_gain_mid = scatter_products(
        middle_back_kernel,
        8,
        (hidden, inverse_mid, gain_mid, cotangent, factor),
        (wide, low, jax.ShapeDtypeStruct((1, width), F32)),
        (dgu_first, w_first, 0),
        (dgu_last, w_last, 0),
    )
    dbranch_all, ffn_sums, grad_last = gather_beside(
        dbranch,
        ((act_first, w_first, 2 * split), (act_last, w_last, 2 * rest)),
        mid_all,
        out_all,
        dgu_last,
        act_last,
    )
    part_last = scatter_grads(grad_last)
    dbranch_all, part_first = lax.optimization_barrier((dbranch_all, part_first))

    theirs_first = their_rows(part_first)
    dattended, dgating, grad_go = gate_back(
        normed_all, dbranch_all, w_go, attended, gate_sig, mixed
    )
    dattended, theirs_first, grad_go = lax.optimization_barrier((dattended, theirs_first, grad_go))
    part_go = scatter_grads(grad_go)
    dqkv, grad_query_gain, grad_key_gain, ffn_branch = attend_back(
        qkv, dattended, logs, query_scale, key_scale, cos_rows, sin_rows, ffn_sums, heads, head, full_len
    )
    grad_query_gain, grad_key_gain = grad_query_gain[0], grad_key_gain[0]
    dqkv, part_last = lax.optimization_barrier((dqkv, part_last))
    theirs_last = their_rows(part_last)
    layer_out = (hidden + ffn_branch).astype(BF16)
    dqkv, layer_out = lax.optimization_barrier((dqkv, layer_out))
    grad_qkv = weight_grads(normed_all, dqkv)
    grad_qkv, theirs_last = lax.optimization_barrier((grad_qkv, theirs_last))
    plan = [(0, i * split, split, i, 0, i == 2) for i in range(3)]
    plan += [(1, i * rest, rest, i, split, i == 2) for i in range(3)]
    grad_gate, grad_up, grad_down = join_grads(
        (part_first, part_last),
        (theirs_first, theirs_last),
        plan,
        [weight.shape for weight in (swiglu_gate, swiglu_up, swiglu_down)],
    )
    grad_qkv, layer_out, grad_gate, grad_up, grad_down = lax.optimization_barrier(
        (grad_qkv, layer_out, grad_gate, grad_up, grad_down)
    )
    input_grad, mine_qkv, theirs_qkv, totals = tail(
        ((dqkv, w_qkv, 0), (dgating, w_go, 0)),
        grad_qkv,
        tokens,
        inverse_in,
        dhidden,
        attention_gain,
        (grad_gain_mid, grad_query_gain, grad_key_gain),
    )
    input_grad, part_go = lax.optimization_barrier((input_grad, part_go))
    theirs_go = their_rows(part_go)
    grad_gating, grad_output = join_grads(
        (part_go,),
        (theirs_go,),
        [(0, 0, q_cols, 0, 0, False), (0, q_cols, q_cols, 1, 0, True)],
        (gating_proj.shape, output_proj.shape),
    )
    widths, starts = (q_cols, kv_cols, kv_cols), (0, q_cols, q_cols + kv_cols)
    *gain_grads, grad_query, grad_key, grad_value = join_last(
        mine_qkv,
        theirs_qkv,
        totals,
        [(0, starts[i], widths[i], i, 0, False) for i in range(3)],
        (width, width, head, head),
        [weight.shape for weight in (query_proj, key_proj, value_proj)],
    )
    gain_grads = [gain.reshape(-1) for gain in gain_grads]
    shape = (seq_count, local_len, width)
    return (
        layer_out.reshape(shape),
        input_grad.reshape(shape),
        gain_grads[0],
        gain_grads[2],
        gain_grads[3],
        grad_query,
        grad_key,
        grad_value,
        grad_gating,
        grad_output,
        gain_grads[1],
        grad_gate,
        grad_up,
        grad_down,
    )


def solution(mesh):
    if (mesh.shape["dp"], mesh.shape["ctx"]) == (8, 4):
        body = per_device
        mesh = Mesh(mesh.devices.reshape(4, 2, 2, 2), ("z", "y", "x", "c"))
        dp, ctx = ("z", "y"), ("x", "c")
    else:
        body = per_device_wide
        dp, ctx = "dp", "ctx"
    tokens, weight, turned = P(dp, ctx, None), P(dp, ctx), P(ctx, dp)
    return jax.shard_map(
        body,
        mesh=mesh,
        in_specs=(tokens, tokens, P(dp), *[P()] * 6, *[weight] * 4, turned, P(), weight, weight, turned),
        out_specs=(tokens, tokens, *[P()] * 3, *[weight] * 4, turned, P(), weight, weight, turned),
        check_vma=False,
    )
```

```python
import functools

import jax
import jax.numpy as jnp
import numpy as np
from jax import lax
from jax.experimental import pallas as pl
from jax.experimental.pallas import tpu as pltpu
from jax.sharding import Mesh
from jax.sharding import PartitionSpec as P

LENGTH = 1024

EPSILON = 1e-06
ROPE_BASE = 1000000.0
MESH = pl.DeviceIdType.MESH
BF16 = jnp.bfloat16
F32 = jnp.float32
VMEM_BYTES = 62 * 2**20


def micros(count):
    return pl.CostEstimate(flops=0, transcendentals=0, bytes_accessed=count * 3_300_000)


def dot_nn(left, right):
    return jnp.dot(left, right, preferred_element_type=F32)


def dot_tn(left, right):
    return lax.dot_general(left, right, (((0,), (0,)), ((), ())), preferred_element_type=F32)


def dot_nt(left, right):
    return lax.dot_general(left, right, (((1,), (1,)), ((), ())), preferred_element_type=F32)


def rope_tables(positions, head_width):
    halfway = head_width // 2
    inverse = 1.0 / ROPE_BASE ** (jnp.arange(halfway, dtype=F32) * (2.0 / head_width))
    angles = positions.astype(F32)[:, None] * inverse[None, :]
    return (jnp.cos(angles), jnp.sin(angles))


def rotate(tensor, cosine, sine):
    halfway = tensor.shape[-1] // 2
    first_half = tensor[..., :halfway]
    second_half = tensor[..., halfway:]
    return jnp.concatenate(
        [first_half * cosine - second_half * sine, second_half * cosine + first_half * sine], -1
    )


def unrotate(grads_in, cosine, sine):
    halfway = grads_in.shape[-1] // 2
    first_half = grads_in[..., :halfway]
    second_half = grads_in[..., halfway:]
    return jnp.concatenate(
        [first_half * cosine + second_half * sine, second_half * cosine - first_half * sine], -1
    )


def norm_back(grads_in, values_in, inverse, gain_vec):
    scaled = grads_in * gain_vec
    return inverse * scaled - values_in * (inverse * inverse * inverse) * jnp.mean(
        scaled * values_in, -1, keepdims=True
    )


def greet(neighbours):
    barrier = pltpu.get_barrier_semaphore()
    for neighbour in neighbours:
        pl.semaphore_signal(barrier, inc=1, device_id=neighbour, device_id_type=MESH)
    pl.semaphore_wait(barrier, len(neighbours))


def remote_copies(send, recv, device):
    def remote(index, source, target, axis):
        return pltpu.make_async_remote_copy(
            src_ref=source,
            dst_ref=target,
            send_sem=send.at[index],
            recv_sem=recv.at[index],
            device_id=device[axis],
            device_id_type=MESH,
        )

    return remote


def place():
    y, x, c = lax.axis_index("y"), lax.axis_index("x"), lax.axis_index("c")
    return y, x, c, {"y": {"y": 1 - y}, "x": {"x": 1 - x}, "c": {"c": 1 - c}}


def gather_steps(s_ref, out_ref, local_sem, send, recv, split=True):
    y, x, c, device = place()
    remote = remote_copies(send, recv, device)
    half = s_ref.shape[0] // 2
    low, high = pl.ds(0, half), pl.ds(half, half)
    mine = out_ref.at[y, x, c]
    from_x = out_ref.at[y, 1 - x, c]
    from_y = out_ref.at[1 - y, x, c]
    diagonal = out_ref.at[1 - y, 1 - x, c]
    x_low = remote(0, s_ref.at[low], mine.at[low], "x")
    y_high = remote(1, s_ref.at[high], mine.at[high], "y")
    x_high = remote(2, s_ref.at[high], mine.at[high], "x")
    y_low = remote(3, s_ref.at[low], mine.at[low], "y")
    c_own = remote(4, s_ref, mine, "c")
    local = pltpu.make_async_copy(s_ref, mine, local_sem)
    forward_y = remote(5, from_x.at[low], from_x.at[low], "y")
    over_x = from_y.at[high] if split else from_y
    forward_x = remote(6, over_x, over_x, "x")
    c_x = remote(7, from_x, from_x, "c")
    c_y = remote(8, from_y, from_y, "c")
    c_low = remote(9, diagonal.at[low], diagonal.at[low], "c")
    over_c = diagonal.at[high] if split else diagonal
    c_high = remote(10, over_c, over_c, "c")

    def begin():
        for copy in (x_low, y_high, x_high, y_low, c_own, local):
            copy.start()

    def forward():
        x_low.wait_recv()
        if split:
            forward_y.start()
        y_high.wait_recv()
        if split:
            forward_x.start()

    def across():
        if not split:
            y_low.wait_recv()
            forward_x.start()
        x_high.wait_recv()
        c_x.start()
        if split:
            y_low.wait_recv()
        c_y.start()

    def finish():
        if split:
            forward_y.wait_recv()
            c_low.start()
        forward_x.wait_recv()
        c_high.start()
        for copy in (c_own, c_x, c_y, *((c_low,) if split else ()), c_high):
            copy.wait()
        for copy in (x_low, y_high, x_high, y_low, *((forward_y,) if split else ()), forward_x):
            copy.wait_send()
        local.wait()

    return begin, forward, across, finish


GATHER_SEMAPHORES = (
    pltpu.SemaphoreType.DMA,
    pltpu.SemaphoreType.DMA((11,)),
    pltpu.SemaphoreType.DMA((11,)),
)


def swap_steps(pieces, sources, outs, local_sem, send, recv, wanted=None):
    y, _, _, device = place()
    remote = remote_copies(send, recv, device)
    copies, locals_ = [], []
    for i, (source, out, first, count, at) in enumerate(pieces):
        if wanted is not None and not wanted(out):
            continue
        rows, cols = sources[source].shape
        target = outs[out].at[pl.ds(pl.multiple_of(y * rows, rows), rows), pl.ds(at, count)]

        def half(which):
            start = pl.multiple_of(which * (cols // 2) + first, 128)
            return sources[source].at[:, pl.ds(start, count)]

        copies.append(remote(i, half(1 - y), target, "y"))
        locals_.append(pltpu.make_async_copy(half(y), target, local_sem.at[i]))

    def begin():
        for copy in (*copies, *locals_):
            copy.start()

    def here():
        for copy in locals_:
            copy.wait()

    def finish():
        for copy in copies:
            copy.wait()

    return begin, here, finish


def line_steps(rows_ref, out_ref, local_sem, send, recv, part, which):
    z = lax.axis_index("z")
    rows, half = rows_ref.shape[0], rows_ref.shape[0] // 2
    first = which * half
    pair, middle = z + 1 - 2 * lax.rem(z, 2), 3 - z
    inner = (z == 1) | (z == 2)

    def at(index):
        return out_ref.at[pl.ds(pl.multiple_of(index * rows + first, half), half)]

    def remote(index, source, target, peer):
        return pltpu.make_async_remote_copy(
            src_ref=source,
            dst_ref=target,
            send_sem=send.at[5 * part + index],
            recv_sem=recv.at[5 * part + index],
            device_id={"z": peer},
            device_id_type=MESH,
        )

    far = middle + 1 - 2 * lax.rem(middle, 2)
    own = rows_ref.at[pl.ds(pl.multiple_of(first, half), half)]
    own_pair = remote(0, own, at(z), pair)
    own_middle = remote(1, own, at(z), middle)
    pair_middle = remote(2, at(pair), at(pair), middle)
    middle_pair = remote(3, at(middle), at(middle), pair)
    far_pair = remote(4, at(far), at(far), pair)
    local = pltpu.make_async_copy(own, at(z), local_sem.at[part])

    def begin():
        local.start()
        own_pair.start()
        pl.when(inner)(own_middle.start)

    def second():
        own_pair.wait_recv()

        @pl.when(inner)
        def _():
            pair_middle.start()
            own_middle.wait_recv()
            middle_pair.start()

    def third():
        @pl.when(inner)
        def _():
            pair_middle.wait_recv()
            far_pair.start()

    def finish():
        @pl.when(inner)
        def _():
            for copy in (own_middle, pair_middle, middle_pair, far_pair):
                copy.wait_send()

        @pl.when(jnp.logical_not(inner))
        def _():
            middle_pair.wait_recv()
            far_pair.wait_recv()

        own_pair.wait_send()
        local.wait()

    def peers():
        return pair, middle, inner

    return begin, second, third, finish, peers


def greet_line(others, pair, middle, inner):
    barrier = pltpu.get_barrier_semaphore()
    for other in (*others, {"z": pair}):
        pl.semaphore_signal(barrier, inc=1, device_id=other, device_id_type=MESH)

    @pl.when(inner)
    def _():
        pl.semaphore_signal(barrier, inc=1, device_id={"z": middle}, device_id_type=MESH)

    count = len(others) + 1
    pl.semaphore_wait(barrier, jnp.where(inner, count + 1, count))


LINE_SEMAPHORES = (
    pltpu.SemaphoreType.DMA((2,)),
    pltpu.SemaphoreType.DMA((10,)),
    pltpu.SemaphoreType.DMA((10,)),
)


def both_halves(rows_ref, out_ref, *sems):
    y = lax.axis_index("y")
    return [line_steps(rows_ref, out_ref, *sems, part, which) for part, which in ((0, y), (1, 1 - y))]


def gather_kernel(source, rows_ref, out, line_ref, *sems):
    begin, forward, across, finish = gather_steps(source, out, *sems[:3])
    lines = both_halves(rows_ref, line_ref, *sems[3:])
    greet_line(tuple(place()[3].values()), *lines[0][4]())
    for steps in lines:
        steps[0]()
    begin()
    for steps in lines:
        steps[1]()
    forward()
    lines[0][2]()
    across()
    lines[1][2]()
    finish()
    for steps in lines:
        steps[3]()


def gather_tokens(shard, line):
    rows, width = shard.shape
    gathered, lined = pl.pallas_call(
        gather_kernel,
        out_shape=(
            jax.ShapeDtypeStruct((2, 2, 2, rows, width), shard.dtype),
            jax.ShapeDtypeStruct((4 * line.shape[0], line.shape[1]), line.dtype),
        ),
        in_specs=[pl.BlockSpec(memory_space=pltpu.VMEM)] * 2,
        out_specs=(pl.BlockSpec(memory_space=pl.ANY),) * 2,
        scratch_shapes=[*GATHER_SEMAPHORES, *LINE_SEMAPHORES],
        compiler_params=pltpu.CompilerParams(collective_id=1, has_side_effects=True),
        cost_estimate=micros(42),
        name="gather_tokens",
    )(shard, line)
    return gathered.reshape(8 * rows, width), lined


def opening_kernel(pieces, tokens, cotangent, gain, ids, counts, numer, denom, turns, *refs):
    sources, refs = list(refs[:8]), refs[8:]
    out, line_q, line_g, first, last_gu, last_d, inverse, low, factor, cosine, sine, *refs = refs
    rows_q, rows_g, normed, output_t, down_t, *sems = refs
    begin, forward, across, finish = gather_steps(normed, out, *sems[:3], False)
    y = lax.axis_index("y")
    steps = [
        line_steps(rows, line, *sems[3 * i + 3 : 3 * i + 6], part, which)
        for part, which in ((0, y), (1, 1 - y))
        for i, (rows, line) in enumerate(((rows_q, line_q), (rows_g, line_g)))
    ]
    output_ref, down_ref = sources[4], sources[7]
    sources[4], sources[7] = output_t, down_t
    swaps = [
        swap_steps(pieces, sources, (rows_q, rows_g, first, last_gu, last_d), *sems[9:], wanted)
        for wanted in (lambda out: out == 0, lambda out: out == 1, lambda out: out > 1)
    ]
    step = 64

    def norm(i):
        at = pl.ds(i * step, step)
        x = tokens[at].astype(F32)
        inv = lax.rsqrt(jnp.mean(x * x, -1, keepdims=True) + EPSILON)
        inverse[at] = inv
        normed[at] = (x * inv * gain[...].astype(F32).reshape(1, -1)).astype(BF16)

    def weigh(i):
        at = pl.ds(i * step, step)
        low[at] = (cotangent[at].astype(F32) * factor[...]).astype(BF16)

    def turn(i):
        at = pl.ds(i * 128, 128)
        places = lax.broadcasted_iota(jnp.int32, (128, cosine.shape[1]), 0) + i * 128
        angles = places.astype(F32) * turns[0:1]
        cosine[at] = jnp.cos(angles)
        sine[at] = jnp.sin(angles) * turns[1:2]

    greet_line(tuple(place()[3].values()), *steps[0][4]())
    swaps[0][0]()
    swaps[0][1]()
    steps[0][0]()
    output_t[...] = output_ref[...].astype(F32).T.astype(BF16)
    swaps[1][0]()
    swaps[1][1]()
    steps[1][0]()
    pl.loop(0, tokens.shape[0] // step)(norm)
    begin()
    for i in range(2):
        swaps[i][2]()
        steps[i + 2][0]()
    steps[0][1]()
    steps[1][1]()
    chosen = lax.broadcasted_iota(jnp.int32, counts.shape, 1) == ids[...]
    ratio = numer[...].astype(F32) / denom[...].astype(F32) * LENGTH / counts[...].astype(F32)
    factor[...] = jnp.sum(jnp.where(chosen, ratio, 0.0), -1, keepdims=True)

    @pl.loop(0, down_ref.shape[0] // 256)
    def _(i):
        at = pl.ds(pl.multiple_of(i * 256, 256), 256)
        down_t[:, at] = down_ref[at].astype(F32).T.astype(BF16)

    steps[2][1]()
    steps[3][1]()
    forward()
    across()
    swaps[2][0]()
    steps[0][2]()
    steps[1][2]()
    pl.loop(0, tokens.shape[0] // step)(weigh)
    steps[2][2]()
    steps[3][2]()
    pl.loop(0, cosine.shape[0] // 128)(turn)
    finish()
    for step_set in steps:
        step_set[3]()
    swaps[2][1]()
    swaps[2][2]()


def opening(tokens, cotangent, gain, domains, weights, split, full_len, head):
    rows, width = tokens.shape
    halves = [weight.shape[0 if i in (4, 7) else 1] // 2 for i, weight in enumerate(weights)]
    groups = (
        [(i, 0, halves[i]) for i in (0, 1, 2)],
        [(i, 0, halves[i]) for i in (3, 4)],
        [(i, 0, split) for i in (5, 6, 7)],
        [(i, split, halves[i] - split) for i in (5, 6)],
        [(7, split, halves[7] - split)],
    )
    pieces, widths = [], []
    for group in groups:
        at = 0
        for source, first, count in group:
            pieces.append((source, len(widths), first, count, at))
            at += count
        widths.append(at)
    inverse = 1.0 / np.float32(ROPE_BASE) ** (np.arange(head // 2, dtype=np.float32) * np.float32(2.0 / head))
    turns = np.stack([np.tile(inverse, 2), np.repeat(np.float32([-1.0, 1.0]), head // 2)]).astype(np.float32)
    whole, loose = pl.BlockSpec(memory_space=pltpu.VMEM), pl.BlockSpec(memory_space=pl.ANY)
    shape = jax.ShapeDtypeStruct
    dma = pltpu.SemaphoreType.DMA
    gathered, *outs = pl.pallas_call(
        functools.partial(opening_kernel, pieces),
        out_shape=(
            shape((2, 2, 2, rows, width), BF16),
            *[shape((8 * rows, size), BF16) for size in widths[:2]],
            *[shape((2 * rows, size), BF16) for size in widths[2:]],
            shape((rows, 1), F32),
            shape((rows, width), BF16),
            shape((1, 1), F32),
            shape((full_len, head), F32),
            shape((full_len, head), F32),
        ),
        in_specs=[whole] * (8 + len(weights)),
        out_specs=(*[loose] * 6, *[whole] * 5),
        scratch_shapes=[
            *[pltpu.VMEM((2 * rows, size), BF16) for size in widths[:2]],
            pltpu.VMEM((rows, width), BF16),
            *[pltpu.VMEM(weights[i].shape[::-1], BF16) for i in (4, 7)],
            *GATHER_SEMAPHORES,
            *[dma((2,)), dma((10,)), dma((10,))] * 2,
            *[dma((len(pieces),))] * 3,
        ],
        compiler_params=pltpu.CompilerParams(
            collective_id=2, has_side_effects=True, vmem_limit_bytes=VMEM_BYTES
        ),
        cost_estimate=micros(80),
        name="opening",
    )(
        tokens,
        cotangent,
        gain,
        *(domain.reshape(1, -1) for domain in domains),
        jnp.asarray(turns),
        *weights,
    )
    return gathered.reshape(8 * rows, width), *outs


def add_rows(target, start, size, other, base, step=64):
    @pl.loop(0, size // step)
    def _(i):
        at, there = pl.ds(start + i * step, step), pl.ds(base + i * step, step)
        target[at] = (target[at].astype(F32) + other[there].astype(F32)).astype(target.dtype)


def product_steps(windows, lefts, rights, left_vmem, right_vmem, own, pairs, got, load_sem, send, recv):
    y, x, c, device = place()
    remote = remote_copies(send, recv, device)
    rows, width = own.shape[1:]
    half, both, tile = rows // 2, 2 * rows, 256
    targets = ((1 - y, 1 - x), (1 - y, x), (y, 1 - x), (y, x))
    pieces = ((0, 0, half), (0, half, half), (1, 0, rows), (2, 0, rows), (3, 0, rows))
    count = len(lefts)
    right_loads = [
        pltpu.make_async_copy(
            rights[j].at[:, pl.ds(windows[j], right_vmem[j].shape[1])], right_vmem[j], load_sem.at[j]
        )
        for j in range(count)
    ]
    left_loads = []
    for i, (a, b) in enumerate(targets):
        start = pl.multiple_of((a * 2 + b) * both, both)
        left_loads.append(
            [
                pltpu.make_async_copy(
                    lefts[j].at[pl.ds(start, both)], left_vmem[j].at[i], load_sem.at[count * (i + 1) + j]
                )
                for j in range(count)
            ]
        )
    crossing = [
        remote(k, pairs.at[i, 1 - c, pl.ds(first, size)], got.at[i, pl.ds(first, size)], "c")
        for k, (i, first, size) in enumerate(pieces)
    ]

    def load():
        for copy in right_loads:
            copy.start()
        for copies in left_loads:
            for copy in copies:
                copy.start()

    def ready():
        for copy in right_loads:
            copy.wait()

    def product(i):
        for copy in left_loads[i]:
            copy.wait()

        @pl.loop(0, width // tile)
        def _(n):
            cols = pl.ds(pl.multiple_of(n * tile, tile), tile)
            total = dot_nt(left_vmem[0][i], right_vmem[0][cols])
            for j in range(1, count):
                total = total + dot_nt(left_vmem[j][i], right_vmem[j][cols])
            pairs[i, :, :, cols] = total.reshape(2, rows, tile).astype(BF16)

        for k, piece in enumerate(pieces):
            if piece[0] == i:
                crossing[k].start()

    def cores(k, step=64):
        i, first, size = pieces[k]
        crossing[k].wait_recv()

        @pl.loop(0, size // step)
        def _(n):
            at = pl.ds(first + n * step, step)
            own[i, at] = (pairs[i, c, at].astype(F32) + got[i, at].astype(F32)).astype(BF16)

    def finish():
        for copy in crossing:
            copy.wait_send()

    return load, ready, product, cores, finish


def axis_steps(own, x_diag, y_diag, x_got, y_got, send, recv):
    remote = remote_copies(send, recv, place()[3])
    rows = own.shape[1]
    half = rows // 2
    low, high = pl.ds(0, half), pl.ds(half, half)
    diag_x = remote(0, own.at[0, low], x_diag, "x")
    diag_y = remote(1, own.at[0, high], y_diag, "y")
    y_high = remote(2, own.at[1, high], y_got.at[high], "y")
    x_low = remote(3, own.at[2, low], x_got.at[low], "x")
    y_low = remote(4, own.at[1, low], y_got.at[low], "y")
    x_high = remote(5, own.at[2, high], x_got.at[high], "x")

    def second():
        diag_x.wait_recv()
        add_rows(own.at[1], 0, half, x_diag, 0)
        y_low.start()
        diag_y.wait_recv()
        add_rows(own.at[2], half, half, y_diag, 0)
        x_high.start()

    def finish(store, step=32):
        for copy in (y_high, x_low, y_low, x_high):
            copy.wait_recv()

        @pl.loop(0, rows // step)
        def _(i):
            at = pl.ds(i * step, step)
            store(at, own[3, at].astype(F32) + x_got[at].astype(F32) + y_got[at].astype(F32))

        for copy in (diag_x, diag_y, y_high, x_low, y_low, x_high):
            copy.wait_send()

    return diag_x, diag_y, x_low, y_high, second, finish


def scatter_steps(windows, lefts, rights, scratch):
    count = len(windows)
    product_scratch, axis_scratch = scratch[: 2 * count + 6], scratch[2 * count + 6 :]
    load, ready, product, cores, crossed = product_steps(
        windows, lefts, rights, product_scratch[:count], product_scratch[count : 2 * count],
        *product_scratch[2 * count :],
    )
    own = product_scratch[2 * count]
    diag_x, diag_y, x_low, y_high, second_axis, finish_axis = axis_steps(own, *axis_scratch)

    def first():
        ready()
        product(0)
        cores(0)
        diag_x.start()
        cores(1)
        diag_y.start()
        product(2)
        product(1)
        cores(3)
        x_low.start()
        cores(2)
        y_high.start()

    def second():
        second_axis()
        product(3)
        cores(4)

    def finish(store):
        finish_axis(store)
        crossed()

    return load, first, second, finish


def product_scratch(group, own=True):
    lefts, rights = [item[0] for item in group], [item[1] for item in group]
    rows, width = lefts[0].shape[0] // 8, rights[0].shape[0]
    return [
        *[pltpu.VMEM((4, 2 * rows, left.shape[1]), BF16) for left in lefts],
        *[pltpu.VMEM((width, left.shape[1]), BF16) for left in lefts],
        *[pltpu.VMEM((4, rows, width), BF16)] * own,
        pltpu.VMEM((4, 2, rows, width), BF16),
        pltpu.VMEM((4, rows, width), BF16),
        pltpu.SemaphoreType.DMA((5 * len(group),)),
        pltpu.SemaphoreType.DMA((5,)),
        pltpu.SemaphoreType.DMA((5,)),
    ]


def axis_scratch(rows, width):
    return [
        pltpu.VMEM((rows // 2, width), BF16),
        pltpu.VMEM((rows // 2, width), BF16),
        pltpu.VMEM((rows, width), BF16),
        pltpu.VMEM((rows, width), BF16),
        pltpu.SemaphoreType.DMA((6,)),
        pltpu.SemaphoreType.DMA((6,)),
    ]


def scatter_scratch(group):
    lefts, rights = [item[0] for item in group], [item[1] for item in group]
    rows, width = lefts[0].shape[0] // 8, rights[0].shape[0]
    scratch = product_scratch(group) + axis_scratch(rows, width)
    return lefts + rights, scratch, jax.ShapeDtypeStruct((rows, width), F32)


def middle_kernel(windows, *refs):
    count = len(windows)
    lefts, rights, refs = refs[:count], refs[count : 2 * count], refs[2 * count :]
    tokens, gain, hidden, inverse, normed, *scratch = refs
    load, first, second, finish = scatter_steps(windows, lefts, rights, scratch)

    def store(at, branch):
        total = tokens[at].astype(F32) + branch
        inv = lax.rsqrt(jnp.mean(total * total, -1, keepdims=True) + EPSILON)
        hidden[at] = total
        inverse[at] = inv
        normed[at] = (total * inv * gain[...].astype(F32)).astype(BF16)

    load()
    greet(tuple(place()[3].values()))
    first()
    second()
    finish(store)


def middle_back_kernel(windows, *refs):
    count = len(windows)
    lefts, rights, refs = refs[:count], refs[count : 2 * count], refs[2 * count :]
    hidden, inverse, gain, cotangent, factor, dhidden, dbranch, gain_grad, *scratch = refs
    load, first, second, finish = scatter_steps(windows, lefts, rights, scratch)
    gain_grad[...] = jnp.zeros_like(gain_grad)

    def store(at, grad):
        state, inv = hidden[at], inverse[at]
        gain_grad[...] += jnp.sum(grad * state * inv, 0, keepdims=True)
        upstream = cotangent[at].astype(F32) * factor[...]
        total = upstream + norm_back(grad, state, inv, gain[...].astype(F32))
        dhidden[at] = total
        dbranch[at] = total.astype(BF16)

    load()
    greet(tuple(place()[3].values()))
    first()
    second()
    finish(store)


def scatter_products(kernel, number, extras, outs, *group):
    operands, scratch, _ = scatter_scratch(group)
    whole = pl.BlockSpec(memory_space=pltpu.VMEM)
    return pl.pallas_call(
        functools.partial(kernel, [item[2] for item in group]),
        out_shape=outs,
        in_specs=[pl.BlockSpec(memory_space=pl.ANY)] * len(operands) + [whole] * len(extras),
        out_specs=(whole,) * len(outs),
        scratch_shapes=scratch,
        compiler_params=pltpu.CompilerParams(
            collective_id=number, has_side_effects=True, vmem_limit_bytes=VMEM_BYTES
        ),
        cost_estimate=micros(48),
        name="scatter_products",
    )(*operands, *extras)


def gather_beside_kernel(windows, tile, shard_ref, *refs):
    count = len(windows)
    lefts, rights, refs = refs[:count], refs[count : 2 * count], refs[2 * count :]
    mid, low, dgu, act, out_ref, sums_ref, grad_ref, *scratch = refs
    size = 2 * count + 5
    products, (mid_buf, low_buf, dgu_vmem, act_vmem, total, tile_sem, side_sem), sems = (
        scratch[:size], scratch[size : size + 7], scratch[size + 7 :],
    )
    load, ready, product, cores, crossed = product_steps(
        windows, lefts, rights, products[:count], products[count : 2 * count], sums_ref,
        *products[2 * count :],
    )
    begin, forward, across, finish = gather_steps(shard_ref, out_ref, *sems)
    tiles = mid.shape[0] // tile
    sides = [
        pltpu.make_async_copy(dgu, dgu_vmem, side_sem.at[0]),
        pltpu.make_async_copy(act, act_vmem, side_sem.at[1]),
    ]

    def tile_copies(t):
        rows, slot = pl.ds(pl.multiple_of(t * tile, tile), tile), lax.rem(t, 2)
        return [
            pltpu.make_async_copy(source.at[rows], buffer.at[slot], tile_sem.at[i, slot])
            for i, (source, buffer) in enumerate(((mid, mid_buf), (low, low_buf)))
        ]

    load()
    greet(tuple(place()[3].values()))
    begin()
    for copy in (*sides, *tile_copies(0), *tile_copies(1)):
        copy.start()
    ready()
    for i in range(4):
        product(i)
    forward()
    for copy in sides:
        copy.wait()
    cores(0)
    cores(1)

    @pl.loop(0, tiles)
    def _(t):
        for copy in tile_copies(t):
            copy.wait()
        rows, slot = pl.ds(pl.multiple_of(t * tile, tile), tile), lax.rem(t, 2)
        add_products(t, total, 0, mid_buf.at[slot], dgu_vmem.at[rows])
        add_products(t, total, dgu_vmem.shape[1], low_buf.at[slot], act_vmem.at[rows])

        @pl.when(t + 2 < tiles)
        def _():
            for copy in tile_copies(t + 2):
                copy.start()

        @pl.when(t == tiles // 2 - 1)
        def _():
            across()
            for k in range(2, 5):
                cores(k)

    @pl.loop(0, total.shape[0] // 256)
    def _(m):
        at = pl.ds(m * 256, 256)
        grad_ref[at] = total[at].astype(BF16)

    crossed()
    finish()


def gather_beside(shard, group, mid, low, dgu, act, tile=512):
    rows, width = shard.shape
    operands = [item[0] for item in group] + [item[1] for item in group] + [mid, low, dgu, act]
    cols = dgu.shape[1] + act.shape[1]
    gathered, sums, grad = pl.pallas_call(
        functools.partial(gather_beside_kernel, [item[2] for item in group], tile),
        out_shape=(
            jax.ShapeDtypeStruct((2, 2, 2, rows, width), shard.dtype),
            jax.ShapeDtypeStruct((4, rows, width), BF16),
            jax.ShapeDtypeStruct((width, cols), BF16),
        ),
        in_specs=[
            pl.BlockSpec(memory_space=pltpu.VMEM),
            *[pl.BlockSpec(memory_space=pl.ANY)] * len(operands),
        ],
        out_specs=(
            pl.BlockSpec(memory_space=pl.ANY),
            pl.BlockSpec(memory_space=pltpu.VMEM),
            pl.BlockSpec(memory_space=pltpu.VMEM),
        ),
        scratch_shapes=[
            *product_scratch(group, own=False),
            pltpu.VMEM((2, tile, width), BF16),
            pltpu.VMEM((2, tile, width), BF16),
            pltpu.VMEM(dgu.shape, BF16),
            pltpu.VMEM(act.shape, BF16),
            pltpu.VMEM((width, cols), F32),
            pltpu.SemaphoreType.DMA((2, 2)),
            pltpu.SemaphoreType.DMA((2,)),
            *GATHER_SEMAPHORES,
        ],
        compiler_params=pltpu.CompilerParams(
            collective_id=6, has_side_effects=True, vmem_limit_bytes=VMEM_BYTES
        ),
        cost_estimate=micros(44),
        name="gather_beside",
    )(shard, *operands)
    return gathered.reshape(8 * rows, width), sums, grad


def line_scatter_steps(grad_ref, own, from_edge, from_middle, inward, load_sem, send, recv, part, which):
    z = lax.axis_index("z")
    rows, half = own.shape[1], own.shape[1] // 2
    pair, middle = z + 1 - 2 * lax.rem(z, 2), 3 - z
    inner = (z == 1) | (z == 2)
    edge = jnp.logical_not(inner)
    far = middle + 1 - 2 * lax.rem(middle, 2)
    first = pl.multiple_of(which * half, half)
    span = pl.ds(first, half)

    def block(index):
        return grad_ref.at[pl.ds(pl.multiple_of(index * rows + first, half), half)]

    def remote(index, source, target, peer):
        return pltpu.make_async_remote_copy(
            src_ref=source,
            dst_ref=target,
            send_sem=send.at[6 * part + index],
            recv_sem=recv.at[6 * part + index],
            device_id={"z": peer},
            device_id_type=MESH,
        )

    indices = (far, middle, pair, z)
    loads = [
        pltpu.make_async_copy(block(index), own.at[i, span], load_sem.at[4 * part + i])
        for i, index in enumerate(indices)
    ]
    edge_far = remote(0, own.at[1, span], from_edge.at[0, span], pair)
    edge_near = remote(1, own.at[0, span], from_edge.at[1, span], pair)
    edge_pair = remote(2, own.at[2, span], from_edge.at[2, span], pair)
    inner_far = remote(3, own.at[0, span], from_middle.at[0, span], middle)
    inner_near = remote(4, own.at[1, span], from_middle.at[1, span], middle)
    outward = remote(5, own.at[2, span], inward.at[span], pair)
    step = 128

    def add_into(target, other):
        @pl.loop(0, half // step)
        def _(i):
            at = pl.ds(first + i * step, step)
            target[at] = (target[at].astype(F32) + other[at].astype(F32)).astype(target.dtype)

    def load():
        for copy in loads:
            copy.start()

    def begin():
        for copy in loads:
            copy.wait()

        @pl.when(edge)
        def _():
            for copy in (edge_far, edge_near, edge_pair):
                copy.start()

    def second():
        @pl.when(inner)
        def _():
            edge_far.wait_recv()
            add_into(own.at[0], from_edge.at[0])
            inner_far.start()

    def third():
        @pl.when(inner)
        def _():
            edge_near.wait_recv()
            add_into(own.at[1], from_edge.at[1])
            inner_near.start()
            inner_far.wait_recv()
            add_into(own.at[2], from_middle.at[0])
            outward.start()

    def finish():
        @pl.when(inner)
        def _():
            edge_pair.wait_recv()
            add_into(own.at[3], from_edge.at[2])
            inner_near.wait_recv()
            add_into(own.at[3], from_middle.at[1])
            for copy in (inner_far, inner_near, outward):
                copy.wait_send()

        @pl.when(edge)
        def _():
            outward.wait_recv()
            add_into(own.at[3], inward)
            for copy in (edge_far, edge_near, edge_pair):
                copy.wait_send()

    return load, begin, second, third, finish


def total_steps(near, far, near_send, near_recv, far_send, far_recv):
    z, y, x, c = (lax.axis_index(name) for name in "zyxc")
    here = (y * 2 + x) * 2 + c
    others = [
        {"y": lax.rem(y + i // 4, 2), "x": lax.rem(x + i // 2 % 2, 2), "c": lax.rem(c + i % 2, 2)}
        for i in range(1, 8)
    ]
    levels = [{"z": lax.rem(z + i, 4)} for i in range(1, 4)]

    def remote(index, source, target, send, recv, device):
        return pltpu.make_async_remote_copy(
            src_ref=source,
            dst_ref=target,
            send_sem=send.at[index],
            recv_sem=recv.at[index],
            device_id=device,
            device_id_type=MESH,
        )

    around = [
        remote(i, near.at[here], near.at[here], near_send, near_recv, other)
        for i, other in enumerate(others)
    ]
    along = [
        remote(i, far.at[z], far.at[z], far_send, far_recv, level) for i, level in enumerate(levels)
    ]

    def begin():
        for copy in around:
            copy.start()

    def second():
        for copy in around:
            copy.wait()
        total = near[0]
        for i in range(1, 8):
            total = total + near[i]
        far[z] = total
        for copy in along:
            copy.start()

    def finish():
        for copy in along:
            copy.wait()
        total = far[0]
        for i in range(1, 4):
            total = total + far[i]
        return total

    return begin, second, finish, here, others, levels


def tail_kernel(windows, *refs):
    count = len(windows)
    lefts, rights, refs = refs[:count], refs[count : 2 * count], refs[2 * count :]
    grad_ref, tokens_ref, inverse_ref, dhidden_ref, gain_ref, *refs = refs
    gains, (out_ref, mine_ref, theirs_ref, total_ref), scratch = refs[:3], refs[3:7], refs[7:]
    size = 2 * count + 12
    load, first, second, finish = scatter_steps(windows, lefts, rights, scratch[:size])
    line, (swap_sem,), total = scratch[size : size + 7], scratch[size + 7 : size + 8], scratch[size + 8 :]
    near, far = total[:2]
    total_begin, total_second, total_finish, here, others, levels = total_steps(*total)
    y = lax.axis_index("y")
    lines = [line_scatter_steps(grad_ref, *line, part, which) for part, which in ((0, 1 - y), (1, y))]
    load()
    for steps in lines:
        steps[0]()
    width = out_ref.shape[1]
    near[here, :, pl.ds(width, width)] = gains[0][...]
    head = gains[1].shape[1]
    near[here, :, pl.ds(2 * width, head)] = gains[1][...]
    near[here, :, pl.ds(2 * width + head, head)] = gains[2][...]
    greet(others + levels)
    for steps in lines:
        steps[1]()
    first()
    lines[0][2]()
    second()
    lines[0][3]()
    lines[1][2]()
    gain_in = near.at[here, :, pl.ds(0, width)]
    gain_in[...] = jnp.zeros((1, width), F32)

    def store(at, grad):
        x, inv = tokens_ref[at].astype(F32), inverse_ref[at]
        gain_in[...] += jnp.sum(grad * x * inv, 0, keepdims=True)
        back = norm_back(grad, x, inv, gain_ref[...].astype(F32))
        out_ref[at] = (dhidden_ref[at] + back).astype(BF16)

    finish(store)
    total_begin()
    lines[1][3]()
    lines[0][4]()
    summed = line[0].at[3]
    half = theirs_ref.shape[0]
    swap = pltpu.make_async_remote_copy(
        src_ref=summed.at[pl.ds(pl.multiple_of((1 - y) * half, half), half)],
        dst_ref=theirs_ref,
        send_sem=swap_sem.at[0],
        recv_sem=swap_sem.at[1],
        device_id={"y": 1 - y},
        device_id_type=MESH,
    )
    swap.start()
    total_second()
    lines[1][4]()
    mine_ref[...] = summed[pl.ds(pl.multiple_of(y * half, half), half)]
    total_ref[...] = total_finish()
    swap.wait()


def tail(group, grad, tokens, inverse, dhidden, gain, gains):
    operands, scratch, total = scatter_scratch(group)
    rows, cols = grad.shape[0] // 4, grad.shape[1]
    length = 2 * total.shape[1] + 2 * gains[1].size
    half = jax.ShapeDtypeStruct((rows // 2, cols), BF16)
    whole = pl.BlockSpec(memory_space=pltpu.VMEM)
    block = lambda count: pltpu.VMEM((count, rows, cols), BF16)
    dma = pltpu.SemaphoreType.DMA
    return pl.pallas_call(
        functools.partial(tail_kernel, [item[2] for item in group]),
        out_shape=(
            jax.ShapeDtypeStruct(total.shape, BF16),
            half,
            half,
            jax.ShapeDtypeStruct((1, length), F32),
        ),
        in_specs=[pl.BlockSpec(memory_space=pl.ANY)] * (len(operands) + 1) + [whole] * 7,
        out_specs=(whole,) * 4,
        scratch_shapes=[
            *scratch,
            block(4), block(3), block(2), pltpu.VMEM((rows, cols), BF16), dma((8,)), dma((12,)), dma((12,)),
            dma((2,)),
            pltpu.VMEM((8, 1, length), F32), pltpu.VMEM((4, 1, length), F32), dma((7,)), dma((7,)), dma((3,)), dma((3,)),
        ],
        compiler_params=pltpu.CompilerParams(
            collective_id=0, has_side_effects=True, vmem_limit_bytes=VMEM_BYTES
        ),
        cost_estimate=micros(52),
        name="tail",
    )(*operands, grad, tokens, inverse, dhidden, gain.reshape(1, -1), *(gain.reshape(1, -1) for gain in gains))


def swap_y(value):
    return lax.ppermute(value, "y", [(0, 1), (1, 0)])


def in_y_order(mine, theirs, axis):
    count = mine.shape[axis]
    return lax.dynamic_slice_in_dim(
        jnp.concatenate([mine, theirs, mine], axis), lax.axis_index("y") * count, 2 * count, axis
    )


def gather_rows(rows):
    return lax.all_gather(rows, "z", axis=0, tiled=True)


def scatter_grads(grad):
    return lax.psum_scatter(grad.astype(BF16), "z", scatter_dimension=0, tiled=True)


def their_rows(part):
    half = part.shape[0] // 2
    return swap_y(
        lax.dynamic_slice_in_dim(part, (1 - lax.axis_index("y")) * half, half, 0)
    )


def join_pieces(plan, y, mine_of, theirs_of, outs):
    for source, first, width, out, at, turned in plan:
        half = outs[out].shape[0 if turned else 1] // 2
        cols = pl.ds(first, width)
        for which, piece in ((y, mine_of(source, cols)), (1 - y, theirs_of(source, cols))):
            target = pl.ds(pl.multiple_of(which * half + at, 128), width)
            if turned:
                outs[out][target, :] = piece.astype(F32).T
            else:
                outs[out][:, target] = piece.astype(F32)


def join_kernel(plan, count, y_rows, *refs):
    y = lax.axis_index("y")
    parts, theirs, outs = refs[:count], refs[count : 2 * count], refs[2 * count :]
    mine = pl.ds(pl.multiple_of(y * y_rows, y_rows), y_rows)
    own = lambda source, cols: parts[source][mine, cols]
    got = lambda source, cols: theirs[source][:, cols]
    join_pieces(plan, y, own, got, outs)


def join_grads(parts, theirs, plan, shapes):
    whole = pl.BlockSpec(memory_space=pltpu.VMEM)
    return pl.pallas_call(
        functools.partial(join_kernel, plan, len(parts), theirs[0].shape[0]),
        out_shape=tuple(jax.ShapeDtypeStruct(shape, F32) for shape in shapes),
        in_specs=[whole] * (2 * len(parts)),
        out_specs=(whole,) * len(shapes),
        compiler_params=pltpu.CompilerParams(vmem_limit_bytes=VMEM_BYTES),
        cost_estimate=micros(5),
        name="join_grads",
    )(*parts, *theirs)


def last_join_kernel(plan, mine, theirs, total, *outs):
    gains, grads, start = outs[:4], outs[4:], 0
    for gain in gains:
        gain[...] = total[:, pl.ds(start, gain.shape[1])]
        start += gain.shape[1]
    y = lax.axis_index("y")
    join_pieces(plan, y, lambda _, cols: mine[:, cols], lambda _, cols: theirs[:, cols], grads)


def join_last(mine, theirs, total, plan, sizes, shapes):
    whole = pl.BlockSpec(memory_space=pltpu.VMEM)
    outs = (*((1, size) for size in sizes), *shapes)
    return pl.pallas_call(
        functools.partial(last_join_kernel, plan),
        out_shape=tuple(jax.ShapeDtypeStruct(shape, F32) for shape in outs),
        in_specs=[whole] * 3,
        out_specs=(whole,) * len(outs),
        cost_estimate=micros(4),
        name="join_last",
    )(mine, theirs, total)


def normed_rope(raw, gain, cosine, sine):
    inverse = lax.rsqrt(jnp.mean(raw * raw, -1, keepdims=True) + EPSILON)
    scaled = raw * inverse * gain
    turned = pltpu.roll(scaled, scaled.shape[-1] // 2, 1)
    return (scaled * cosine + turned * sine).astype(BF16)


def normed_rope_back(grad, raw, gain, cosine, sine):
    inverse = lax.rsqrt(jnp.mean(raw * raw, -1, keepdims=True) + EPSILON)
    straight = grad * cosine - pltpu.roll(grad, grad.shape[-1] // 2, 1) * sine
    gain_part = jnp.sum(straight * (raw * inverse), 0, keepdims=True)
    return norm_back(straight, raw, inverse, gain).astype(BF16), gain_part


def causal_scores(query, keys, first, scaling):
    scores = dot_nt(query, keys) * scaling
    rows = lax.broadcasted_iota(jnp.int32, scores.shape, 0) + first
    columns = lax.broadcasted_iota(jnp.int32, scores.shape, 1)
    return jnp.where(rows >= columns, scores, -1e30)


def attend_kernel(
    heads, head, block, normed_ref, w_ref, wg_ref, low_ref, qg_ref, kg_ref, cos_ref, sin_ref,
    raw_ref, out_ref, log_ref, gate_ref, mixed_ref, all_ref, key_ref, value_ref, *sems,
):
    seq, step, steps = pl.program_id(0), pl.program_id(1), pl.num_programs(1)
    tick = seq * steps + step
    scaling = head**-0.5
    at = heads * head
    begin, forward, across, finish = gather_steps(low_ref, all_ref, *sems)

    @pl.when(tick == 0)
    def _():
        greet(tuple(place()[3].values()))
        begin()

    pl.when(tick == 3)(forward)
    pl.when(tick == 6)(across)
    raw_ref[...] = dot_nn(normed_ref[...], w_ref[...])
    here = pl.ds(pl.multiple_of(step * block, block), block)
    cosine, sine = cos_ref[here], sin_ref[here]

    @pl.when(tick == 0)
    def _():
        key_ref[...] = jnp.zeros_like(key_ref)
        value_ref[...] = jnp.zeros_like(value_ref)

    key_ref[here] = normed_rope(raw_ref[:, at : at + head], kg_ref[...], cosine, sine)
    value_ref[here] = raw_ref[:, at + head :].astype(BF16)

    for i in range(0, key_ref.shape[0] // block, 2):

        @pl.when(step // 2 == i // 2)
        def _():
            seen = pl.ds(0, (i + 2) * block)

            @pl.loop(0, heads)
            def _(h):
                cols = pl.ds(pl.multiple_of(h * head, head), head)
                query = normed_rope(raw_ref[:, cols], qg_ref[...], cosine, sine)
                scores = causal_scores(query, key_ref[seen], step * block, scaling)
                highest = jnp.max(scores, -1, keepdims=True)
                exp_vals = jnp.exp(scores - highest)
                total = jnp.sum(exp_vals, -1, keepdims=True)
                probs = (exp_vals / total).astype(BF16)
                out_ref[:, cols] = dot_nn(probs, value_ref[seen])
                log_ref[h] = highest + jnp.log(total)

    gate = jax.nn.sigmoid(dot_nn(normed_ref[...], wg_ref[...]))
    gate_ref[...] = gate
    mixed_ref[...] = (out_ref[...] * gate).astype(BF16)
    pl.when(tick == pl.num_programs(0) * steps - 1)(finish)


def attend(normed, weights, gates, low, query_gain, key_gain, cosine, sine, heads, head, length, block=256):
    rows, width = normed.shape
    cols = weights.shape[1]
    seqs, steps = rows // length, length // block
    whole = lambda shape: pl.BlockSpec(
        shape, lambda s, i: (0,) * len(shape), pipeline_mode=pl.Buffered(1)
    )
    part = lambda cols: pl.BlockSpec((block, cols), lambda s, i: (s * steps + i, 0))
    *outs, gathered = pl.pallas_call(
        functools.partial(attend_kernel, heads, head, block),
        out_shape=(
            jax.ShapeDtypeStruct((rows, cols), F32),
            jax.ShapeDtypeStruct((rows, heads * head), F32),
            jax.ShapeDtypeStruct((heads, rows, 1), F32),
            jax.ShapeDtypeStruct((rows, heads * head), F32),
            jax.ShapeDtypeStruct((rows, heads * head), BF16),
            jax.ShapeDtypeStruct((2, 2, 2, *low.shape), low.dtype),
        ),
        grid=(seqs, steps),
        in_specs=[
            part(width),
            whole((width, cols)),
            whole((width, heads * head)),
            pl.BlockSpec(memory_space=pl.ANY),
            whole((1, head)),
            whole((1, head)),
            whole((length, head)),
            whole((length, head)),
        ],
        out_specs=(
            part(cols),
            part(heads * head),
            pl.BlockSpec((heads, block, 1), lambda s, i: (0, s * steps + i, 0)),
            part(heads * head),
            part(heads * head),
            pl.BlockSpec(memory_space=pl.ANY),
        ),
        scratch_shapes=[
            pltpu.VMEM((length, head), BF16),
            pltpu.VMEM((length, head), BF16),
            *GATHER_SEMAPHORES,
        ],
        compiler_params=pltpu.CompilerParams(collective_id=3, has_side_effects=True),
        cost_estimate=micros(42),
        name="attend",
    )(normed, weights, gates, low, query_gain, key_gain, cosine, sine)
    return *outs, gathered.reshape(rows, width)


def add_products(step, total_ref, start, left_ref, right_ref, tile=1024):
    wide = min(512, right_ref.shape[1])

    @pl.loop(0, left_ref.shape[1] // tile)
    def _(m):
        at = pl.ds(pl.multiple_of(m * tile, tile), tile)

        @pl.loop(0, right_ref.shape[1] // wide)
        def _(n):
            cols = pl.ds(pl.multiple_of(start + n * wide, wide), wide)
            part = dot_tn(left_ref[:, at], right_ref[:, pl.ds(pl.multiple_of(n * wide, wide), wide)])

            @pl.when(step == 0)
            def _():
                total_ref[at, cols] = part

            @pl.when(step > 0)
            def _():
                total_ref[at, cols] += part


def store_low(step, total_ref, out_ref, tile=256):
    @pl.when(step == pl.num_programs(0) - 1)
    def _():
        @pl.loop(0, total_ref.shape[0] // tile)
        def _(m):
            at = pl.ds(m * tile, tile)
            out_ref[at] = total_ref[at].astype(BF16)


def grads_kernel(left_ref, right_ref, out_ref, total_ref):
    step = pl.program_id(0)
    add_products(step, total_ref, 0, left_ref, right_ref)
    store_low(step, total_ref, out_ref)


def weight_grads(left, right, block=1024):
    (rows, width), cols = left.shape, right.shape[1]
    part = lambda cols: pl.BlockSpec((block, cols), lambda i: (i, 0))
    return pl.pallas_call(
        grads_kernel,
        out_shape=jax.ShapeDtypeStruct((width, cols), BF16),
        grid=(rows // block,),
        in_specs=[part(width), part(cols)],
        out_specs=pl.BlockSpec((width, cols), lambda i: (0, 0)),
        scratch_shapes=[pltpu.VMEM((width, cols), F32)],
        cost_estimate=micros(11),
        name="weight_grads",
    )(left, right)


def gate_back_kernel(
    normed_ref, branch_ref, w_ref, attended_ref, gate_ref, mixed_ref,
    dattended_ref, dgating_ref, grad_ref, total_ref,
):
    step = pl.program_id(0)
    dmixed = dot_nn(branch_ref[...], w_ref[...])
    gate = gate_ref[...]
    dattended_ref[...] = (dmixed * gate).astype(BF16)
    dgating_ref[...] = (dmixed * attended_ref[...] * gate * (1.0 - gate)).astype(BF16)
    add_products(step, total_ref, 0, normed_ref, dgating_ref)
    add_products(step, total_ref, dgating_ref.shape[1], branch_ref, mixed_ref)
    store_low(step, total_ref, grad_ref)


def gate_back(normed, branch, weights, attended, gate, mixed, block=1024):
    rows, width = normed.shape
    cols = attended.shape[1]
    part = lambda cols: pl.BlockSpec((block, cols), lambda i: (i, 0))
    return pl.pallas_call(
        gate_back_kernel,
        out_shape=(
            jax.ShapeDtypeStruct((rows, cols), BF16),
            jax.ShapeDtypeStruct((rows, cols), BF16),
            jax.ShapeDtypeStruct((width, 2 * cols), BF16),
        ),
        grid=(rows // block,),
        in_specs=[
            part(width),
            part(width),
            pl.BlockSpec((width, cols), lambda i: (0, 1)),
            part(cols),
            part(cols),
            part(cols),
        ],
        out_specs=(part(cols), part(cols), pl.BlockSpec((width, 2 * cols), lambda i: (0, 0))),
        scratch_shapes=[pltpu.VMEM((width, 2 * cols), F32)],
        compiler_params=pltpu.CompilerParams(vmem_limit_bytes=VMEM_BYTES),
        cost_estimate=micros(25),
        name="gate_back",
    )(normed, branch, weights, attended, gate, mixed)


def feed_units(count, tile, mid_ref, low_ref, gu_ref, down_ref, first, act_ref, dgu_ref):
    @pl.loop(0, count // tile)
    def _(j):
        start = pl.multiple_of(j * tile, tile)
        at, after = pl.ds(start, tile), pl.ds(pl.multiple_of(count + start, tile), tile)
        last = pl.ds(pl.multiple_of(first + start, tile), tile)
        gate = dot_nn(mid_ref[...], gu_ref[:, at])
        up = dot_nn(mid_ref[...], gu_ref[:, after])
        dact = dot_nn(low_ref[...], down_ref[:, last])
        sigma = jax.nn.sigmoid(gate)
        silu = gate * sigma
        act_ref[:, at] = (silu * up).astype(BF16)
        dgu_ref[:, at] = (dact * up * sigma * (1.0 + gate * (1.0 - sigma))).astype(BF16)
        dgu_ref[:, after] = (dact * silu).astype(BF16)


def feed_kernel(count, tile, mid_ref, low_ref, gu_ref, down_ref, act_ref, dgu_ref):
    feed_units(count, tile, mid_ref, low_ref, gu_ref, down_ref, 0, act_ref, dgu_ref)


def feed_grads_kernel(
    count, tile, mid_ref, low_ref, w_ref, rows_ref, act_ref, dgu_ref, grad_ref, line_ref, total_ref, *sems
):
    step = pl.program_id(0)
    lines = both_halves(rows_ref, line_ref, *sems)

    @pl.when(step == 0)
    def _():
        greet_line((), *lines[0][4]())
        for steps in lines:
            steps[0]()

    feed_units(count, tile, mid_ref, low_ref, w_ref, w_ref, 2 * count, act_ref, dgu_ref)

    @pl.when(step == 0)
    def _():
        lines[0][1]()

    @pl.when(step == pl.num_programs(0) - 1)
    def _():
        lines[1][2]()

    add_products(step, total_ref, 0, mid_ref, dgu_ref)
    add_products(step, total_ref, 2 * count, low_ref, act_ref)

    @pl.when(step == 0)
    def _():
        lines[1][1]()
        lines[0][2]()

    store_low(step, total_ref, grad_ref)

    @pl.when(step == pl.num_programs(0) - 1)
    def _():
        for steps in lines:
            steps[3]()


def feed_forward(mid, low, weights, down, block=512):
    rows, width = mid.shape
    count = down.shape[1]
    part = lambda cols: pl.BlockSpec((block, cols), lambda i: (i, 0))
    whole = lambda array: pl.BlockSpec(array.shape, lambda i: (0, 0), pipeline_mode=pl.Buffered(1))
    return pl.pallas_call(
        functools.partial(feed_kernel, count, 256),
        out_shape=(
            jax.ShapeDtypeStruct((rows, count), BF16),
            jax.ShapeDtypeStruct((rows, 2 * count), BF16),
        ),
        grid=(rows // block,),
        in_specs=[part(width), part(width), whole(weights), whole(down)],
        out_specs=(part(count), part(2 * count)),
        compiler_params=pltpu.CompilerParams(vmem_limit_bytes=VMEM_BYTES),
        cost_estimate=micros(14),
        name="feed_forward",
    )(mid, low, weights, down)


def feed_forward_grads(mid, low, weights, line, block=1024):
    rows, width = mid.shape
    count = weights.shape[1] // 3
    part = lambda cols: pl.BlockSpec((block, cols), lambda i: (i, 0))
    whole = pl.BlockSpec(weights.shape, lambda i: (0, 0), pipeline_mode=pl.Buffered(1))
    return pl.pallas_call(
        functools.partial(feed_grads_kernel, count, 256),
        out_shape=(
            jax.ShapeDtypeStruct((rows, count), BF16),
            jax.ShapeDtypeStruct((rows, 2 * count), BF16),
            jax.ShapeDtypeStruct(weights.shape, BF16),
            jax.ShapeDtypeStruct((4 * line.shape[0], line.shape[1]), BF16),
        ),
        grid=(rows // block,),
        in_specs=[part(width), part(width), whole, pl.BlockSpec(memory_space=pltpu.VMEM)],
        out_specs=(part(count), part(2 * count), whole, pl.BlockSpec(memory_space=pl.ANY)),
        scratch_shapes=[pltpu.VMEM(weights.shape, F32), *LINE_SEMAPHORES],
        compiler_params=pltpu.CompilerParams(
            collective_id=9, has_side_effects=True, vmem_limit_bytes=VMEM_BYTES
        ),
        cost_estimate=micros(41),
        name="feed_forward_grads",
    )(mid, low, weights, line)


def attend_back_kernel(
    heads, head, block, raw_ref, up_ref, log_ref, qg_ref, kg_ref, cos_ref, sin_ref, sums_ref,
    out_ref, qg_out, kg_out, sum_ref, key_ref, value_ref, dkey_ref, dvalue_ref, own, load_sem, *scratch,
):
    seq, step, steps = pl.program_id(0), pl.program_id(1), pl.num_programs(1)
    tick = seq * steps + step
    scaling = head**-0.5
    at = heads * head
    blocks = raw_ref.shape[0] // block
    diag_x, diag_y, x_low, y_high, second, finish = axis_steps(own, *scratch)

    @pl.when(tick == 0)
    def _():
        load = pltpu.make_async_copy(sums_ref, own, load_sem)
        load.start()
        device = place()[3]
        greet((device["y"], device["x"]))
        load.wait()
        for copy in (diag_x, diag_y, x_low, y_high):
            copy.start()
        qg_out[...] = jnp.zeros_like(qg_out)
        kg_out[...] = jnp.zeros_like(kg_out)

    pl.when(tick == 4)(second)

    @pl.when(step == 0)
    def _():
        key_ref[...] = normed_rope(
            raw_ref[:, at : at + head], kg_ref[...], cos_ref[...], sin_ref[...]
        )
        value_ref[...] = raw_ref[:, at + head :].astype(BF16)
        dkey_ref[...] = jnp.zeros_like(dkey_ref)
        dvalue_ref[...] = jnp.zeros_like(dvalue_ref)

    rows = pl.ds(pl.multiple_of(step * block, block), block)

    for i in range(0, blocks, 2):

        @pl.when(step // 2 == i // 2)
        def _():
            seen = pl.ds(0, (i + 2) * block)

            @pl.loop(0, heads)
            def _(h):
                cols = pl.ds(pl.multiple_of(h * head, head), head)
                raw = raw_ref[rows, cols]
                query = normed_rope(raw, qg_ref[...], cos_ref[rows], sin_ref[rows])
                scores = causal_scores(query, key_ref[seen], step * block, scaling)
                probs = jnp.exp(scores - log_ref[h])
                upstream = up_ref[:, cols]
                dprobs = dot_nt(upstream, value_ref[seen])
                centre = jnp.sum(dprobs * probs, -1, keepdims=True)
                dscores = (probs * (dprobs - centre)).astype(BF16)
                dkey_ref[seen] += dot_tn(dscores, query)
                dvalue_ref[seen] += dot_tn(probs.astype(BF16), upstream)
                dquery = dot_nn(dscores, key_ref[seen]) * scaling
                grad, part = normed_rope_back(
                    dquery, raw, qg_ref[...], cos_ref[rows], sin_ref[rows]
                )
                out_ref[rows, cols] = grad
                qg_out[...] += part

    @pl.when(step == blocks - 1)
    def _():
        grad, part = normed_rope_back(
            dkey_ref[...] * scaling,
            raw_ref[:, at : at + head],
            kg_ref[...],
            cos_ref[...],
            sin_ref[...],
        )
        out_ref[:, at : at + head] = grad
        out_ref[:, at + head :] = dvalue_ref[...].astype(BF16)
        kg_out[...] += part

    @pl.when(tick == pl.num_programs(0) * steps - 1)
    def _():
        def store(rows, value):
            sum_ref[rows] = value

        finish(store)


def attend_back(
    raw, upstream, logs, query_gain, key_gain, cosine, sine, sums, heads, head, length, block=256
):
    rows = raw.shape[0]
    total = jax.ShapeDtypeStruct(sums.shape[1:], F32)
    seqs, steps = rows // length, length // block
    whole = lambda shape: pl.BlockSpec(shape, lambda s, i: (0,) * len(shape))
    return pl.pallas_call(
        functools.partial(attend_back_kernel, heads, head, block),
        out_shape=(
            jax.ShapeDtypeStruct(raw.shape, BF16),
            jax.ShapeDtypeStruct((1, head), F32),
            jax.ShapeDtypeStruct((1, head), F32),
            total,
        ),
        grid=(seqs, steps),
        in_specs=[
            pl.BlockSpec((length, raw.shape[1]), lambda s, i: (s, 0)),
            pl.BlockSpec((block, heads * head), lambda s, i: (s * steps + i, 0)),
            pl.BlockSpec((heads, block, 1), lambda s, i: (0, s * steps + i, 0)),
            whole((1, head)),
            whole((1, head)),
            whole((length, head)),
            whole((length, head)),
            pl.BlockSpec(memory_space=pl.ANY),
        ],
        out_specs=(
            pl.BlockSpec((length, raw.shape[1]), lambda s, i: (s, 0)),
            whole((1, head)),
            whole((1, head)),
            whole(total.shape),
        ),
        scratch_shapes=[
            pltpu.VMEM((length, head), BF16),
            pltpu.VMEM((length, head), BF16),
            pltpu.VMEM((length, head), F32),
            pltpu.VMEM((length, head), F32),
            pltpu.VMEM(sums.shape, BF16),
            pltpu.SemaphoreType.DMA,
            *axis_scratch(*sums.shape[1:]),
        ],
        compiler_params=pltpu.CompilerParams(
            collective_id=5, has_side_effects=True, vmem_limit_bytes=VMEM_BYTES
        ),
        cost_estimate=micros(40),
        name="attend_back",
    )(raw, upstream, logs, query_gain, key_gain, cosine, sine, sums)


def attention_weights(query_proj, key_proj, value_proj, gating_proj, output_proj):
    return (
        lax.all_gather(query_proj, "dp", axis=0, tiled=True),
        lax.all_gather(key_proj, "dp", axis=0, tiled=True),
        lax.all_gather(value_proj, "dp", axis=0, tiled=True),
        lax.all_gather(gating_proj, "dp", axis=0, tiled=True),
        lax.all_gather(output_proj, "dp", axis=1, tiled=True),
    )


def swiglu_weights(swiglu_gate, swiglu_up, swiglu_down):
    return (
        lax.all_gather(swiglu_gate, "dp", axis=0, tiled=True),
        lax.all_gather(swiglu_up, "dp", axis=0, tiled=True),
        lax.all_gather(swiglu_down, "dp", axis=1, tiled=True),
    )


def softmax_forward_mapped(seq_items, causal):
    queries, keys_seq, values_seq = seq_items
    scaling = queries.shape[-1] ** (-0.5)
    scores = (
        jnp.einsum("qgjd,kgd->gjqk", queries, keys_seq, preferred_element_type=jnp.float32)
        * scaling
    )
    scores = jnp.where(causal, scores, -1e30)
    highest = jnp.max(scores, -1, keepdims=True)
    exp_vals = jnp.exp(scores - highest)
    row_totals = jnp.sum(exp_vals, -1, keepdims=True)
    attn_probs = (exp_vals / row_totals).astype(jnp.bfloat16)
    attended = jnp.einsum(
        "gjqk,kgd->qgjd", attn_probs, values_seq, preferred_element_type=jnp.float32
    )
    return (attended, highest[..., 0] + jnp.log(row_totals[..., 0]))


def softmax_backward_mapped(seq_items, causal):
    queries, keys_seq, values_seq, log_total, upstream = seq_items
    scaling = queries.shape[-1] ** (-0.5)
    scores = (
        jnp.einsum("qgjd,kgd->gjqk", queries, keys_seq, preferred_element_type=jnp.float32)
        * scaling
    )
    scores = jnp.where(causal, scores, -1e30)
    attn_probs = jnp.exp(scores - log_total[..., None])
    dprobs = jnp.einsum("qgjd,kgd->gjqk", upstream, values_seq, preferred_element_type=jnp.float32)
    centre = jnp.sum(dprobs * attn_probs, -1, keepdims=True)
    dscores = (attn_probs * (dprobs - centre)).astype(jnp.bfloat16)
    dqueries = (
        jnp.einsum("gjqk,kgd->qgjd", dscores, keys_seq, preferred_element_type=jnp.float32)
        * scaling
    )
    key_grads = (
        jnp.einsum("gjqk,qgjd->kgd", dscores, queries, preferred_element_type=jnp.float32) * scaling
    )
    value_grads = jnp.einsum(
        "gjqk,qgjd->kgd",
        attn_probs.astype(jnp.bfloat16),
        upstream,
        preferred_element_type=jnp.float32,
    )
    key_rows = key_grads.shape[0]
    return (dqueries, key_grads.reshape(key_rows, -1), value_grads.reshape(key_rows, -1))


def per_device_wide(
    tokens,
    cotangent,
    domain_ids,
    domain_counts,
    domain_numer,
    domain_denom,
    attention_gain,
    query_gain,
    key_gain,
    query_proj,
    key_proj,
    value_proj,
    gating_proj,
    output_proj,
    swiglu_gain,
    swiglu_gate,
    swiglu_up,
    swiglu_down,
):
    seq_count, local_len, model_width = tokens.shape
    full_len = local_len * lax.axis_size("ctx")
    local_rows = seq_count * local_len
    all_rows = seq_count * full_len
    head_dim = query_gain.shape[0]
    local_heads = query_proj.shape[1] // head_dim
    local_kv = key_proj.shape[1] // head_dim
    group_size = local_heads // local_kv
    positions = jnp.arange(full_len, dtype=jnp.int32)
    causal = positions[:, None] >= positions[None, :]
    cosine, sine = rope_tables(positions, head_dim)
    cos_rows = cosine[:, None, :]
    sin_rows = sine[:, None, :]
    inputs = tokens.reshape(local_rows, model_width).astype(jnp.float32)
    inverse_in = lax.rsqrt(jnp.mean(inputs * inputs, -1, keepdims=True) + EPSILON)
    gain_in = attention_gain.astype(jnp.float32)
    normed = (inputs * inverse_in * gain_in).astype(jnp.bfloat16)
    normed_all = lax.all_gather(
        normed.reshape(seq_count, local_len, model_width), "ctx", axis=1, tiled=True
    ).reshape(all_rows, model_width)
    attn_full = attention_weights(query_proj, key_proj, value_proj, gating_proj, output_proj)
    query_raw = dot_nn(normed_all, attn_full[0]).reshape(
        seq_count, full_len, local_heads, head_dim
    )
    key_raw = dot_nn(normed_all, attn_full[1]).reshape(seq_count, full_len, local_kv, head_dim)
    value_low = (
        dot_nn(normed_all, attn_full[2])
        .astype(jnp.bfloat16)
        .reshape(seq_count, full_len, local_kv, head_dim)
    )
    gate_pre = dot_nn(normed_all, attn_full[3])
    query_scale = query_gain.astype(jnp.float32)
    key_scale = key_gain.astype(jnp.float32)
    query_inv = lax.rsqrt(jnp.mean(query_raw * query_raw, -1, keepdims=True) + EPSILON)
    key_inv = lax.rsqrt(jnp.mean(key_raw * key_raw, -1, keepdims=True) + EPSILON)
    query_low = rotate(query_raw * query_inv * query_scale, cos_rows, sin_rows).astype(jnp.bfloat16)
    key_low = rotate(key_raw * key_inv * key_scale, cos_rows, sin_rows).astype(jnp.bfloat16)
    query_groups = query_low.reshape(seq_count, full_len, local_kv, group_size, head_dim)
    attended, log_total = lax.map(
        lambda seq_items: softmax_forward_mapped(seq_items, causal), (query_groups, key_low, value_low)
    )
    attended = attended.reshape(all_rows, local_heads * head_dim)
    gate_sig = jax.nn.sigmoid(gate_pre)
    mixed = (attended * gate_sig).astype(jnp.bfloat16)
    branch_part = dot_nn(mixed, attn_full[4]).reshape(seq_count, full_len, model_width)
    branch = lax.psum_scatter(branch_part, "ctx", scatter_dimension=1, tiled=True).reshape(
        local_rows, model_width
    )
    hidden = inputs + branch
    inverse_mid = lax.rsqrt(jnp.mean(hidden * hidden, -1, keepdims=True) + EPSILON)
    gain_mid = swiglu_gain.astype(jnp.float32)
    normed_mid = (hidden * inverse_mid * gain_mid).astype(jnp.bfloat16)
    normed_mid_all = lax.all_gather(
        normed_mid.reshape(seq_count, local_len, model_width), "ctx", axis=1, tiled=True
    ).reshape(all_rows, model_width)
    swiglu_full = swiglu_weights(swiglu_gate, swiglu_up, swiglu_down)
    gate_ff = dot_nn(normed_mid_all, swiglu_full[0])
    up_val = dot_nn(normed_mid_all, swiglu_full[1])
    gate_sigma = jax.nn.sigmoid(gate_ff)
    silu_val = gate_ff * gate_sigma
    activation = (silu_val * up_val).astype(jnp.bfloat16)
    down_part = dot_nn(activation, swiglu_full[2]).reshape(seq_count, full_len, model_width)
    ffn_branch = (
        lax.psum_scatter(down_part.astype(jnp.bfloat16), "ctx", scatter_dimension=1, tiled=True)
        .astype(jnp.float32)
        .reshape(local_rows, model_width)
    )
    layer_out = (hidden + ffn_branch).astype(jnp.bfloat16)
    domain_table = (
        domain_ids[:, None] == jnp.arange(domain_counts.shape[0], dtype=jnp.int32)[None, :]
    ).astype(jnp.float32)
    ratio = (
        domain_numer.astype(jnp.float32)
        / domain_denom.astype(jnp.float32)
        * LENGTH
        / domain_counts.astype(jnp.float32)
    )
    factor = jnp.sum(domain_table * ratio[None, :], 1)
    upstream = (cotangent.astype(jnp.float32) * factor[:, None, None]).reshape(
        local_rows, model_width
    )
    swiglu_back = swiglu_weights(swiglu_gate, swiglu_up, swiglu_down)
    out_low = upstream.astype(jnp.bfloat16)
    out_all = lax.all_gather(
        out_low.reshape(seq_count, local_len, model_width), "ctx", axis=1, tiled=True
    ).reshape(all_rows, model_width)
    dactivation = dot_nt(out_all, swiglu_back[2])
    dgate_low = (dactivation * up_val * gate_sigma * (1.0 + gate_ff * (1.0 - gate_sigma))).astype(
        jnp.bfloat16
    )
    dup_low = (dactivation * silu_val).astype(jnp.bfloat16)
    grad_down = dot_tn(activation, out_all)
    grad_gate = dot_tn(normed_mid_all, dgate_low)
    grad_up = dot_tn(normed_mid_all, dup_low)
    dmid_part = dot_nt(dgate_low, swiglu_back[0]) + dot_nt(dup_low, swiglu_back[1])
    dnormed_mid = lax.psum_scatter(
        dmid_part.reshape(seq_count, full_len, model_width), "ctx", scatter_dimension=1, tiled=True
    ).reshape(local_rows, model_width)
    grad_gain_mid = jnp.sum(dnormed_mid * hidden * inverse_mid, 0)
    dhidden = upstream + norm_back(dnormed_mid, hidden, inverse_mid, gain_mid)
    swiglu_grads = (
        lax.psum_scatter(
            grad_gate.astype(jnp.bfloat16), "dp", scatter_dimension=0, tiled=True
        ).astype(jnp.float32),
        lax.psum_scatter(
            grad_up.astype(jnp.bfloat16), "dp", scatter_dimension=0, tiled=True
        ).astype(jnp.float32),
        lax.psum_scatter(
            grad_down.astype(jnp.bfloat16), "dp", scatter_dimension=1, tiled=True
        ).astype(jnp.float32),
    )
    attn_back = attention_weights(query_proj, key_proj, value_proj, gating_proj, output_proj)
    dbranch_low = dhidden.astype(jnp.bfloat16)
    dbranch_all = lax.all_gather(
        dbranch_low.reshape(seq_count, local_len, model_width), "ctx", axis=1, tiled=True
    ).reshape(all_rows, model_width)
    grad_output = dot_tn(mixed, dbranch_all)
    dmixed = dot_nt(dbranch_all, attn_back[4])
    dattended_low = (dmixed * gate_sig).astype(jnp.bfloat16)
    dgating_low = (dmixed * attended * gate_sig * (1.0 - gate_sig)).astype(jnp.bfloat16)
    upstream_heads = dattended_low.reshape(seq_count, full_len, local_kv, group_size, head_dim)
    dquery_rot, dkey_rot, dvalue_sum = lax.map(
        lambda seq_items: softmax_backward_mapped(seq_items, causal),
        (query_groups, key_low, value_low, log_total, upstream_heads),
    )
    dvalue_low = dvalue_sum.reshape(all_rows, local_kv * head_dim).astype(jnp.bfloat16)
    dquery_normed = unrotate(
        dquery_rot.reshape(seq_count, full_len, local_heads, head_dim), cos_rows, sin_rows
    )
    dkey_normed = unrotate(
        dkey_rot.reshape(seq_count, full_len, local_kv, head_dim), cos_rows, sin_rows
    )
    grad_query_gain = jnp.sum(dquery_normed * query_raw * query_inv, (0, 1, 2))
    grad_key_gain = jnp.sum(dkey_normed * key_raw * key_inv, (0, 1, 2))
    dquery_low = (
        norm_back(dquery_normed, query_raw, query_inv, query_scale)
        .reshape(all_rows, -1)
        .astype(jnp.bfloat16)
    )
    dkey_low = (
        norm_back(dkey_normed, key_raw, key_inv, key_scale)
        .reshape(all_rows, -1)
        .astype(jnp.bfloat16)
    )
    dnormed_part = (
        dot_nt(dquery_low, attn_back[0])
        + dot_nt(dkey_low, attn_back[1])
        + dot_nt(dvalue_low, attn_back[2])
        + dot_nt(dgating_low, attn_back[3])
    )
    dnormed = (
        lax.psum_scatter(
            dnormed_part.reshape(seq_count, full_len, model_width).astype(jnp.bfloat16),
            "ctx",
            scatter_dimension=1,
            tiled=True,
        )
        .astype(jnp.float32)
        .reshape(local_rows, model_width)
    )
    grad_gain_in = jnp.sum(dnormed * inputs * inverse_in, 0)
    input_grad = (dhidden + norm_back(dnormed, inputs, inverse_in, gain_in)).astype(jnp.bfloat16)
    grad_query = dot_tn(normed_all, dquery_low)
    grad_key = dot_tn(normed_all, dkey_low)
    grad_value = dot_tn(normed_all, dvalue_low)
    grad_gating = dot_tn(normed_all, dgating_low)
    attention_grads = (
        lax.psum_scatter(
            grad_query.astype(jnp.bfloat16), "dp", scatter_dimension=0, tiled=True
        ).astype(jnp.float32),
        lax.psum_scatter(
            grad_key.astype(jnp.bfloat16), "dp", scatter_dimension=0, tiled=True
        ).astype(jnp.float32),
        lax.psum_scatter(
            grad_value.astype(jnp.bfloat16), "dp", scatter_dimension=0, tiled=True
        ).astype(jnp.float32),
        lax.psum_scatter(
            grad_gating.astype(jnp.bfloat16), "dp", scatter_dimension=0, tiled=True
        ).astype(jnp.float32),
        lax.psum_scatter(
            grad_output.astype(jnp.bfloat16), "dp", scatter_dimension=1, tiled=True
        ).astype(jnp.float32),
    )
    gain_grads = lax.psum(
        (grad_gain_in, grad_gain_mid, grad_query_gain, grad_key_gain), ("dp", "ctx")
    )
    return (
        layer_out.reshape(seq_count, local_len, model_width),
        input_grad.reshape(seq_count, local_len, model_width),
        gain_grads[0],
        gain_grads[2],
        gain_grads[3],
        attention_grads[0],
        attention_grads[1],
        attention_grads[2],
        attention_grads[3],
        attention_grads[4],
        gain_grads[1],
        swiglu_grads[0],
        swiglu_grads[1],
        swiglu_grads[2],
    )


def per_device(
    tokens,
    cotangent,
    domain_ids,
    domain_counts,
    domain_numer,
    domain_denom,
    attention_gain,
    query_gain,
    key_gain,
    query_proj,
    key_proj,
    value_proj,
    gating_proj,
    output_proj,
    swiglu_gain,
    swiglu_gate,
    swiglu_up,
    swiglu_down,
):
    seq_count, local_len, width = tokens.shape
    rows = seq_count * local_len
    full_len = local_len * lax.axis_size("x") * lax.axis_size("c")
    seqs = seq_count * lax.axis_size("y")
    head = query_gain.shape[0]
    kv_cols = key_proj.shape[1] // 2
    q_cols = query_proj.shape[1] // 2
    ff_cols = swiglu_gate.shape[1] // 2
    heads = q_cols // head
    split, rest = ff_cols * 2 // 3, ff_cols - ff_cols * 2 // 3
    tokens, cotangent = tokens.reshape(rows, width), cotangent.reshape(rows, width)
    (
        normed_all, w_qkv, w_go, rows_first, rows_gu, rows_d, inverse_in, out_low, factor, cos_rows, sin_rows,
    ) = opening(
        tokens,
        cotangent,
        attention_gain,
        (domain_ids, domain_counts, domain_numer, domain_denom),
        (
            query_proj, key_proj, value_proj, gating_proj, output_proj, swiglu_gate, swiglu_up, swiglu_down,
        ),
        split,
        full_len,
        head,
    )
    w_first = gather_rows(rows_first)

    query_scale, key_scale = query_gain.astype(F32)[None], key_gain.astype(F32)[None]
    qkv, attended, logs, gate_sig, mixed, out_all = attend(
        normed_all, w_qkv, w_go, out_low, query_scale, key_scale, cos_rows, sin_rows, heads, head, full_len
    )
    wide, column = jax.ShapeDtypeStruct((rows, width), F32), jax.ShapeDtypeStruct((rows, 1), F32)
    low = jax.ShapeDtypeStruct((rows, width), BF16)
    gain_mid = swiglu_gain.reshape(1, -1)
    hidden, inverse_mid, normed_mid = scatter_products(
        middle_kernel, 7, (tokens, gain_mid), (wide, column, low), (mixed, w_go, q_cols)
    )
    mid_all, w_last_d = gather_tokens(normed_mid, rows_d)

    act_first, dgu_first, grad_first, w_last_gu = feed_forward_grads(mid_all, out_all, w_first, rows_gu)
    part_first = scatter_grads(grad_first)
    act_last, dgu_last = feed_forward(mid_all, out_all, w_last_gu, w_last_d)
    dhidden, dbranch, grad_gain_mid = scatter_products(
        middle_back_kernel,
        8,
        (hidden, inverse_mid, gain_mid, cotangent, factor),
        (wide, low, jax.ShapeDtypeStruct((1, width), F32)),
        (dgu_first, w_first, 0),
        (dgu_last, w_last_gu, 0),
    )
    dbranch_all, ffn_sums, grad_last = gather_beside(
        dbranch,
        ((act_first, w_first, 2 * split), (act_last, w_last_d, 0)),
        mid_all,
        out_all,
        dgu_last,
        act_last,
    )
    part_last = scatter_grads(grad_last)
    dbranch_all, part_first = lax.optimization_barrier((dbranch_all, part_first))

    theirs_first = their_rows(part_first)
    dattended, dgating, grad_go = gate_back(
        normed_all, dbranch_all, w_go, attended, gate_sig, mixed
    )
    dattended, theirs_first, grad_go = lax.optimization_barrier((dattended, theirs_first, grad_go))
    part_go = scatter_grads(grad_go)
    dqkv, grad_query_gain, grad_key_gain, ffn_branch = attend_back(
        qkv, dattended, logs, query_scale, key_scale, cos_rows, sin_rows, ffn_sums, heads, head, full_len
    )
    grad_query_gain, grad_key_gain = grad_query_gain[0], grad_key_gain[0]
    dqkv, part_last = lax.optimization_barrier((dqkv, part_last))
    theirs_last = their_rows(part_last)
    layer_out = (hidden + ffn_branch).astype(BF16)
    dqkv, layer_out = lax.optimization_barrier((dqkv, layer_out))
    grad_qkv = weight_grads(normed_all, dqkv)
    grad_qkv, theirs_last = lax.optimization_barrier((grad_qkv, theirs_last))
    plan = [(0, i * split, split, i, 0, i == 2) for i in range(3)]
    plan += [(1, i * rest, rest, i, split, i == 2) for i in range(3)]
    grad_gate, grad_up, grad_down = join_grads(
        (part_first, part_last),
        (theirs_first, theirs_last),
        plan,
        [weight.shape for weight in (swiglu_gate, swiglu_up, swiglu_down)],
    )
    grad_qkv, layer_out, grad_gate, grad_up, grad_down = lax.optimization_barrier(
        (grad_qkv, layer_out, grad_gate, grad_up, grad_down)
    )
    input_grad, mine_qkv, theirs_qkv, totals = tail(
        ((dqkv, w_qkv, 0), (dgating, w_go, 0)),
        grad_qkv,
        tokens,
        inverse_in,
        dhidden,
        attention_gain,
        (grad_gain_mid, grad_query_gain, grad_key_gain),
    )
    input_grad, part_go = lax.optimization_barrier((input_grad, part_go))
    theirs_go = their_rows(part_go)
    grad_gating, grad_output = join_grads(
        (part_go,),
        (theirs_go,),
        [(0, 0, q_cols, 0, 0, False), (0, q_cols, q_cols, 1, 0, True)],
        (gating_proj.shape, output_proj.shape),
    )
    widths, starts = (q_cols, kv_cols, kv_cols), (0, q_cols, q_cols + kv_cols)
    *gain_grads, grad_query, grad_key, grad_value = join_last(
        mine_qkv,
        theirs_qkv,
        totals,
        [(0, starts[i], widths[i], i, 0, False) for i in range(3)],
        (width, width, head, head),
        [weight.shape for weight in (query_proj, key_proj, value_proj)],
    )
    gain_grads = [gain.reshape(-1) for gain in gain_grads]
    shape = (seq_count, local_len, width)
    return (
        layer_out.reshape(shape),
        input_grad.reshape(shape),
        gain_grads[0],
        gain_grads[2],
        gain_grads[3],
        grad_query,
        grad_key,
        grad_value,
        grad_gating,
        grad_output,
        gain_grads[1],
        grad_gate,
        grad_up,
        grad_down,
    )


def solution(mesh):
    if (mesh.shape["dp"], mesh.shape["ctx"]) == (8, 4):
        body = per_device
        mesh = Mesh(mesh.devices.reshape(4, 2, 2, 2), ("z", "y", "x", "c"))
        dp, ctx = ("z", "y"), ("x", "c")
    else:
        body = per_device_wide
        dp, ctx = "dp", "ctx"
    tokens, weight, turned = P(dp, ctx, None), P(dp, ctx), P(ctx, dp)
    return jax.shard_map(
        body,
        mesh=mesh,
        in_specs=(tokens, tokens, P(dp), *[P()] * 6, *[weight] * 4, turned, P(), weight, weight, turned),
        out_specs=(tokens, tokens, *[P()] * 3, *[weight] * 4, turned, P(), weight, weight, turned),
        check_vma=False,
    )
```

```python
import functools

import jax
import jax.numpy as jnp
import numpy as np
from jax import lax
from jax.experimental import pallas as pl
from jax.experimental.pallas import tpu as pltpu
from jax.sharding import Mesh
from jax.sharding import PartitionSpec as P

LENGTH = 1024

EPSILON = 1e-06
ROPE_BASE = 1000000.0
MESH = pl.DeviceIdType.MESH
BF16 = jnp.bfloat16
F32 = jnp.float32
VMEM_BYTES = 62 * 2**20


def micros(count):
    return pl.CostEstimate(flops=0, transcendentals=0, bytes_accessed=count * 3_300_000)


def dot_nn(left, right):
    return jnp.dot(left, right, preferred_element_type=F32)


def dot_tn(left, right):
    return lax.dot_general(left, right, (((0,), (0,)), ((), ())), preferred_element_type=F32)


def dot_nt(left, right):
    return lax.dot_general(left, right, (((1,), (1,)), ((), ())), preferred_element_type=F32)


def rope_tables(positions, head_width):
    halfway = head_width // 2
    inverse = 1.0 / ROPE_BASE ** (jnp.arange(halfway, dtype=F32) * (2.0 / head_width))
    angles = positions.astype(F32)[:, None] * inverse[None, :]
    return (jnp.cos(angles), jnp.sin(angles))


def rotate(tensor, cosine, sine):
    halfway = tensor.shape[-1] // 2
    first_half = tensor[..., :halfway]
    second_half = tensor[..., halfway:]
    return jnp.concatenate(
        [first_half * cosine - second_half * sine, second_half * cosine + first_half * sine], -1
    )


def unrotate(grads_in, cosine, sine):
    halfway = grads_in.shape[-1] // 2
    first_half = grads_in[..., :halfway]
    second_half = grads_in[..., halfway:]
    return jnp.concatenate(
        [first_half * cosine + second_half * sine, second_half * cosine - first_half * sine], -1
    )


def norm_back(grads_in, values_in, inverse, gain_vec):
    scaled = grads_in * gain_vec
    return inverse * scaled - values_in * (inverse * inverse * inverse) * jnp.mean(
        scaled * values_in, -1, keepdims=True
    )


def greet(neighbours):
    barrier = pltpu.get_barrier_semaphore()
    for neighbour in neighbours:
        pl.semaphore_signal(barrier, inc=1, device_id=neighbour, device_id_type=MESH)
    pl.semaphore_wait(barrier, len(neighbours))


def remote_copies(send, recv, device):
    def remote(index, source, target, axis):
        return pltpu.make_async_remote_copy(
            src_ref=source,
            dst_ref=target,
            send_sem=send.at[index],
            recv_sem=recv.at[index],
            device_id=device[axis],
            device_id_type=MESH,
        )

    return remote


def place():
    y, x, c = lax.axis_index("y"), lax.axis_index("x"), lax.axis_index("c")
    return y, x, c, {"y": {"y": 1 - y}, "x": {"x": 1 - x}, "c": {"c": 1 - c}}


def gather_steps(s_ref, out_ref, local_sem, send, recv, split=True):
    y, x, c, device = place()
    remote = remote_copies(send, recv, device)
    half = s_ref.shape[0] // 2
    low, high = pl.ds(0, half), pl.ds(half, half)
    mine = out_ref.at[y, x, c]
    from_x = out_ref.at[y, 1 - x, c]
    from_y = out_ref.at[1 - y, x, c]
    diagonal = out_ref.at[1 - y, 1 - x, c]
    x_low = remote(0, s_ref.at[low], mine.at[low], "x")
    y_high = remote(1, s_ref.at[high], mine.at[high], "y")
    x_high = remote(2, s_ref.at[high], mine.at[high], "x")
    y_low = remote(3, s_ref.at[low], mine.at[low], "y")
    c_own = remote(4, s_ref, mine, "c")
    local = pltpu.make_async_copy(s_ref, mine, local_sem)
    forward_y = remote(5, from_x.at[low], from_x.at[low], "y")
    over_x = from_y.at[high] if split else from_y
    forward_x = remote(6, over_x, over_x, "x")
    c_x = remote(7, from_x, from_x, "c")
    c_y = remote(8, from_y, from_y, "c")
    c_low = remote(9, diagonal.at[low], diagonal.at[low], "c")
    over_c = diagonal.at[high] if split else diagonal
    c_high = remote(10, over_c, over_c, "c")

    def begin():
        for copy in (x_low, y_high, x_high, y_low, c_own, local):
            copy.start()

    def forward():
        x_low.wait_recv()
        if split:
            forward_y.start()
        y_high.wait_recv()
        if split:
            forward_x.start()

    def across():
        if not split:
            y_low.wait_recv()
            forward_x.start()
        x_high.wait_recv()
        c_x.start()
        if split:
            y_low.wait_recv()
        c_y.start()

    def finish():
        if split:
            forward_y.wait_recv()
            c_low.start()
        forward_x.wait_recv()
        c_high.start()
        for copy in (c_own, c_x, c_y, *((c_low,) if split else ()), c_high):
            copy.wait()
        for copy in (x_low, y_high, x_high, y_low, *((forward_y,) if split else ()), forward_x):
            copy.wait_send()
        local.wait()

    return begin, forward, across, finish


GATHER_SEMAPHORES = (
    pltpu.SemaphoreType.DMA,
    pltpu.SemaphoreType.DMA((11,)),
    pltpu.SemaphoreType.DMA((11,)),
)


def swap_steps(pieces, sources, outs, local_sem, send, recv, wanted=None):
    y, _, _, device = place()
    remote = remote_copies(send, recv, device)
    copies, locals_ = [], []
    for i, (source, out, first, count, at) in enumerate(pieces):
        if wanted is not None and not wanted(out):
            continue
        rows, cols = sources[source].shape
        target = outs[out].at[pl.ds(pl.multiple_of(y * rows, rows), rows), pl.ds(at, count)]

        def half(which):
            start = pl.multiple_of(which * (cols // 2) + first, 128)
            return sources[source].at[:, pl.ds(start, count)]

        copies.append(remote(i, half(1 - y), target, "y"))
        locals_.append(pltpu.make_async_copy(half(y), target, local_sem.at[i]))

    def begin():
        for copy in (*copies, *locals_):
            copy.start()

    def here():
        for copy in locals_:
            copy.wait()

    def finish():
        for copy in copies:
            copy.wait()

    return begin, here, finish


def line_steps(rows_ref, out_ref, local_sem, send, recv, part, which):
    z = lax.axis_index("z")
    rows, half = rows_ref.shape[0], rows_ref.shape[0] // 2
    first = which * half
    pair, middle = z + 1 - 2 * lax.rem(z, 2), 3 - z
    inner = (z == 1) | (z == 2)

    def at(index):
        return out_ref.at[pl.ds(pl.multiple_of(index * rows + first, half), half)]

    def remote(index, source, target, peer):
        return pltpu.make_async_remote_copy(
            src_ref=source,
            dst_ref=target,
            send_sem=send.at[5 * part + index],
            recv_sem=recv.at[5 * part + index],
            device_id={"z": peer},
            device_id_type=MESH,
        )

    far = middle + 1 - 2 * lax.rem(middle, 2)
    own = rows_ref.at[pl.ds(pl.multiple_of(first, half), half)]
    own_pair = remote(0, own, at(z), pair)
    own_middle = remote(1, own, at(z), middle)
    pair_middle = remote(2, at(pair), at(pair), middle)
    middle_pair = remote(3, at(middle), at(middle), pair)
    far_pair = remote(4, at(far), at(far), pair)
    local = pltpu.make_async_copy(own, at(z), local_sem.at[part])

    def begin():
        local.start()
        own_pair.start()
        pl.when(inner)(own_middle.start)

    def second():
        own_pair.wait_recv()

        @pl.when(inner)
        def _():
            pair_middle.start()
            own_middle.wait_recv()
            middle_pair.start()

    def third():
        @pl.when(inner)
        def _():
            pair_middle.wait_recv()
            far_pair.start()

    def finish():
        @pl.when(inner)
        def _():
            for copy in (own_middle, pair_middle, middle_pair, far_pair):
                copy.wait_send()

        @pl.when(jnp.logical_not(inner))
        def _():
            middle_pair.wait_recv()
            far_pair.wait_recv()

        own_pair.wait_send()
        local.wait()

    def peers():
        return pair, middle, inner

    return begin, second, third, finish, peers


def greet_line(others, pair, middle, inner):
    barrier = pltpu.get_barrier_semaphore()
    for other in (*others, {"z": pair}):
        pl.semaphore_signal(barrier, inc=1, device_id=other, device_id_type=MESH)

    @pl.when(inner)
    def _():
        pl.semaphore_signal(barrier, inc=1, device_id={"z": middle}, device_id_type=MESH)

    count = len(others) + 1
    pl.semaphore_wait(barrier, jnp.where(inner, count + 1, count))


LINE_SEMAPHORES = (
    pltpu.SemaphoreType.DMA((2,)),
    pltpu.SemaphoreType.DMA((10,)),
    pltpu.SemaphoreType.DMA((10,)),
)


def both_halves(rows_ref, out_ref, *sems):
    y = lax.axis_index("y")
    return [line_steps(rows_ref, out_ref, *sems, part, which) for part, which in ((0, y), (1, 1 - y))]


def gather_kernel(source, rows_ref, out, line_ref, *sems):
    begin, forward, across, finish = gather_steps(source, out, *sems[:3])
    lines = both_halves(rows_ref, line_ref, *sems[3:])
    greet_line(tuple(place()[3].values()), *lines[0][4]())
    for steps in lines:
        steps[0]()
    begin()
    for steps in lines:
        steps[1]()
    forward()
    lines[0][2]()
    across()
    lines[1][2]()
    finish()
    for steps in lines:
        steps[3]()


def gather_tokens(shard, line):
    rows, width = shard.shape
    gathered, lined = pl.pallas_call(
        gather_kernel,
        out_shape=(
            jax.ShapeDtypeStruct((2, 2, 2, rows, width), shard.dtype),
            jax.ShapeDtypeStruct((4 * line.shape[0], line.shape[1]), line.dtype),
        ),
        in_specs=[pl.BlockSpec(memory_space=pltpu.VMEM)] * 2,
        out_specs=(pl.BlockSpec(memory_space=pl.ANY),) * 2,
        scratch_shapes=[*GATHER_SEMAPHORES, *LINE_SEMAPHORES],
        compiler_params=pltpu.CompilerParams(collective_id=1, has_side_effects=True),
        cost_estimate=micros(42),
        name="gather_tokens",
    )(shard, line)
    return gathered.reshape(8 * rows, width), lined


def opening_kernel(pieces, tokens, cotangent, gain, ids, counts, numer, denom, turns, *refs):
    sources, refs = list(refs[:8]), refs[8:]
    out, line_q, line_g, first, last_gu, last_d, inverse, low, factor, cosine, sine, *refs = refs
    rows_q, rows_g, normed, output_t, down_t, *sems = refs
    begin, forward, across, finish = gather_steps(normed, out, *sems[:3], False)
    y = lax.axis_index("y")
    steps = [
        line_steps(rows, line, *sems[3 * i + 3 : 3 * i + 6], part, which)
        for part, which in ((0, y), (1, 1 - y))
        for i, (rows, line) in enumerate(((rows_q, line_q), (rows_g, line_g)))
    ]
    output_ref, down_ref = sources[4], sources[7]
    sources[4], sources[7] = output_t, down_t
    swaps = [
        swap_steps(pieces, sources, (rows_q, rows_g, first, last_gu, last_d), *sems[9:], wanted)
        for wanted in (lambda out: out == 0, lambda out: out == 1, lambda out: out > 1)
    ]
    step = 64

    def norm(i):
        at = pl.ds(i * step, step)
        x = tokens[at].astype(F32)
        inv = lax.rsqrt(jnp.mean(x * x, -1, keepdims=True) + EPSILON)
        inverse[at] = inv
        normed[at] = (x * inv * gain[...].astype(F32).reshape(1, -1)).astype(BF16)

    def weigh(i):
        at = pl.ds(i * step, step)
        low[at] = (cotangent[at].astype(F32) * factor[...]).astype(BF16)

    def turn(i):
        at = pl.ds(i * 128, 128)
        places = lax.broadcasted_iota(jnp.int32, (128, cosine.shape[1]), 0) + i * 128
        angles = places.astype(F32) * turns[0:1]
        cosine[at] = jnp.cos(angles)
        sine[at] = jnp.sin(angles) * turns[1:2]

    greet_line(tuple(place()[3].values()), *steps[0][4]())
    swaps[0][0]()
    swaps[0][1]()
    steps[0][0]()
    output_t[...] = output_ref[...].astype(F32).T.astype(BF16)
    swaps[1][0]()
    swaps[1][1]()
    steps[1][0]()
    pl.loop(0, tokens.shape[0] // step)(norm)
    begin()
    for i in range(2):
        swaps[i][2]()
        steps[i + 2][0]()
    steps[0][1]()
    steps[1][1]()
    chosen = lax.broadcasted_iota(jnp.int32, counts.shape, 1) == ids[...]
    ratio = numer[...].astype(F32) / denom[...].astype(F32) * LENGTH / counts[...].astype(F32)
    factor[...] = jnp.sum(jnp.where(chosen, ratio, 0.0), -1, keepdims=True)

    @pl.loop(0, down_ref.shape[0] // 256)
    def _(i):
        at = pl.ds(pl.multiple_of(i * 256, 256), 256)
        down_t[:, at] = down_ref[at].astype(F32).T.astype(BF16)

    steps[2][1]()
    steps[3][1]()
    forward()
    across()
    swaps[2][0]()
    steps[0][2]()
    steps[1][2]()
    pl.loop(0, tokens.shape[0] // step)(weigh)
    steps[2][2]()
    steps[3][2]()
    pl.loop(0, cosine.shape[0] // 128)(turn)
    finish()
    for step_set in steps:
        step_set[3]()
    swaps[2][1]()
    swaps[2][2]()


def opening(tokens, cotangent, gain, domains, weights, split, full_len, head):
    rows, width = tokens.shape
    halves = [weight.shape[0 if i in (4, 7) else 1] // 2 for i, weight in enumerate(weights)]
    groups = (
        [(i, 0, halves[i]) for i in (0, 1, 2)],
        [(i, 0, halves[i]) for i in (3, 4)],
        [(i, 0, split) for i in (5, 6, 7)],
        [(i, split, halves[i] - split) for i in (5, 6)],
        [(7, split, halves[7] - split)],
    )
    pieces, widths = [], []
    for group in groups:
        at = 0
        for source, first, count in group:
            pieces.append((source, len(widths), first, count, at))
            at += count
        widths.append(at)
    inverse = 1.0 / np.float32(ROPE_BASE) ** (np.arange(head // 2, dtype=np.float32) * np.float32(2.0 / head))
    turns = np.stack([np.tile(inverse, 2), np.repeat(np.float32([-1.0, 1.0]), head // 2)]).astype(np.float32)
    whole, loose = pl.BlockSpec(memory_space=pltpu.VMEM), pl.BlockSpec(memory_space=pl.ANY)
    shape = jax.ShapeDtypeStruct
    dma = pltpu.SemaphoreType.DMA
    gathered, *outs = pl.pallas_call(
        functools.partial(opening_kernel, pieces),
        out_shape=(
            shape((2, 2, 2, rows, width), BF16),
            *[shape((8 * rows, size), BF16) for size in widths[:2]],
            *[shape((2 * rows, size), BF16) for size in widths[2:]],
            shape((rows, 1), F32),
            shape((rows, width), BF16),
            shape((1, 1), F32),
            shape((full_len, head), F32),
            shape((full_len, head), F32),
        ),
        in_specs=[whole] * (8 + len(weights)),
        out_specs=(*[loose] * 6, *[whole] * 5),
        scratch_shapes=[
            *[pltpu.VMEM((2 * rows, size), BF16) for size in widths[:2]],
            pltpu.VMEM((rows, width), BF16),
            *[pltpu.VMEM(weights[i].shape[::-1], BF16) for i in (4, 7)],
            *GATHER_SEMAPHORES,
            *[dma((2,)), dma((10,)), dma((10,))] * 2,
            *[dma((len(pieces),))] * 3,
        ],
        compiler_params=pltpu.CompilerParams(
            collective_id=2, has_side_effects=True, vmem_limit_bytes=VMEM_BYTES
        ),
        cost_estimate=micros(80),
        name="opening",
    )(
        tokens,
        cotangent,
        gain,
        *(domain.reshape(1, -1) for domain in domains),
        jnp.asarray(turns),
        *weights,
    )
    return gathered.reshape(8 * rows, width), *outs


def add_rows(target, start, size, other, base, step=64):
    @pl.loop(0, size // step)
    def _(i):
        at, there = pl.ds(start + i * step, step), pl.ds(base + i * step, step)
        target[at] = (target[at].astype(F32) + other[there].astype(F32)).astype(target.dtype)


def product_steps(windows, lefts, rights, left_vmem, right_vmem, own, pairs, got, load_sem, send, recv):
    y, x, c, device = place()
    remote = remote_copies(send, recv, device)
    rows, width = own.shape[1:]
    half, both, tile = rows // 2, 2 * rows, 256
    targets = ((1 - y, 1 - x), (1 - y, x), (y, 1 - x), (y, x))
    pieces = ((0, 0, half), (0, half, half), (1, 0, rows), (2, 0, rows), (3, 0, rows))
    count = len(lefts)
    right_loads = [
        pltpu.make_async_copy(
            rights[j].at[:, pl.ds(windows[j], right_vmem[j].shape[1])], right_vmem[j], load_sem.at[j]
        )
        for j in range(count)
    ]
    left_loads = []
    for i, (a, b) in enumerate(targets):
        start = pl.multiple_of((a * 2 + b) * both, both)
        left_loads.append(
            [
                pltpu.make_async_copy(
                    lefts[j].at[pl.ds(start, both)], left_vmem[j].at[i], load_sem.at[count * (i + 1) + j]
                )
                for j in range(count)
            ]
        )
    crossing = [
        remote(k, pairs.at[i, 1 - c, pl.ds(first, size)], got.at[i, pl.ds(first, size)], "c")
        for k, (i, first, size) in enumerate(pieces)
    ]

    def load():
        for copy in right_loads:
            copy.start()
        for copies in left_loads:
            for copy in copies:
                copy.start()

    def ready():
        for copy in right_loads:
            copy.wait()

    def product(i):
        for copy in left_loads[i]:
            copy.wait()

        @pl.loop(0, width // tile)
        def _(n):
            cols = pl.ds(pl.multiple_of(n * tile, tile), tile)
            total = dot_nt(left_vmem[0][i], right_vmem[0][cols])
            for j in range(1, count):
                total = total + dot_nt(left_vmem[j][i], right_vmem[j][cols])
            pairs[i, :, :, cols] = total.reshape(2, rows, tile).astype(BF16)

        for k, piece in enumerate(pieces):
            if piece[0] == i:
                crossing[k].start()

    def cores(k, step=64):
        i, first, size = pieces[k]
        crossing[k].wait_recv()

        @pl.loop(0, size // step)
        def _(n):
            at = pl.ds(first + n * step, step)
            own[i, at] = (pairs[i, c, at].astype(F32) + got[i, at].astype(F32)).astype(BF16)

    def finish():
        for copy in crossing:
            copy.wait_send()

    return load, ready, product, cores, finish


def axis_steps(own, x_diag, y_diag, x_got, y_got, send, recv):
    remote = remote_copies(send, recv, place()[3])
    rows = own.shape[1]
    half = rows // 2
    low, high = pl.ds(0, half), pl.ds(half, half)
    diag_x = remote(0, own.at[0, low], x_diag, "x")
    diag_y = remote(1, own.at[0, high], y_diag, "y")
    y_high = remote(2, own.at[1, high], y_got.at[high], "y")
    x_low = remote(3, own.at[2, low], x_got.at[low], "x")
    size = half // 2
    spans = [pl.ds(i * size, size) for i in range(4)]
    y_low = [remote(4 + i, own.at[1, spans[i]], y_got.at[spans[i]], "y") for i in range(2)]
    x_high = [remote(6 + i, own.at[2, spans[2 + i]], x_got.at[spans[2 + i]], "x") for i in range(2)]

    def second():
        diag_x.wait_recv()
        for i in range(2):
            add_rows(own.at[1], i * size, size, x_diag, i * size)
            y_low[i].start()
        diag_y.wait_recv()
        for i in range(2):
            add_rows(own.at[2], half + i * size, size, y_diag, i * size)
            x_high[i].start()

    def finish(store, step=32):
        needed = ((x_low, y_low[0]), (y_high, x_high[0]), (y_low[1],), (x_high[1],))

        @pl.loop(0, 4)
        def _(part):
            for k, copies in enumerate(needed):

                @pl.when(part == k)
                def _():
                    for copy in copies:
                        copy.wait_recv()

            start = lax.rem(part, 2) * half + lax.div(part, 2) * size

            @pl.loop(0, size // step)
            def _(i):
                at = pl.ds(pl.multiple_of(start + i * step, step), step)
                store(at, own[3, at].astype(F32) + x_got[at].astype(F32) + y_got[at].astype(F32))

        for copy in (diag_x, diag_y, y_high, x_low, *y_low, *x_high):
            copy.wait_send()

    return diag_x, diag_y, x_low, y_high, second, finish


def scatter_steps(windows, lefts, rights, scratch):
    count = len(windows)
    product_scratch, axis_scratch = scratch[: 2 * count + 6], scratch[2 * count + 6 :]
    load, ready, product, cores, crossed = product_steps(
        windows, lefts, rights, product_scratch[:count], product_scratch[count : 2 * count],
        *product_scratch[2 * count :],
    )
    own = product_scratch[2 * count]
    diag_x, diag_y, x_low, y_high, second_axis, finish_axis = axis_steps(own, *axis_scratch)

    def first():
        ready()
        product(0)
        cores(0)
        diag_x.start()
        cores(1)
        diag_y.start()
        product(2)
        product(1)
        cores(3)
        x_low.start()
        cores(2)
        y_high.start()

    def second():
        second_axis()
        product(3)
        cores(4)

    def finish(store):
        finish_axis(store)
        crossed()

    return load, first, second, finish


def product_scratch(group, own=True):
    lefts, rights = [item[0] for item in group], [item[1] for item in group]
    rows, width = lefts[0].shape[0] // 8, rights[0].shape[0]
    return [
        *[pltpu.VMEM((4, 2 * rows, left.shape[1]), BF16) for left in lefts],
        *[pltpu.VMEM((width, left.shape[1]), BF16) for left in lefts],
        *[pltpu.VMEM((4, rows, width), BF16)] * own,
        pltpu.VMEM((4, 2, rows, width), BF16),
        pltpu.VMEM((4, rows, width), BF16),
        pltpu.SemaphoreType.DMA((5 * len(group),)),
        pltpu.SemaphoreType.DMA((5,)),
        pltpu.SemaphoreType.DMA((5,)),
    ]


def axis_scratch(rows, width):
    return [
        pltpu.VMEM((rows // 2, width), BF16),
        pltpu.VMEM((rows // 2, width), BF16),
        pltpu.VMEM((rows, width), BF16),
        pltpu.VMEM((rows, width), BF16),
        pltpu.SemaphoreType.DMA((8,)),
        pltpu.SemaphoreType.DMA((8,)),
    ]


def scatter_scratch(group):
    lefts, rights = [item[0] for item in group], [item[1] for item in group]
    rows, width = lefts[0].shape[0] // 8, rights[0].shape[0]
    scratch = product_scratch(group) + axis_scratch(rows, width)
    return lefts + rights, scratch, jax.ShapeDtypeStruct((rows, width), F32)


def middle_kernel(windows, *refs):
    count = len(windows)
    lefts, rights, refs = refs[:count], refs[count : 2 * count], refs[2 * count :]
    tokens, gain, hidden, inverse, normed, *scratch = refs
    load, first, second, finish = scatter_steps(windows, lefts, rights, scratch)

    def store(at, branch):
        total = tokens[at].astype(F32) + branch
        inv = lax.rsqrt(jnp.mean(total * total, -1, keepdims=True) + EPSILON)
        hidden[at] = total
        inverse[at] = inv
        normed[at] = (total * inv * gain[...].astype(F32)).astype(BF16)

    load()
    greet(tuple(place()[3].values()))
    first()
    second()
    finish(store)


def middle_back_kernel(windows, *refs):
    count = len(windows)
    lefts, rights, refs = refs[:count], refs[count : 2 * count], refs[2 * count :]
    hidden, inverse, gain, cotangent, factor, dhidden, dbranch, gain_grad, *scratch = refs
    load, first, second, finish = scatter_steps(windows, lefts, rights, scratch)
    gain_grad[...] = jnp.zeros_like(gain_grad)

    def store(at, grad):
        state, inv = hidden[at], inverse[at]
        gain_grad[...] += jnp.sum(grad * state * inv, 0, keepdims=True)
        upstream = cotangent[at].astype(F32) * factor[...]
        total = upstream + norm_back(grad, state, inv, gain[...].astype(F32))
        dhidden[at] = total
        dbranch[at] = total.astype(BF16)

    load()
    greet(tuple(place()[3].values()))
    first()
    second()
    finish(store)


def scatter_products(kernel, number, extras, outs, *group):
    operands, scratch, _ = scatter_scratch(group)
    whole = pl.BlockSpec(memory_space=pltpu.VMEM)
    return pl.pallas_call(
        functools.partial(kernel, [item[2] for item in group]),
        out_shape=outs,
        in_specs=[pl.BlockSpec(memory_space=pl.ANY)] * len(operands) + [whole] * len(extras),
        out_specs=(whole,) * len(outs),
        scratch_shapes=scratch,
        compiler_params=pltpu.CompilerParams(
            collective_id=number, has_side_effects=True, vmem_limit_bytes=VMEM_BYTES
        ),
        cost_estimate=micros(48),
        name="scatter_products",
    )(*operands, *extras)


def gather_beside_kernel(windows, tile, shard_ref, *refs):
    count = len(windows)
    lefts, rights, refs = refs[:count], refs[count : 2 * count], refs[2 * count :]
    mid, low, dgu, act, out_ref, sums_ref, grad_ref, *scratch = refs
    size = 2 * count + 5
    products, (mid_buf, low_buf, dgu_vmem, act_vmem, total, tile_sem, side_sem), sems = (
        scratch[:size], scratch[size : size + 7], scratch[size + 7 :],
    )
    load, ready, product, cores, crossed = product_steps(
        windows, lefts, rights, products[:count], products[count : 2 * count], sums_ref,
        *products[2 * count :],
    )
    begin, forward, across, finish = gather_steps(shard_ref, out_ref, *sems)
    tiles = mid.shape[0] // tile
    sides = [
        pltpu.make_async_copy(dgu, dgu_vmem, side_sem.at[0]),
        pltpu.make_async_copy(act, act_vmem, side_sem.at[1]),
    ]

    def tile_copies(t):
        rows, slot = pl.ds(pl.multiple_of(t * tile, tile), tile), lax.rem(t, 2)
        return [
            pltpu.make_async_copy(source.at[rows], buffer.at[slot], tile_sem.at[i, slot])
            for i, (source, buffer) in enumerate(((mid, mid_buf), (low, low_buf)))
        ]

    load()
    greet(tuple(place()[3].values()))
    begin()
    for copy in (*sides, *tile_copies(0), *tile_copies(1)):
        copy.start()
    ready()
    for i in range(4):
        product(i)
    forward()
    for copy in sides:
        copy.wait()
    cores(0)
    cores(1)

    @pl.loop(0, tiles)
    def _(t):
        for copy in tile_copies(t):
            copy.wait()
        rows, slot = pl.ds(pl.multiple_of(t * tile, tile), tile), lax.rem(t, 2)
        add_products(t, total, 0, mid_buf.at[slot], dgu_vmem.at[rows])
        add_products(t, total, dgu_vmem.shape[1], low_buf.at[slot], act_vmem.at[rows])

        @pl.when(t + 2 < tiles)
        def _():
            for copy in tile_copies(t + 2):
                copy.start()

        @pl.when(t == tiles // 2 - 1)
        def _():
            across()
            for k in range(2, 5):
                cores(k)

    @pl.loop(0, total.shape[0] // 256)
    def _(m):
        at = pl.ds(m * 256, 256)
        grad_ref[at] = total[at].astype(BF16)

    crossed()
    finish()


def gather_beside(shard, group, mid, low, dgu, act, tile=512):
    rows, width = shard.shape
    operands = [item[0] for item in group] + [item[1] for item in group] + [mid, low, dgu, act]
    cols = dgu.shape[1] + act.shape[1]
    gathered, sums, grad = pl.pallas_call(
        functools.partial(gather_beside_kernel, [item[2] for item in group], tile),
        out_shape=(
            jax.ShapeDtypeStruct((2, 2, 2, rows, width), shard.dtype),
            jax.ShapeDtypeStruct((4, rows, width), BF16),
            jax.ShapeDtypeStruct((width, cols), BF16),
        ),
        in_specs=[
            pl.BlockSpec(memory_space=pltpu.VMEM),
            *[pl.BlockSpec(memory_space=pl.ANY)] * len(operands),
        ],
        out_specs=(
            pl.BlockSpec(memory_space=pl.ANY),
            pl.BlockSpec(memory_space=pltpu.VMEM),
            pl.BlockSpec(memory_space=pltpu.VMEM),
        ),
        scratch_shapes=[
            *product_scratch(group, own=False),
            pltpu.VMEM((2, tile, width), BF16),
            pltpu.VMEM((2, tile, width), BF16),
            pltpu.VMEM(dgu.shape, BF16),
            pltpu.VMEM(act.shape, BF16),
            pltpu.VMEM((width, cols), F32),
            pltpu.SemaphoreType.DMA((2, 2)),
            pltpu.SemaphoreType.DMA((2,)),
            *GATHER_SEMAPHORES,
        ],
        compiler_params=pltpu.CompilerParams(
            collective_id=6, has_side_effects=True, vmem_limit_bytes=VMEM_BYTES
        ),
        cost_estimate=micros(44),
        name="gather_beside",
    )(shard, *operands)
    return gathered.reshape(8 * rows, width), sums, grad


def line_scatter_steps(grad_ref, own, from_edge, from_middle, inward, load_sem, send, recv, part, which):
    z = lax.axis_index("z")
    rows, half = own.shape[1], own.shape[1] // 2
    pair, middle = z + 1 - 2 * lax.rem(z, 2), 3 - z
    inner = (z == 1) | (z == 2)
    edge = jnp.logical_not(inner)
    far = middle + 1 - 2 * lax.rem(middle, 2)
    first = pl.multiple_of(which * half, half)
    span = pl.ds(first, half)

    def block(index):
        return grad_ref.at[pl.ds(pl.multiple_of(index * rows + first, half), half)]

    def remote(index, source, target, peer):
        return pltpu.make_async_remote_copy(
            src_ref=source,
            dst_ref=target,
            send_sem=send.at[6 * part + index],
            recv_sem=recv.at[6 * part + index],
            device_id={"z": peer},
            device_id_type=MESH,
        )

    indices = (far, middle, pair, z)
    loads = [
        pltpu.make_async_copy(block(index), own.at[i, span], load_sem.at[4 * part + i])
        for i, index in enumerate(indices)
    ]
    edge_far = remote(0, own.at[1, span], from_edge.at[0, span], pair)
    edge_near = remote(1, own.at[0, span], from_edge.at[1, span], pair)
    edge_pair = remote(2, own.at[2, span], from_edge.at[2, span], pair)
    inner_far = remote(3, own.at[0, span], from_middle.at[0, span], middle)
    inner_near = remote(4, own.at[1, span], from_middle.at[1, span], middle)
    outward = remote(5, own.at[2, span], inward.at[span], pair)
    step = 128

    def add_into(target, other):
        @pl.loop(0, half // step)
        def _(i):
            at = pl.ds(first + i * step, step)
            target[at] = (target[at].astype(F32) + other[at].astype(F32)).astype(target.dtype)

    def load():
        for copy in loads:
            copy.start()

    def begin():
        for copy in loads:
            copy.wait()

        @pl.when(edge)
        def _():
            for copy in (edge_far, edge_near, edge_pair):
                copy.start()

    def second():
        @pl.when(inner)
        def _():
            edge_far.wait_recv()
            add_into(own.at[0], from_edge.at[0])
            inner_far.start()

    def third():
        @pl.when(inner)
        def _():
            edge_near.wait_recv()
            add_into(own.at[1], from_edge.at[1])
            inner_near.start()
            inner_far.wait_recv()
            add_into(own.at[2], from_middle.at[0])
            outward.start()

    def finish():
        @pl.when(inner)
        def _():
            edge_pair.wait_recv()
            add_into(own.at[3], from_edge.at[2])
            inner_near.wait_recv()
            add_into(own.at[3], from_middle.at[1])
            for copy in (inner_far, inner_near, outward):
                copy.wait_send()

        @pl.when(edge)
        def _():
            outward.wait_recv()
            add_into(own.at[3], inward)
            for copy in (edge_far, edge_near, edge_pair):
                copy.wait_send()

    return load, begin, second, third, finish


def total_steps(near, far, near_send, near_recv, far_send, far_recv):
    z, y, x, c = (lax.axis_index(name) for name in "zyxc")
    here = (y * 2 + x) * 2 + c
    others = [
        {"y": lax.rem(y + i // 4, 2), "x": lax.rem(x + i // 2 % 2, 2), "c": lax.rem(c + i % 2, 2)}
        for i in range(1, 8)
    ]
    levels = [{"z": lax.rem(z + i, 4)} for i in range(1, 4)]

    def remote(index, source, target, send, recv, device):
        return pltpu.make_async_remote_copy(
            src_ref=source,
            dst_ref=target,
            send_sem=send.at[index],
            recv_sem=recv.at[index],
            device_id=device,
            device_id_type=MESH,
        )

    around = [
        remote(i, near.at[here], near.at[here], near_send, near_recv, other)
        for i, other in enumerate(others)
    ]
    along = [
        remote(i, far.at[z], far.at[z], far_send, far_recv, level) for i, level in enumerate(levels)
    ]

    def begin():
        for copy in around:
            copy.start()

    def second():
        for copy in around:
            copy.wait()
        total = near[0]
        for i in range(1, 8):
            total = total + near[i]
        far[z] = total
        for copy in along:
            copy.start()

    def finish():
        for copy in along:
            copy.wait()
        total = far[0]
        for i in range(1, 4):
            total = total + far[i]
        return total

    return begin, second, finish, here, others, levels


def tail_kernel(windows, *refs):
    count = len(windows)
    lefts, rights, refs = refs[:count], refs[count : 2 * count], refs[2 * count :]
    grad_ref, tokens_ref, inverse_ref, dhidden_ref, gain_ref, *refs = refs
    gains, (out_ref, mine_ref, theirs_ref, total_ref), scratch = refs[:3], refs[3:7], refs[7:]
    size = 2 * count + 12
    load, first, second, finish = scatter_steps(windows, lefts, rights, scratch[:size])
    line, (swap_sem,), total = scratch[size : size + 7], scratch[size + 7 : size + 8], scratch[size + 8 :]
    near, far = total[:2]
    total_begin, total_second, total_finish, here, others, levels = total_steps(*total)
    y = lax.axis_index("y")
    lines = [line_scatter_steps(grad_ref, *line, part, which) for part, which in ((0, 1 - y), (1, y))]
    load()
    for steps in lines:
        steps[0]()
    width = out_ref.shape[1]
    near[here, :, pl.ds(width, width)] = gains[0][...]
    head = gains[1].shape[1]
    near[here, :, pl.ds(2 * width, head)] = gains[1][...]
    near[here, :, pl.ds(2 * width + head, head)] = gains[2][...]
    greet(others + levels)
    for steps in lines:
        steps[1]()
    first()
    lines[0][2]()
    second()
    lines[0][3]()
    lines[1][2]()
    gain_in = near.at[here, :, pl.ds(0, width)]
    gain_in[...] = jnp.zeros((1, width), F32)

    def store(at, grad):
        x, inv = tokens_ref[at].astype(F32), inverse_ref[at]
        gain_in[...] += jnp.sum(grad * x * inv, 0, keepdims=True)
        back = norm_back(grad, x, inv, gain_ref[...].astype(F32))
        out_ref[at] = (dhidden_ref[at] + back).astype(BF16)

    finish(store)
    total_begin()
    lines[1][3]()
    lines[0][4]()
    summed = line[0].at[3]
    half = theirs_ref.shape[0]
    swap = pltpu.make_async_remote_copy(
        src_ref=summed.at[pl.ds(pl.multiple_of((1 - y) * half, half), half)],
        dst_ref=theirs_ref,
        send_sem=swap_sem.at[0],
        recv_sem=swap_sem.at[1],
        device_id={"y": 1 - y},
        device_id_type=MESH,
    )
    swap.start()
    total_second()
    lines[1][4]()
    mine_ref[...] = summed[pl.ds(pl.multiple_of(y * half, half), half)]
    total_ref[...] = total_finish()
    swap.wait()


def tail(group, grad, tokens, inverse, dhidden, gain, gains):
    operands, scratch, total = scatter_scratch(group)
    rows, cols = grad.shape[0] // 4, grad.shape[1]
    length = 2 * total.shape[1] + 2 * gains[1].size
    half = jax.ShapeDtypeStruct((rows // 2, cols), BF16)
    whole = pl.BlockSpec(memory_space=pltpu.VMEM)
    block = lambda count: pltpu.VMEM((count, rows, cols), BF16)
    dma = pltpu.SemaphoreType.DMA
    return pl.pallas_call(
        functools.partial(tail_kernel, [item[2] for item in group]),
        out_shape=(
            jax.ShapeDtypeStruct(total.shape, BF16),
            half,
            half,
            jax.ShapeDtypeStruct((1, length), F32),
        ),
        in_specs=[pl.BlockSpec(memory_space=pl.ANY)] * (len(operands) + 1) + [whole] * 7,
        out_specs=(whole,) * 4,
        scratch_shapes=[
            *scratch,
            block(4), block(3), block(2), pltpu.VMEM((rows, cols), BF16), dma((8,)), dma((12,)), dma((12,)),
            dma((2,)),
            pltpu.VMEM((8, 1, length), F32), pltpu.VMEM((4, 1, length), F32), dma((7,)), dma((7,)), dma((3,)), dma((3,)),
        ],
        compiler_params=pltpu.CompilerParams(
            collective_id=0, has_side_effects=True, vmem_limit_bytes=VMEM_BYTES
        ),
        cost_estimate=micros(52),
        name="tail",
    )(*operands, grad, tokens, inverse, dhidden, gain.reshape(1, -1), *(gain.reshape(1, -1) for gain in gains))


def swap_y(value):
    return lax.ppermute(value, "y", [(0, 1), (1, 0)])


def in_y_order(mine, theirs, axis):
    count = mine.shape[axis]
    return lax.dynamic_slice_in_dim(
        jnp.concatenate([mine, theirs, mine], axis), lax.axis_index("y") * count, 2 * count, axis
    )


def gather_rows(rows):
    return lax.all_gather(rows, "z", axis=0, tiled=True)


def scatter_grads(grad):
    return lax.psum_scatter(grad.astype(BF16), "z", scatter_dimension=0, tiled=True)


def their_rows(part):
    half = part.shape[0] // 2
    return swap_y(
        lax.dynamic_slice_in_dim(part, (1 - lax.axis_index("y")) * half, half, 0)
    )


def join_pieces(plan, y, mine_of, theirs_of, outs):
    for source, first, width, out, at, turned in plan:
        half = outs[out].shape[0 if turned else 1] // 2
        cols = pl.ds(first, width)
        for which, piece in ((y, mine_of(source, cols)), (1 - y, theirs_of(source, cols))):
            target = pl.ds(pl.multiple_of(which * half + at, 128), width)
            if turned:
                outs[out][target, :] = piece.astype(F32).T
            else:
                outs[out][:, target] = piece.astype(F32)


def join_kernel(plan, count, y_rows, *refs):
    y = lax.axis_index("y")
    parts, theirs, outs = refs[:count], refs[count : 2 * count], refs[2 * count :]
    mine = pl.ds(pl.multiple_of(y * y_rows, y_rows), y_rows)
    own = lambda source, cols: parts[source][mine, cols]
    got = lambda source, cols: theirs[source][:, cols]
    join_pieces(plan, y, own, got, outs)


def join_grads(parts, theirs, plan, shapes):
    whole = pl.BlockSpec(memory_space=pltpu.VMEM)
    return pl.pallas_call(
        functools.partial(join_kernel, plan, len(parts), theirs[0].shape[0]),
        out_shape=tuple(jax.ShapeDtypeStruct(shape, F32) for shape in shapes),
        in_specs=[whole] * (2 * len(parts)),
        out_specs=(whole,) * len(shapes),
        compiler_params=pltpu.CompilerParams(vmem_limit_bytes=VMEM_BYTES),
        cost_estimate=micros(5),
        name="join_grads",
    )(*parts, *theirs)


def last_join_kernel(plan, mine, theirs, total, *outs):
    gains, grads, start = outs[:4], outs[4:], 0
    for gain in gains:
        gain[...] = total[:, pl.ds(start, gain.shape[1])]
        start += gain.shape[1]
    y = lax.axis_index("y")
    join_pieces(plan, y, lambda _, cols: mine[:, cols], lambda _, cols: theirs[:, cols], grads)


def join_last(mine, theirs, total, plan, sizes, shapes):
    whole = pl.BlockSpec(memory_space=pltpu.VMEM)
    outs = (*((1, size) for size in sizes), *shapes)
    return pl.pallas_call(
        functools.partial(last_join_kernel, plan),
        out_shape=tuple(jax.ShapeDtypeStruct(shape, F32) for shape in outs),
        in_specs=[whole] * 3,
        out_specs=(whole,) * len(outs),
        cost_estimate=micros(4),
        name="join_last",
    )(mine, theirs, total)


def normed_rope(raw, gain, cosine, sine):
    inverse = lax.rsqrt(jnp.mean(raw * raw, -1, keepdims=True) + EPSILON)
    scaled = raw * inverse * gain
    turned = pltpu.roll(scaled, scaled.shape[-1] // 2, 1)
    return (scaled * cosine + turned * sine).astype(BF16)


def normed_rope_back(grad, raw, gain, cosine, sine):
    inverse = lax.rsqrt(jnp.mean(raw * raw, -1, keepdims=True) + EPSILON)
    straight = grad * cosine - pltpu.roll(grad, grad.shape[-1] // 2, 1) * sine
    gain_part = jnp.sum(straight * (raw * inverse), 0, keepdims=True)
    return norm_back(straight, raw, inverse, gain).astype(BF16), gain_part


def causal_scores(query, keys, first, scaling):
    scores = dot_nt(query, keys) * scaling
    rows = lax.broadcasted_iota(jnp.int32, scores.shape, 0) + first
    columns = lax.broadcasted_iota(jnp.int32, scores.shape, 1)
    return jnp.where(rows >= columns, scores, -1e30)


def attend_kernel(
    heads, head, block, normed_ref, w_ref, wg_ref, low_ref, qg_ref, kg_ref, cos_ref, sin_ref,
    raw_ref, out_ref, log_ref, gate_ref, mixed_ref, all_ref, key_ref, value_ref, *sems,
):
    seq, step, steps = pl.program_id(0), pl.program_id(1), pl.num_programs(1)
    tick = seq * steps + step
    scaling = head**-0.5
    at = heads * head
    begin, forward, across, finish = gather_steps(low_ref, all_ref, *sems)

    @pl.when(tick == 0)
    def _():
        greet(tuple(place()[3].values()))
        begin()

    pl.when(tick == 3)(forward)
    pl.when(tick == 6)(across)
    raw_ref[...] = dot_nn(normed_ref[...], w_ref[...])
    here = pl.ds(pl.multiple_of(step * block, block), block)
    cosine, sine = cos_ref[here], sin_ref[here]

    @pl.when(tick == 0)
    def _():
        key_ref[...] = jnp.zeros_like(key_ref)
        value_ref[...] = jnp.zeros_like(value_ref)

    key_ref[here] = normed_rope(raw_ref[:, at : at + head], kg_ref[...], cosine, sine)
    value_ref[here] = raw_ref[:, at + head :].astype(BF16)

    for i in range(0, key_ref.shape[0] // block, 2):

        @pl.when(step // 2 == i // 2)
        def _():
            seen = pl.ds(0, (i + 2) * block)

            @pl.loop(0, heads)
            def _(h):
                cols = pl.ds(pl.multiple_of(h * head, head), head)
                query = normed_rope(raw_ref[:, cols], qg_ref[...], cosine, sine)
                scores = causal_scores(query, key_ref[seen], step * block, scaling)
                highest = jnp.max(scores, -1, keepdims=True)
                exp_vals = jnp.exp(scores - highest)
                total = jnp.sum(exp_vals, -1, keepdims=True)
                probs = (exp_vals / total).astype(BF16)
                out_ref[:, cols] = dot_nn(probs, value_ref[seen])
                log_ref[h] = highest + jnp.log(total)

    gate = jax.nn.sigmoid(dot_nn(normed_ref[...], wg_ref[...]))
    gate_ref[...] = gate
    mixed_ref[...] = (out_ref[...] * gate).astype(BF16)
    pl.when(tick == pl.num_programs(0) * steps - 1)(finish)


def attend(normed, weights, gates, low, query_gain, key_gain, cosine, sine, heads, head, length, block=256):
    rows, width = normed.shape
    cols = weights.shape[1]
    seqs, steps = rows // length, length // block
    whole = lambda shape: pl.BlockSpec(
        shape, lambda s, i: (0,) * len(shape), pipeline_mode=pl.Buffered(1)
    )
    part = lambda cols: pl.BlockSpec((block, cols), lambda s, i: (s * steps + i, 0))
    *outs, gathered = pl.pallas_call(
        functools.partial(attend_kernel, heads, head, block),
        out_shape=(
            jax.ShapeDtypeStruct((rows, cols), F32),
            jax.ShapeDtypeStruct((rows, heads * head), F32),
            jax.ShapeDtypeStruct((heads, rows, 1), F32),
            jax.ShapeDtypeStruct((rows, heads * head), F32),
            jax.ShapeDtypeStruct((rows, heads * head), BF16),
            jax.ShapeDtypeStruct((2, 2, 2, *low.shape), low.dtype),
        ),
        grid=(seqs, steps),
        in_specs=[
            part(width),
            whole((width, cols)),
            whole((width, heads * head)),
            pl.BlockSpec(memory_space=pl.ANY),
            whole((1, head)),
            whole((1, head)),
            whole((length, head)),
            whole((length, head)),
        ],
        out_specs=(
            part(cols),
            part(heads * head),
            pl.BlockSpec((heads, block, 1), lambda s, i: (0, s * steps + i, 0)),
            part(heads * head),
            part(heads * head),
            pl.BlockSpec(memory_space=pl.ANY),
        ),
        scratch_shapes=[
            pltpu.VMEM((length, head), BF16),
            pltpu.VMEM((length, head), BF16),
            *GATHER_SEMAPHORES,
        ],
        compiler_params=pltpu.CompilerParams(collective_id=3, has_side_effects=True),
        cost_estimate=micros(42),
        name="attend",
    )(normed, weights, gates, low, query_gain, key_gain, cosine, sine)
    return *outs, gathered.reshape(rows, width)


def add_products(step, total_ref, start, left_ref, right_ref, tile=1024):
    wide = min(512, right_ref.shape[1])

    @pl.loop(0, left_ref.shape[1] // tile)
    def _(m):
        at = pl.ds(pl.multiple_of(m * tile, tile), tile)

        @pl.loop(0, right_ref.shape[1] // wide)
        def _(n):
            cols = pl.ds(pl.multiple_of(start + n * wide, wide), wide)
            part = dot_tn(left_ref[:, at], right_ref[:, pl.ds(pl.multiple_of(n * wide, wide), wide)])

            @pl.when(step == 0)
            def _():
                total_ref[at, cols] = part

            @pl.when(step > 0)
            def _():
                total_ref[at, cols] += part


def store_low(step, total_ref, out_ref, tile=256):
    @pl.when(step == pl.num_programs(0) - 1)
    def _():
        @pl.loop(0, total_ref.shape[0] // tile)
        def _(m):
            at = pl.ds(m * tile, tile)
            out_ref[at] = total_ref[at].astype(BF16)


def grads_kernel(left_ref, right_ref, out_ref, total_ref):
    step = pl.program_id(0)
    add_products(step, total_ref, 0, left_ref, right_ref)
    store_low(step, total_ref, out_ref)


def weight_grads(left, right, block=1024):
    (rows, width), cols = left.shape, right.shape[1]
    part = lambda cols: pl.BlockSpec((block, cols), lambda i: (i, 0))
    return pl.pallas_call(
        grads_kernel,
        out_shape=jax.ShapeDtypeStruct((width, cols), BF16),
        grid=(rows // block,),
        in_specs=[part(width), part(cols)],
        out_specs=pl.BlockSpec((width, cols), lambda i: (0, 0)),
        scratch_shapes=[pltpu.VMEM((width, cols), F32)],
        cost_estimate=micros(11),
        name="weight_grads",
    )(left, right)


def gate_back_kernel(
    normed_ref, branch_ref, w_ref, attended_ref, gate_ref, mixed_ref,
    dattended_ref, dgating_ref, grad_ref, total_ref,
):
    step = pl.program_id(0)
    dmixed = dot_nn(branch_ref[...], w_ref[...])
    gate = gate_ref[...]
    dattended_ref[...] = (dmixed * gate).astype(BF16)
    dgating_ref[...] = (dmixed * attended_ref[...] * gate * (1.0 - gate)).astype(BF16)
    add_products(step, total_ref, 0, normed_ref, dgating_ref)
    add_products(step, total_ref, dgating_ref.shape[1], branch_ref, mixed_ref)
    store_low(step, total_ref, grad_ref)


def gate_back(normed, branch, weights, attended, gate, mixed, block=1024):
    rows, width = normed.shape
    cols = attended.shape[1]
    part = lambda cols: pl.BlockSpec((block, cols), lambda i: (i, 0))
    return pl.pallas_call(
        gate_back_kernel,
        out_shape=(
            jax.ShapeDtypeStruct((rows, cols), BF16),
            jax.ShapeDtypeStruct((rows, cols), BF16),
            jax.ShapeDtypeStruct((width, 2 * cols), BF16),
        ),
        grid=(rows // block,),
        in_specs=[
            part(width),
            part(width),
            pl.BlockSpec((width, cols), lambda i: (0, 1)),
            part(cols),
            part(cols),
            part(cols),
        ],
        out_specs=(part(cols), part(cols), pl.BlockSpec((width, 2 * cols), lambda i: (0, 0))),
        scratch_shapes=[pltpu.VMEM((width, 2 * cols), F32)],
        compiler_params=pltpu.CompilerParams(vmem_limit_bytes=VMEM_BYTES),
        cost_estimate=micros(25),
        name="gate_back",
    )(normed, branch, weights, attended, gate, mixed)


def feed_units(count, tile, mid_ref, low_ref, gu_ref, down_ref, first, act_ref, dgu_ref):
    @pl.loop(0, count // tile)
    def _(j):
        start = pl.multiple_of(j * tile, tile)
        at, after = pl.ds(start, tile), pl.ds(pl.multiple_of(count + start, tile), tile)
        last = pl.ds(pl.multiple_of(first + start, tile), tile)
        gate = dot_nn(mid_ref[...], gu_ref[:, at])
        up = dot_nn(mid_ref[...], gu_ref[:, after])
        dact = dot_nn(low_ref[...], down_ref[:, last])
        sigma = jax.nn.sigmoid(gate)
        silu = gate * sigma
        act_ref[:, at] = (silu * up).astype(BF16)
        dgu_ref[:, at] = (dact * up * sigma * (1.0 + gate * (1.0 - sigma))).astype(BF16)
        dgu_ref[:, after] = (dact * silu).astype(BF16)


def feed_kernel(count, tile, mid_ref, low_ref, gu_ref, down_ref, act_ref, dgu_ref):
    feed_units(count, tile, mid_ref, low_ref, gu_ref, down_ref, 0, act_ref, dgu_ref)


def feed_grads_kernel(
    count, tile, mid_ref, low_ref, w_ref, act_ref, dgu_ref, grad_ref, total_ref
):
    step = pl.program_id(0)
    feed_units(count, tile, mid_ref, low_ref, w_ref, w_ref, 2 * count, act_ref, dgu_ref)
    add_products(step, total_ref, 0, mid_ref, dgu_ref)
    add_products(step, total_ref, 2 * count, low_ref, act_ref)
    store_low(step, total_ref, grad_ref)


def feed_forward(mid, low, weights, down, block=512):
    rows, width = mid.shape
    count = down.shape[1]
    part = lambda cols: pl.BlockSpec((block, cols), lambda i: (i, 0))
    whole = lambda array: pl.BlockSpec(array.shape, lambda i: (0, 0), pipeline_mode=pl.Buffered(1))
    return pl.pallas_call(
        functools.partial(feed_kernel, count, 256),
        out_shape=(
            jax.ShapeDtypeStruct((rows, count), BF16),
            jax.ShapeDtypeStruct((rows, 2 * count), BF16),
        ),
        grid=(rows // block,),
        in_specs=[part(width), part(width), whole(weights), whole(down)],
        out_specs=(part(count), part(2 * count)),
        compiler_params=pltpu.CompilerParams(vmem_limit_bytes=VMEM_BYTES),
        cost_estimate=micros(14),
        name="feed_forward",
    )(mid, low, weights, down)


def feed_forward_grads(mid, low, weights, block=1024):
    rows, width = mid.shape
    count = weights.shape[1] // 3
    part = lambda cols: pl.BlockSpec((block, cols), lambda i: (i, 0))
    whole = pl.BlockSpec(weights.shape, lambda i: (0, 0), pipeline_mode=pl.Buffered(1))
    return pl.pallas_call(
        functools.partial(feed_grads_kernel, count, 256),
        out_shape=(
            jax.ShapeDtypeStruct((rows, count), BF16),
            jax.ShapeDtypeStruct((rows, 2 * count), BF16),
            jax.ShapeDtypeStruct(weights.shape, BF16),
        ),
        grid=(rows // block,),
        in_specs=[part(width), part(width), whole],
        out_specs=(part(count), part(2 * count), whole),
        scratch_shapes=[pltpu.VMEM(weights.shape, F32)],
        compiler_params=pltpu.CompilerParams(vmem_limit_bytes=VMEM_BYTES),
        cost_estimate=micros(41),
        name="feed_forward_grads",
    )(mid, low, weights)


def attend_back_kernel(
    heads, head, block, raw_ref, up_ref, log_ref, qg_ref, kg_ref, cos_ref, sin_ref, sums_ref,
    out_ref, qg_out, kg_out, sum_ref, key_ref, value_ref, dkey_ref, dvalue_ref, own, load_sem, *scratch,
):
    seq, step, steps = pl.program_id(0), pl.program_id(1), pl.num_programs(1)
    tick = seq * steps + step
    scaling = head**-0.5
    at = heads * head
    blocks = raw_ref.shape[0] // block
    diag_x, diag_y, x_low, y_high, second, finish = axis_steps(own, *scratch)

    @pl.when(tick == 0)
    def _():
        load = pltpu.make_async_copy(sums_ref, own, load_sem)
        load.start()
        device = place()[3]
        greet((device["y"], device["x"]))
        load.wait()
        for copy in (diag_x, diag_y, x_low, y_high):
            copy.start()
        qg_out[...] = jnp.zeros_like(qg_out)
        kg_out[...] = jnp.zeros_like(kg_out)

    pl.when(tick == 4)(second)

    @pl.when(step == 0)
    def _():
        key_ref[...] = normed_rope(
            raw_ref[:, at : at + head], kg_ref[...], cos_ref[...], sin_ref[...]
        )
        value_ref[...] = raw_ref[:, at + head :].astype(BF16)
        dkey_ref[...] = jnp.zeros_like(dkey_ref)
        dvalue_ref[...] = jnp.zeros_like(dvalue_ref)

    rows = pl.ds(pl.multiple_of(step * block, block), block)

    for i in range(0, blocks, 2):

        @pl.when(step // 2 == i // 2)
        def _():
            seen = pl.ds(0, (i + 2) * block)

            @pl.loop(0, heads)
            def _(h):
                cols = pl.ds(pl.multiple_of(h * head, head), head)
                raw = raw_ref[rows, cols]
                query = normed_rope(raw, qg_ref[...], cos_ref[rows], sin_ref[rows])
                scores = causal_scores(query, key_ref[seen], step * block, scaling)
                probs = jnp.exp(scores - log_ref[h])
                upstream = up_ref[:, cols]
                dprobs = dot_nt(upstream, value_ref[seen])
                centre = jnp.sum(dprobs * probs, -1, keepdims=True)
                dscores = (probs * (dprobs - centre)).astype(BF16)
                dkey_ref[seen] += dot_tn(dscores, query)
                dvalue_ref[seen] += dot_tn(probs.astype(BF16), upstream)
                dquery = dot_nn(dscores, key_ref[seen]) * scaling
                grad, part = normed_rope_back(
                    dquery, raw, qg_ref[...], cos_ref[rows], sin_ref[rows]
                )
                out_ref[rows, cols] = grad
                qg_out[...] += part

    @pl.when(step == blocks - 1)
    def _():
        grad, part = normed_rope_back(
            dkey_ref[...] * scaling,
            raw_ref[:, at : at + head],
            kg_ref[...],
            cos_ref[...],
            sin_ref[...],
        )
        out_ref[:, at : at + head] = grad
        out_ref[:, at + head :] = dvalue_ref[...].astype(BF16)
        kg_out[...] += part

    @pl.when(tick == pl.num_programs(0) * steps - 1)
    def _():
        def store(rows, value):
            sum_ref[rows] = value

        finish(store)


def attend_back(
    raw, upstream, logs, query_gain, key_gain, cosine, sine, sums, heads, head, length, block=256
):
    rows = raw.shape[0]
    total = jax.ShapeDtypeStruct(sums.shape[1:], F32)
    seqs, steps = rows // length, length // block
    whole = lambda shape: pl.BlockSpec(shape, lambda s, i: (0,) * len(shape))
    return pl.pallas_call(
        functools.partial(attend_back_kernel, heads, head, block),
        out_shape=(
            jax.ShapeDtypeStruct(raw.shape, BF16),
            jax.ShapeDtypeStruct((1, head), F32),
            jax.ShapeDtypeStruct((1, head), F32),
            total,
        ),
        grid=(seqs, steps),
        in_specs=[
            pl.BlockSpec((length, raw.shape[1]), lambda s, i: (s, 0)),
            pl.BlockSpec((block, heads * head), lambda s, i: (s * steps + i, 0)),
            pl.BlockSpec((heads, block, 1), lambda s, i: (0, s * steps + i, 0)),
            whole((1, head)),
            whole((1, head)),
            whole((length, head)),
            whole((length, head)),
            pl.BlockSpec(memory_space=pl.ANY),
        ],
        out_specs=(
            pl.BlockSpec((length, raw.shape[1]), lambda s, i: (s, 0)),
            whole((1, head)),
            whole((1, head)),
            whole(total.shape),
        ),
        scratch_shapes=[
            pltpu.VMEM((length, head), BF16),
            pltpu.VMEM((length, head), BF16),
            pltpu.VMEM((length, head), F32),
            pltpu.VMEM((length, head), F32),
            pltpu.VMEM(sums.shape, BF16),
            pltpu.SemaphoreType.DMA,
            *axis_scratch(*sums.shape[1:]),
        ],
        compiler_params=pltpu.CompilerParams(
            collective_id=5, has_side_effects=True, vmem_limit_bytes=VMEM_BYTES
        ),
        cost_estimate=micros(40),
        name="attend_back",
    )(raw, upstream, logs, query_gain, key_gain, cosine, sine, sums)


def attention_weights(query_proj, key_proj, value_proj, gating_proj, output_proj):
    return (
        lax.all_gather(query_proj, "dp", axis=0, tiled=True),
        lax.all_gather(key_proj, "dp", axis=0, tiled=True),
        lax.all_gather(value_proj, "dp", axis=0, tiled=True),
        lax.all_gather(gating_proj, "dp", axis=0, tiled=True),
        lax.all_gather(output_proj, "dp", axis=1, tiled=True),
    )


def swiglu_weights(swiglu_gate, swiglu_up, swiglu_down):
    return (
        lax.all_gather(swiglu_gate, "dp", axis=0, tiled=True),
        lax.all_gather(swiglu_up, "dp", axis=0, tiled=True),
        lax.all_gather(swiglu_down, "dp", axis=1, tiled=True),
    )


def softmax_forward_mapped(seq_items, causal):
    queries, keys_seq, values_seq = seq_items
    scaling = queries.shape[-1] ** (-0.5)
    scores = (
        jnp.einsum("qgjd,kgd->gjqk", queries, keys_seq, preferred_element_type=jnp.float32)
        * scaling
    )
    scores = jnp.where(causal, scores, -1e30)
    highest = jnp.max(scores, -1, keepdims=True)
    exp_vals = jnp.exp(scores - highest)
    row_totals = jnp.sum(exp_vals, -1, keepdims=True)
    attn_probs = (exp_vals / row_totals).astype(jnp.bfloat16)
    attended = jnp.einsum(
        "gjqk,kgd->qgjd", attn_probs, values_seq, preferred_element_type=jnp.float32
    )
    return (attended, highest[..., 0] + jnp.log(row_totals[..., 0]))


def softmax_backward_mapped(seq_items, causal):
    queries, keys_seq, values_seq, log_total, upstream = seq_items
    scaling = queries.shape[-1] ** (-0.5)
    scores = (
        jnp.einsum("qgjd,kgd->gjqk", queries, keys_seq, preferred_element_type=jnp.float32)
        * scaling
    )
    scores = jnp.where(causal, scores, -1e30)
    attn_probs = jnp.exp(scores - log_total[..., None])
    dprobs = jnp.einsum("qgjd,kgd->gjqk", upstream, values_seq, preferred_element_type=jnp.float32)
    centre = jnp.sum(dprobs * attn_probs, -1, keepdims=True)
    dscores = (attn_probs * (dprobs - centre)).astype(jnp.bfloat16)
    dqueries = (
        jnp.einsum("gjqk,kgd->qgjd", dscores, keys_seq, preferred_element_type=jnp.float32)
        * scaling
    )
    key_grads = (
        jnp.einsum("gjqk,qgjd->kgd", dscores, queries, preferred_element_type=jnp.float32) * scaling
    )
    value_grads = jnp.einsum(
        "gjqk,qgjd->kgd",
        attn_probs.astype(jnp.bfloat16),
        upstream,
        preferred_element_type=jnp.float32,
    )
    key_rows = key_grads.shape[0]
    return (dqueries, key_grads.reshape(key_rows, -1), value_grads.reshape(key_rows, -1))


def per_device_wide(
    tokens,
    cotangent,
    domain_ids,
    domain_counts,
    domain_numer,
    domain_denom,
    attention_gain,
    query_gain,
    key_gain,
    query_proj,
    key_proj,
    value_proj,
    gating_proj,
    output_proj,
    swiglu_gain,
    swiglu_gate,
    swiglu_up,
    swiglu_down,
):
    seq_count, local_len, model_width = tokens.shape
    full_len = local_len * lax.axis_size("ctx")
    local_rows = seq_count * local_len
    all_rows = seq_count * full_len
    head_dim = query_gain.shape[0]
    local_heads = query_proj.shape[1] // head_dim
    local_kv = key_proj.shape[1] // head_dim
    group_size = local_heads // local_kv
    positions = jnp.arange(full_len, dtype=jnp.int32)
    causal = positions[:, None] >= positions[None, :]
    cosine, sine = rope_tables(positions, head_dim)
    cos_rows = cosine[:, None, :]
    sin_rows = sine[:, None, :]
    inputs = tokens.reshape(local_rows, model_width).astype(jnp.float32)
    inverse_in = lax.rsqrt(jnp.mean(inputs * inputs, -1, keepdims=True) + EPSILON)
    gain_in = attention_gain.astype(jnp.float32)
    normed = (inputs * inverse_in * gain_in).astype(jnp.bfloat16)
    normed_all = lax.all_gather(
        normed.reshape(seq_count, local_len, model_width), "ctx", axis=1, tiled=True
    ).reshape(all_rows, model_width)
    attn_full = attention_weights(query_proj, key_proj, value_proj, gating_proj, output_proj)
    query_raw = dot_nn(normed_all, attn_full[0]).reshape(
        seq_count, full_len, local_heads, head_dim
    )
    key_raw = dot_nn(normed_all, attn_full[1]).reshape(seq_count, full_len, local_kv, head_dim)
    value_low = (
        dot_nn(normed_all, attn_full[2])
        .astype(jnp.bfloat16)
        .reshape(seq_count, full_len, local_kv, head_dim)
    )
    gate_pre = dot_nn(normed_all, attn_full[3])
    query_scale = query_gain.astype(jnp.float32)
    key_scale = key_gain.astype(jnp.float32)
    query_inv = lax.rsqrt(jnp.mean(query_raw * query_raw, -1, keepdims=True) + EPSILON)
    key_inv = lax.rsqrt(jnp.mean(key_raw * key_raw, -1, keepdims=True) + EPSILON)
    query_low = rotate(query_raw * query_inv * query_scale, cos_rows, sin_rows).astype(jnp.bfloat16)
    key_low = rotate(key_raw * key_inv * key_scale, cos_rows, sin_rows).astype(jnp.bfloat16)
    query_groups = query_low.reshape(seq_count, full_len, local_kv, group_size, head_dim)
    attended, log_total = lax.map(
        lambda seq_items: softmax_forward_mapped(seq_items, causal), (query_groups, key_low, value_low)
    )
    attended = attended.reshape(all_rows, local_heads * head_dim)
    gate_sig = jax.nn.sigmoid(gate_pre)
    mixed = (attended * gate_sig).astype(jnp.bfloat16)
    branch_part = dot_nn(mixed, attn_full[4]).reshape(seq_count, full_len, model_width)
    branch = lax.psum_scatter(branch_part, "ctx", scatter_dimension=1, tiled=True).reshape(
        local_rows, model_width
    )
    hidden = inputs + branch
    inverse_mid = lax.rsqrt(jnp.mean(hidden * hidden, -1, keepdims=True) + EPSILON)
    gain_mid = swiglu_gain.astype(jnp.float32)
    normed_mid = (hidden * inverse_mid * gain_mid).astype(jnp.bfloat16)
    normed_mid_all = lax.all_gather(
        normed_mid.reshape(seq_count, local_len, model_width), "ctx", axis=1, tiled=True
    ).reshape(all_rows, model_width)
    swiglu_full = swiglu_weights(swiglu_gate, swiglu_up, swiglu_down)
    gate_ff = dot_nn(normed_mid_all, swiglu_full[0])
    up_val = dot_nn(normed_mid_all, swiglu_full[1])
    gate_sigma = jax.nn.sigmoid(gate_ff)
    silu_val = gate_ff * gate_sigma
    activation = (silu_val * up_val).astype(jnp.bfloat16)
    down_part = dot_nn(activation, swiglu_full[2]).reshape(seq_count, full_len, model_width)
    ffn_branch = (
        lax.psum_scatter(down_part.astype(jnp.bfloat16), "ctx", scatter_dimension=1, tiled=True)
        .astype(jnp.float32)
        .reshape(local_rows, model_width)
    )
    layer_out = (hidden + ffn_branch).astype(jnp.bfloat16)
    domain_table = (
        domain_ids[:, None] == jnp.arange(domain_counts.shape[0], dtype=jnp.int32)[None, :]
    ).astype(jnp.float32)
    ratio = (
        domain_numer.astype(jnp.float32)
        / domain_denom.astype(jnp.float32)
        * LENGTH
        / domain_counts.astype(jnp.float32)
    )
    factor = jnp.sum(domain_table * ratio[None, :], 1)
    upstream = (cotangent.astype(jnp.float32) * factor[:, None, None]).reshape(
        local_rows, model_width
    )
    swiglu_back = swiglu_weights(swiglu_gate, swiglu_up, swiglu_down)
    out_low = upstream.astype(jnp.bfloat16)
    out_all = lax.all_gather(
        out_low.reshape(seq_count, local_len, model_width), "ctx", axis=1, tiled=True
    ).reshape(all_rows, model_width)
    dactivation = dot_nt(out_all, swiglu_back[2])
    dgate_low = (dactivation * up_val * gate_sigma * (1.0 + gate_ff * (1.0 - gate_sigma))).astype(
        jnp.bfloat16
    )
    dup_low = (dactivation * silu_val).astype(jnp.bfloat16)
    grad_down = dot_tn(activation, out_all)
    grad_gate = dot_tn(normed_mid_all, dgate_low)
    grad_up = dot_tn(normed_mid_all, dup_low)
    dmid_part = dot_nt(dgate_low, swiglu_back[0]) + dot_nt(dup_low, swiglu_back[1])
    dnormed_mid = lax.psum_scatter(
        dmid_part.reshape(seq_count, full_len, model_width), "ctx", scatter_dimension=1, tiled=True
    ).reshape(local_rows, model_width)
    grad_gain_mid = jnp.sum(dnormed_mid * hidden * inverse_mid, 0)
    dhidden = upstream + norm_back(dnormed_mid, hidden, inverse_mid, gain_mid)
    swiglu_grads = (
        lax.psum_scatter(
            grad_gate.astype(jnp.bfloat16), "dp", scatter_dimension=0, tiled=True
        ).astype(jnp.float32),
        lax.psum_scatter(
            grad_up.astype(jnp.bfloat16), "dp", scatter_dimension=0, tiled=True
        ).astype(jnp.float32),
        lax.psum_scatter(
            grad_down.astype(jnp.bfloat16), "dp", scatter_dimension=1, tiled=True
        ).astype(jnp.float32),
    )
    attn_back = attention_weights(query_proj, key_proj, value_proj, gating_proj, output_proj)
    dbranch_low = dhidden.astype(jnp.bfloat16)
    dbranch_all = lax.all_gather(
        dbranch_low.reshape(seq_count, local_len, model_width), "ctx", axis=1, tiled=True
    ).reshape(all_rows, model_width)
    grad_output = dot_tn(mixed, dbranch_all)
    dmixed = dot_nt(dbranch_all, attn_back[4])
    dattended_low = (dmixed * gate_sig).astype(jnp.bfloat16)
    dgating_low = (dmixed * attended * gate_sig * (1.0 - gate_sig)).astype(jnp.bfloat16)
    upstream_heads = dattended_low.reshape(seq_count, full_len, local_kv, group_size, head_dim)
    dquery_rot, dkey_rot, dvalue_sum = lax.map(
        lambda seq_items: softmax_backward_mapped(seq_items, causal),
        (query_groups, key_low, value_low, log_total, upstream_heads),
    )
    dvalue_low = dvalue_sum.reshape(all_rows, local_kv * head_dim).astype(jnp.bfloat16)
    dquery_normed = unrotate(
        dquery_rot.reshape(seq_count, full_len, local_heads, head_dim), cos_rows, sin_rows
    )
    dkey_normed = unrotate(
        dkey_rot.reshape(seq_count, full_len, local_kv, head_dim), cos_rows, sin_rows
    )
    grad_query_gain = jnp.sum(dquery_normed * query_raw * query_inv, (0, 1, 2))
    grad_key_gain = jnp.sum(dkey_normed * key_raw * key_inv, (0, 1, 2))
    dquery_low = (
        norm_back(dquery_normed, query_raw, query_inv, query_scale)
        .reshape(all_rows, -1)
        .astype(jnp.bfloat16)
    )
    dkey_low = (
        norm_back(dkey_normed, key_raw, key_inv, key_scale)
        .reshape(all_rows, -1)
        .astype(jnp.bfloat16)
    )
    dnormed_part = (
        dot_nt(dquery_low, attn_back[0])
        + dot_nt(dkey_low, attn_back[1])
        + dot_nt(dvalue_low, attn_back[2])
        + dot_nt(dgating_low, attn_back[3])
    )
    dnormed = (
        lax.psum_scatter(
            dnormed_part.reshape(seq_count, full_len, model_width).astype(jnp.bfloat16),
            "ctx",
            scatter_dimension=1,
            tiled=True,
        )
        .astype(jnp.float32)
        .reshape(local_rows, model_width)
    )
    grad_gain_in = jnp.sum(dnormed * inputs * inverse_in, 0)
    input_grad = (dhidden + norm_back(dnormed, inputs, inverse_in, gain_in)).astype(jnp.bfloat16)
    grad_query = dot_tn(normed_all, dquery_low)
    grad_key = dot_tn(normed_all, dkey_low)
    grad_value = dot_tn(normed_all, dvalue_low)
    grad_gating = dot_tn(normed_all, dgating_low)
    attention_grads = (
        lax.psum_scatter(
            grad_query.astype(jnp.bfloat16), "dp", scatter_dimension=0, tiled=True
        ).astype(jnp.float32),
        lax.psum_scatter(
            grad_key.astype(jnp.bfloat16), "dp", scatter_dimension=0, tiled=True
        ).astype(jnp.float32),
        lax.psum_scatter(
            grad_value.astype(jnp.bfloat16), "dp", scatter_dimension=0, tiled=True
        ).astype(jnp.float32),
        lax.psum_scatter(
            grad_gating.astype(jnp.bfloat16), "dp", scatter_dimension=0, tiled=True
        ).astype(jnp.float32),
        lax.psum_scatter(
            grad_output.astype(jnp.bfloat16), "dp", scatter_dimension=1, tiled=True
        ).astype(jnp.float32),
    )
    gain_grads = lax.psum(
        (grad_gain_in, grad_gain_mid, grad_query_gain, grad_key_gain), ("dp", "ctx")
    )
    return (
        layer_out.reshape(seq_count, local_len, model_width),
        input_grad.reshape(seq_count, local_len, model_width),
        gain_grads[0],
        gain_grads[2],
        gain_grads[3],
        attention_grads[0],
        attention_grads[1],
        attention_grads[2],
        attention_grads[3],
        attention_grads[4],
        gain_grads[1],
        swiglu_grads[0],
        swiglu_grads[1],
        swiglu_grads[2],
    )


def per_device(
    tokens,
    cotangent,
    domain_ids,
    domain_counts,
    domain_numer,
    domain_denom,
    attention_gain,
    query_gain,
    key_gain,
    query_proj,
    key_proj,
    value_proj,
    gating_proj,
    output_proj,
    swiglu_gain,
    swiglu_gate,
    swiglu_up,
    swiglu_down,
):
    seq_count, local_len, width = tokens.shape
    rows = seq_count * local_len
    full_len = local_len * lax.axis_size("x") * lax.axis_size("c")
    seqs = seq_count * lax.axis_size("y")
    head = query_gain.shape[0]
    kv_cols = key_proj.shape[1] // 2
    q_cols = query_proj.shape[1] // 2
    ff_cols = swiglu_gate.shape[1] // 2
    heads = q_cols // head
    split, rest = ff_cols * 2 // 3, ff_cols - ff_cols * 2 // 3
    tokens, cotangent = tokens.reshape(rows, width), cotangent.reshape(rows, width)
    (
        normed_all, w_qkv, w_go, rows_first, rows_gu, rows_d, inverse_in, out_low, factor, cos_rows, sin_rows,
    ) = opening(
        tokens,
        cotangent,
        attention_gain,
        (domain_ids, domain_counts, domain_numer, domain_denom),
        (
            query_proj, key_proj, value_proj, gating_proj, output_proj, swiglu_gate, swiglu_up, swiglu_down,
        ),
        split,
        full_len,
        head,
    )
    w_first = gather_rows(rows_first)
    w_last_gu = gather_rows(rows_gu)

    query_scale, key_scale = query_gain.astype(F32)[None], key_gain.astype(F32)[None]
    qkv, attended, logs, gate_sig, mixed, out_all = attend(
        normed_all, w_qkv, w_go, out_low, query_scale, key_scale, cos_rows, sin_rows, heads, head, full_len
    )
    wide, column = jax.ShapeDtypeStruct((rows, width), F32), jax.ShapeDtypeStruct((rows, 1), F32)
    low = jax.ShapeDtypeStruct((rows, width), BF16)
    gain_mid = swiglu_gain.reshape(1, -1)
    hidden, inverse_mid, normed_mid = scatter_products(
        middle_kernel, 7, (tokens, gain_mid), (wide, column, low), (mixed, w_go, q_cols)
    )
    mid_all, w_last_d = gather_tokens(normed_mid, rows_d)

    act_first, dgu_first, grad_first = feed_forward_grads(mid_all, out_all, w_first)
    part_first = scatter_grads(grad_first)
    w_last_gu, grad_first = lax.optimization_barrier((w_last_gu, grad_first))
    act_last, dgu_last = feed_forward(mid_all, out_all, w_last_gu, w_last_d)
    dhidden, dbranch, grad_gain_mid = scatter_products(
        middle_back_kernel,
        8,
        (hidden, inverse_mid, gain_mid, cotangent, factor),
        (wide, low, jax.ShapeDtypeStruct((1, width), F32)),
        (dgu_first, w_first, 0),
        (dgu_last, w_last_gu, 0),
    )
    dbranch_all, ffn_sums, grad_last = gather_beside(
        dbranch,
        ((act_first, w_first, 2 * split), (act_last, w_last_d, 0)),
        mid_all,
        out_all,
        dgu_last,
        act_last,
    )
    part_last = scatter_grads(grad_last)
    dbranch_all, part_first = lax.optimization_barrier((dbranch_all, part_first))

    theirs_first = their_rows(part_first)
    dattended, dgating, grad_go = gate_back(
        normed_all, dbranch_all, w_go, attended, gate_sig, mixed
    )
    dattended, theirs_first, grad_go = lax.optimization_barrier((dattended, theirs_first, grad_go))
    part_go = scatter_grads(grad_go)
    dqkv, grad_query_gain, grad_key_gain, ffn_branch = attend_back(
        qkv, dattended, logs, query_scale, key_scale, cos_rows, sin_rows, ffn_sums, heads, head, full_len
    )
    grad_query_gain, grad_key_gain = grad_query_gain[0], grad_key_gain[0]
    dqkv, part_last = lax.optimization_barrier((dqkv, part_last))
    theirs_last = their_rows(part_last)
    layer_out = (hidden + ffn_branch).astype(BF16)
    dqkv, layer_out = lax.optimization_barrier((dqkv, layer_out))
    grad_qkv = weight_grads(normed_all, dqkv)
    grad_qkv, theirs_last = lax.optimization_barrier((grad_qkv, theirs_last))
    plan = [(0, i * split, split, i, 0, i == 2) for i in range(3)]
    plan += [(1, i * rest, rest, i, split, i == 2) for i in range(3)]
    grad_gate, grad_up, grad_down = join_grads(
        (part_first, part_last),
        (theirs_first, theirs_last),
        plan,
        [weight.shape for weight in (swiglu_gate, swiglu_up, swiglu_down)],
    )
    grad_qkv, layer_out, grad_gate, grad_up, grad_down = lax.optimization_barrier(
        (grad_qkv, layer_out, grad_gate, grad_up, grad_down)
    )
    input_grad, mine_qkv, theirs_qkv, totals = tail(
        ((dqkv, w_qkv, 0), (dgating, w_go, 0)),
        grad_qkv,
        tokens,
        inverse_in,
        dhidden,
        attention_gain,
        (grad_gain_mid, grad_query_gain, grad_key_gain),
    )
    input_grad, part_go = lax.optimization_barrier((input_grad, part_go))
    theirs_go = their_rows(part_go)
    grad_gating, grad_output = join_grads(
        (part_go,),
        (theirs_go,),
        [(0, 0, q_cols, 0, 0, False), (0, q_cols, q_cols, 1, 0, True)],
        (gating_proj.shape, output_proj.shape),
    )
    widths, starts = (q_cols, kv_cols, kv_cols), (0, q_cols, q_cols + kv_cols)
    *gain_grads, grad_query, grad_key, grad_value = join_last(
        mine_qkv,
        theirs_qkv,
        totals,
        [(0, starts[i], widths[i], i, 0, False) for i in range(3)],
        (width, width, head, head),
        [weight.shape for weight in (query_proj, key_proj, value_proj)],
    )
    gain_grads = [gain.reshape(-1) for gain in gain_grads]
    shape = (seq_count, local_len, width)
    return (
        layer_out.reshape(shape),
        input_grad.reshape(shape),
        gain_grads[0],
        gain_grads[2],
        gain_grads[3],
        grad_query,
        grad_key,
        grad_value,
        grad_gating,
        grad_output,
        gain_grads[1],
        grad_gate,
        grad_up,
        grad_down,
    )


def solution(mesh):
    if (mesh.shape["dp"], mesh.shape["ctx"]) == (8, 4):
        body = per_device
        mesh = Mesh(mesh.devices.reshape(4, 2, 2, 2), ("z", "y", "x", "c"))
        dp, ctx = ("z", "y"), ("x", "c")
    else:
        body = per_device_wide
        dp, ctx = "dp", "ctx"
    tokens, weight, turned = P(dp, ctx, None), P(dp, ctx), P(ctx, dp)
    return jax.shard_map(
        body,
        mesh=mesh,
        in_specs=(tokens, tokens, P(dp), *[P()] * 6, *[weight] * 4, turned, P(), weight, weight, turned),
        out_specs=(tokens, tokens, *[P()] * 3, *[weight] * 4, turned, P(), weight, weight, turned),
        check_vma=False,
    )
```

```python
import functools

import jax
import jax.numpy as jnp
import numpy as np
from jax import lax
from jax.experimental import pallas as pl
from jax.experimental.pallas import tpu as pltpu
from jax.sharding import Mesh
from jax.sharding import PartitionSpec as P

LENGTH = 1024

EPSILON = 1e-06
ROPE_BASE = 1000000.0
MESH = pl.DeviceIdType.MESH
BF16 = jnp.bfloat16
F32 = jnp.float32
VMEM_BYTES = 62 * 2**20


def micros(count):
    return pl.CostEstimate(flops=0, transcendentals=0, bytes_accessed=count * 3_300_000)


def dot_nn(left, right):
    return jnp.dot(left, right, preferred_element_type=F32)


def dot_tn(left, right):
    return lax.dot_general(left, right, (((0,), (0,)), ((), ())), preferred_element_type=F32)


def dot_nt(left, right):
    return lax.dot_general(left, right, (((1,), (1,)), ((), ())), preferred_element_type=F32)


def rope_tables(positions, head_width):
    halfway = head_width // 2
    inverse = 1.0 / ROPE_BASE ** (jnp.arange(halfway, dtype=F32) * (2.0 / head_width))
    angles = positions.astype(F32)[:, None] * inverse[None, :]
    return (jnp.cos(angles), jnp.sin(angles))


def rotate(tensor, cosine, sine):
    halfway = tensor.shape[-1] // 2
    first_half = tensor[..., :halfway]
    second_half = tensor[..., halfway:]
    return jnp.concatenate(
        [first_half * cosine - second_half * sine, second_half * cosine + first_half * sine], -1
    )


def unrotate(grads_in, cosine, sine):
    halfway = grads_in.shape[-1] // 2
    first_half = grads_in[..., :halfway]
    second_half = grads_in[..., halfway:]
    return jnp.concatenate(
        [first_half * cosine + second_half * sine, second_half * cosine - first_half * sine], -1
    )


def norm_back(grads_in, values_in, inverse, gain_vec):
    scaled = grads_in * gain_vec
    return inverse * scaled - values_in * (inverse * inverse * inverse) * jnp.mean(
        scaled * values_in, -1, keepdims=True
    )


def greet(neighbours):
    barrier = pltpu.get_barrier_semaphore()
    for neighbour in neighbours:
        pl.semaphore_signal(barrier, inc=1, device_id=neighbour, device_id_type=MESH)
    pl.semaphore_wait(barrier, len(neighbours))


def remote_copies(send, recv, device):
    def remote(index, source, target, axis):
        return pltpu.make_async_remote_copy(
            src_ref=source,
            dst_ref=target,
            send_sem=send.at[index],
            recv_sem=recv.at[index],
            device_id=device[axis],
            device_id_type=MESH,
        )

    return remote


def place():
    y, x, c = lax.axis_index("y"), lax.axis_index("x"), lax.axis_index("c")
    return y, x, c, {"y": {"y": 1 - y}, "x": {"x": 1 - x}, "c": {"c": 1 - c}}


def gather_steps(s_ref, out_ref, local_sem, send, recv, split=True):
    y, x, c, device = place()
    remote = remote_copies(send, recv, device)
    half = s_ref.shape[0] // 2
    low, high = pl.ds(0, half), pl.ds(half, half)
    mine = out_ref.at[y, x, c]
    from_x = out_ref.at[y, 1 - x, c]
    from_y = out_ref.at[1 - y, x, c]
    diagonal = out_ref.at[1 - y, 1 - x, c]
    x_low = remote(0, s_ref.at[low], mine.at[low], "x")
    y_high = remote(1, s_ref.at[high], mine.at[high], "y")
    x_high = remote(2, s_ref.at[high], mine.at[high], "x")
    y_low = remote(3, s_ref.at[low], mine.at[low], "y")
    c_own = remote(4, s_ref, mine, "c")
    local = pltpu.make_async_copy(s_ref, mine, local_sem)
    forward_y = remote(5, from_x.at[low], from_x.at[low], "y")
    over_x = from_y.at[high] if split else from_y
    forward_x = remote(6, over_x, over_x, "x")
    c_x = remote(7, from_x, from_x, "c")
    c_y = remote(8, from_y, from_y, "c")
    c_low = remote(9, diagonal.at[low], diagonal.at[low], "c")
    over_c = diagonal.at[high] if split else diagonal
    c_high = remote(10, over_c, over_c, "c")

    def begin():
        for copy in (x_low, y_high, x_high, y_low, c_own, local):
            copy.start()

    def forward():
        x_low.wait_recv()
        if split:
            forward_y.start()
        y_high.wait_recv()
        if split:
            forward_x.start()

    def across():
        if not split:
            y_low.wait_recv()
            forward_x.start()
        x_high.wait_recv()
        c_x.start()
        if split:
            y_low.wait_recv()
        c_y.start()

    def finish():
        if split:
            forward_y.wait_recv()
            c_low.start()
        forward_x.wait_recv()
        c_high.start()
        for copy in (c_own, c_x, c_y, *((c_low,) if split else ()), c_high):
            copy.wait()
        for copy in (x_low, y_high, x_high, y_low, *((forward_y,) if split else ()), forward_x):
            copy.wait_send()
        local.wait()

    return begin, forward, across, finish


GATHER_SEMAPHORES = (
    pltpu.SemaphoreType.DMA,
    pltpu.SemaphoreType.DMA((11,)),
    pltpu.SemaphoreType.DMA((11,)),
)


def swap_steps(pieces, sources, outs, local_sem, send, recv, wanted=None):
    y, _, _, device = place()
    remote = remote_copies(send, recv, device)
    copies, locals_ = [], []
    for i, (source, out, first, count, at) in enumerate(pieces):
        if wanted is not None and not wanted(out):
            continue
        rows, cols = sources[source].shape
        target = outs[out].at[pl.ds(pl.multiple_of(y * rows, rows), rows), pl.ds(at, count)]

        def half(which):
            start = pl.multiple_of(which * (cols // 2) + first, 128)
            return sources[source].at[:, pl.ds(start, count)]

        copies.append(remote(i, half(1 - y), target, "y"))
        locals_.append(pltpu.make_async_copy(half(y), target, local_sem.at[i]))

    def begin():
        for copy in (*copies, *locals_):
            copy.start()

    def here():
        for copy in locals_:
            copy.wait()

    def finish():
        for copy in copies:
            copy.wait()

    return begin, here, finish


def line_steps(rows_ref, out_ref, local_sem, send, recv, part, which):
    z = lax.axis_index("z")
    rows, half = rows_ref.shape[0], rows_ref.shape[0] // 2
    first = which * half
    pair, middle = z + 1 - 2 * lax.rem(z, 2), 3 - z
    inner = (z == 1) | (z == 2)

    def at(index):
        return out_ref.at[pl.ds(pl.multiple_of(index * rows + first, half), half)]

    def remote(index, source, target, peer):
        return pltpu.make_async_remote_copy(
            src_ref=source,
            dst_ref=target,
            send_sem=send.at[5 * part + index],
            recv_sem=recv.at[5 * part + index],
            device_id={"z": peer},
            device_id_type=MESH,
        )

    far = middle + 1 - 2 * lax.rem(middle, 2)
    own = rows_ref.at[pl.ds(pl.multiple_of(first, half), half)]
    own_pair = remote(0, own, at(z), pair)
    own_middle = remote(1, own, at(z), middle)
    pair_middle = remote(2, at(pair), at(pair), middle)
    middle_pair = remote(3, at(middle), at(middle), pair)
    far_pair = remote(4, at(far), at(far), pair)
    local = pltpu.make_async_copy(own, at(z), local_sem.at[part])

    def begin():
        local.start()
        own_pair.start()
        pl.when(inner)(own_middle.start)

    def second():
        own_pair.wait_recv()

        @pl.when(inner)
        def _():
            pair_middle.start()
            own_middle.wait_recv()
            middle_pair.start()

    def third():
        @pl.when(inner)
        def _():
            pair_middle.wait_recv()
            far_pair.start()

    def finish():
        @pl.when(inner)
        def _():
            for copy in (own_middle, pair_middle, middle_pair, far_pair):
                copy.wait_send()

        @pl.when(jnp.logical_not(inner))
        def _():
            middle_pair.wait_recv()
            far_pair.wait_recv()

        own_pair.wait_send()
        local.wait()

    def peers():
        return pair, middle, inner

    return begin, second, third, finish, peers


def greet_line(others, pair, middle, inner):
    barrier = pltpu.get_barrier_semaphore()
    for other in (*others, {"z": pair}):
        pl.semaphore_signal(barrier, inc=1, device_id=other, device_id_type=MESH)

    @pl.when(inner)
    def _():
        pl.semaphore_signal(barrier, inc=1, device_id={"z": middle}, device_id_type=MESH)

    count = len(others) + 1
    pl.semaphore_wait(barrier, jnp.where(inner, count + 1, count))


LINE_SEMAPHORES = (
    pltpu.SemaphoreType.DMA((2,)),
    pltpu.SemaphoreType.DMA((10,)),
    pltpu.SemaphoreType.DMA((10,)),
)


def both_halves(rows_ref, out_ref, *sems):
    y = lax.axis_index("y")
    return [line_steps(rows_ref, out_ref, *sems, part, which) for part, which in ((0, y), (1, 1 - y))]


def gather_kernel(source, rows_ref, out, line_ref, *sems):
    begin, forward, across, finish = gather_steps(source, out, *sems[:3])
    lines = both_halves(rows_ref, line_ref, *sems[3:])
    greet_line(tuple(place()[3].values()), *lines[0][4]())
    for steps in lines:
        steps[0]()
    begin()
    for steps in lines:
        steps[1]()
    forward()
    lines[0][2]()
    across()
    lines[1][2]()
    finish()
    for steps in lines:
        steps[3]()


def gather_tokens(shard, line):
    rows, width = shard.shape
    gathered, lined = pl.pallas_call(
        gather_kernel,
        out_shape=(
            jax.ShapeDtypeStruct((2, 2, 2, rows, width), shard.dtype),
            jax.ShapeDtypeStruct((4 * line.shape[0], line.shape[1]), line.dtype),
        ),
        in_specs=[pl.BlockSpec(memory_space=pltpu.VMEM)] * 2,
        out_specs=(pl.BlockSpec(memory_space=pl.ANY),) * 2,
        scratch_shapes=[*GATHER_SEMAPHORES, *LINE_SEMAPHORES],
        compiler_params=pltpu.CompilerParams(collective_id=1, has_side_effects=True),
        cost_estimate=micros(42),
        name="gather_tokens",
    )(shard, line)
    return gathered.reshape(8 * rows, width), lined


def opening_kernel(pieces, tokens, cotangent, gain, ids, counts, numer, denom, turns, *refs):
    sources, refs = list(refs[:8]), refs[8:]
    out, line_q, line_g, first, last_gu, last_d, inverse, low, factor, cosine, sine, *refs = refs
    rows_q, rows_g, normed, output_t, down_t, *sems = refs
    begin, forward, across, finish = gather_steps(normed, out, *sems[:3], False)
    y = lax.axis_index("y")
    steps = [
        line_steps(rows, line, *sems[3 * i + 3 : 3 * i + 6], part, which)
        for part, which in ((0, y), (1, 1 - y))
        for i, (rows, line) in enumerate(((rows_q, line_q), (rows_g, line_g)))
    ]
    output_ref, down_ref = sources[4], sources[7]
    sources[4], sources[7] = output_t, down_t
    swaps = [
        swap_steps(pieces, sources, (rows_q, rows_g, first, last_gu, last_d), *sems[9:], wanted)
        for wanted in (lambda out: out == 0, lambda out: out == 1, lambda out: out > 1)
    ]
    step = 64

    def norm(i):
        at = pl.ds(i * step, step)
        x = tokens[at].astype(F32)
        inv = lax.rsqrt(jnp.mean(x * x, -1, keepdims=True) + EPSILON)
        inverse[at] = inv
        normed[at] = (x * inv * gain[...].astype(F32).reshape(1, -1)).astype(BF16)

    def weigh(i):
        at = pl.ds(i * step, step)
        low[at] = (cotangent[at].astype(F32) * factor[...]).astype(BF16)

    def turn(i):
        at = pl.ds(i * 128, 128)
        places = lax.broadcasted_iota(jnp.int32, (128, cosine.shape[1]), 0) + i * 128
        angles = places.astype(F32) * turns[0:1]
        cosine[at] = jnp.cos(angles)
        sine[at] = jnp.sin(angles) * turns[1:2]

    greet_line(tuple(place()[3].values()), *steps[0][4]())
    swaps[0][0]()
    swaps[0][1]()
    steps[0][0]()
    output_t[...] = output_ref[...].astype(F32).T.astype(BF16)
    swaps[1][0]()
    swaps[1][1]()
    steps[1][0]()
    pl.loop(0, tokens.shape[0] // step)(norm)
    begin()
    for i in range(2):
        swaps[i][2]()
        steps[i + 2][0]()
    steps[0][1]()
    steps[1][1]()
    chosen = lax.broadcasted_iota(jnp.int32, counts.shape, 1) == ids[...]
    ratio = numer[...].astype(F32) / denom[...].astype(F32) * LENGTH / counts[...].astype(F32)
    factor[...] = jnp.sum(jnp.where(chosen, ratio, 0.0), -1, keepdims=True)

    @pl.loop(0, down_ref.shape[0] // 256)
    def _(i):
        at = pl.ds(pl.multiple_of(i * 256, 256), 256)
        down_t[:, at] = down_ref[at].astype(F32).T.astype(BF16)

    steps[2][1]()
    steps[3][1]()
    forward()
    across()
    swaps[2][0]()
    steps[0][2]()
    steps[1][2]()
    pl.loop(0, tokens.shape[0] // step)(weigh)
    steps[2][2]()
    steps[3][2]()
    pl.loop(0, cosine.shape[0] // 128)(turn)
    finish()
    for step_set in steps:
        step_set[3]()
    swaps[2][1]()
    swaps[2][2]()


def opening(tokens, cotangent, gain, domains, weights, split, full_len, head):
    rows, width = tokens.shape
    halves = [weight.shape[0 if i in (4, 7) else 1] // 2 for i, weight in enumerate(weights)]
    groups = (
        [(i, 0, halves[i]) for i in (0, 1, 2)],
        [(i, 0, halves[i]) for i in (3, 4)],
        [(i, 0, split) for i in (5, 6, 7)],
        [(i, split, halves[i] - split) for i in (5, 6)],
        [(7, split, halves[7] - split)],
    )
    pieces, widths = [], []
    for group in groups:
        at = 0
        for source, first, count in group:
            pieces.append((source, len(widths), first, count, at))
            at += count
        widths.append(at)
    inverse = 1.0 / np.float32(ROPE_BASE) ** (np.arange(head // 2, dtype=np.float32) * np.float32(2.0 / head))
    turns = np.stack([np.tile(inverse, 2), np.repeat(np.float32([-1.0, 1.0]), head // 2)]).astype(np.float32)
    whole, loose = pl.BlockSpec(memory_space=pltpu.VMEM), pl.BlockSpec(memory_space=pl.ANY)
    shape = jax.ShapeDtypeStruct
    dma = pltpu.SemaphoreType.DMA
    gathered, *outs = pl.pallas_call(
        functools.partial(opening_kernel, pieces),
        out_shape=(
            shape((2, 2, 2, rows, width), BF16),
            *[shape((8 * rows, size), BF16) for size in widths[:2]],
            *[shape((2 * rows, size), BF16) for size in widths[2:]],
            shape((rows, 1), F32),
            shape((rows, width), BF16),
            shape((1, 1), F32),
            shape((full_len, head), F32),
            shape((full_len, head), F32),
        ),
        in_specs=[whole] * (8 + len(weights)),
        out_specs=(*[loose] * 6, *[whole] * 5),
        scratch_shapes=[
            *[pltpu.VMEM((2 * rows, size), BF16) for size in widths[:2]],
            pltpu.VMEM((rows, width), BF16),
            *[pltpu.VMEM(weights[i].shape[::-1], BF16) for i in (4, 7)],
            *GATHER_SEMAPHORES,
            *[dma((2,)), dma((10,)), dma((10,))] * 2,
            *[dma((len(pieces),))] * 3,
        ],
        compiler_params=pltpu.CompilerParams(
            collective_id=2, has_side_effects=True, vmem_limit_bytes=VMEM_BYTES
        ),
        cost_estimate=micros(80),
        name="opening",
    )(
        tokens,
        cotangent,
        gain,
        *(domain.reshape(1, -1) for domain in domains),
        jnp.asarray(turns),
        *weights,
    )
    return gathered.reshape(8 * rows, width), *outs


def add_rows(target, start, size, other, base, step=64):
    @pl.loop(0, size // step)
    def _(i):
        at, there = pl.ds(start + i * step, step), pl.ds(base + i * step, step)
        target[at] = (target[at].astype(F32) + other[there].astype(F32)).astype(target.dtype)


def product_steps(windows, lefts, rights, left_vmem, right_vmem, own, pairs, got, load_sem, send, recv):
    y, x, c, device = place()
    remote = remote_copies(send, recv, device)
    rows, width = own.shape[1:]
    half, both = rows // 2, 2 * rows
    tile = 512 if sum(ref.shape[2] for ref in left_vmem) <= 256 else 256
    targets = ((1 - y, 1 - x), (1 - y, x), (y, 1 - x), (y, x))
    pieces = ((0, 0, half), (0, half, half), (1, 0, rows), (2, 0, rows), (3, 0, rows))
    count = len(lefts)
    right_loads = [
        pltpu.make_async_copy(
            rights[j].at[:, pl.ds(windows[j], right_vmem[j].shape[1])], right_vmem[j], load_sem.at[j]
        )
        for j in range(count)
    ]
    left_loads = []
    for i, (a, b) in enumerate(targets):
        start = pl.multiple_of((a * 2 + b) * both, both)
        left_loads.append(
            [
                pltpu.make_async_copy(
                    lefts[j].at[pl.ds(start, both)], left_vmem[j].at[i], load_sem.at[count * (i + 1) + j]
                )
                for j in range(count)
            ]
        )
    crossing = [
        remote(k, pairs.at[i, 1 - c, pl.ds(first, size)], got.at[i, pl.ds(first, size)], "c")
        for k, (i, first, size) in enumerate(pieces)
    ]

    def load():
        for copy in right_loads:
            copy.start()
        for copies in left_loads:
            for copy in copies:
                copy.start()

    def ready():
        for copy in right_loads:
            copy.wait()

    def product(i):
        for copy in left_loads[i]:
            copy.wait()

        @pl.loop(0, width // tile)
        def _(n):
            cols = pl.ds(pl.multiple_of(n * tile, tile), tile)
            total = dot_nt(left_vmem[0][i], right_vmem[0][cols])
            for j in range(1, count):
                total = total + dot_nt(left_vmem[j][i], right_vmem[j][cols])
            pairs[i, :, :, cols] = total.reshape(2, rows, tile).astype(BF16)

        for k, piece in enumerate(pieces):
            if piece[0] == i:
                crossing[k].start()

    def cores(k, step=64):
        i, first, size = pieces[k]
        crossing[k].wait_recv()

        @pl.loop(0, size // step)
        def _(n):
            at = pl.ds(first + n * step, step)
            own[i, at] = (pairs[i, c, at].astype(F32) + got[i, at].astype(F32)).astype(BF16)

    def finish():
        for copy in crossing:
            copy.wait_send()

    return load, ready, product, cores, finish


def axis_steps(own, x_diag, y_diag, x_got, y_got, send, recv):
    remote = remote_copies(send, recv, place()[3])
    rows = own.shape[1]
    half = rows // 2
    low, high = pl.ds(0, half), pl.ds(half, half)
    diag_x = remote(0, own.at[0, low], x_diag, "x")
    diag_y = remote(1, own.at[0, high], y_diag, "y")
    y_high = remote(2, own.at[1, high], y_got.at[high], "y")
    x_low = remote(3, own.at[2, low], x_got.at[low], "x")
    size = half // 2
    spans = [pl.ds(i * size, size) for i in range(4)]
    y_low = [remote(4 + i, own.at[1, spans[i]], y_got.at[spans[i]], "y") for i in range(2)]
    x_high = [remote(6 + i, own.at[2, spans[2 + i]], x_got.at[spans[2 + i]], "x") for i in range(2)]

    def second():
        diag_x.wait_recv()
        for i in range(2):
            add_rows(own.at[1], i * size, size, x_diag, i * size)
            y_low[i].start()
        diag_y.wait_recv()
        for i in range(2):
            add_rows(own.at[2], half + i * size, size, y_diag, i * size)
            x_high[i].start()

    def finish(store, step=32):
        needed = ((x_low, y_low[0]), (y_high, x_high[0]), (y_low[1],), (x_high[1],))

        @pl.loop(0, 4)
        def _(part):
            for k, copies in enumerate(needed):

                @pl.when(part == k)
                def _():
                    for copy in copies:
                        copy.wait_recv()

            start = lax.rem(part, 2) * half + lax.div(part, 2) * size

            @pl.loop(0, size // step)
            def _(i):
                at = pl.ds(pl.multiple_of(start + i * step, step), step)
                store(at, own[3, at].astype(F32) + x_got[at].astype(F32) + y_got[at].astype(F32))

        for copy in (diag_x, diag_y, y_high, x_low, *y_low, *x_high):
            copy.wait_send()

    return diag_x, diag_y, x_low, y_high, second, finish


def scatter_steps(windows, lefts, rights, scratch):
    count = len(windows)
    product_scratch, axis_scratch = scratch[: 2 * count + 6], scratch[2 * count + 6 :]
    load, ready, product, cores, crossed = product_steps(
        windows, lefts, rights, product_scratch[:count], product_scratch[count : 2 * count],
        *product_scratch[2 * count :],
    )
    own = product_scratch[2 * count]
    diag_x, diag_y, x_low, y_high, second_axis, finish_axis = axis_steps(own, *axis_scratch)

    def first():
        ready()
        product(0)
        cores(0)
        diag_x.start()
        cores(1)
        diag_y.start()
        product(2)
        product(1)
        cores(3)
        x_low.start()
        cores(2)
        y_high.start()

    def second():
        second_axis()
        product(3)
        cores(4)

    def finish(store):
        finish_axis(store)
        crossed()

    return load, first, second, finish


def product_scratch(group, own=True):
    lefts, rights = [item[0] for item in group], [item[1] for item in group]
    rows, width = lefts[0].shape[0] // 8, rights[0].shape[0]
    return [
        *[pltpu.VMEM((4, 2 * rows, left.shape[1]), BF16) for left in lefts],
        *[pltpu.VMEM((width, left.shape[1]), BF16) for left in lefts],
        *[pltpu.VMEM((4, rows, width), BF16)] * own,
        pltpu.VMEM((4, 2, rows, width), BF16),
        pltpu.VMEM((4, rows, width), BF16),
        pltpu.SemaphoreType.DMA((5 * len(group),)),
        pltpu.SemaphoreType.DMA((5,)),
        pltpu.SemaphoreType.DMA((5,)),
    ]


def axis_scratch(rows, width):
    return [
        pltpu.VMEM((rows // 2, width), BF16),
        pltpu.VMEM((rows // 2, width), BF16),
        pltpu.VMEM((rows, width), BF16),
        pltpu.VMEM((rows, width), BF16),
        pltpu.SemaphoreType.DMA((8,)),
        pltpu.SemaphoreType.DMA((8,)),
    ]


def scatter_scratch(group):
    lefts, rights = [item[0] for item in group], [item[1] for item in group]
    rows, width = lefts[0].shape[0] // 8, rights[0].shape[0]
    scratch = product_scratch(group) + axis_scratch(rows, width)
    return lefts + rights, scratch, jax.ShapeDtypeStruct((rows, width), F32)


def middle_kernel(windows, *refs):
    count = len(windows)
    lefts, rights, refs = refs[:count], refs[count : 2 * count], refs[2 * count :]
    tokens, gain, hidden, inverse, normed, *scratch = refs
    load, first, second, finish = scatter_steps(windows, lefts, rights, scratch)

    def store(at, branch):
        total = tokens[at].astype(F32) + branch
        inv = lax.rsqrt(jnp.mean(total * total, -1, keepdims=True) + EPSILON)
        hidden[at] = total
        inverse[at] = inv
        normed[at] = (total * inv * gain[...].astype(F32)).astype(BF16)

    load()
    greet(tuple(place()[3].values()))
    first()
    second()
    finish(store)


def middle_back_kernel(windows, *refs):
    count = len(windows)
    lefts, rights, refs = refs[:count], refs[count : 2 * count], refs[2 * count :]
    hidden, inverse, gain, cotangent, factor, dhidden, dbranch, gain_grad, *scratch = refs
    load, first, second, finish = scatter_steps(windows, lefts, rights, scratch)
    gain_grad[...] = jnp.zeros_like(gain_grad)

    def store(at, grad):
        state, inv = hidden[at], inverse[at]
        gain_grad[...] += jnp.sum(grad * state * inv, 0, keepdims=True)
        upstream = cotangent[at].astype(F32) * factor[...]
        total = upstream + norm_back(grad, state, inv, gain[...].astype(F32))
        dhidden[at] = total
        dbranch[at] = total.astype(BF16)

    load()
    greet(tuple(place()[3].values()))
    first()
    second()
    finish(store)


def scatter_products(kernel, number, extras, outs, *group):
    operands, scratch, _ = scatter_scratch(group)
    whole = pl.BlockSpec(memory_space=pltpu.VMEM)
    return pl.pallas_call(
        functools.partial(kernel, [item[2] for item in group]),
        out_shape=outs,
        in_specs=[pl.BlockSpec(memory_space=pl.ANY)] * len(operands) + [whole] * len(extras),
        out_specs=(whole,) * len(outs),
        scratch_shapes=scratch,
        compiler_params=pltpu.CompilerParams(
            collective_id=number, has_side_effects=True, vmem_limit_bytes=VMEM_BYTES
        ),
        cost_estimate=micros(48),
        name="scatter_products",
    )(*operands, *extras)


def gather_beside_kernel(windows, tile, shard_ref, *refs):
    count = len(windows)
    lefts, rights, refs = refs[:count], refs[count : 2 * count], refs[2 * count :]
    mid, low, dgu, act, out_ref, sums_ref, grad_ref, *scratch = refs
    size = 2 * count + 5
    products, (mid_buf, low_buf, dgu_vmem, act_vmem, total, tile_sem, side_sem), sems = (
        scratch[:size], scratch[size : size + 7], scratch[size + 7 :],
    )
    load, ready, product, cores, crossed = product_steps(
        windows, lefts, rights, products[:count], products[count : 2 * count], sums_ref,
        *products[2 * count :],
    )
    begin, forward, across, finish = gather_steps(shard_ref, out_ref, *sems)
    tiles = mid.shape[0] // tile
    sides = [
        pltpu.make_async_copy(dgu, dgu_vmem, side_sem.at[0]),
        pltpu.make_async_copy(act, act_vmem, side_sem.at[1]),
    ]

    def tile_copies(t):
        rows, slot = pl.ds(pl.multiple_of(t * tile, tile), tile), lax.rem(t, 2)
        return [
            pltpu.make_async_copy(source.at[rows], buffer.at[slot], tile_sem.at[i, slot])
            for i, (source, buffer) in enumerate(((mid, mid_buf), (low, low_buf)))
        ]

    load()
    greet(tuple(place()[3].values()))
    begin()
    for copy in (*sides, *tile_copies(0), *tile_copies(1)):
        copy.start()
    ready()
    for i in range(4):
        product(i)
    forward()
    for copy in sides:
        copy.wait()
    cores(0)
    cores(1)

    @pl.loop(0, tiles)
    def _(t):
        for copy in tile_copies(t):
            copy.wait()
        rows, slot = pl.ds(pl.multiple_of(t * tile, tile), tile), lax.rem(t, 2)
        add_products(t, total, 0, mid_buf.at[slot], dgu_vmem.at[rows])
        add_products(t, total, dgu_vmem.shape[1], low_buf.at[slot], act_vmem.at[rows])

        @pl.when(t + 2 < tiles)
        def _():
            for copy in tile_copies(t + 2):
                copy.start()

        @pl.when(t == tiles // 2 - 1)
        def _():
            across()
            for k in range(2, 5):
                cores(k)

    @pl.loop(0, total.shape[0] // 256)
    def _(m):
        at = pl.ds(m * 256, 256)
        grad_ref[at] = total[at].astype(BF16)

    crossed()
    finish()


def gather_beside(shard, group, mid, low, dgu, act, tile=512):
    rows, width = shard.shape
    operands = [item[0] for item in group] + [item[1] for item in group] + [mid, low, dgu, act]
    cols = dgu.shape[1] + act.shape[1]
    gathered, sums, grad = pl.pallas_call(
        functools.partial(gather_beside_kernel, [item[2] for item in group], tile),
        out_shape=(
            jax.ShapeDtypeStruct((2, 2, 2, rows, width), shard.dtype),
            jax.ShapeDtypeStruct((4, rows, width), BF16),
            jax.ShapeDtypeStruct((width, cols), BF16),
        ),
        in_specs=[
            pl.BlockSpec(memory_space=pltpu.VMEM),
            *[pl.BlockSpec(memory_space=pl.ANY)] * len(operands),
        ],
        out_specs=(
            pl.BlockSpec(memory_space=pl.ANY),
            pl.BlockSpec(memory_space=pltpu.VMEM),
            pl.BlockSpec(memory_space=pltpu.VMEM),
        ),
        scratch_shapes=[
            *product_scratch(group, own=False),
            pltpu.VMEM((2, tile, width), BF16),
            pltpu.VMEM((2, tile, width), BF16),
            pltpu.VMEM(dgu.shape, BF16),
            pltpu.VMEM(act.shape, BF16),
            pltpu.VMEM((width, cols), F32),
            pltpu.SemaphoreType.DMA((2, 2)),
            pltpu.SemaphoreType.DMA((2,)),
            *GATHER_SEMAPHORES,
        ],
        compiler_params=pltpu.CompilerParams(
            collective_id=6, has_side_effects=True, vmem_limit_bytes=VMEM_BYTES
        ),
        cost_estimate=micros(44),
        name="gather_beside",
    )(shard, *operands)
    return gathered.reshape(8 * rows, width), sums, grad


def line_scatter_steps(grad_ref, own, from_edge, from_middle, inward, load_sem, send, recv, part, which):
    z = lax.axis_index("z")
    rows, half = own.shape[1], own.shape[1] // 2
    pair, middle = z + 1 - 2 * lax.rem(z, 2), 3 - z
    inner = (z == 1) | (z == 2)
    edge = jnp.logical_not(inner)
    far = middle + 1 - 2 * lax.rem(middle, 2)
    first = pl.multiple_of(which * half, half)
    span = pl.ds(first, half)

    def block(index):
        return grad_ref.at[pl.ds(pl.multiple_of(index * rows + first, half), half)]

    def remote(index, source, target, peer):
        return pltpu.make_async_remote_copy(
            src_ref=source,
            dst_ref=target,
            send_sem=send.at[6 * part + index],
            recv_sem=recv.at[6 * part + index],
            device_id={"z": peer},
            device_id_type=MESH,
        )

    indices = (far, middle, pair, z)
    loads = [
        pltpu.make_async_copy(block(index), own.at[i, span], load_sem.at[4 * part + i])
        for i, index in enumerate(indices)
    ]
    edge_far = remote(0, own.at[1, span], from_edge.at[0, span], pair)
    edge_near = remote(1, own.at[0, span], from_edge.at[1, span], pair)
    edge_pair = remote(2, own.at[2, span], from_edge.at[2, span], pair)
    inner_far = remote(3, own.at[0, span], from_middle.at[0, span], middle)
    inner_near = remote(4, own.at[1, span], from_middle.at[1, span], middle)
    outward = remote(5, own.at[2, span], inward.at[span], pair)
    step = 128

    def add_into(target, other):
        @pl.loop(0, half // step)
        def _(i):
            at = pl.ds(first + i * step, step)
            target[at] = (target[at].astype(F32) + other[at].astype(F32)).astype(target.dtype)

    def load():
        for copy in loads:
            copy.start()

    def begin():
        for copy in loads:
            copy.wait()

        @pl.when(edge)
        def _():
            for copy in (edge_far, edge_near, edge_pair):
                copy.start()

    def second():
        @pl.when(inner)
        def _():
            edge_far.wait_recv()
            add_into(own.at[0], from_edge.at[0])
            inner_far.start()

    def third():
        @pl.when(inner)
        def _():
            edge_near.wait_recv()
            add_into(own.at[1], from_edge.at[1])
            inner_near.start()
            inner_far.wait_recv()
            add_into(own.at[2], from_middle.at[0])
            outward.start()

    def finish():
        @pl.when(inner)
        def _():
            edge_pair.wait_recv()
            add_into(own.at[3], from_edge.at[2])
            inner_near.wait_recv()
            add_into(own.at[3], from_middle.at[1])
            for copy in (inner_far, inner_near, outward):
                copy.wait_send()

        @pl.when(edge)
        def _():
            outward.wait_recv()
            add_into(own.at[3], inward)
            for copy in (edge_far, edge_near, edge_pair):
                copy.wait_send()

    return load, begin, second, third, finish


def total_steps(near, far, near_send, near_recv, far_send, far_recv):
    z, y, x, c = (lax.axis_index(name) for name in "zyxc")
    here = (y * 2 + x) * 2 + c
    others = [
        {"y": lax.rem(y + i // 4, 2), "x": lax.rem(x + i // 2 % 2, 2), "c": lax.rem(c + i % 2, 2)}
        for i in range(1, 8)
    ]
    levels = [{"z": lax.rem(z + i, 4)} for i in range(1, 4)]

    def remote(index, source, target, send, recv, device):
        return pltpu.make_async_remote_copy(
            src_ref=source,
            dst_ref=target,
            send_sem=send.at[index],
            recv_sem=recv.at[index],
            device_id=device,
            device_id_type=MESH,
        )

    around = [
        remote(i, near.at[here], near.at[here], near_send, near_recv, other)
        for i, other in enumerate(others)
    ]
    along = [
        remote(i, far.at[z], far.at[z], far_send, far_recv, level) for i, level in enumerate(levels)
    ]

    def begin():
        for copy in around:
            copy.start()

    def second():
        for copy in around:
            copy.wait()
        total = near[0]
        for i in range(1, 8):
            total = total + near[i]
        far[z] = total
        for copy in along:
            copy.start()

    def finish():
        for copy in along:
            copy.wait()
        total = far[0]
        for i in range(1, 4):
            total = total + far[i]
        return total

    return begin, second, finish, here, others, levels


def tail_kernel(windows, *refs):
    count = len(windows)
    lefts, rights, refs = refs[:count], refs[count : 2 * count], refs[2 * count :]
    grad_ref, tokens_ref, inverse_ref, dhidden_ref, gain_ref, *refs = refs
    gains, (out_ref, mine_ref, theirs_ref, total_ref), scratch = refs[:3], refs[3:7], refs[7:]
    size = 2 * count + 12
    load, first, second, finish = scatter_steps(windows, lefts, rights, scratch[:size])
    line, (swap_sem,), total = scratch[size : size + 7], scratch[size + 7 : size + 8], scratch[size + 8 :]
    near, far = total[:2]
    total_begin, total_second, total_finish, here, others, levels = total_steps(*total)
    y = lax.axis_index("y")
    lines = [line_scatter_steps(grad_ref, *line, part, which) for part, which in ((0, 1 - y), (1, y))]
    load()
    for steps in lines:
        steps[0]()
    width = out_ref.shape[1]
    near[here, :, pl.ds(width, width)] = gains[0][...]
    head = gains[1].shape[1]
    near[here, :, pl.ds(2 * width, head)] = gains[1][...]
    near[here, :, pl.ds(2 * width + head, head)] = gains[2][...]
    greet(others + levels)
    for steps in lines:
        steps[1]()
    first()
    lines[0][2]()
    second()
    lines[0][3]()
    lines[1][2]()
    gain_in = near.at[here, :, pl.ds(0, width)]
    gain_in[...] = jnp.zeros((1, width), F32)

    def store(at, grad):
        x, inv = tokens_ref[at].astype(F32), inverse_ref[at]
        gain_in[...] += jnp.sum(grad * x * inv, 0, keepdims=True)
        back = norm_back(grad, x, inv, gain_ref[...].astype(F32))
        out_ref[at] = (dhidden_ref[at] + back).astype(BF16)

    finish(store)
    total_begin()
    lines[1][3]()
    lines[0][4]()
    summed = line[0].at[3]
    half = theirs_ref.shape[0]
    swap = pltpu.make_async_remote_copy(
        src_ref=summed.at[pl.ds(pl.multiple_of((1 - y) * half, half), half)],
        dst_ref=theirs_ref,
        send_sem=swap_sem.at[0],
        recv_sem=swap_sem.at[1],
        device_id={"y": 1 - y},
        device_id_type=MESH,
    )
    swap.start()
    total_second()
    lines[1][4]()
    mine_ref[...] = summed[pl.ds(pl.multiple_of(y * half, half), half)]
    total_ref[...] = total_finish()
    swap.wait()


def tail(group, grad, tokens, inverse, dhidden, gain, gains):
    operands, scratch, total = scatter_scratch(group)
    rows, cols = grad.shape[0] // 4, grad.shape[1]
    length = 2 * total.shape[1] + 2 * gains[1].size
    half = jax.ShapeDtypeStruct((rows // 2, cols), BF16)
    whole = pl.BlockSpec(memory_space=pltpu.VMEM)
    block = lambda count: pltpu.VMEM((count, rows, cols), BF16)
    dma = pltpu.SemaphoreType.DMA
    return pl.pallas_call(
        functools.partial(tail_kernel, [item[2] for item in group]),
        out_shape=(
            jax.ShapeDtypeStruct(total.shape, BF16),
            half,
            half,
            jax.ShapeDtypeStruct((1, length), F32),
        ),
        in_specs=[pl.BlockSpec(memory_space=pl.ANY)] * (len(operands) + 1) + [whole] * 7,
        out_specs=(whole,) * 4,
        scratch_shapes=[
            *scratch,
            block(4), block(3), block(2), pltpu.VMEM((rows, cols), BF16), dma((8,)), dma((12,)), dma((12,)),
            dma((2,)),
            pltpu.VMEM((8, 1, length), F32), pltpu.VMEM((4, 1, length), F32), dma((7,)), dma((7,)), dma((3,)), dma((3,)),
        ],
        compiler_params=pltpu.CompilerParams(
            collective_id=0, has_side_effects=True, vmem_limit_bytes=VMEM_BYTES
        ),
        cost_estimate=micros(52),
        name="tail",
    )(*operands, grad, tokens, inverse, dhidden, gain.reshape(1, -1), *(gain.reshape(1, -1) for gain in gains))


def swap_y(value):
    return lax.ppermute(value, "y", [(0, 1), (1, 0)])


def in_y_order(mine, theirs, axis):
    count = mine.shape[axis]
    return lax.dynamic_slice_in_dim(
        jnp.concatenate([mine, theirs, mine], axis), lax.axis_index("y") * count, 2 * count, axis
    )


def gather_rows(rows):
    return lax.all_gather(rows, "z", axis=0, tiled=True)


def scatter_grads(grad):
    return lax.psum_scatter(grad.astype(BF16), "z", scatter_dimension=0, tiled=True)


def their_rows(part):
    half = part.shape[0] // 2
    return swap_y(
        lax.dynamic_slice_in_dim(part, (1 - lax.axis_index("y")) * half, half, 0)
    )


def join_pieces(plan, y, mine_of, theirs_of, outs):
    for source, first, width, out, at, turned in plan:
        half = outs[out].shape[0 if turned else 1] // 2
        cols = pl.ds(first, width)
        for which, piece in ((y, mine_of(source, cols)), (1 - y, theirs_of(source, cols))):
            target = pl.ds(pl.multiple_of(which * half + at, 128), width)
            if turned:
                outs[out][target, :] = piece.astype(F32).T
            else:
                outs[out][:, target] = piece.astype(F32)


def join_kernel(plan, count, y_rows, *refs):
    y = lax.axis_index("y")
    parts, theirs, outs = refs[:count], refs[count : 2 * count], refs[2 * count :]
    mine = pl.ds(pl.multiple_of(y * y_rows, y_rows), y_rows)
    own = lambda source, cols: parts[source][mine, cols]
    got = lambda source, cols: theirs[source][:, cols]
    join_pieces(plan, y, own, got, outs)


def join_grads(parts, theirs, plan, shapes):
    whole = pl.BlockSpec(memory_space=pltpu.VMEM)
    return pl.pallas_call(
        functools.partial(join_kernel, plan, len(parts), theirs[0].shape[0]),
        out_shape=tuple(jax.ShapeDtypeStruct(shape, F32) for shape in shapes),
        in_specs=[whole] * (2 * len(parts)),
        out_specs=(whole,) * len(shapes),
        compiler_params=pltpu.CompilerParams(vmem_limit_bytes=VMEM_BYTES),
        cost_estimate=micros(5),
        name="join_grads",
    )(*parts, *theirs)


def last_join_kernel(plan, mine, theirs, total, *outs):
    gains, grads, start = outs[:4], outs[4:], 0
    for gain in gains:
        gain[...] = total[:, pl.ds(start, gain.shape[1])]
        start += gain.shape[1]
    y = lax.axis_index("y")
    join_pieces(plan, y, lambda _, cols: mine[:, cols], lambda _, cols: theirs[:, cols], grads)


def join_last(mine, theirs, total, plan, sizes, shapes):
    whole = pl.BlockSpec(memory_space=pltpu.VMEM)
    outs = (*((1, size) for size in sizes), *shapes)
    return pl.pallas_call(
        functools.partial(last_join_kernel, plan),
        out_shape=tuple(jax.ShapeDtypeStruct(shape, F32) for shape in outs),
        in_specs=[whole] * 3,
        out_specs=(whole,) * len(outs),
        cost_estimate=micros(4),
        name="join_last",
    )(mine, theirs, total)


def normed_rope(raw, gain, cosine, sine):
    inverse = lax.rsqrt(jnp.mean(raw * raw, -1, keepdims=True) + EPSILON)
    scaled = raw * inverse * gain
    turned = pltpu.roll(scaled, scaled.shape[-1] // 2, 1)
    return (scaled * cosine + turned * sine).astype(BF16)


def normed_rope_back(grad, raw, gain, cosine, sine):
    inverse = lax.rsqrt(jnp.mean(raw * raw, -1, keepdims=True) + EPSILON)
    straight = grad * cosine - pltpu.roll(grad, grad.shape[-1] // 2, 1) * sine
    gain_part = jnp.sum(straight * (raw * inverse), 0, keepdims=True)
    return norm_back(straight, raw, inverse, gain).astype(BF16), gain_part


def causal_scores(query, keys, first, scaling):
    scores = dot_nt(query, keys) * scaling
    rows = lax.broadcasted_iota(jnp.int32, scores.shape, 0) + first
    columns = lax.broadcasted_iota(jnp.int32, scores.shape, 1)
    return jnp.where(rows >= columns, scores, -1e30)


def attend_kernel(
    heads, head, block, normed_ref, w_ref, wg_ref, low_ref, qg_ref, kg_ref, cos_ref, sin_ref,
    raw_ref, out_ref, log_ref, gate_ref, mixed_ref, all_ref, key_ref, value_ref, *sems,
):
    seq, step, steps = pl.program_id(0), pl.program_id(1), pl.num_programs(1)
    tick = seq * steps + step
    scaling = head**-0.5
    at = heads * head
    begin, forward, across, finish = gather_steps(low_ref, all_ref, *sems)

    @pl.when(tick == 0)
    def _():
        greet(tuple(place()[3].values()))
        begin()

    pl.when(tick == 3)(forward)
    pl.when(tick == 6)(across)
    raw_ref[...] = dot_nn(normed_ref[...], w_ref[...])
    here = pl.ds(pl.multiple_of(step * block, block), block)
    cosine, sine = cos_ref[here], sin_ref[here]

    @pl.when(tick == 0)
    def _():
        key_ref[...] = jnp.zeros_like(key_ref)
        value_ref[...] = jnp.zeros_like(value_ref)

    key_ref[here] = normed_rope(raw_ref[:, at : at + head], kg_ref[...], cosine, sine)
    value_ref[here] = raw_ref[:, at + head :].astype(BF16)

    for i in range(0, key_ref.shape[0] // block, 2):

        @pl.when(step // 2 == i // 2)
        def _():
            seen = pl.ds(0, (i + 2) * block)

            @pl.loop(0, heads)
            def _(h):
                cols = pl.ds(pl.multiple_of(h * head, head), head)
                query = normed_rope(raw_ref[:, cols], qg_ref[...], cosine, sine)
                scores = causal_scores(query, key_ref[seen], step * block, scaling)
                highest = jnp.max(scores, -1, keepdims=True)
                exp_vals = jnp.exp(scores - highest)
                total = jnp.sum(exp_vals, -1, keepdims=True)
                probs = (exp_vals / total).astype(BF16)
                out_ref[:, cols] = dot_nn(probs, value_ref[seen])
                log_ref[h] = highest + jnp.log(total)

    gate = jax.nn.sigmoid(dot_nn(normed_ref[...], wg_ref[...]))
    gate_ref[...] = gate
    mixed_ref[...] = (out_ref[...] * gate).astype(BF16)
    pl.when(tick == pl.num_programs(0) * steps - 1)(finish)


def attend(normed, weights, gates, low, query_gain, key_gain, cosine, sine, heads, head, length, block=256):
    rows, width = normed.shape
    cols = weights.shape[1]
    seqs, steps = rows // length, length // block
    whole = lambda shape: pl.BlockSpec(
        shape, lambda s, i: (0,) * len(shape), pipeline_mode=pl.Buffered(1)
    )
    part = lambda cols: pl.BlockSpec((block, cols), lambda s, i: (s * steps + i, 0))
    *outs, gathered = pl.pallas_call(
        functools.partial(attend_kernel, heads, head, block),
        out_shape=(
            jax.ShapeDtypeStruct((rows, cols), F32),
            jax.ShapeDtypeStruct((rows, heads * head), F32),
            jax.ShapeDtypeStruct((heads, rows, 1), F32),
            jax.ShapeDtypeStruct((rows, heads * head), F32),
            jax.ShapeDtypeStruct((rows, heads * head), BF16),
            jax.ShapeDtypeStruct((2, 2, 2, *low.shape), low.dtype),
        ),
        grid=(seqs, steps),
        in_specs=[
            part(width),
            whole((width, cols)),
            whole((width, heads * head)),
            pl.BlockSpec(memory_space=pl.ANY),
            whole((1, head)),
            whole((1, head)),
            whole((length, head)),
            whole((length, head)),
        ],
        out_specs=(
            part(cols),
            part(heads * head),
            pl.BlockSpec((heads, block, 1), lambda s, i: (0, s * steps + i, 0)),
            part(heads * head),
            part(heads * head),
            pl.BlockSpec(memory_space=pl.ANY),
        ),
        scratch_shapes=[
            pltpu.VMEM((length, head), BF16),
            pltpu.VMEM((length, head), BF16),
            *GATHER_SEMAPHORES,
        ],
        compiler_params=pltpu.CompilerParams(collective_id=3, has_side_effects=True),
        cost_estimate=micros(42),
        name="attend",
    )(normed, weights, gates, low, query_gain, key_gain, cosine, sine)
    return *outs, gathered.reshape(rows, width)


def add_products(step, total_ref, start, left_ref, right_ref, tile=1024):
    wide = min(512, right_ref.shape[1])

    @pl.loop(0, left_ref.shape[1] // tile)
    def _(m):
        at = pl.ds(pl.multiple_of(m * tile, tile), tile)

        @pl.loop(0, right_ref.shape[1] // wide)
        def _(n):
            cols = pl.ds(pl.multiple_of(start + n * wide, wide), wide)
            part = dot_tn(left_ref[:, at], right_ref[:, pl.ds(pl.multiple_of(n * wide, wide), wide)])

            @pl.when(step == 0)
            def _():
                total_ref[at, cols] = part

            @pl.when(step > 0)
            def _():
                total_ref[at, cols] += part


def store_low(step, total_ref, out_ref, tile=256):
    @pl.when(step == pl.num_programs(0) - 1)
    def _():
        @pl.loop(0, total_ref.shape[0] // tile)
        def _(m):
            at = pl.ds(m * tile, tile)
            out_ref[at] = total_ref[at].astype(BF16)


def grads_kernel(left_ref, right_ref, out_ref, total_ref):
    step = pl.program_id(0)
    add_products(step, total_ref, 0, left_ref, right_ref)
    store_low(step, total_ref, out_ref)


def weight_grads(left, right, block=1024):
    (rows, width), cols = left.shape, right.shape[1]
    part = lambda cols: pl.BlockSpec((block, cols), lambda i: (i, 0))
    return pl.pallas_call(
        grads_kernel,
        out_shape=jax.ShapeDtypeStruct((width, cols), BF16),
        grid=(rows // block,),
        in_specs=[part(width), part(cols)],
        out_specs=pl.BlockSpec((width, cols), lambda i: (0, 0)),
        scratch_shapes=[pltpu.VMEM((width, cols), F32)],
        cost_estimate=micros(11),
        name="weight_grads",
    )(left, right)


def gate_back_kernel(
    normed_ref, branch_ref, w_ref, attended_ref, gate_ref, mixed_ref,
    dattended_ref, dgating_ref, grad_ref, total_ref,
):
    step = pl.program_id(0)
    dmixed = dot_nn(branch_ref[...], w_ref[...])
    gate = gate_ref[...]
    dattended_ref[...] = (dmixed * gate).astype(BF16)
    dgating_ref[...] = (dmixed * attended_ref[...] * gate * (1.0 - gate)).astype(BF16)
    add_products(step, total_ref, 0, normed_ref, dgating_ref)
    add_products(step, total_ref, dgating_ref.shape[1], branch_ref, mixed_ref)
    store_low(step, total_ref, grad_ref)


def gate_back(normed, branch, weights, attended, gate, mixed, block=1024):
    rows, width = normed.shape
    cols = attended.shape[1]
    part = lambda cols: pl.BlockSpec((block, cols), lambda i: (i, 0))
    return pl.pallas_call(
        gate_back_kernel,
        out_shape=(
            jax.ShapeDtypeStruct((rows, cols), BF16),
            jax.ShapeDtypeStruct((rows, cols), BF16),
            jax.ShapeDtypeStruct((width, 2 * cols), BF16),
        ),
        grid=(rows // block,),
        in_specs=[
            part(width),
            part(width),
            pl.BlockSpec((width, cols), lambda i: (0, 1)),
            part(cols),
            part(cols),
            part(cols),
        ],
        out_specs=(part(cols), part(cols), pl.BlockSpec((width, 2 * cols), lambda i: (0, 0))),
        scratch_shapes=[pltpu.VMEM((width, 2 * cols), F32)],
        compiler_params=pltpu.CompilerParams(vmem_limit_bytes=VMEM_BYTES),
        cost_estimate=micros(25),
        name="gate_back",
    )(normed, branch, weights, attended, gate, mixed)


def feed_units(count, tile, mid_ref, low_ref, gu_ref, down_ref, first, act_ref, dgu_ref):
    @pl.loop(0, count // tile)
    def _(j):
        start = pl.multiple_of(j * tile, tile)
        at, after = pl.ds(start, tile), pl.ds(pl.multiple_of(count + start, tile), tile)
        last = pl.ds(pl.multiple_of(first + start, tile), tile)
        gate = dot_nn(mid_ref[...], gu_ref[:, at])
        up = dot_nn(mid_ref[...], gu_ref[:, after])
        dact = dot_nn(low_ref[...], down_ref[:, last])
        sigma = jax.nn.sigmoid(gate)
        silu = gate * sigma
        act_ref[:, at] = (silu * up).astype(BF16)
        dgu_ref[:, at] = (dact * up * sigma * (1.0 + gate * (1.0 - sigma))).astype(BF16)
        dgu_ref[:, after] = (dact * silu).astype(BF16)


def feed_kernel(count, tile, mid_ref, low_ref, gu_ref, down_ref, act_ref, dgu_ref):
    feed_units(count, tile, mid_ref, low_ref, gu_ref, down_ref, 0, act_ref, dgu_ref)


def feed_grads_kernel(
    count, tile, mid_ref, low_ref, w_ref, act_ref, dgu_ref, grad_ref, total_ref
):
    step = pl.program_id(0)
    feed_units(count, tile, mid_ref, low_ref, w_ref, w_ref, 2 * count, act_ref, dgu_ref)
    add_products(step, total_ref, 0, mid_ref, dgu_ref)
    add_products(step, total_ref, 2 * count, low_ref, act_ref)
    store_low(step, total_ref, grad_ref)


def feed_forward(mid, low, weights, down, block=256):
    rows, width = mid.shape
    count = down.shape[1]
    part = lambda cols: pl.BlockSpec((block, cols), lambda i: (i, 0))
    whole = lambda array: pl.BlockSpec(array.shape, lambda i: (0, 0), pipeline_mode=pl.Buffered(1))
    return pl.pallas_call(
        functools.partial(feed_kernel, count, 256),
        out_shape=(
            jax.ShapeDtypeStruct((rows, count), BF16),
            jax.ShapeDtypeStruct((rows, 2 * count), BF16),
        ),
        grid=(rows // block,),
        in_specs=[part(width), part(width), whole(weights), whole(down)],
        out_specs=(part(count), part(2 * count)),
        compiler_params=pltpu.CompilerParams(vmem_limit_bytes=VMEM_BYTES),
        cost_estimate=micros(14),
        name="feed_forward",
    )(mid, low, weights, down)


def feed_forward_grads(mid, low, weights, block=1024):
    rows, width = mid.shape
    count = weights.shape[1] // 3
    part = lambda cols: pl.BlockSpec((block, cols), lambda i: (i, 0))
    whole = pl.BlockSpec(weights.shape, lambda i: (0, 0), pipeline_mode=pl.Buffered(1))
    return pl.pallas_call(
        functools.partial(feed_grads_kernel, count, 256),
        out_shape=(
            jax.ShapeDtypeStruct((rows, count), BF16),
            jax.ShapeDtypeStruct((rows, 2 * count), BF16),
            jax.ShapeDtypeStruct(weights.shape, BF16),
        ),
        grid=(rows // block,),
        in_specs=[part(width), part(width), whole],
        out_specs=(part(count), part(2 * count), whole),
        scratch_shapes=[pltpu.VMEM(weights.shape, F32)],
        compiler_params=pltpu.CompilerParams(vmem_limit_bytes=VMEM_BYTES),
        cost_estimate=micros(41),
        name="feed_forward_grads",
    )(mid, low, weights)


def attend_back_kernel(
    heads, head, block, raw_ref, up_ref, log_ref, qg_ref, kg_ref, cos_ref, sin_ref, sums_ref,
    out_ref, qg_out, kg_out, sum_ref, key_ref, value_ref, dkey_ref, dvalue_ref, own, load_sem, *scratch,
):
    seq, step, steps = pl.program_id(0), pl.program_id(1), pl.num_programs(1)
    tick = seq * steps + step
    scaling = head**-0.5
    at = heads * head
    blocks = raw_ref.shape[0] // block
    diag_x, diag_y, x_low, y_high, second, finish = axis_steps(own, *scratch)

    @pl.when(tick == 0)
    def _():
        load = pltpu.make_async_copy(sums_ref, own, load_sem)
        load.start()
        device = place()[3]
        greet((device["y"], device["x"]))
        load.wait()
        for copy in (diag_x, diag_y, x_low, y_high):
            copy.start()
        qg_out[...] = jnp.zeros_like(qg_out)
        kg_out[...] = jnp.zeros_like(kg_out)

    pl.when(tick == 4)(second)

    @pl.when(step == 0)
    def _():
        key_ref[...] = normed_rope(
            raw_ref[:, at : at + head], kg_ref[...], cos_ref[...], sin_ref[...]
        )
        value_ref[...] = raw_ref[:, at + head :].astype(BF16)
        dkey_ref[...] = jnp.zeros_like(dkey_ref)
        dvalue_ref[...] = jnp.zeros_like(dvalue_ref)

    rows = pl.ds(pl.multiple_of(step * block, block), block)

    for i in range(0, blocks, 2):

        @pl.when(step // 2 == i // 2)
        def _():
            seen = pl.ds(0, (i + 2) * block)

            @pl.loop(0, heads)
            def _(h):
                cols = pl.ds(pl.multiple_of(h * head, head), head)
                raw = raw_ref[rows, cols]
                query = normed_rope(raw, qg_ref[...], cos_ref[rows], sin_ref[rows])
                scores = causal_scores(query, key_ref[seen], step * block, scaling)
                probs = jnp.exp(scores - log_ref[h])
                upstream = up_ref[:, cols]
                dprobs = dot_nt(upstream, value_ref[seen])
                centre = jnp.sum(dprobs * probs, -1, keepdims=True)
                dscores = (probs * (dprobs - centre)).astype(BF16)
                dkey_ref[seen] += dot_tn(dscores, query)
                dvalue_ref[seen] += dot_tn(probs.astype(BF16), upstream)
                dquery = dot_nn(dscores, key_ref[seen]) * scaling
                grad, part = normed_rope_back(
                    dquery, raw, qg_ref[...], cos_ref[rows], sin_ref[rows]
                )
                out_ref[rows, cols] = grad
                qg_out[...] += part

    @pl.when(step == blocks - 1)
    def _():
        grad, part = normed_rope_back(
            dkey_ref[...] * scaling,
            raw_ref[:, at : at + head],
            kg_ref[...],
            cos_ref[...],
            sin_ref[...],
        )
        out_ref[:, at : at + head] = grad
        out_ref[:, at + head :] = dvalue_ref[...].astype(BF16)
        kg_out[...] += part

    @pl.when(tick == pl.num_programs(0) * steps - 1)
    def _():
        def store(rows, value):
            sum_ref[rows] = value

        finish(store)


def attend_back(
    raw, upstream, logs, query_gain, key_gain, cosine, sine, sums, heads, head, length, block=256
):
    rows = raw.shape[0]
    total = jax.ShapeDtypeStruct(sums.shape[1:], F32)
    seqs, steps = rows // length, length // block
    whole = lambda shape: pl.BlockSpec(shape, lambda s, i: (0,) * len(shape))
    return pl.pallas_call(
        functools.partial(attend_back_kernel, heads, head, block),
        out_shape=(
            jax.ShapeDtypeStruct(raw.shape, BF16),
            jax.ShapeDtypeStruct((1, head), F32),
            jax.ShapeDtypeStruct((1, head), F32),
            total,
        ),
        grid=(seqs, steps),
        in_specs=[
            pl.BlockSpec((length, raw.shape[1]), lambda s, i: (s, 0)),
            pl.BlockSpec((block, heads * head), lambda s, i: (s * steps + i, 0)),
            pl.BlockSpec((heads, block, 1), lambda s, i: (0, s * steps + i, 0)),
            whole((1, head)),
            whole((1, head)),
            whole((length, head)),
            whole((length, head)),
            pl.BlockSpec(memory_space=pl.ANY),
        ],
        out_specs=(
            pl.BlockSpec((length, raw.shape[1]), lambda s, i: (s, 0)),
            whole((1, head)),
            whole((1, head)),
            whole(total.shape),
        ),
        scratch_shapes=[
            pltpu.VMEM((length, head), BF16),
            pltpu.VMEM((length, head), BF16),
            pltpu.VMEM((length, head), F32),
            pltpu.VMEM((length, head), F32),
            pltpu.VMEM(sums.shape, BF16),
            pltpu.SemaphoreType.DMA,
            *axis_scratch(*sums.shape[1:]),
        ],
        compiler_params=pltpu.CompilerParams(
            collective_id=5, has_side_effects=True, vmem_limit_bytes=VMEM_BYTES
        ),
        cost_estimate=micros(40),
        name="attend_back",
    )(raw, upstream, logs, query_gain, key_gain, cosine, sine, sums)


def attention_weights(query_proj, key_proj, value_proj, gating_proj, output_proj):
    return (
        lax.all_gather(query_proj, "dp", axis=0, tiled=True),
        lax.all_gather(key_proj, "dp", axis=0, tiled=True),
        lax.all_gather(value_proj, "dp", axis=0, tiled=True),
        lax.all_gather(gating_proj, "dp", axis=0, tiled=True),
        lax.all_gather(output_proj, "dp", axis=1, tiled=True),
    )


def swiglu_weights(swiglu_gate, swiglu_up, swiglu_down):
    return (
        lax.all_gather(swiglu_gate, "dp", axis=0, tiled=True),
        lax.all_gather(swiglu_up, "dp", axis=0, tiled=True),
        lax.all_gather(swiglu_down, "dp", axis=1, tiled=True),
    )


def softmax_forward_mapped(seq_items, causal):
    queries, keys_seq, values_seq = seq_items
    scaling = queries.shape[-1] ** (-0.5)
    scores = (
        jnp.einsum("qgjd,kgd->gjqk", queries, keys_seq, preferred_element_type=jnp.float32)
        * scaling
    )
    scores = jnp.where(causal, scores, -1e30)
    highest = jnp.max(scores, -1, keepdims=True)
    exp_vals = jnp.exp(scores - highest)
    row_totals = jnp.sum(exp_vals, -1, keepdims=True)
    attn_probs = (exp_vals / row_totals).astype(jnp.bfloat16)
    attended = jnp.einsum(
        "gjqk,kgd->qgjd", attn_probs, values_seq, preferred_element_type=jnp.float32
    )
    return (attended, highest[..., 0] + jnp.log(row_totals[..., 0]))


def softmax_backward_mapped(seq_items, causal):
    queries, keys_seq, values_seq, log_total, upstream = seq_items
    scaling = queries.shape[-1] ** (-0.5)
    scores = (
        jnp.einsum("qgjd,kgd->gjqk", queries, keys_seq, preferred_element_type=jnp.float32)
        * scaling
    )
    scores = jnp.where(causal, scores, -1e30)
    attn_probs = jnp.exp(scores - log_total[..., None])
    dprobs = jnp.einsum("qgjd,kgd->gjqk", upstream, values_seq, preferred_element_type=jnp.float32)
    centre = jnp.sum(dprobs * attn_probs, -1, keepdims=True)
    dscores = (attn_probs * (dprobs - centre)).astype(jnp.bfloat16)
    dqueries = (
        jnp.einsum("gjqk,kgd->qgjd", dscores, keys_seq, preferred_element_type=jnp.float32)
        * scaling
    )
    key_grads = (
        jnp.einsum("gjqk,qgjd->kgd", dscores, queries, preferred_element_type=jnp.float32) * scaling
    )
    value_grads = jnp.einsum(
        "gjqk,qgjd->kgd",
        attn_probs.astype(jnp.bfloat16),
        upstream,
        preferred_element_type=jnp.float32,
    )
    key_rows = key_grads.shape[0]
    return (dqueries, key_grads.reshape(key_rows, -1), value_grads.reshape(key_rows, -1))


def per_device_wide(
    tokens,
    cotangent,
    domain_ids,
    domain_counts,
    domain_numer,
    domain_denom,
    attention_gain,
    query_gain,
    key_gain,
    query_proj,
    key_proj,
    value_proj,
    gating_proj,
    output_proj,
    swiglu_gain,
    swiglu_gate,
    swiglu_up,
    swiglu_down,
):
    seq_count, local_len, model_width = tokens.shape
    full_len = local_len * lax.axis_size("ctx")
    local_rows = seq_count * local_len
    all_rows = seq_count * full_len
    head_dim = query_gain.shape[0]
    local_heads = query_proj.shape[1] // head_dim
    local_kv = key_proj.shape[1] // head_dim
    group_size = local_heads // local_kv
    positions = jnp.arange(full_len, dtype=jnp.int32)
    causal = positions[:, None] >= positions[None, :]
    cosine, sine = rope_tables(positions, head_dim)
    cos_rows = cosine[:, None, :]
    sin_rows = sine[:, None, :]
    inputs = tokens.reshape(local_rows, model_width).astype(jnp.float32)
    inverse_in = lax.rsqrt(jnp.mean(inputs * inputs, -1, keepdims=True) + EPSILON)
    gain_in = attention_gain.astype(jnp.float32)
    normed = (inputs * inverse_in * gain_in).astype(jnp.bfloat16)
    normed_all = lax.all_gather(
        normed.reshape(seq_count, local_len, model_width), "ctx", axis=1, tiled=True
    ).reshape(all_rows, model_width)
    attn_full = attention_weights(query_proj, key_proj, value_proj, gating_proj, output_proj)
    query_raw = dot_nn(normed_all, attn_full[0]).reshape(
        seq_count, full_len, local_heads, head_dim
    )
    key_raw = dot_nn(normed_all, attn_full[1]).reshape(seq_count, full_len, local_kv, head_dim)
    value_low = (
        dot_nn(normed_all, attn_full[2])
        .astype(jnp.bfloat16)
        .reshape(seq_count, full_len, local_kv, head_dim)
    )
    gate_pre = dot_nn(normed_all, attn_full[3])
    query_scale = query_gain.astype(jnp.float32)
    key_scale = key_gain.astype(jnp.float32)
    query_inv = lax.rsqrt(jnp.mean(query_raw * query_raw, -1, keepdims=True) + EPSILON)
    key_inv = lax.rsqrt(jnp.mean(key_raw * key_raw, -1, keepdims=True) + EPSILON)
    query_low = rotate(query_raw * query_inv * query_scale, cos_rows, sin_rows).astype(jnp.bfloat16)
    key_low = rotate(key_raw * key_inv * key_scale, cos_rows, sin_rows).astype(jnp.bfloat16)
    query_groups = query_low.reshape(seq_count, full_len, local_kv, group_size, head_dim)
    attended, log_total = lax.map(
        lambda seq_items: softmax_forward_mapped(seq_items, causal), (query_groups, key_low, value_low)
    )
    attended = attended.reshape(all_rows, local_heads * head_dim)
    gate_sig = jax.nn.sigmoid(gate_pre)
    mixed = (attended * gate_sig).astype(jnp.bfloat16)
    branch_part = dot_nn(mixed, attn_full[4]).reshape(seq_count, full_len, model_width)
    branch = lax.psum_scatter(branch_part, "ctx", scatter_dimension=1, tiled=True).reshape(
        local_rows, model_width
    )
    hidden = inputs + branch
    inverse_mid = lax.rsqrt(jnp.mean(hidden * hidden, -1, keepdims=True) + EPSILON)
    gain_mid = swiglu_gain.astype(jnp.float32)
    normed_mid = (hidden * inverse_mid * gain_mid).astype(jnp.bfloat16)
    normed_mid_all = lax.all_gather(
        normed_mid.reshape(seq_count, local_len, model_width), "ctx", axis=1, tiled=True
    ).reshape(all_rows, model_width)
    swiglu_full = swiglu_weights(swiglu_gate, swiglu_up, swiglu_down)
    gate_ff = dot_nn(normed_mid_all, swiglu_full[0])
    up_val = dot_nn(normed_mid_all, swiglu_full[1])
    gate_sigma = jax.nn.sigmoid(gate_ff)
    silu_val = gate_ff * gate_sigma
    activation = (silu_val * up_val).astype(jnp.bfloat16)
    down_part = dot_nn(activation, swiglu_full[2]).reshape(seq_count, full_len, model_width)
    ffn_branch = (
        lax.psum_scatter(down_part.astype(jnp.bfloat16), "ctx", scatter_dimension=1, tiled=True)
        .astype(jnp.float32)
        .reshape(local_rows, model_width)
    )
    layer_out = (hidden + ffn_branch).astype(jnp.bfloat16)
    domain_table = (
        domain_ids[:, None] == jnp.arange(domain_counts.shape[0], dtype=jnp.int32)[None, :]
    ).astype(jnp.float32)
    ratio = (
        domain_numer.astype(jnp.float32)
        / domain_denom.astype(jnp.float32)
        * LENGTH
        / domain_counts.astype(jnp.float32)
    )
    factor = jnp.sum(domain_table * ratio[None, :], 1)
    upstream = (cotangent.astype(jnp.float32) * factor[:, None, None]).reshape(
        local_rows, model_width
    )
    swiglu_back = swiglu_weights(swiglu_gate, swiglu_up, swiglu_down)
    out_low = upstream.astype(jnp.bfloat16)
    out_all = lax.all_gather(
        out_low.reshape(seq_count, local_len, model_width), "ctx", axis=1, tiled=True
    ).reshape(all_rows, model_width)
    dactivation = dot_nt(out_all, swiglu_back[2])
    dgate_low = (dactivation * up_val * gate_sigma * (1.0 + gate_ff * (1.0 - gate_sigma))).astype(
        jnp.bfloat16
    )
    dup_low = (dactivation * silu_val).astype(jnp.bfloat16)
    grad_down = dot_tn(activation, out_all)
    grad_gate = dot_tn(normed_mid_all, dgate_low)
    grad_up = dot_tn(normed_mid_all, dup_low)
    dmid_part = dot_nt(dgate_low, swiglu_back[0]) + dot_nt(dup_low, swiglu_back[1])
    dnormed_mid = lax.psum_scatter(
        dmid_part.reshape(seq_count, full_len, model_width), "ctx", scatter_dimension=1, tiled=True
    ).reshape(local_rows, model_width)
    grad_gain_mid = jnp.sum(dnormed_mid * hidden * inverse_mid, 0)
    dhidden = upstream + norm_back(dnormed_mid, hidden, inverse_mid, gain_mid)
    swiglu_grads = (
        lax.psum_scatter(
            grad_gate.astype(jnp.bfloat16), "dp", scatter_dimension=0, tiled=True
        ).astype(jnp.float32),
        lax.psum_scatter(
            grad_up.astype(jnp.bfloat16), "dp", scatter_dimension=0, tiled=True
        ).astype(jnp.float32),
        lax.psum_scatter(
            grad_down.astype(jnp.bfloat16), "dp", scatter_dimension=1, tiled=True
        ).astype(jnp.float32),
    )
    attn_back = attention_weights(query_proj, key_proj, value_proj, gating_proj, output_proj)
    dbranch_low = dhidden.astype(jnp.bfloat16)
    dbranch_all = lax.all_gather(
        dbranch_low.reshape(seq_count, local_len, model_width), "ctx", axis=1, tiled=True
    ).reshape(all_rows, model_width)
    grad_output = dot_tn(mixed, dbranch_all)
    dmixed = dot_nt(dbranch_all, attn_back[4])
    dattended_low = (dmixed * gate_sig).astype(jnp.bfloat16)
    dgating_low = (dmixed * attended * gate_sig * (1.0 - gate_sig)).astype(jnp.bfloat16)
    upstream_heads = dattended_low.reshape(seq_count, full_len, local_kv, group_size, head_dim)
    dquery_rot, dkey_rot, dvalue_sum = lax.map(
        lambda seq_items: softmax_backward_mapped(seq_items, causal),
        (query_groups, key_low, value_low, log_total, upstream_heads),
    )
    dvalue_low = dvalue_sum.reshape(all_rows, local_kv * head_dim).astype(jnp.bfloat16)
    dquery_normed = unrotate(
        dquery_rot.reshape(seq_count, full_len, local_heads, head_dim), cos_rows, sin_rows
    )
    dkey_normed = unrotate(
        dkey_rot.reshape(seq_count, full_len, local_kv, head_dim), cos_rows, sin_rows
    )
    grad_query_gain = jnp.sum(dquery_normed * query_raw * query_inv, (0, 1, 2))
    grad_key_gain = jnp.sum(dkey_normed * key_raw * key_inv, (0, 1, 2))
    dquery_low = (
        norm_back(dquery_normed, query_raw, query_inv, query_scale)
        .reshape(all_rows, -1)
        .astype(jnp.bfloat16)
    )
    dkey_low = (
        norm_back(dkey_normed, key_raw, key_inv, key_scale)
        .reshape(all_rows, -1)
        .astype(jnp.bfloat16)
    )
    dnormed_part = (
        dot_nt(dquery_low, attn_back[0])
        + dot_nt(dkey_low, attn_back[1])
        + dot_nt(dvalue_low, attn_back[2])
        + dot_nt(dgating_low, attn_back[3])
    )
    dnormed = (
        lax.psum_scatter(
            dnormed_part.reshape(seq_count, full_len, model_width).astype(jnp.bfloat16),
            "ctx",
            scatter_dimension=1,
            tiled=True,
        )
        .astype(jnp.float32)
        .reshape(local_rows, model_width)
    )
    grad_gain_in = jnp.sum(dnormed * inputs * inverse_in, 0)
    input_grad = (dhidden + norm_back(dnormed, inputs, inverse_in, gain_in)).astype(jnp.bfloat16)
    grad_query = dot_tn(normed_all, dquery_low)
    grad_key = dot_tn(normed_all, dkey_low)
    grad_value = dot_tn(normed_all, dvalue_low)
    grad_gating = dot_tn(normed_all, dgating_low)
    attention_grads = (
        lax.psum_scatter(
            grad_query.astype(jnp.bfloat16), "dp", scatter_dimension=0, tiled=True
        ).astype(jnp.float32),
        lax.psum_scatter(
            grad_key.astype(jnp.bfloat16), "dp", scatter_dimension=0, tiled=True
        ).astype(jnp.float32),
        lax.psum_scatter(
            grad_value.astype(jnp.bfloat16), "dp", scatter_dimension=0, tiled=True
        ).astype(jnp.float32),
        lax.psum_scatter(
            grad_gating.astype(jnp.bfloat16), "dp", scatter_dimension=0, tiled=True
        ).astype(jnp.float32),
        lax.psum_scatter(
            grad_output.astype(jnp.bfloat16), "dp", scatter_dimension=1, tiled=True
        ).astype(jnp.float32),
    )
    gain_grads = lax.psum(
        (grad_gain_in, grad_gain_mid, grad_query_gain, grad_key_gain), ("dp", "ctx")
    )
    return (
        layer_out.reshape(seq_count, local_len, model_width),
        input_grad.reshape(seq_count, local_len, model_width),
        gain_grads[0],
        gain_grads[2],
        gain_grads[3],
        attention_grads[0],
        attention_grads[1],
        attention_grads[2],
        attention_grads[3],
        attention_grads[4],
        gain_grads[1],
        swiglu_grads[0],
        swiglu_grads[1],
        swiglu_grads[2],
    )


def per_device(
    tokens,
    cotangent,
    domain_ids,
    domain_counts,
    domain_numer,
    domain_denom,
    attention_gain,
    query_gain,
    key_gain,
    query_proj,
    key_proj,
    value_proj,
    gating_proj,
    output_proj,
    swiglu_gain,
    swiglu_gate,
    swiglu_up,
    swiglu_down,
):
    seq_count, local_len, width = tokens.shape
    rows = seq_count * local_len
    full_len = local_len * lax.axis_size("x") * lax.axis_size("c")
    seqs = seq_count * lax.axis_size("y")
    head = query_gain.shape[0]
    kv_cols = key_proj.shape[1] // 2
    q_cols = query_proj.shape[1] // 2
    ff_cols = swiglu_gate.shape[1] // 2
    heads = q_cols // head
    split, rest = ff_cols * 2 // 3, ff_cols - ff_cols * 2 // 3
    tokens, cotangent = tokens.reshape(rows, width), cotangent.reshape(rows, width)
    (
        normed_all, w_qkv, w_go, rows_first, rows_gu, rows_d, inverse_in, out_low, factor, cos_rows, sin_rows,
    ) = opening(
        tokens,
        cotangent,
        attention_gain,
        (domain_ids, domain_counts, domain_numer, domain_denom),
        (
            query_proj, key_proj, value_proj, gating_proj, output_proj, swiglu_gate, swiglu_up, swiglu_down,
        ),
        split,
        full_len,
        head,
    )
    w_first = gather_rows(rows_first)
    w_last_gu = gather_rows(rows_gu)

    query_scale, key_scale = query_gain.astype(F32)[None], key_gain.astype(F32)[None]
    qkv, attended, logs, gate_sig, mixed, out_all = attend(
        normed_all, w_qkv, w_go, out_low, query_scale, key_scale, cos_rows, sin_rows, heads, head, full_len
    )
    wide, column = jax.ShapeDtypeStruct((rows, width), F32), jax.ShapeDtypeStruct((rows, 1), F32)
    low = jax.ShapeDtypeStruct((rows, width), BF16)
    gain_mid = swiglu_gain.reshape(1, -1)
    hidden, inverse_mid, normed_mid = scatter_products(
        middle_kernel, 7, (tokens, gain_mid), (wide, column, low), (mixed, w_go, q_cols)
    )
    mid_all, w_last_d = gather_tokens(normed_mid, rows_d)

    act_first, dgu_first, grad_first = feed_forward_grads(mid_all, out_all, w_first)
    part_first = scatter_grads(grad_first)
    w_last_gu, grad_first = lax.optimization_barrier((w_last_gu, grad_first))
    act_last, dgu_last = feed_forward(mid_all, out_all, w_last_gu, w_last_d)
    dhidden, dbranch, grad_gain_mid = scatter_products(
        middle_back_kernel,
        8,
        (hidden, inverse_mid, gain_mid, cotangent, factor),
        (wide, low, jax.ShapeDtypeStruct((1, width), F32)),
        (dgu_first, w_first, 0),
        (dgu_last, w_last_gu, 0),
    )
    dbranch_all, ffn_sums, grad_last = gather_beside(
        dbranch,
        ((act_first, w_first, 2 * split), (act_last, w_last_d, 0)),
        mid_all,
        out_all,
        dgu_last,
        act_last,
    )
    part_last = scatter_grads(grad_last)
    dbranch_all, part_first = lax.optimization_barrier((dbranch_all, part_first))

    theirs_first = their_rows(part_first)
    dattended, dgating, grad_go = gate_back(
        normed_all, dbranch_all, w_go, attended, gate_sig, mixed
    )
    dattended, theirs_first, grad_go = lax.optimization_barrier((dattended, theirs_first, grad_go))
    part_go = scatter_grads(grad_go)
    dqkv, grad_query_gain, grad_key_gain, ffn_branch = attend_back(
        qkv, dattended, logs, query_scale, key_scale, cos_rows, sin_rows, ffn_sums, heads, head, full_len
    )
    grad_query_gain, grad_key_gain = grad_query_gain[0], grad_key_gain[0]
    dqkv, part_last = lax.optimization_barrier((dqkv, part_last))
    theirs_last = their_rows(part_last)
    layer_out = (hidden + ffn_branch).astype(BF16)
    dqkv, layer_out = lax.optimization_barrier((dqkv, layer_out))
    grad_qkv = weight_grads(normed_all, dqkv)
    grad_qkv, theirs_last = lax.optimization_barrier((grad_qkv, theirs_last))
    plan = [(0, i * split, split, i, 0, i == 2) for i in range(3)]
    plan += [(1, i * rest, rest, i, split, i == 2) for i in range(3)]
    grad_gate, grad_up, grad_down = join_grads(
        (part_first, part_last),
        (theirs_first, theirs_last),
        plan,
        [weight.shape for weight in (swiglu_gate, swiglu_up, swiglu_down)],
    )
    grad_qkv, layer_out, grad_gate, grad_up, grad_down = lax.optimization_barrier(
        (grad_qkv, layer_out, grad_gate, grad_up, grad_down)
    )
    input_grad, mine_qkv, theirs_qkv, totals = tail(
        ((dqkv, w_qkv, 0), (dgating, w_go, 0)),
        grad_qkv,
        tokens,
        inverse_in,
        dhidden,
        attention_gain,
        (grad_gain_mid, grad_query_gain, grad_key_gain),
    )
    input_grad, part_go = lax.optimization_barrier((input_grad, part_go))
    theirs_go = their_rows(part_go)
    grad_gating, grad_output = join_grads(
        (part_go,),
        (theirs_go,),
        [(0, 0, q_cols, 0, 0, False), (0, q_cols, q_cols, 1, 0, True)],
        (gating_proj.shape, output_proj.shape),
    )
    widths, starts = (q_cols, kv_cols, kv_cols), (0, q_cols, q_cols + kv_cols)
    *gain_grads, grad_query, grad_key, grad_value = join_last(
        mine_qkv,
        theirs_qkv,
        totals,
        [(0, starts[i], widths[i], i, 0, False) for i in range(3)],
        (width, width, head, head),
        [weight.shape for weight in (query_proj, key_proj, value_proj)],
    )
    gain_grads = [gain.reshape(-1) for gain in gain_grads]
    shape = (seq_count, local_len, width)
    return (
        layer_out.reshape(shape),
        input_grad.reshape(shape),
        gain_grads[0],
        gain_grads[2],
        gain_grads[3],
        grad_query,
        grad_key,
        grad_value,
        grad_gating,
        grad_output,
        gain_grads[1],
        grad_gate,
        grad_up,
        grad_down,
    )


def solution(mesh):
    if (mesh.shape["dp"], mesh.shape["ctx"]) == (8, 4):
        body = per_device
        mesh = Mesh(mesh.devices.reshape(4, 2, 2, 2), ("z", "y", "x", "c"))
        dp, ctx = ("z", "y"), ("x", "c")
    else:
        body = per_device_wide
        dp, ctx = "dp", "ctx"
    tokens, weight, turned = P(dp, ctx, None), P(dp, ctx), P(ctx, dp)
    return jax.shard_map(
        body,
        mesh=mesh,
        in_specs=(tokens, tokens, P(dp), *[P()] * 6, *[weight] * 4, turned, P(), weight, weight, turned),
        out_specs=(tokens, tokens, *[P()] * 3, *[weight] * 4, turned, P(), weight, weight, turned),
        check_vma=False,
    )
```
